128 devices in a mesh: fsdp: 32 (over x, z_lo, y), tok: 4 (over z_hi, core).
Axes of the slice: x: 4, y: 4, z: 4 (z_hi: 2, z_lo: 2; z = z_hi * 2 + z_lo), core: 2. Of those that a mesh axis runs over, the one named last changes fastest.
Arguments:
- tokens: bfloat16 [64, 256, 2048], P('fsdp', 'tok'), may hold values from -6 to 6
- cotangent: bfloat16 [64, 256, 2048], P('fsdp', 'tok'), may hold values from -6 to 6
- segments: int32 [64, 256], P('fsdp'), may hold values from 0 to 7, never falling along the last dimension, each value on 1 to 128 neighbouring positions
- adapter_id: int32 [64], P('fsdp'), may hold values from 0 to 7
- w_qkv: bfloat16 [3, 2048, 2048], P(None, 'fsdp', 'tok'), may hold values from -0.125 to 0.125
- w_out: bfloat16 [2048, 2048], P('tok', 'fsdp'), may hold values from -0.125 to 0.125
- w_gateup: bfloat16 [2, 2048, 5632], P(None, 'fsdp', 'tok'), may hold values from -0.125 to 0.125
- w_down: bfloat16 [5632, 2048], P('tok', 'fsdp'), may hold values from -0.078125 to 0.078125
- gain_attn: float32 [2048], replicated, may hold values from 0.5 to 1.5
- gain_ffn: float32 [2048], replicated, may hold values from 0.5 to 1.5
- gain_sub: float32 [256], replicated, may hold values from 0.5 to 1.5
- lambda_head: float32 [8], replicated, may hold values from 0.2 to 0.7
- a_in: bfloat16 [5, 2048, 128], P(None, ('fsdp', 'tok')), may hold values from -0.125 to 0.125
- b_qkv: bfloat16 [3, 128, 2048], P(None, 'fsdp', 'tok'), may hold values from -0.75 to 0.75
- b_gateup: bfloat16 [2, 128, 5632], P(None, 'fsdp', 'tok'), may hold values from -0.75 to 0.75
- a_out: bfloat16 [2048, 128], P('tok', 'fsdp'), may hold values from -0.125 to 0.125
- a_down: bfloat16 [5632, 128], P('tok', 'fsdp'), may hold values from -0.078125 to 0.078125
- b_rows: bfloat16 [2, 128, 2048], P(None, None, ('fsdp', 'tok')), may hold values from -0.75 to 0.75
Outputs:
- output: bfloat16 [64, 256, 2048], P('fsdp', 'tok')
- grad_tokens: float32 [64, 256, 2048], P('fsdp', 'tok')
- grad_a_in: float32 [5, 2048, 128], P(None, ('fsdp', 'tok'))
- grad_b_qkv: float32 [3, 128, 2048], P(None, 'fsdp', 'tok')
- grad_b_gateup: float32 [2, 128, 5632], P(None, 'fsdp', 'tok')
- grad_a_out: float32 [2048, 128], P('tok', 'fsdp')
- grad_a_down: float32 [5632, 128], P('tok', 'fsdp')
- grad_b_rows: float32 [2, 128, 2048], P(None, None, ('fsdp', 'tok'))
The draws below stay inside these ranges and needn't reach their ends.
Inputs may be any that keep to these rules, and one draw needn't show every extreme that they name: `segments`: segment numbers never fall along a sequence; a document holds at most 128 tokens.
All inputs are finite; a program needn't handle non-finite values.
Results may differ from the reference program's by a relative error of at most 0.02.
The reference program's roundings to bfloat16 on the way count: a program that leaves them out, or rounds other values in their place, can miss the bound.
Values may be sent and summed in bfloat16 or wider, within the bound.
No kernel may reach another device: no remote copies, remote signals or barrier semaphores. Data moves between devices by JAX's collectives and lax.ppermute only.
A program may use at most 192 MiB of HBM per device.

```python
import math
import jax
import jax.numpy as jnp
import numpy as np
from jax import lax

D = 2048
HEADS = 8
HEAD_DIM = 128
VALUE_DIM = 256
FF = 5632
RANK = 16
ADAPTERS = 8
LEN = 256
QW = 2048
COLS = 128
SEQS = 64


def plant(values, stream_key, smallest, high):
    dims = values.shape
    spot = [jax.random.randint(jax.random.fold_in(stream_key, axis), (), 0, dims[axis]) for axis in range(len(dims))]
    values = values.at[tuple(spot)].set(smallest)
    longest = dims.index(max(dims))
    spot[longest] = (spot[longest] + 1) % dims[longest]
    return values.at[tuple(spot)].set(high)


def shard_levels(key, extent, pieces, low, largest):
    def one(position, shards_of):
        heights = jax.random.uniform(jax.random.fold_in(jax.random.fold_in(key, 6), position), (shards_of,), jnp.float32, low / len(pieces), largest / len(pieces))
        return jnp.repeat(jnp.exp(heights), extent[position] // shards_of).reshape((-1,) + (1,) * (len(extent) - position - 1))

    gain = one(*pieces[0])
    for cut in pieces[1:]:
        gain = gain * one(*cut)
    return gain


def profile(count, total, reach, skew):
    loads = [(1 << 20) // math.isqrt(standing ** skew) + 1 for standing in range(2, count + 1)]
    surplus, counts = total - reach - (count - 1), [1] * (count - 1)
    while surplus > 0:
        candidates = [i for i in range(count - 1) if counts[i] < reach]
        whole, remaining = sum([loads[i] for i in candidates]), surplus
        for i in candidates:
            addition = min(reach - counts[i], max(1, remaining * loads[i] // whole), surplus)
            counts[i] = counts[i] + addition
            surplus = surplus - addition
    return np.array([reach] + counts)


def uneven(rng, amount, total, limit, skew):
    if amount == 2:
        one = jax.random.randint(rng, (), max(1, total - limit), min(limit, total - 1) + 1)
        return jnp.stack([one, total - one])
    sizes = jnp.asarray(profile(amount, total, limit, skew), jnp.int32)
    pairs = (amount - 1) // 2
    donor, taker = sizes[1:1 + 2 * pairs:2], sizes[2:2 + 2 * pairs:2]
    room = jnp.minimum(donor - 1, limit - taker)
    moved = jax.random.randint(jax.random.fold_in(rng, 1), (pairs,), 0, 1 << 20) % (room + 1)
    sizes = sizes.at[1:1 + 2 * pairs:2].set(donor - moved).at[2:2 + 2 * pairs:2].set(taker + moved)
    return sizes[jax.random.permutation(jax.random.fold_in(rng, 2), amount)]


def centred(stream_key, dims, spread, limit, pieces=(), kind=jnp.bfloat16):
    array = jax.random.normal(stream_key, dims, jnp.float32) * spread
    if len(pieces) > 0:
        array = shard_levels(stream_key, dims, pieces, -0.22, 0.18) * array
    return jnp.clip(array, min=-limit, max=limit).astype(kind)


def setup_inputs(seed: int = 0) -> dict:
    key_of = jax.random.split(jax.random.key(seed), 19)
    return {
        "tokens": centred(key_of[0], (SEQS, LEN, D), 1.0, 6.0, ((0, 32), (1, 4))),
        "cotangent": centred(key_of[1], (SEQS, LEN, D), 1.0, 6.0, ((0, 32), (1, 4))),
        "segments": jax.vmap(lambda own: jnp.searchsorted(jnp.cumsum(uneven(own, 8, LEN, LEN // 2, 2)), jnp.arange(LEN), side="right"))(jax.random.split(key_of[2], SEQS)).reshape((SEQS, LEN)).astype(jnp.int32),
        "adapter_id": plant(jax.random.randint(key_of[3], (SEQS,), 0, ADAPTERS), jax.random.fold_in(key_of[3], 1), 0, ADAPTERS - 1).astype(jnp.int32),
        "w_qkv": centred(key_of[4], (3, D, QW), D ** -0.5, 0.125, ((1, 32), (2, 4))),
        "w_out": centred(key_of[5], (QW, D), QW ** -0.5, 0.125, ((0, 4), (1, 32))),
        "w_gateup": centred(key_of[6], (2, D, FF), D ** -0.5, 0.125, ((1, 32), (2, 4))),
        "w_down": centred(key_of[7], (FF, D), FF ** -0.5, 0.078125, ((0, 4), (1, 32))),
        "gain_attn": jnp.clip(1.0 + 0.1 * jax.random.normal(key_of[8], (D,), jnp.float32), 0.5, 1.5),
        "gain_ffn": jnp.clip(1.0 + 0.1 * jax.random.normal(key_of[9], (D,), jnp.float32), 0.5, 1.5),
        "gain_sub": jnp.clip(1.0 + 0.1 * jax.random.normal(key_of[10], (VALUE_DIM,), jnp.float32), 0.5, 1.5),
        "lambda_head": jnp.clip(jax.random.uniform(key_of[11], (HEADS,), jnp.float32, 0.2, 0.7), 0.2, 0.7),
        "a_in": centred(key_of[12], (5, D, COLS), D ** -0.5, 0.125, ((1, 128),)),
        "b_qkv": centred(key_of[13], (3, COLS, QW), (4 * RANK) ** -0.5, 0.75, ((1, 32), (2, 4))),
        "b_gateup": centred(key_of[14], (2, COLS, FF), (4 * RANK) ** -0.5, 0.75, ((1, 32), (2, 4))),
        "a_out": centred(key_of[15], (QW, COLS), QW ** -0.5, 0.125, ((0, 4), (1, 32))),
        "a_down": centred(key_of[16], (FF, COLS), FF ** -0.5, 0.078125, ((0, 4), (1, 32))),
        "b_rows": centred(key_of[17], (2, COLS, D), (4 * RANK) ** -0.5, 0.75, ((2, 128),)),
    }


@jax.custom_vjp
def low(v):
    return lax.optimization_barrier(v.astype(jnp.bfloat16)).astype(jnp.float32)

@jax.custom_vjp
def low_back(v):
    return v

def low_keep(v):
    return (low(v), None)

def low_pass(kept, grad):
    return (grad,)

def back_keep(v):
    return (v, None)

def back_low(kept, grad):
    return (low(grad),)
low.defvjp(low_keep, low_pass)
low_back.defvjp(back_keep, back_low)
highest = lax.Precision.HIGHEST
negative = -1e+30
adapter_scale = 2.0
lambda_init = 0.2
rotary_base = 10000.0
row_epsilon = 1e-06
head_epsilon = 1e-05

def rows_norm(values, gain_vector):
    return values * lax.rsqrt(lax.optimization_barrier(jnp.mean(values * values, axis=-1, keepdims=True)) + row_epsilon) * gain_vector

def head_norm(values, gain_vector):
    scaled = values * lax.rsqrt(lax.optimization_barrier(jnp.mean(values * values, axis=-1, keepdims=True)) + head_epsilon)
    return scaled * gain_vector * (1.0 - lambda_init)

def rotary_heads(values, positions, head_dim):
    length = values.shape[0]
    groups = values.reshape(length, -1, head_dim)
    half_dim = head_dim // 2
    frequency = rotary_base ** (-jnp.arange(half_dim, dtype=jnp.float32) / half_dim)
    angles = positions.astype(jnp.float32)[:, None] * frequency[None, :]
    cosine = jnp.cos(angles)[:, None, :]
    sine_part = jnp.sin(angles)[:, None, :]
    first_half = groups[..., :half_dim]
    second = groups[..., half_dim:]
    turned = jnp.concatenate([first_half * cosine - second * sine_part, second * cosine + first_half * sine_part], axis=-1)
    return turned.reshape(length, -1)

def swiglu(gate_rows, up_rows):
    return gate_rows * jax.nn.sigmoid(gate_rows) * up_rows

def project(row_block, weight, down_sel, up_sel):
    lowrank = jnp.dot(row_block, down_sel, precision=highest)
    return jnp.dot(row_block, weight, precision=highest) + adapter_scale * jnp.dot(lowrank, up_sel, precision=highest)

def layer_forward(inputs, adapters, frozen, segment_row, offset):
    a_in, b_qkv, b_gateup, a_out, a_down, b_rows = adapters
    w_qkv, w_out, w_gateup, w_down, gain_attn, gain_ffn, gain_sub, lambda_head = frozen
    length = inputs.shape[0]
    ain_sel = lax.dynamic_slice_in_dim(a_in, offset, RANK, 2)
    bqkv_sel = lax.dynamic_slice_in_dim(b_qkv, offset, RANK, 1)
    bgu_sel = lax.dynamic_slice_in_dim(b_gateup, offset, RANK, 1)
    aout_sel = lax.dynamic_slice_in_dim(a_out, offset, RANK, 1)
    adown_sel = lax.dynamic_slice_in_dim(a_down, offset, RANK, 1)
    brows_sel = lax.dynamic_slice_in_dim(b_rows, offset, RANK, 1)
    positions = jnp.arange(length)
    normed = low(rows_norm(inputs, gain_attn))
    queries = low_back(project(normed, w_qkv[0], ain_sel[0], bqkv_sel[0]))
    keys_lin = low_back(project(normed, w_qkv[1], ain_sel[1], bqkv_sel[1]))
    values_lin = low_back(project(normed, w_qkv[2], ain_sel[2], bqkv_sel[2]))
    query_in = low(rotary_heads(queries, positions, HEAD_DIM)).reshape(length, HEADS, 2, HEAD_DIM)
    key_in = low(rotary_heads(keys_lin, positions, HEAD_DIM)).reshape(length, HEADS, 2, HEAD_DIM)
    value_in = low(values_lin).reshape(length, HEADS, VALUE_DIM)
    allowed = (segment_row[:, None] == segment_row[None, :]) & (positions[:, None] >= positions[None, :])
    raw_scores = jnp.einsum('qhmd,khmd->hmqk', query_in, key_in, precision=highest) * HEAD_DIM ** (-0.5)
    scores = low_back(jnp.where(allowed, raw_scores, negative))
    row_max = lax.optimization_barrier(jnp.max(scores, axis=-1, keepdims=True))
    expo = jnp.exp(scores - row_max)
    soft_max = expo / lax.optimization_barrier(jnp.sum(expo, axis=-1, keepdims=True))
    differ = low(soft_max[:, 0] - lambda_head[:, None, None] * soft_max[:, 1])
    heads_out = low_back(jnp.einsum('hqk,khd->qhd', differ, value_in, precision=highest))
    mixed_rows = low(head_norm(heads_out, gain_sub).reshape(length, HEADS * VALUE_DIM))
    attn_branch = low_back(project(mixed_rows, w_out, aout_sel, brows_sel[0]))
    hidden = inputs + attn_branch
    normed_ffn = low(rows_norm(hidden, gain_ffn))
    gate_rows = low_back(project(normed_ffn, w_gateup[0], ain_sel[3], bgu_sel[0]))
    up_rows = low_back(project(normed_ffn, w_gateup[1], ain_sel[4], bgu_sel[1]))
    product = low(swiglu(gate_rows, up_rows))
    ffn_branch = low_back(project(product, w_down, adown_sel, brows_sel[1]))
    return hidden + ffn_branch

def add_pair(first_term, second_term):
    return first_term + second_term

def reference(tokens, cotangent, segments, adapter_id, w_qkv, w_out, w_gateup, w_down, gain_attn, gain_ffn, gain_sub, lambda_head, a_in, b_qkv, b_gateup, a_out, a_down, b_rows):
    frozen = (w_qkv.astype(jnp.float32), w_out.astype(jnp.float32), w_gateup.astype(jnp.float32), w_down.astype(jnp.float32), gain_attn.astype(jnp.float32), gain_ffn.astype(jnp.float32), gain_sub.astype(jnp.float32), lambda_head.astype(jnp.float32))
    adapters = (a_in.astype(jnp.float32), b_qkv.astype(jnp.float32), b_gateup.astype(jnp.float32), a_out.astype(jnp.float32), a_down.astype(jnp.float32), b_rows.astype(jnp.float32))

    def one_sequence(totals, seq_items):
        inputs, tangent, segment_row, chosen = seq_items
        offset = (chosen * RANK).astype(jnp.int32)

        def wrapped(layer_in, adapter_set):
            return layer_forward(layer_in, adapter_set, frozen, segment_row, offset)
        output, pullback = jax.vjp(wrapped, inputs.astype(jnp.float32), adapters)
        grad_inputs, grad_adapters = pullback(tangent.astype(jnp.float32))
        totals = jax.tree.map(add_pair, totals, grad_adapters)
        return (totals, (output.astype(jnp.bfloat16), grad_inputs))
    zero_grads = tuple((jnp.zeros_like(entry) for entry in adapters))
    totals, (outputs, grads) = lax.scan(one_sequence, zero_grads, (tokens, cotangent, segments, adapter_id))
    return (outputs, grads, totals[0], totals[1], totals[2], totals[3], totals[4], totals[5])
```

```python
from functools import partial

import jax
import jax.numpy as jnp
from jax import lax
from jax.sharding import PartitionSpec as P

D = 2048
HEAD_DIM = 128
VALUE_DIM = 256
RANK = 16
COLS = 128


highest = lax.Precision.HIGHEST
negative = -1e30
adapter_scale = 2.0
lambda_init = 0.2
rotary_base = 10000.0
row_epsilon = 1e-06
head_epsilon = 1e-05


def rows_norm(values, gain_vector):
    return (
        values
        * lax.rsqrt(jnp.mean(values * values, axis=-1, keepdims=True) + row_epsilon)
        * gain_vector
    )


def head_norm(values, gain_vector):
    scaled = values * lax.rsqrt(jnp.mean(values * values, axis=-1, keepdims=True) + head_epsilon)
    return scaled * gain_vector * (1.0 - lambda_init)


def rotary_heads(values, positions, head_dim):
    lead = values.shape[:-1]
    groups = values.reshape(lead + (-1, head_dim))
    half_dim = head_dim // 2
    frequency = rotary_base ** (-jnp.arange(half_dim, dtype=jnp.float32) / half_dim)
    angles = positions.astype(jnp.float32)[:, None] * frequency[None, :]
    cosine = jnp.cos(angles)[:, None, :]
    sine_part = jnp.sin(angles)[:, None, :]
    first_half = groups[..., :half_dim]
    second = groups[..., half_dim:]
    turned = jnp.concatenate(
        [first_half * cosine - second * sine_part, second * cosine + first_half * sine_part],
        axis=-1,
    )
    return turned.reshape(values.shape)


def swiglu(gate_rows, up_rows):
    return gate_rows * jax.nn.sigmoid(gate_rows) * up_rows


def attention_scores(query_in, key_in, allowed):
    raw_scores = jnp.einsum(
        "qhmd,khmd->hmqk", query_in, key_in, preferred_element_type=jnp.float32
    ) * query_in.shape[-1] ** (-0.5)
    return jnp.where(allowed[None, None], raw_scores, negative)


def attend(query_in, key_in, value_in, allowed, lambda_here):
    scores = attention_scores(query_in, key_in, allowed)
    row_max = jnp.max(scores, axis=-1, keepdims=True)
    log_total = row_max + jnp.log(jnp.sum(jnp.exp(scores - row_max), axis=-1, keepdims=True))
    soft_max = jnp.exp(scores - log_total)
    differ = (soft_max[:, 0] - lambda_here[:, None, None] * soft_max[:, 1]).astype(jnp.bfloat16)
    heads_out = jnp.einsum("hqk,khd->qhd", differ, value_in, preferred_element_type=jnp.float32)
    return (heads_out, log_total)


def attend_back(query_in, key_in, value_in, allowed, lambda_here, log_total, grad_heads):
    scale = query_in.shape[-1] ** (-0.5)
    scores = attention_scores(query_in, key_in, allowed)
    soft_max = jnp.exp(scores - log_total)
    differ = (soft_max[:, 0] - lambda_here[:, None, None] * soft_max[:, 1]).astype(jnp.bfloat16)
    grad_values = jnp.einsum("hqk,qhd->khd", differ, grad_heads, preferred_element_type=jnp.float32)
    grad_differ = jnp.einsum(
        "qhd,khd->hqk", grad_heads, value_in, preferred_element_type=jnp.float32
    )
    grad_soft = jnp.stack([grad_differ, -lambda_here[:, None, None] * grad_differ], axis=1)
    grad_scores = (
        soft_max * (grad_soft - jnp.sum(grad_soft * soft_max, axis=-1, keepdims=True))
    ).astype(jnp.bfloat16)
    grad_query = (
        jnp.einsum("hmqk,khmd->qhmd", grad_scores, key_in, preferred_element_type=jnp.float32)
        * scale
    )
    grad_key = (
        jnp.einsum("hmqk,qhmd->khmd", grad_scores, query_in, preferred_element_type=jnp.float32)
        * scale
    )
    return (grad_query, grad_key, grad_values.astype(jnp.bfloat16))


def xor_pairs(count, bit):
    return [(i, i ^ bit) for i in range(count)]


def tok_gather(values):
    count = lax.axis_size("tok")
    me = lax.axis_index("tok")
    far = lax.ppermute(values, "tok", xor_pairs(count, 2))
    pair = jnp.where((me & 2) == 0, jnp.stack([values, far]), jnp.stack([far, values]))
    near = lax.ppermute(pair, "tok", xor_pairs(count, 1))
    full = jnp.where((me & 1) == 0, jnp.stack([pair, near], 1), jnp.stack([near, pair], 1))
    return full.reshape((count,) + values.shape)


def tok_scatter(blocks):
    count = lax.axis_size("tok")
    me = lax.axis_index("tok")
    core = me & 1
    half = (me >> 1) & 1
    split = blocks.reshape((2, 2) + blocks.shape[1:])
    mine = lax.dynamic_index_in_dim(split, core, 1, keepdims=False)
    theirs = lax.dynamic_index_in_dim(split, 1 - core, 1, keepdims=False)
    chip_sum = mine + lax.ppermute(theirs, "tok", xor_pairs(count, 1))
    keep = lax.dynamic_index_in_dim(chip_sum, half, 0, keepdims=False)
    send = lax.dynamic_index_in_dim(chip_sum, 1 - half, 0, keepdims=False)
    return keep + lax.ppermute(send, "tok", xor_pairs(count, 2))


def tok_sum(values):
    count = lax.axis_size("tok")
    chip_sum = values + lax.ppermute(values, "tok", xor_pairs(count, 1))
    return chip_sum + lax.ppermute(chip_sum, "tok", xor_pairs(count, 2))


def hp_dot(left, right, spec):
    return jnp.einsum(spec, left, right, precision=highest, preferred_element_type=jnp.float32)


def per_device(
    tokens,
    cotangent,
    segments,
    adapter_id,
    w_qkv,
    w_out,
    w_gateup,
    w_down,
    gain_attn,
    gain_ffn,
    gain_sub,
    lambda_head,
    a_in,
    b_qkv,
    b_gateup,
    a_out,
    a_down,
    b_rows,
):
    tok_count = lax.axis_size("tok")
    fsdp_count = lax.axis_size("fsdp")
    me_tok = lax.axis_index("tok")
    seqs, local_len, _ = tokens.shape
    length = local_len * tok_count
    qw_here = w_qkv.shape[2]
    ff_here = w_gateup.shape[2]
    heads_here = qw_here // VALUE_DIM
    lambda_here = lax.dynamic_slice_in_dim(lambda_head, me_tok * heads_here, heads_here)
    positions = jnp.arange(length)
    offsets = adapter_id * RANK
    fsdp_rows = w_qkv.shape[1]
    groups_per_adapter = RANK // b_qkv.shape[1]

    a_in_tok = tok_gather(a_in)
    b_rows_tok = tok_gather(b_rows)
    pieces = [w_qkv, w_out, w_gateup, w_down, b_qkv, b_gateup, a_out, a_down, a_in_tok, b_rows_tok]
    flat = jnp.concatenate([p.reshape(-1) for p in pieces])
    gathered = lax.all_gather(flat, "fsdp", axis=0, tiled=False)
    unpacked = []
    start = 0
    for p in pieces:
        size = p.size
        unpacked.append(gathered[:, start : start + size].reshape((fsdp_count,) + p.shape))
        start += size
    (g_qkv, g_out, g_gateup, g_down, g_bqkv, g_bgateup, g_aout, g_adown, g_ain, g_brows) = unpacked
    w_qkv_full = jnp.moveaxis(g_qkv, 0, 1).reshape(3, fsdp_count * fsdp_rows, qw_here)
    w_out_full = jnp.moveaxis(g_out, 0, 1).reshape(qw_here, fsdp_count * fsdp_rows)
    w_gateup_full = jnp.moveaxis(g_gateup, 0, 1).reshape(2, fsdp_count * fsdp_rows, ff_here)
    w_down_full = jnp.moveaxis(g_down, 0, 1).reshape(ff_here, fsdp_count * fsdp_rows)
    a_in_full = jnp.transpose(g_ain, (2, 0, 1, 3, 4)).reshape(5, D, COLS)
    b_rows_full = jnp.transpose(g_brows, (2, 3, 0, 1, 4)).reshape(2, COLS, D)

    def pick_cols(values, axis):
        return jnp.stack(
            [lax.dynamic_slice_in_dim(values, offsets[s], RANK, axis) for s in range(seqs)]
        )

    def pick_groups(values):
        return jnp.stack(
            [
                lax.dynamic_slice_in_dim(values, adapter_id[s] * groups_per_adapter, groups_per_adapter, 0)
                for s in range(seqs)
            ]
        )

    a_in_sel = pick_cols(a_in_full, 2)
    b_rows_sel = pick_cols(b_rows_full, 1)
    b_qkv_sel = jnp.moveaxis(pick_groups(g_bqkv), 1, 2).reshape(seqs, 3, RANK, qw_here)
    b_gateup_sel = jnp.moveaxis(pick_groups(g_bgateup), 1, 2).reshape(seqs, 2, RANK, ff_here)
    a_out_sel = jnp.moveaxis(pick_groups(g_aout), 1, 2).reshape(seqs, qw_here, RANK)
    a_down_sel = jnp.moveaxis(pick_groups(g_adown), 1, 2).reshape(seqs, ff_here, RANK)

    def gather_rows(values):
        full = tok_gather(values)
        return jnp.moveaxis(full, 0, 1).reshape(seqs, length, values.shape[-1])

    def scatter_rows(values):
        blocks = jnp.moveaxis(values.reshape(seqs, tok_count, local_len, values.shape[-1]), 1, 0)
        return tok_scatter(blocks)

    def column_forward(rows_full, weight, down_sel, up_sel):
        lowrank = jnp.einsum("std,sdr->str", rows_full, down_sel, preferred_element_type=jnp.float32)
        linear = jnp.einsum("std,de->ste", rows_full, weight, preferred_element_type=jnp.float32)
        return linear + adapter_scale * hp_dot(lowrank, up_sel.astype(jnp.float32), "str,sre->ste"), lowrank

    def row_forward(rows_here, weight, down_sel, up_sel):
        lowrank = jnp.einsum("std,sdr->str", rows_here, down_sel, preferred_element_type=jnp.float32)
        main_part = jnp.einsum("std,de->ste", rows_here, weight, preferred_element_type=jnp.float32)
        total = main_part + adapter_scale * hp_dot(lowrank, up_sel.astype(jnp.float32), "str,sre->ste")
        return scatter_rows(total), lowrank

    inputs_rows = tokens.astype(jnp.float32)
    allowed = (segments[:, :, None] == segments[:, None, :]) & (
        positions[:, None] >= positions[None, :]
    )[None]
    grad_ffn_full = gather_rows(cotangent)
    normed_rows, norm_attn_pull = jax.vjp(partial(rows_norm, gain_vector=gain_attn), inputs_rows)
    normed_full = gather_rows(normed_rows.astype(jnp.bfloat16))
    proj_lin = []
    proj_low = []
    for p in range(3):
        lin, lowr = column_forward(normed_full, w_qkv_full[p], a_in_sel[:, p], b_qkv_sel[:, p])
        proj_lin.append(lin)
        proj_low.append(lowr)
    rotate = partial(rotary_heads, positions=positions, head_dim=HEAD_DIM)
    query_rot, query_pull = jax.vjp(rotate, proj_lin[0])
    key_rot, key_pull = jax.vjp(rotate, proj_lin[1])
    query_in = query_rot.astype(jnp.bfloat16).reshape(seqs, length, heads_here, 2, HEAD_DIM)
    key_in = key_rot.astype(jnp.bfloat16).reshape(seqs, length, heads_here, 2, HEAD_DIM)
    value_in = proj_lin[2].astype(jnp.bfloat16).reshape(seqs, length, heads_here, VALUE_DIM)
    heads_out, log_total = jax.vmap(attend, in_axes=(0, 0, 0, 0, None))(
        query_in, key_in, value_in, allowed, lambda_here
    )
    mixed_float, head_pull = jax.vjp(partial(head_norm, gain_vector=gain_sub), heads_out)
    mixed_rows = mixed_float.reshape(seqs, length, qw_here).astype(jnp.bfloat16)
    attn_rows, out_low = row_forward(mixed_rows, w_out_full, a_out_sel, b_rows_sel[:, 0])
    hidden = inputs_rows + attn_rows
    normed_ffn, norm_ffn_pull = jax.vjp(partial(rows_norm, gain_vector=gain_ffn), hidden)
    ffn_full = gather_rows(normed_ffn.astype(jnp.bfloat16))
    gate_lin, gate_low = column_forward(ffn_full, w_gateup_full[0], a_in_sel[:, 3], b_gateup_sel[:, 0])
    up_lin, up_low = column_forward(ffn_full, w_gateup_full[1], a_in_sel[:, 4], b_gateup_sel[:, 1])
    product_float, swiglu_pull = jax.vjp(swiglu, gate_lin, up_lin)
    product = product_float.astype(jnp.bfloat16)
    ffn_rows, down_low = row_forward(product, w_down_full, a_down_sel, b_rows_sel[:, 1])
    output = (hidden + ffn_rows).astype(jnp.bfloat16)
    row_lows = tok_sum(jnp.stack([out_low, down_low]))

    tangent = cotangent.astype(jnp.float32)

    def row_backward(grad_full, rows_here, weight, down_sel, up_sel):
        grad_float = grad_full.astype(jnp.float32)
        grad_low = adapter_scale * hp_dot(grad_float, up_sel.astype(jnp.float32), "ste,sre->str")
        grad_down = hp_dot(rows_here.astype(jnp.float32), grad_low, "std,str->sdr")
        grad_inputs = jnp.einsum(
            "ste,de->std", grad_full, weight, preferred_element_type=jnp.float32
        ) + hp_dot(grad_low, down_sel.astype(jnp.float32), "str,sdr->std")
        return grad_inputs, grad_down

    def column_backward(rows_full, entries):
        running = None
        grad_lows = []
        grads_up = []
        for grad_rows, weight, down_sel, up_sel, lowrank in entries:
            grad_float = grad_rows.astype(jnp.float32)
            grad_low = adapter_scale * hp_dot(grad_float, up_sel.astype(jnp.float32), "ste,sre->str")
            grads_up.append(adapter_scale * hp_dot(lowrank, grad_float, "str,ste->sre"))
            grad_lows.append(grad_low)
            term = jnp.einsum(
                "ste,de->std", grad_rows, weight, preferred_element_type=jnp.float32
            ) + hp_dot(grad_low, down_sel.astype(jnp.float32), "str,sdr->std")
            running = term if running is None else running + term
        return scatter_rows(running), grad_lows, grads_up

    def rows_of_mine(rows_full):
        split = rows_full.reshape(seqs, length, fsdp_count, tok_count, D // (fsdp_count * tok_count))
        return lax.dynamic_index_in_dim(split, me_tok, 3, keepdims=False)

    grad_product, grad_a_down = row_backward(
        grad_ffn_full, product, w_down_full, a_down_sel, b_rows_sel[:, 1]
    )
    grad_gate, grad_up = swiglu_pull(grad_product)
    grad_ffn_rows, ffn_grad_lows, ffn_grads_up = column_backward(
        ffn_full,
        (
            (grad_gate.astype(jnp.bfloat16), w_gateup_full[0], a_in_sel[:, 3], b_gateup_sel[:, 0], gate_low),
            (grad_up.astype(jnp.bfloat16), w_gateup_full[1], a_in_sel[:, 4], b_gateup_sel[:, 1], up_low),
        ),
    )
    grad_hidden = tangent + norm_ffn_pull(grad_ffn_rows)[0]
    grad_attn_full = gather_rows(grad_hidden.astype(jnp.bfloat16))
    grad_mixed, grad_a_out = row_backward(
        grad_attn_full, mixed_rows, w_out_full, a_out_sel, b_rows_sel[:, 0]
    )
    grad_heads = head_pull(grad_mixed.reshape(seqs, length, heads_here, VALUE_DIM))[0].astype(
        jnp.bfloat16
    )
    grad_query_rot, grad_key_rot, grad_values = jax.vmap(
        attend_back, in_axes=(0, 0, 0, 0, None, 0, 0)
    )(query_in, key_in, value_in, allowed, lambda_here, log_total, grad_heads)
    grad_query = query_pull(grad_query_rot.reshape(seqs, length, qw_here))[0].astype(jnp.bfloat16)
    grad_key = key_pull(grad_key_rot.reshape(seqs, length, qw_here))[0].astype(jnp.bfloat16)
    grad_attn_rows, attn_grad_lows, attn_grads_up = column_backward(
        normed_full,
        (
            (grad_query, w_qkv_full[0], a_in_sel[:, 0], b_qkv_sel[:, 0], proj_low[0]),
            (grad_key, w_qkv_full[1], a_in_sel[:, 1], b_qkv_sel[:, 1], proj_low[1]),
            (grad_values.reshape(seqs, length, qw_here), w_qkv_full[2], a_in_sel[:, 2], b_qkv_sel[:, 2], proj_low[2]),
        ),
    )
    grad_tokens = grad_hidden + norm_attn_pull(grad_attn_rows)[0]

    grad_lows = tok_sum(jnp.stack(attn_grad_lows + ffn_grad_lows))
    attn_mine = rows_of_mine(normed_full)
    ffn_mine = rows_of_mine(ffn_full)
    grad_a_in_part = jnp.concatenate(
        [
            hp_dot(attn_mine.astype(jnp.float32), grad_lows[:3], "stfi,pstr->psfir"),
            hp_dot(ffn_mine.astype(jnp.float32), grad_lows[3:], "stfi,pstr->psfir"),
        ]
    )
    e_attn_mine = rows_of_mine(grad_attn_full).astype(jnp.float32)
    e_ffn_mine = rows_of_mine(grad_ffn_full).astype(jnp.float32)
    grad_b_rows_part = adapter_scale * jnp.stack(
        [
            hp_dot(row_lows[0], e_attn_mine, "str,stfj->srfj"),
            hp_dot(row_lows[1], e_ffn_mine, "str,stfj->srfj"),
        ]
    )

    def place(part, axis, total):
        shape = list(part.shape[1:])
        shape[axis] = total
        dense = jnp.zeros(shape, jnp.float32)
        for s in range(seqs):
            current = lax.dynamic_slice_in_dim(dense, offsets[s], RANK, axis)
            dense = lax.dynamic_update_slice_in_dim(dense, current + part[s], offsets[s], axis)
        return dense

    dense_a_in = place(jnp.moveaxis(grad_a_in_part, 1, 0), 3, COLS)
    dense_b_rows = place(jnp.moveaxis(grad_b_rows_part, 1, 0), 1, COLS)
    wide = jnp.concatenate(
        [
            jnp.moveaxis(dense_a_in, 1, 0).reshape(fsdp_count, -1),
            jnp.moveaxis(dense_b_rows, 2, 0).reshape(fsdp_count, -1),
        ],
        axis=1,
    )
    wide_sum = lax.all_to_all(wide, "fsdp", 0, 0, tiled=False).sum(0)
    a_in_block = wide_sum[: 5 * 16 * COLS].reshape(5, 16, COLS)
    b_rows_block = wide_sum[5 * 16 * COLS :].reshape(2, COLS, 16)

    dense_b_qkv = place(jnp.stack(attn_grads_up, 1), 1, COLS)
    dense_b_gateup = place(jnp.stack(ffn_grads_up, 1), 1, COLS)
    dense_a_out = place(grad_a_out, 1, COLS)
    dense_a_down = place(grad_a_down, 1, COLS)
    per = COLS // fsdp_count
    narrow = jnp.concatenate(
        [
            jnp.moveaxis(dense_b_qkv.reshape(3, fsdp_count, per, qw_here), 1, 0).reshape(fsdp_count, -1),
            jnp.moveaxis(dense_b_gateup.reshape(2, fsdp_count, per, ff_here), 1, 0).reshape(fsdp_count, -1),
            jnp.moveaxis(dense_a_out.reshape(qw_here, fsdp_count, per), 1, 0).reshape(fsdp_count, -1),
            jnp.moveaxis(dense_a_down.reshape(ff_here, fsdp_count, per), 1, 0).reshape(fsdp_count, -1),
        ],
        axis=1,
    ).astype(jnp.bfloat16)
    narrow_sum = lax.all_to_all(narrow, "fsdp", 0, 0, tiled=False).astype(jnp.float32).sum(0)
    sizes = [3 * per * qw_here, 2 * per * ff_here, qw_here * per, ff_here * per]
    cuts = [0]
    for size in sizes:
        cuts.append(cuts[-1] + size)
    b_qkv_block = narrow_sum[cuts[0] : cuts[1]].reshape(3, per, qw_here)
    b_gateup_block = narrow_sum[cuts[1] : cuts[2]].reshape(2, per, ff_here)
    a_out_block = narrow_sum[cuts[2] : cuts[3]].reshape(qw_here, per)
    a_down_block = narrow_sum[cuts[3] : cuts[4]].reshape(ff_here, per)

    return (
        output,
        grad_tokens,
        a_in_block,
        b_qkv_block,
        b_gateup_block,
        a_out_block,
        a_down_block,
        b_rows_block,
    )


def solution(mesh):
    return jax.shard_map(
        per_device,
        mesh=mesh,
        in_specs=(
            P("fsdp", "tok", None),
            P("fsdp", "tok", None),
            P("fsdp", None),
            P("fsdp"),
            P(None, "fsdp", "tok"),
            P("tok", "fsdp"),
            P(None, "fsdp", "tok"),
            P("tok", "fsdp"),
            P(),
            P(),
            P(),
            P(),
            P(None, ("fsdp", "tok"), None),
            P(None, "fsdp", "tok"),
            P(None, "fsdp", "tok"),
            P("tok", "fsdp"),
            P("tok", "fsdp"),
            P(None, None, ("fsdp", "tok")),
        ),
        out_specs=(
            P("fsdp", "tok", None),
            P("fsdp", "tok", None),
            P(None, ("fsdp", "tok"), None),
            P(None, "fsdp", "tok"),
            P(None, "fsdp", "tok"),
            P("tok", "fsdp"),
            P("tok", "fsdp"),
            P(None, None, ("fsdp", "tok")),
        ),
        check_vma=False,
    )
```

```python
from functools import partial

import jax
import jax.numpy as jnp
from jax import lax
from jax.sharding import PartitionSpec as P

D = 2048
HEAD_DIM = 128
VALUE_DIM = 256
RANK = 16
COLS = 128


highest = lax.Precision.HIGHEST
negative = -1e30
adapter_scale = 2.0
lambda_init = 0.2
rotary_base = 10000.0
row_epsilon = 1e-06
head_epsilon = 1e-05


def rows_norm(values, gain_vector):
    return (
        values
        * lax.rsqrt(jnp.mean(values * values, axis=-1, keepdims=True) + row_epsilon)
        * gain_vector
    )


def head_norm(values, gain_vector):
    scaled = values * lax.rsqrt(jnp.mean(values * values, axis=-1, keepdims=True) + head_epsilon)
    return scaled * gain_vector * (1.0 - lambda_init)


def rotary_heads(values, positions, head_dim):
    lead = values.shape[:-1]
    groups = values.reshape(lead + (-1, head_dim))
    half_dim = head_dim // 2
    frequency = rotary_base ** (-jnp.arange(half_dim, dtype=jnp.float32) / half_dim)
    angles = positions.astype(jnp.float32)[:, None] * frequency[None, :]
    cosine = jnp.cos(angles)[:, None, :]
    sine_part = jnp.sin(angles)[:, None, :]
    first_half = groups[..., :half_dim]
    second = groups[..., half_dim:]
    turned = jnp.concatenate(
        [first_half * cosine - second * sine_part, second * cosine + first_half * sine_part],
        axis=-1,
    )
    return turned.reshape(values.shape)


def swiglu(gate_rows, up_rows):
    return gate_rows * jax.nn.sigmoid(gate_rows) * up_rows


def attention_scores(query_in, key_in, allowed):
    raw_scores = jnp.einsum(
        "qhmd,khmd->hmqk", query_in, key_in, preferred_element_type=jnp.float32
    ) * query_in.shape[-1] ** (-0.5)
    return jnp.where(allowed[None, None], raw_scores, negative)


def attend(query_in, key_in, value_in, allowed, lambda_here):
    scores = attention_scores(query_in, key_in, allowed)
    row_max = jnp.max(scores, axis=-1, keepdims=True)
    log_total = row_max + jnp.log(jnp.sum(jnp.exp(scores - row_max), axis=-1, keepdims=True))
    soft_max = jnp.exp(scores - log_total)
    differ = (soft_max[:, 0] - lambda_here[:, None, None] * soft_max[:, 1]).astype(jnp.bfloat16)
    heads_out = jnp.einsum("hqk,khd->qhd", differ, value_in, preferred_element_type=jnp.float32)
    return (heads_out, log_total)


def attend_back(query_in, key_in, value_in, allowed, lambda_here, log_total, grad_heads):
    scale = query_in.shape[-1] ** (-0.5)
    scores = attention_scores(query_in, key_in, allowed)
    soft_max = jnp.exp(scores - log_total)
    differ = (soft_max[:, 0] - lambda_here[:, None, None] * soft_max[:, 1]).astype(jnp.bfloat16)
    grad_values = jnp.einsum("hqk,qhd->khd", differ, grad_heads, preferred_element_type=jnp.float32)
    grad_differ = jnp.einsum(
        "qhd,khd->hqk", grad_heads, value_in, preferred_element_type=jnp.float32
    )
    grad_soft = jnp.stack([grad_differ, -lambda_here[:, None, None] * grad_differ], axis=1)
    grad_scores = (
        soft_max * (grad_soft - jnp.sum(grad_soft * soft_max, axis=-1, keepdims=True))
    ).astype(jnp.bfloat16)
    grad_query = (
        jnp.einsum("hmqk,khmd->qhmd", grad_scores, key_in, preferred_element_type=jnp.float32)
        * scale
    )
    grad_key = (
        jnp.einsum("hmqk,qhmd->khmd", grad_scores, query_in, preferred_element_type=jnp.float32)
        * scale
    )
    return (grad_query, grad_key, grad_values.astype(jnp.bfloat16))


def xor_pairs(count, bit):
    return [(i, i ^ bit) for i in range(count)]


def tok_gather(values):
    count = lax.axis_size("tok")
    me = lax.axis_index("tok")
    far = lax.ppermute(values, "tok", xor_pairs(count, 2))
    pair = jnp.where((me & 2) == 0, jnp.stack([values, far]), jnp.stack([far, values]))
    near = lax.ppermute(pair, "tok", xor_pairs(count, 1))
    full = jnp.where((me & 1) == 0, jnp.stack([pair, near], 1), jnp.stack([near, pair], 1))
    return full.reshape((count,) + values.shape)


def tok_scatter(blocks):
    count = lax.axis_size("tok")
    me = lax.axis_index("tok")
    core = me & 1
    half = (me >> 1) & 1
    split = blocks.reshape((2, 2) + blocks.shape[1:])
    mine = lax.dynamic_index_in_dim(split, core, 1, keepdims=False)
    theirs = lax.dynamic_index_in_dim(split, 1 - core, 1, keepdims=False)
    chip_sum = mine + lax.ppermute(theirs, "tok", xor_pairs(count, 1))
    keep = lax.dynamic_index_in_dim(chip_sum, half, 0, keepdims=False)
    send = lax.dynamic_index_in_dim(chip_sum, 1 - half, 0, keepdims=False)
    return keep + lax.ppermute(send, "tok", xor_pairs(count, 2))


def tok_sum(values):
    count = lax.axis_size("tok")
    chip_sum = values + lax.ppermute(values, "tok", xor_pairs(count, 1))
    return chip_sum + lax.ppermute(chip_sum, "tok", xor_pairs(count, 2))


def hp_dot(left, right, spec):
    return jnp.einsum(spec, left, right, precision=highest, preferred_element_type=jnp.float32)


def per_device(
    tokens,
    cotangent,
    segments,
    adapter_id,
    w_qkv,
    w_out,
    w_gateup,
    w_down,
    gain_attn,
    gain_ffn,
    gain_sub,
    lambda_head,
    a_in,
    b_qkv,
    b_gateup,
    a_out,
    a_down,
    b_rows,
):
    tok_count = lax.axis_size("tok")
    fsdp_count = lax.axis_size("fsdp")
    me_tok = lax.axis_index("tok")
    seqs, local_len, _ = tokens.shape
    length = local_len * tok_count
    qw_here = w_qkv.shape[2]
    ff_here = w_gateup.shape[2]
    heads_here = qw_here // VALUE_DIM
    lambda_here = lax.dynamic_slice_in_dim(lambda_head, me_tok * heads_here, heads_here)
    positions = jnp.arange(length)
    offsets = adapter_id * RANK
    fsdp_rows = w_qkv.shape[1]
    groups_per_adapter = RANK // b_qkv.shape[1]

    def fsdp_gather(values, axis):
        tiled_in = jnp.concatenate([values] * fsdp_count, axis=0)
        return lax.all_to_all(tiled_in, "fsdp", 0, axis, tiled=True)

    a_in_tok = tok_gather(a_in)
    b_rows_tok = tok_gather(b_rows)
    small = [b_qkv, b_gateup, a_out, a_down, a_in_tok, b_rows_tok]
    small_flat = jnp.concatenate([p.reshape(1, -1) for p in small], axis=1)
    small_all = fsdp_gather(small_flat, 0)
    unpacked = []
    start = 0
    for p in small:
        unpacked.append(small_all[:, start : start + p.size].reshape((fsdp_count,) + p.shape))
        start += p.size
    (g_bqkv, g_bgateup, g_aout, g_adown, g_ain, g_brows) = unpacked
    w_qkv_full = fsdp_gather(w_qkv, 1)
    w_out_full = fsdp_gather(w_out, 1)
    w_gateup_full = fsdp_gather(w_gateup, 1)
    w_down_full = fsdp_gather(w_down, 1)
    a_in_full = jnp.transpose(g_ain, (2, 0, 1, 3, 4)).reshape(5, D, COLS)
    b_rows_full = jnp.transpose(g_brows, (2, 3, 0, 1, 4)).reshape(2, COLS, D)

    def pick_cols(values, axis):
        return jnp.stack(
            [lax.dynamic_slice_in_dim(values, offsets[s], RANK, axis) for s in range(seqs)]
        )

    def pick_groups(values):
        return jnp.stack(
            [
                lax.dynamic_slice_in_dim(values, adapter_id[s] * groups_per_adapter, groups_per_adapter, 0)
                for s in range(seqs)
            ]
        )

    a_in_sel = pick_cols(a_in_full, 2)
    b_rows_sel = pick_cols(b_rows_full, 1)
    b_qkv_sel = jnp.moveaxis(pick_groups(g_bqkv), 1, 2).reshape(seqs, 3, RANK, qw_here)
    b_gateup_sel = jnp.moveaxis(pick_groups(g_bgateup), 1, 2).reshape(seqs, 2, RANK, ff_here)
    a_out_sel = jnp.moveaxis(pick_groups(g_aout), 1, 2).reshape(seqs, qw_here, RANK)
    a_down_sel = jnp.moveaxis(pick_groups(g_adown), 1, 2).reshape(seqs, ff_here, RANK)

    def gather_rows(values):
        full = tok_gather(values)
        return jnp.moveaxis(full, 0, 1).reshape(seqs, length, values.shape[-1])

    def scatter_rows(values):
        blocks = jnp.moveaxis(values.reshape(seqs, tok_count, local_len, values.shape[-1]), 1, 0)
        return tok_scatter(blocks)

    def column_forward(rows_full, weight, down_sel, up_sel):
        lowrank = jnp.einsum("std,sdr->str", rows_full, down_sel, preferred_element_type=jnp.float32)
        linear = jnp.einsum("std,de->ste", rows_full, weight, preferred_element_type=jnp.float32)
        return linear + adapter_scale * hp_dot(lowrank, up_sel.astype(jnp.float32), "str,sre->ste"), lowrank

    def row_forward(rows_here, weight, down_sel, up_sel):
        lowrank = jnp.einsum("std,sdr->str", rows_here, down_sel, preferred_element_type=jnp.float32)
        main_part = jnp.einsum("std,de->ste", rows_here, weight, preferred_element_type=jnp.float32)
        total = main_part + adapter_scale * hp_dot(lowrank, up_sel.astype(jnp.float32), "str,sre->ste")
        return scatter_rows(total), lowrank

    inputs_rows = tokens.astype(jnp.float32)
    allowed = (segments[:, :, None] == segments[:, None, :]) & (
        positions[:, None] >= positions[None, :]
    )[None]
    grad_ffn_full = gather_rows(cotangent)
    normed_rows, norm_attn_pull = jax.vjp(partial(rows_norm, gain_vector=gain_attn), inputs_rows)
    normed_full = gather_rows(normed_rows.astype(jnp.bfloat16))
    proj_lin = []
    proj_low = []
    for p in range(3):
        lin, lowr = column_forward(normed_full, w_qkv_full[p], a_in_sel[:, p], b_qkv_sel[:, p])
        proj_lin.append(lin)
        proj_low.append(lowr)
    rotate = partial(rotary_heads, positions=positions, head_dim=HEAD_DIM)
    query_rot, query_pull = jax.vjp(rotate, proj_lin[0])
    key_rot, key_pull = jax.vjp(rotate, proj_lin[1])
    query_in = query_rot.astype(jnp.bfloat16).reshape(seqs, length, heads_here, 2, HEAD_DIM)
    key_in = key_rot.astype(jnp.bfloat16).reshape(seqs, length, heads_here, 2, HEAD_DIM)
    value_in = proj_lin[2].astype(jnp.bfloat16).reshape(seqs, length, heads_here, VALUE_DIM)
    heads_out, log_total = jax.vmap(attend, in_axes=(0, 0, 0, 0, None))(
        query_in, key_in, value_in, allowed, lambda_here
    )
    mixed_float, head_pull = jax.vjp(partial(head_norm, gain_vector=gain_sub), heads_out)
    mixed_rows = mixed_float.reshape(seqs, length, qw_here).astype(jnp.bfloat16)
    attn_rows, out_low = row_forward(mixed_rows, w_out_full, a_out_sel, b_rows_sel[:, 0])
    hidden = inputs_rows + attn_rows
    normed_ffn, norm_ffn_pull = jax.vjp(partial(rows_norm, gain_vector=gain_ffn), hidden)
    ffn_full = gather_rows(normed_ffn.astype(jnp.bfloat16))
    gate_lin, gate_low = column_forward(ffn_full, w_gateup_full[0], a_in_sel[:, 3], b_gateup_sel[:, 0])
    up_lin, up_low = column_forward(ffn_full, w_gateup_full[1], a_in_sel[:, 4], b_gateup_sel[:, 1])
    product_float, swiglu_pull = jax.vjp(swiglu, gate_lin, up_lin)
    product = product_float.astype(jnp.bfloat16)
    ffn_rows, down_low = row_forward(product, w_down_full, a_down_sel, b_rows_sel[:, 1])
    output = (hidden + ffn_rows).astype(jnp.bfloat16)
    row_lows = tok_sum(jnp.stack([out_low, down_low]))

    tangent = cotangent.astype(jnp.float32)

    def row_backward(grad_full, rows_here, weight, down_sel, up_sel):
        grad_float = grad_full.astype(jnp.float32)
        grad_low = adapter_scale * hp_dot(grad_float, up_sel.astype(jnp.float32), "ste,sre->str")
        grad_down = hp_dot(rows_here.astype(jnp.float32), grad_low, "std,str->sdr")
        grad_inputs = jnp.einsum(
            "ste,de->std", grad_full, weight, preferred_element_type=jnp.float32
        ) + hp_dot(grad_low, down_sel.astype(jnp.float32), "str,sdr->std")
        return grad_inputs, grad_down

    def column_backward(rows_full, entries):
        running = None
        grad_lows = []
        grads_up = []
        for grad_rows, weight, down_sel, up_sel, lowrank in entries:
            grad_float = grad_rows.astype(jnp.float32)
            grad_low = adapter_scale * hp_dot(grad_float, up_sel.astype(jnp.float32), "ste,sre->str")
            grads_up.append(adapter_scale * hp_dot(lowrank, grad_float, "str,ste->sre"))
            grad_lows.append(grad_low)
            term = jnp.einsum(
                "ste,de->std", grad_rows, weight, preferred_element_type=jnp.float32
            ) + hp_dot(grad_low, down_sel.astype(jnp.float32), "str,sdr->std")
            running = term if running is None else running + term
        return scatter_rows(running), grad_lows, grads_up

    def rows_of_mine(rows_full):
        split = rows_full.reshape(seqs, length, fsdp_count, tok_count, D // (fsdp_count * tok_count))
        return lax.dynamic_index_in_dim(split, me_tok, 3, keepdims=False)

    grad_product, grad_a_down = row_backward(
        grad_ffn_full, product, w_down_full, a_down_sel, b_rows_sel[:, 1]
    )
    grad_gate, grad_up = swiglu_pull(grad_product)
    grad_ffn_rows, ffn_grad_lows, ffn_grads_up = column_backward(
        ffn_full,
        (
            (grad_gate.astype(jnp.bfloat16), w_gateup_full[0], a_in_sel[:, 3], b_gateup_sel[:, 0], gate_low),
            (grad_up.astype(jnp.bfloat16), w_gateup_full[1], a_in_sel[:, 4], b_gateup_sel[:, 1], up_low),
        ),
    )
    grad_hidden = tangent + norm_ffn_pull(grad_ffn_rows)[0]
    grad_attn_full = gather_rows(grad_hidden.astype(jnp.bfloat16))
    grad_mixed, grad_a_out = row_backward(
        grad_attn_full, mixed_rows, w_out_full, a_out_sel, b_rows_sel[:, 0]
    )
    grad_heads = head_pull(grad_mixed.reshape(seqs, length, heads_here, VALUE_DIM))[0].astype(
        jnp.bfloat16
    )
    grad_query_rot, grad_key_rot, grad_values = jax.vmap(
        attend_back, in_axes=(0, 0, 0, 0, None, 0, 0)
    )(query_in, key_in, value_in, allowed, lambda_here, log_total, grad_heads)
    grad_query = query_pull(grad_query_rot.reshape(seqs, length, qw_here))[0].astype(jnp.bfloat16)
    grad_key = key_pull(grad_key_rot.reshape(seqs, length, qw_here))[0].astype(jnp.bfloat16)
    grad_attn_rows, attn_grad_lows, attn_grads_up = column_backward(
        normed_full,
        (
            (grad_query, w_qkv_full[0], a_in_sel[:, 0], b_qkv_sel[:, 0], proj_low[0]),
            (grad_key, w_qkv_full[1], a_in_sel[:, 1], b_qkv_sel[:, 1], proj_low[1]),
            (grad_values.reshape(seqs, length, qw_here), w_qkv_full[2], a_in_sel[:, 2], b_qkv_sel[:, 2], proj_low[2]),
        ),
    )
    grad_tokens = grad_hidden + norm_attn_pull(grad_attn_rows)[0]

    grad_lows = tok_sum(jnp.stack(attn_grad_lows + ffn_grad_lows))
    attn_mine = rows_of_mine(normed_full)
    ffn_mine = rows_of_mine(ffn_full)
    grad_a_in_part = jnp.concatenate(
        [
            hp_dot(attn_mine.astype(jnp.float32), grad_lows[:3], "stfi,pstr->psfir"),
            hp_dot(ffn_mine.astype(jnp.float32), grad_lows[3:], "stfi,pstr->psfir"),
        ]
    )
    e_attn_mine = rows_of_mine(grad_attn_full).astype(jnp.float32)
    e_ffn_mine = rows_of_mine(grad_ffn_full).astype(jnp.float32)
    grad_b_rows_part = adapter_scale * jnp.stack(
        [
            hp_dot(row_lows[0], e_attn_mine, "str,stfj->srfj"),
            hp_dot(row_lows[1], e_ffn_mine, "str,stfj->srfj"),
        ]
    )

    def place(part, axis, total):
        shape = list(part.shape[1:])
        shape[axis] = total
        dense = jnp.zeros(shape, jnp.float32)
        for s in range(seqs):
            current = lax.dynamic_slice_in_dim(dense, offsets[s], RANK, axis)
            dense = lax.dynamic_update_slice_in_dim(dense, current + part[s], offsets[s], axis)
        return dense

    dense_a_in = place(jnp.moveaxis(grad_a_in_part, 1, 0), 3, COLS)
    dense_b_rows = place(jnp.moveaxis(grad_b_rows_part, 1, 0), 1, COLS)
    wide = jnp.concatenate(
        [
            jnp.moveaxis(dense_a_in, 1, 0).reshape(fsdp_count, -1),
            jnp.moveaxis(dense_b_rows, 2, 0).reshape(fsdp_count, -1),
        ],
        axis=1,
    )
    wide_sum = lax.all_to_all(wide, "fsdp", 0, 0, tiled=False).sum(0)
    a_in_block = wide_sum[: 5 * 16 * COLS].reshape(5, 16, COLS)
    b_rows_block = wide_sum[5 * 16 * COLS :].reshape(2, COLS, 16)

    dense_b_qkv = place(jnp.stack(attn_grads_up, 1), 1, COLS)
    dense_b_gateup = place(jnp.stack(ffn_grads_up, 1), 1, COLS)
    dense_a_out = place(grad_a_out, 1, COLS)
    dense_a_down = place(grad_a_down, 1, COLS)
    per = COLS // fsdp_count
    narrow = jnp.concatenate(
        [
            jnp.moveaxis(dense_b_qkv.reshape(3, fsdp_count, per, qw_here), 1, 0).reshape(fsdp_count, -1),
            jnp.moveaxis(dense_b_gateup.reshape(2, fsdp_count, per, ff_here), 1, 0).reshape(fsdp_count, -1),
            jnp.moveaxis(dense_a_out.reshape(qw_here, fsdp_count, per), 1, 0).reshape(fsdp_count, -1),
            jnp.moveaxis(dense_a_down.reshape(ff_here, fsdp_count, per), 1, 0).reshape(fsdp_count, -1),
        ],
        axis=1,
    ).astype(jnp.bfloat16)
    narrow_sum = lax.all_to_all(narrow, "fsdp", 0, 0, tiled=False).astype(jnp.float32).sum(0)
    sizes = [3 * per * qw_here, 2 * per * ff_here, qw_here * per, ff_here * per]
    cuts = [0]
    for size in sizes:
        cuts.append(cuts[-1] + size)
    b_qkv_block = narrow_sum[cuts[0] : cuts[1]].reshape(3, per, qw_here)
    b_gateup_block = narrow_sum[cuts[1] : cuts[2]].reshape(2, per, ff_here)
    a_out_block = narrow_sum[cuts[2] : cuts[3]].reshape(qw_here, per)
    a_down_block = narrow_sum[cuts[3] : cuts[4]].reshape(ff_here, per)

    return (
        output,
        grad_tokens,
        a_in_block,
        b_qkv_block,
        b_gateup_block,
        a_out_block,
        a_down_block,
        b_rows_block,
    )


def solution(mesh):
    return jax.shard_map(
        per_device,
        mesh=mesh,
        in_specs=(
            P("fsdp", "tok", None),
            P("fsdp", "tok", None),
            P("fsdp", None),
            P("fsdp"),
            P(None, "fsdp", "tok"),
            P("tok", "fsdp"),
            P(None, "fsdp", "tok"),
            P("tok", "fsdp"),
            P(),
            P(),
            P(),
            P(),
            P(None, ("fsdp", "tok"), None),
            P(None, "fsdp", "tok"),
            P(None, "fsdp", "tok"),
            P("tok", "fsdp"),
            P("tok", "fsdp"),
            P(None, None, ("fsdp", "tok")),
        ),
        out_specs=(
            P("fsdp", "tok", None),
            P("fsdp", "tok", None),
            P(None, ("fsdp", "tok"), None),
            P(None, "fsdp", "tok"),
            P(None, "fsdp", "tok"),
            P("tok", "fsdp"),
            P("tok", "fsdp"),
            P(None, None, ("fsdp", "tok")),
        ),
        check_vma=False,
    )
```

```python
from functools import partial

import jax
import jax.numpy as jnp
from jax import lax
from jax.sharding import PartitionSpec as P

D = 2048
HEAD_DIM = 128
VALUE_DIM = 256
RANK = 16
COLS = 128


highest = lax.Precision.HIGHEST
negative = -1e30
adapter_scale = 2.0
lambda_init = 0.2
rotary_base = 10000.0
row_epsilon = 1e-06
head_epsilon = 1e-05


def rows_norm(values, gain_vector):
    return (
        values
        * lax.rsqrt(jnp.mean(values * values, axis=-1, keepdims=True) + row_epsilon)
        * gain_vector
    )


def head_norm(values, gain_vector):
    scaled = values * lax.rsqrt(jnp.mean(values * values, axis=-1, keepdims=True) + head_epsilon)
    return scaled * gain_vector * (1.0 - lambda_init)


def rotary_heads(values, positions, head_dim):
    lead = values.shape[:-1]
    groups = values.reshape(lead + (-1, head_dim))
    half_dim = head_dim // 2
    frequency = rotary_base ** (-jnp.arange(half_dim, dtype=jnp.float32) / half_dim)
    angles = positions.astype(jnp.float32)[:, None] * frequency[None, :]
    cosine = jnp.cos(angles)[:, None, :]
    sine_part = jnp.sin(angles)[:, None, :]
    first_half = groups[..., :half_dim]
    second = groups[..., half_dim:]
    turned = jnp.concatenate(
        [first_half * cosine - second * sine_part, second * cosine + first_half * sine_part],
        axis=-1,
    )
    return turned.reshape(values.shape)


def swiglu(gate_rows, up_rows):
    return gate_rows * jax.nn.sigmoid(gate_rows) * up_rows


def attention_scores(query_in, key_in, allowed):
    raw_scores = jnp.einsum(
        "qhmd,khmd->hmqk", query_in, key_in, preferred_element_type=jnp.float32
    ) * query_in.shape[-1] ** (-0.5)
    return jnp.where(allowed[None, None], raw_scores, negative)


def attend(query_in, key_in, value_in, allowed, lambda_here):
    scores = attention_scores(query_in, key_in, allowed)
    row_max = jnp.max(scores, axis=-1, keepdims=True)
    log_total = row_max + jnp.log(jnp.sum(jnp.exp(scores - row_max), axis=-1, keepdims=True))
    soft_max = jnp.exp(scores - log_total)
    differ = (soft_max[:, 0] - lambda_here[:, None, None] * soft_max[:, 1]).astype(jnp.bfloat16)
    heads_out = jnp.einsum("hqk,khd->qhd", differ, value_in, preferred_element_type=jnp.float32)
    return (heads_out, log_total)


def attend_back(query_in, key_in, value_in, allowed, lambda_here, log_total, grad_heads):
    scale = query_in.shape[-1] ** (-0.5)
    scores = attention_scores(query_in, key_in, allowed)
    soft_max = jnp.exp(scores - log_total)
    differ = (soft_max[:, 0] - lambda_here[:, None, None] * soft_max[:, 1]).astype(jnp.bfloat16)
    grad_values = jnp.einsum("hqk,qhd->khd", differ, grad_heads, preferred_element_type=jnp.float32)
    grad_differ = jnp.einsum(
        "qhd,khd->hqk", grad_heads, value_in, preferred_element_type=jnp.float32
    )
    grad_soft = jnp.stack([grad_differ, -lambda_here[:, None, None] * grad_differ], axis=1)
    grad_scores = (
        soft_max * (grad_soft - jnp.sum(grad_soft * soft_max, axis=-1, keepdims=True))
    ).astype(jnp.bfloat16)
    grad_query = (
        jnp.einsum("hmqk,khmd->qhmd", grad_scores, key_in, preferred_element_type=jnp.float32)
        * scale
    )
    grad_key = (
        jnp.einsum("hmqk,qhmd->khmd", grad_scores, query_in, preferred_element_type=jnp.float32)
        * scale
    )
    return (grad_query, grad_key, grad_values.astype(jnp.bfloat16))


def xor_pairs(count, bit):
    return [(i, i ^ bit) for i in range(count)]


def tok_gather(values):
    count = lax.axis_size("tok")
    me = lax.axis_index("tok")
    far = lax.ppermute(values, "tok", xor_pairs(count, 2))
    pair = jnp.where((me & 2) == 0, jnp.stack([values, far]), jnp.stack([far, values]))
    near = lax.ppermute(pair, "tok", xor_pairs(count, 1))
    full = jnp.where((me & 1) == 0, jnp.stack([pair, near], 1), jnp.stack([near, pair], 1))
    return full.reshape((count,) + values.shape)


def tok_scatter(blocks):
    count = lax.axis_size("tok")
    me = lax.axis_index("tok")
    core = me & 1
    half = (me >> 1) & 1
    split = blocks.reshape((2, 2) + blocks.shape[1:])
    mine = lax.dynamic_index_in_dim(split, core, 1, keepdims=False)
    theirs = lax.dynamic_index_in_dim(split, 1 - core, 1, keepdims=False)
    chip_sum = mine + lax.ppermute(theirs, "tok", xor_pairs(count, 1))
    keep = lax.dynamic_index_in_dim(chip_sum, half, 0, keepdims=False)
    send = lax.dynamic_index_in_dim(chip_sum, 1 - half, 0, keepdims=False)
    return keep + lax.ppermute(send, "tok", xor_pairs(count, 2))


def tok_sum(values):
    count = lax.axis_size("tok")
    chip_sum = values + lax.ppermute(values, "tok", xor_pairs(count, 1))
    return chip_sum + lax.ppermute(chip_sum, "tok", xor_pairs(count, 2))


def hp_dot(left, right, spec):
    return jnp.einsum(spec, left, right, precision=highest, preferred_element_type=jnp.float32)


def per_device(
    tokens,
    cotangent,
    segments,
    adapter_id,
    w_qkv,
    w_out,
    w_gateup,
    w_down,
    gain_attn,
    gain_ffn,
    gain_sub,
    lambda_head,
    a_in,
    b_qkv,
    b_gateup,
    a_out,
    a_down,
    b_rows,
):
    tok_count = lax.axis_size("tok")
    fsdp_count = lax.axis_size("fsdp")
    me_tok = lax.axis_index("tok")
    seqs, local_len, _ = tokens.shape
    length = local_len * tok_count
    qw_here = w_qkv.shape[2]
    ff_here = w_gateup.shape[2]
    heads_here = qw_here // VALUE_DIM
    lambda_here = lax.dynamic_slice_in_dim(lambda_head, me_tok * heads_here, heads_here)
    positions = jnp.arange(length)
    offsets = adapter_id * RANK
    fsdp_rows = w_qkv.shape[1]
    groups_per_adapter = RANK // b_qkv.shape[1]

    def fsdp_gather(values, axis):
        tiled_in = jnp.concatenate([values] * fsdp_count, axis=0)
        return lax.all_to_all(tiled_in, "fsdp", 0, axis, tiled=True)

    def packed_gather(small, axes):
        count = 1
        for name in axes:
            count *= lax.axis_size(name)
        flat = jnp.concatenate([p.reshape(-1, COLS) for p in small], axis=0)
        tiled_in = jnp.broadcast_to(flat[None], (count,) + flat.shape).reshape(-1, COLS)
        got = lax.all_to_all(tiled_in, axes, 0, 0, tiled=True).reshape((count,) + flat.shape)
        out = []
        start = 0
        for p in small:
            rows = p.size // COLS
            out.append(got[:, start : start + rows].reshape((count,) + p.shape))
            start += rows
        return out

    w_qkv_full = fsdp_gather(w_qkv, 1)
    g_ain, g_brows = packed_gather([a_in, b_rows], ("fsdp", "tok"))
    g_bqkv, g_bgateup, g_aout, g_adown = packed_gather([b_qkv, b_gateup, a_out, a_down], ("fsdp",))
    w_out_full = fsdp_gather(w_out, 1)
    w_gateup_full = fsdp_gather(w_gateup, 1)
    w_down_full = fsdp_gather(w_down, 1)
    a_in_full = jnp.moveaxis(g_ain, 0, 1).reshape(5, D, COLS)
    b_rows_full = jnp.moveaxis(g_brows, 0, 2).reshape(2, COLS, D)

    def pick_cols(values, axis):
        return jnp.stack(
            [lax.dynamic_slice_in_dim(values, offsets[s], RANK, axis) for s in range(seqs)]
        )

    def pick_groups(values):
        return jnp.stack(
            [
                lax.dynamic_slice_in_dim(values, adapter_id[s] * groups_per_adapter, groups_per_adapter, 0)
                for s in range(seqs)
            ]
        )

    a_in_sel = pick_cols(a_in_full, 2)
    b_rows_sel = pick_cols(b_rows_full, 1)
    b_qkv_sel = jnp.moveaxis(pick_groups(g_bqkv), 1, 2).reshape(seqs, 3, RANK, qw_here)
    b_gateup_sel = jnp.moveaxis(pick_groups(g_bgateup), 1, 2).reshape(seqs, 2, RANK, ff_here)
    a_out_sel = jnp.moveaxis(pick_groups(g_aout), 1, 2).reshape(seqs, qw_here, RANK)
    a_down_sel = jnp.moveaxis(pick_groups(g_adown), 1, 2).reshape(seqs, ff_here, RANK)

    def gather_rows(values):
        full = tok_gather(values)
        return jnp.moveaxis(full, 0, 1).reshape(seqs, length, values.shape[-1])

    def scatter_rows(values):
        blocks = jnp.moveaxis(values.reshape(seqs, tok_count, local_len, values.shape[-1]), 1, 0)
        return tok_scatter(blocks)

    def column_forward(rows_full, weight, down_sel, up_sel):
        lowrank = jnp.einsum("std,sdr->str", rows_full, down_sel, preferred_element_type=jnp.float32)
        linear = jnp.einsum("std,de->ste", rows_full, weight, preferred_element_type=jnp.float32)
        return linear + adapter_scale * hp_dot(lowrank, up_sel.astype(jnp.float32), "str,sre->ste"), lowrank

    def row_forward(rows_here, weight, down_sel, up_sel):
        lowrank = jnp.einsum("std,sdr->str", rows_here, down_sel, preferred_element_type=jnp.float32)
        main_part = jnp.einsum("std,de->ste", rows_here, weight, preferred_element_type=jnp.float32)
        total = main_part + adapter_scale * hp_dot(lowrank, up_sel.astype(jnp.float32), "str,sre->ste")
        return scatter_rows(total), lowrank

    inputs_rows = tokens.astype(jnp.float32)
    allowed = (segments[:, :, None] == segments[:, None, :]) & (
        positions[:, None] >= positions[None, :]
    )[None]
    grad_ffn_full = gather_rows(cotangent)
    normed_rows, norm_attn_pull = jax.vjp(partial(rows_norm, gain_vector=gain_attn), inputs_rows)
    normed_full = gather_rows(normed_rows.astype(jnp.bfloat16))
    proj_lin = []
    proj_low = []
    for p in range(3):
        lin, lowr = column_forward(normed_full, w_qkv_full[p], a_in_sel[:, p], b_qkv_sel[:, p])
        proj_lin.append(lin)
        proj_low.append(lowr)
    rotate = partial(rotary_heads, positions=positions, head_dim=HEAD_DIM)
    query_rot, query_pull = jax.vjp(rotate, proj_lin[0])
    key_rot, key_pull = jax.vjp(rotate, proj_lin[1])
    query_in = query_rot.astype(jnp.bfloat16).reshape(seqs, length, heads_here, 2, HEAD_DIM)
    key_in = key_rot.astype(jnp.bfloat16).reshape(seqs, length, heads_here, 2, HEAD_DIM)
    value_in = proj_lin[2].astype(jnp.bfloat16).reshape(seqs, length, heads_here, VALUE_DIM)
    heads_out, log_total = jax.vmap(attend, in_axes=(0, 0, 0, 0, None))(
        query_in, key_in, value_in, allowed, lambda_here
    )
    mixed_float, head_pull = jax.vjp(partial(head_norm, gain_vector=gain_sub), heads_out)
    mixed_rows = mixed_float.reshape(seqs, length, qw_here).astype(jnp.bfloat16)
    attn_rows, out_low = row_forward(mixed_rows, w_out_full, a_out_sel, b_rows_sel[:, 0])
    hidden = inputs_rows + attn_rows
    normed_ffn, norm_ffn_pull = jax.vjp(partial(rows_norm, gain_vector=gain_ffn), hidden)
    ffn_full = gather_rows(normed_ffn.astype(jnp.bfloat16))
    gate_lin, gate_low = column_forward(ffn_full, w_gateup_full[0], a_in_sel[:, 3], b_gateup_sel[:, 0])
    up_lin, up_low = column_forward(ffn_full, w_gateup_full[1], a_in_sel[:, 4], b_gateup_sel[:, 1])
    product_float, swiglu_pull = jax.vjp(swiglu, gate_lin, up_lin)
    product = product_float.astype(jnp.bfloat16)
    ffn_rows, down_low = row_forward(product, w_down_full, a_down_sel, b_rows_sel[:, 1])
    output = (hidden + ffn_rows).astype(jnp.bfloat16)
    row_lows = tok_sum(jnp.stack([out_low, down_low]))

    tangent = cotangent.astype(jnp.float32)

    def row_backward(grad_full, rows_here, weight, down_sel, up_sel):
        grad_float = grad_full.astype(jnp.float32)
        grad_low = adapter_scale * hp_dot(grad_float, up_sel.astype(jnp.float32), "ste,sre->str")
        grad_down = hp_dot(rows_here.astype(jnp.float32), grad_low, "std,str->sdr")
        grad_inputs = jnp.einsum(
            "ste,de->std", grad_full, weight, preferred_element_type=jnp.float32
        ) + hp_dot(grad_low, down_sel.astype(jnp.float32), "str,sdr->std")
        return grad_inputs, grad_down

    def column_backward(rows_full, entries):
        running = None
        grad_lows = []
        grads_up = []
        for grad_rows, weight, down_sel, up_sel, lowrank in entries:
            grad_float = grad_rows.astype(jnp.float32)
            grad_low = adapter_scale * hp_dot(grad_float, up_sel.astype(jnp.float32), "ste,sre->str")
            grads_up.append(adapter_scale * hp_dot(lowrank, grad_float, "str,ste->sre"))
            grad_lows.append(grad_low)
            term = jnp.einsum(
                "ste,de->std", grad_rows, weight, preferred_element_type=jnp.float32
            ) + hp_dot(grad_low, down_sel.astype(jnp.float32), "str,sdr->std")
            running = term if running is None else running + term
        return scatter_rows(running), grad_lows, grads_up

    def rows_of_mine(rows_full):
        split = rows_full.reshape(seqs, length, fsdp_count, tok_count, D // (fsdp_count * tok_count))
        return lax.dynamic_index_in_dim(split, me_tok, 3, keepdims=False)

    grad_product, grad_a_down = row_backward(
        grad_ffn_full, product, w_down_full, a_down_sel, b_rows_sel[:, 1]
    )
    grad_gate, grad_up = swiglu_pull(grad_product)
    grad_ffn_rows, ffn_grad_lows, ffn_grads_up = column_backward(
        ffn_full,
        (
            (grad_gate.astype(jnp.bfloat16), w_gateup_full[0], a_in_sel[:, 3], b_gateup_sel[:, 0], gate_low),
            (grad_up.astype(jnp.bfloat16), w_gateup_full[1], a_in_sel[:, 4], b_gateup_sel[:, 1], up_low),
        ),
    )
    grad_hidden = tangent + norm_ffn_pull(grad_ffn_rows)[0]
    grad_attn_full = gather_rows(grad_hidden.astype(jnp.bfloat16))
    grad_mixed, grad_a_out = row_backward(
        grad_attn_full, mixed_rows, w_out_full, a_out_sel, b_rows_sel[:, 0]
    )
    grad_heads = head_pull(grad_mixed.reshape(seqs, length, heads_here, VALUE_DIM))[0].astype(
        jnp.bfloat16
    )
    grad_query_rot, grad_key_rot, grad_values = jax.vmap(
        attend_back, in_axes=(0, 0, 0, 0, None, 0, 0)
    )(query_in, key_in, value_in, allowed, lambda_here, log_total, grad_heads)
    grad_query = query_pull(grad_query_rot.reshape(seqs, length, qw_here))[0].astype(jnp.bfloat16)
    grad_key = key_pull(grad_key_rot.reshape(seqs, length, qw_here))[0].astype(jnp.bfloat16)
    grad_attn_rows, attn_grad_lows, attn_grads_up = column_backward(
        normed_full,
        (
            (grad_query, w_qkv_full[0], a_in_sel[:, 0], b_qkv_sel[:, 0], proj_low[0]),
            (grad_key, w_qkv_full[1], a_in_sel[:, 1], b_qkv_sel[:, 1], proj_low[1]),
            (grad_values.reshape(seqs, length, qw_here), w_qkv_full[2], a_in_sel[:, 2], b_qkv_sel[:, 2], proj_low[2]),
        ),
    )
    grad_tokens = grad_hidden + norm_attn_pull(grad_attn_rows)[0]

    grad_lows = tok_sum(jnp.stack(attn_grad_lows + ffn_grad_lows))
    attn_mine = rows_of_mine(normed_full)
    ffn_mine = rows_of_mine(ffn_full)
    grad_a_in_part = jnp.concatenate(
        [
            hp_dot(attn_mine.astype(jnp.float32), grad_lows[:3], "stfi,pstr->psfir"),
            hp_dot(ffn_mine.astype(jnp.float32), grad_lows[3:], "stfi,pstr->psfir"),
        ]
    )
    e_attn_mine = rows_of_mine(grad_attn_full).astype(jnp.float32)
    e_ffn_mine = rows_of_mine(grad_ffn_full).astype(jnp.float32)
    grad_b_rows_part = adapter_scale * jnp.stack(
        [
            hp_dot(row_lows[0], e_attn_mine, "str,stfj->srfj"),
            hp_dot(row_lows[1], e_ffn_mine, "str,stfj->srfj"),
        ]
    )

    def place(part, axis, total):
        shape = list(part.shape[1:])
        shape[axis] = total
        dense = jnp.zeros(shape, jnp.float32)
        for s in range(seqs):
            current = lax.dynamic_slice_in_dim(dense, offsets[s], RANK, axis)
            dense = lax.dynamic_update_slice_in_dim(dense, current + part[s], offsets[s], axis)
        return dense

    dense_a_in = place(jnp.moveaxis(grad_a_in_part, 1, 0), 3, COLS)
    dense_b_rows = place(jnp.moveaxis(grad_b_rows_part, 1, 0), 1, COLS)
    wide = jnp.concatenate(
        [
            jnp.moveaxis(dense_a_in, 1, 0).reshape(fsdp_count, -1),
            jnp.moveaxis(dense_b_rows, 2, 0).reshape(fsdp_count, -1),
        ],
        axis=1,
    )
    wide_sum = lax.all_to_all(wide, "fsdp", 0, 0, tiled=False).sum(0)
    a_in_block = wide_sum[: 5 * 16 * COLS].reshape(5, 16, COLS)
    b_rows_block = wide_sum[5 * 16 * COLS :].reshape(2, COLS, 16)

    dense_b_qkv = place(jnp.stack(attn_grads_up, 1), 1, COLS)
    dense_b_gateup = place(jnp.stack(ffn_grads_up, 1), 1, COLS)
    dense_a_out = place(grad_a_out, 1, COLS)
    dense_a_down = place(grad_a_down, 1, COLS)
    per = COLS // fsdp_count
    narrow = jnp.concatenate(
        [
            jnp.moveaxis(dense_b_qkv.reshape(3, fsdp_count, per, qw_here), 1, 0).reshape(fsdp_count, -1),
            jnp.moveaxis(dense_b_gateup.reshape(2, fsdp_count, per, ff_here), 1, 0).reshape(fsdp_count, -1),
            jnp.moveaxis(dense_a_out.reshape(qw_here, fsdp_count, per), 1, 0).reshape(fsdp_count, -1),
            jnp.moveaxis(dense_a_down.reshape(ff_here, fsdp_count, per), 1, 0).reshape(fsdp_count, -1),
        ],
        axis=1,
    ).astype(jnp.bfloat16)
    narrow_sum = lax.all_to_all(narrow, "fsdp", 0, 0, tiled=False).astype(jnp.float32).sum(0)
    sizes = [3 * per * qw_here, 2 * per * ff_here, qw_here * per, ff_here * per]
    cuts = [0]
    for size in sizes:
        cuts.append(cuts[-1] + size)
    b_qkv_block = narrow_sum[cuts[0] : cuts[1]].reshape(3, per, qw_here)
    b_gateup_block = narrow_sum[cuts[1] : cuts[2]].reshape(2, per, ff_here)
    a_out_block = narrow_sum[cuts[2] : cuts[3]].reshape(qw_here, per)
    a_down_block = narrow_sum[cuts[3] : cuts[4]].reshape(ff_here, per)

    return (
        output,
        grad_tokens,
        a_in_block,
        b_qkv_block,
        b_gateup_block,
        a_out_block,
        a_down_block,
        b_rows_block,
    )


def solution(mesh):
    return jax.shard_map(
        per_device,
        mesh=mesh,
        in_specs=(
            P("fsdp", "tok", None),
            P("fsdp", "tok", None),
            P("fsdp", None),
            P("fsdp"),
            P(None, "fsdp", "tok"),
            P("tok", "fsdp"),
            P(None, "fsdp", "tok"),
            P("tok", "fsdp"),
            P(),
            P(),
            P(),
            P(),
            P(None, ("fsdp", "tok"), None),
            P(None, "fsdp", "tok"),
            P(None, "fsdp", "tok"),
            P("tok", "fsdp"),
            P("tok", "fsdp"),
            P(None, None, ("fsdp", "tok")),
        ),
        out_specs=(
            P("fsdp", "tok", None),
            P("fsdp", "tok", None),
            P(None, ("fsdp", "tok"), None),
            P(None, "fsdp", "tok"),
            P(None, "fsdp", "tok"),
            P("tok", "fsdp"),
            P("tok", "fsdp"),
            P(None, None, ("fsdp", "tok")),
        ),
        check_vma=False,
    )
```

```python
from functools import partial

import jax
import jax.numpy as jnp
from jax import lax
from jax.sharding import PartitionSpec as P

D = 2048
HEAD_DIM = 128
VALUE_DIM = 256
RANK = 16
COLS = 128


highest = lax.Precision.HIGHEST
negative = -1e30
adapter_scale = 2.0
lambda_init = 0.2
rotary_base = 10000.0
row_epsilon = 1e-06
head_epsilon = 1e-05


def rows_norm(values, gain_vector):
    return (
        values
        * lax.rsqrt(jnp.mean(values * values, axis=-1, keepdims=True) + row_epsilon)
        * gain_vector
    )


def head_norm(values, gain_vector):
    scaled = values * lax.rsqrt(jnp.mean(values * values, axis=-1, keepdims=True) + head_epsilon)
    return scaled * gain_vector * (1.0 - lambda_init)


def rotary_heads(values, positions, head_dim):
    lead = values.shape[:-1]
    groups = values.reshape(lead + (-1, head_dim))
    half_dim = head_dim // 2
    frequency = rotary_base ** (-jnp.arange(half_dim, dtype=jnp.float32) / half_dim)
    angles = positions.astype(jnp.float32)[:, None] * frequency[None, :]
    cosine = jnp.cos(angles)[:, None, :]
    sine_part = jnp.sin(angles)[:, None, :]
    first_half = groups[..., :half_dim]
    second = groups[..., half_dim:]
    turned = jnp.concatenate(
        [first_half * cosine - second * sine_part, second * cosine + first_half * sine_part],
        axis=-1,
    )
    return turned.reshape(values.shape)


def swiglu(gate_rows, up_rows):
    return gate_rows * jax.nn.sigmoid(gate_rows) * up_rows


def attention_scores(query_in, key_in, allowed):
    raw_scores = jnp.einsum(
        "qhmd,khmd->hmqk", query_in, key_in, preferred_element_type=jnp.float32
    ) * query_in.shape[-1] ** (-0.5)
    return jnp.where(allowed[None, None], raw_scores, negative)


def attend(query_in, key_in, value_in, allowed, lambda_here):
    scores = attention_scores(query_in, key_in, allowed)
    row_max = jnp.max(scores, axis=-1, keepdims=True)
    log_total = row_max + jnp.log(jnp.sum(jnp.exp(scores - row_max), axis=-1, keepdims=True))
    soft_max = jnp.exp(scores - log_total)
    differ = (soft_max[:, 0] - lambda_here[:, None, None] * soft_max[:, 1]).astype(jnp.bfloat16)
    heads_out = jnp.einsum("hqk,khd->qhd", differ, value_in, preferred_element_type=jnp.float32)
    return (heads_out, log_total)


def attend_back(query_in, key_in, value_in, allowed, lambda_here, log_total, grad_heads):
    scale = query_in.shape[-1] ** (-0.5)
    scores = attention_scores(query_in, key_in, allowed)
    soft_max = jnp.exp(scores - log_total)
    differ = (soft_max[:, 0] - lambda_here[:, None, None] * soft_max[:, 1]).astype(jnp.bfloat16)
    grad_values = jnp.einsum("hqk,qhd->khd", differ, grad_heads, preferred_element_type=jnp.float32)
    grad_differ = jnp.einsum(
        "qhd,khd->hqk", grad_heads, value_in, preferred_element_type=jnp.float32
    )
    grad_soft = jnp.stack([grad_differ, -lambda_here[:, None, None] * grad_differ], axis=1)
    grad_scores = (
        soft_max * (grad_soft - jnp.sum(grad_soft * soft_max, axis=-1, keepdims=True))
    ).astype(jnp.bfloat16)
    grad_query = (
        jnp.einsum("hmqk,khmd->qhmd", grad_scores, key_in, preferred_element_type=jnp.float32)
        * scale
    )
    grad_key = (
        jnp.einsum("hmqk,qhmd->khmd", grad_scores, query_in, preferred_element_type=jnp.float32)
        * scale
    )
    return (grad_query, grad_key, grad_values.astype(jnp.bfloat16))


def xor_pairs(count, bit):
    return [(i, i ^ bit) for i in range(count)]


def tok_gather(values, axis=0):
    count = lax.axis_size("tok")
    me = lax.axis_index("tok")
    far = lax.ppermute(values, "tok", xor_pairs(count, 2))
    pair = jnp.where(
        (me & 2) == 0, jnp.stack([values, far], axis), jnp.stack([far, values], axis)
    )
    near = lax.ppermute(pair, "tok", xor_pairs(count, 1))
    full = jnp.where(
        (me & 1) == 0, jnp.stack([pair, near], axis + 1), jnp.stack([near, pair], axis + 1)
    )
    return full.reshape(values.shape[:axis] + (count,) + values.shape[axis:])


def tok_scatter(blocks, axis=0):
    count = lax.axis_size("tok")
    me = lax.axis_index("tok")
    core = me & 1
    half = (me >> 1) & 1
    split = blocks.reshape(blocks.shape[:axis] + (2, 2) + blocks.shape[axis + 1 :])
    mine = lax.dynamic_index_in_dim(split, core, axis + 1, keepdims=False)
    theirs = lax.dynamic_index_in_dim(split, 1 - core, axis + 1, keepdims=False)
    chip_sum = mine + lax.ppermute(theirs, "tok", xor_pairs(count, 1))
    keep = lax.dynamic_index_in_dim(chip_sum, half, axis, keepdims=False)
    send = lax.dynamic_index_in_dim(chip_sum, 1 - half, axis, keepdims=False)
    return keep + lax.ppermute(send, "tok", xor_pairs(count, 2))


def tok_sum(values):
    count = lax.axis_size("tok")
    chip_sum = values + lax.ppermute(values, "tok", xor_pairs(count, 1))
    return chip_sum + lax.ppermute(chip_sum, "tok", xor_pairs(count, 2))


def hp_dot(left, right, spec):
    return jnp.einsum(spec, left, right, precision=highest, preferred_element_type=jnp.float32)


def per_device(
    tokens,
    cotangent,
    segments,
    adapter_id,
    w_qkv,
    w_out,
    w_gateup,
    w_down,
    gain_attn,
    gain_ffn,
    gain_sub,
    lambda_head,
    a_in,
    b_qkv,
    b_gateup,
    a_out,
    a_down,
    b_rows,
):
    tok_count = lax.axis_size("tok")
    fsdp_count = lax.axis_size("fsdp")
    me_tok = lax.axis_index("tok")
    seqs, local_len, _ = tokens.shape
    length = local_len * tok_count
    qw_here = w_qkv.shape[2]
    ff_here = w_gateup.shape[2]
    heads_here = qw_here // VALUE_DIM
    lambda_here = lax.dynamic_slice_in_dim(lambda_head, me_tok * heads_here, heads_here)
    positions = jnp.arange(length)
    offsets = adapter_id * RANK
    fsdp_rows = w_qkv.shape[1]
    groups_per_adapter = RANK // b_qkv.shape[1]

    def fsdp_gather(values, axis):
        tiled_in = jnp.broadcast_to(values[None], (fsdp_count,) + values.shape)
        tiled_in = tiled_in.reshape((fsdp_count * values.shape[0],) + values.shape[1:])
        return lax.all_to_all(tiled_in, "fsdp", 0, axis, tiled=True)

    def packed_gather(small, axes):
        count = 1
        for name in axes:
            count *= lax.axis_size(name)
        flat = jnp.concatenate([p.reshape(-1, COLS) for p in small], axis=0)
        tiled_in = jnp.broadcast_to(flat[None], (count,) + flat.shape).reshape(-1, COLS)
        got = lax.all_to_all(tiled_in, axes, 0, 0, tiled=True).reshape((count,) + flat.shape)
        out = []
        start = 0
        for p in small:
            rows = p.size // COLS
            out.append(got[:, start : start + rows].reshape((count,) + p.shape))
            start += rows
        return out

    w_qkv_full = fsdp_gather(w_qkv, 1)
    g_ain, g_brows = packed_gather([a_in, b_rows], ("fsdp", "tok"))
    g_bqkv, g_bgateup, g_aout, g_adown = packed_gather([b_qkv, b_gateup, a_out, a_down], ("fsdp",))
    w_out_full = fsdp_gather(w_out, 1)
    w_gateup_full = fsdp_gather(w_gateup, 1)
    w_down_full = fsdp_gather(w_down, 1)
    a_in_full = jnp.moveaxis(g_ain, 0, 1).reshape(5, D, COLS)
    b_rows_full = jnp.moveaxis(g_brows, 0, 2).reshape(2, COLS, D)

    def pick_cols(values, axis):
        return jnp.stack(
            [lax.dynamic_slice_in_dim(values, offsets[s], RANK, axis) for s in range(seqs)]
        )

    def pick_groups(values):
        return jnp.stack(
            [
                lax.dynamic_slice_in_dim(values, adapter_id[s] * groups_per_adapter, groups_per_adapter, 0)
                for s in range(seqs)
            ]
        )

    a_in_sel = pick_cols(a_in_full, 2)
    b_rows_sel = pick_cols(b_rows_full, 1)
    b_qkv_sel = jnp.moveaxis(pick_groups(g_bqkv), 1, 2).reshape(seqs, 3, RANK, qw_here)
    b_gateup_sel = jnp.moveaxis(pick_groups(g_bgateup), 1, 2).reshape(seqs, 2, RANK, ff_here)
    a_out_sel = jnp.moveaxis(pick_groups(g_aout), 1, 2).reshape(seqs, qw_here, RANK)
    a_down_sel = jnp.moveaxis(pick_groups(g_adown), 1, 2).reshape(seqs, ff_here, RANK)

    def gather_rows(values):
        full = tok_gather(values, 1)
        return full.reshape(seqs, length, values.shape[-1])

    def scatter_rows(values):
        return tok_scatter(values.reshape(seqs, tok_count, local_len, values.shape[-1]), 1)

    def column_forward(rows_full, weight, down_sel, up_sel):
        lowrank = jnp.einsum("std,sdr->str", rows_full, down_sel, preferred_element_type=jnp.float32)
        linear = jnp.einsum("std,de->ste", rows_full, weight, preferred_element_type=jnp.float32)
        return linear + adapter_scale * hp_dot(lowrank, up_sel.astype(jnp.float32), "str,sre->ste"), lowrank

    def row_forward(rows_here, weight, down_sel, up_sel):
        lowrank = jnp.einsum("std,sdr->str", rows_here, down_sel, preferred_element_type=jnp.float32)
        main_part = jnp.einsum("std,de->ste", rows_here, weight, preferred_element_type=jnp.float32)
        total = main_part + adapter_scale * hp_dot(lowrank, up_sel.astype(jnp.float32), "str,sre->ste")
        return scatter_rows(total), lowrank

    inputs_rows = tokens.astype(jnp.float32)
    allowed = (segments[:, :, None] == segments[:, None, :]) & (
        positions[:, None] >= positions[None, :]
    )[None]
    grad_ffn_full = gather_rows(cotangent)
    normed_rows, norm_attn_pull = jax.vjp(partial(rows_norm, gain_vector=gain_attn), inputs_rows)
    normed_full = gather_rows(normed_rows.astype(jnp.bfloat16))
    proj_lin = []
    proj_low = []
    for p in range(3):
        lin, lowr = column_forward(normed_full, w_qkv_full[p], a_in_sel[:, p], b_qkv_sel[:, p])
        proj_lin.append(lin)
        proj_low.append(lowr)
    rotate = partial(rotary_heads, positions=positions, head_dim=HEAD_DIM)
    query_rot, query_pull = jax.vjp(rotate, proj_lin[0])
    key_rot, key_pull = jax.vjp(rotate, proj_lin[1])
    query_in = query_rot.astype(jnp.bfloat16).reshape(seqs, length, heads_here, 2, HEAD_DIM)
    key_in = key_rot.astype(jnp.bfloat16).reshape(seqs, length, heads_here, 2, HEAD_DIM)
    value_in = proj_lin[2].astype(jnp.bfloat16).reshape(seqs, length, heads_here, VALUE_DIM)
    heads_out, log_total = jax.vmap(attend, in_axes=(0, 0, 0, 0, None))(
        query_in, key_in, value_in, allowed, lambda_here
    )
    mixed_float, head_pull = jax.vjp(partial(head_norm, gain_vector=gain_sub), heads_out)
    mixed_rows = mixed_float.reshape(seqs, length, qw_here).astype(jnp.bfloat16)
    attn_rows, out_low = row_forward(mixed_rows, w_out_full, a_out_sel, b_rows_sel[:, 0])
    hidden = inputs_rows + attn_rows
    normed_ffn, norm_ffn_pull = jax.vjp(partial(rows_norm, gain_vector=gain_ffn), hidden)
    ffn_full = gather_rows(normed_ffn.astype(jnp.bfloat16))
    gate_lin, gate_low = column_forward(ffn_full, w_gateup_full[0], a_in_sel[:, 3], b_gateup_sel[:, 0])
    up_lin, up_low = column_forward(ffn_full, w_gateup_full[1], a_in_sel[:, 4], b_gateup_sel[:, 1])
    product_float, swiglu_pull = jax.vjp(swiglu, gate_lin, up_lin)
    product = product_float.astype(jnp.bfloat16)
    ffn_rows, down_low = row_forward(product, w_down_full, a_down_sel, b_rows_sel[:, 1])
    output = (hidden + ffn_rows).astype(jnp.bfloat16)
    row_lows = tok_sum(jnp.stack([out_low, down_low]))

    tangent = cotangent.astype(jnp.float32)

    def row_backward(grad_full, rows_here, weight, down_sel, up_sel):
        grad_float = grad_full.astype(jnp.float32)
        grad_low = adapter_scale * hp_dot(grad_float, up_sel.astype(jnp.float32), "ste,sre->str")
        grad_down = hp_dot(rows_here.astype(jnp.float32), grad_low, "std,str->sdr")
        grad_inputs = jnp.einsum(
            "ste,de->std", grad_full, weight, preferred_element_type=jnp.float32
        ) + hp_dot(grad_low, down_sel.astype(jnp.float32), "str,sdr->std")
        return grad_inputs, grad_down

    def column_backward(rows_full, entries):
        running = None
        grad_lows = []
        grads_up = []
        for grad_rows, weight, down_sel, up_sel, lowrank in entries:
            grad_float = grad_rows.astype(jnp.float32)
            grad_low = adapter_scale * hp_dot(grad_float, up_sel.astype(jnp.float32), "ste,sre->str")
            grads_up.append(adapter_scale * hp_dot(lowrank, grad_float, "str,ste->sre"))
            grad_lows.append(grad_low)
            term = jnp.einsum(
                "ste,de->std", grad_rows, weight, preferred_element_type=jnp.float32
            ) + hp_dot(grad_low, down_sel.astype(jnp.float32), "str,sdr->std")
            running = term if running is None else running + term
        return scatter_rows(running), grad_lows, grads_up

    def mine_of(values, axis):
        shape = values.shape
        split = values.reshape(
            shape[:axis] + (fsdp_count, tok_count, D // (fsdp_count * tok_count)) + shape[axis + 1 :]
        )
        return lax.dynamic_index_in_dim(split, me_tok, axis + 1, keepdims=False)

    grad_product, grad_a_down = row_backward(
        grad_ffn_full, product, w_down_full, a_down_sel, b_rows_sel[:, 1]
    )
    grad_gate, grad_up = swiglu_pull(grad_product)
    grad_ffn_rows, ffn_grad_lows, ffn_grads_up = column_backward(
        ffn_full,
        (
            (grad_gate.astype(jnp.bfloat16), w_gateup_full[0], a_in_sel[:, 3], b_gateup_sel[:, 0], gate_low),
            (grad_up.astype(jnp.bfloat16), w_gateup_full[1], a_in_sel[:, 4], b_gateup_sel[:, 1], up_low),
        ),
    )
    grad_hidden = tangent + norm_ffn_pull(grad_ffn_rows)[0]
    grad_attn_full = gather_rows(grad_hidden.astype(jnp.bfloat16))
    grad_mixed, grad_a_out = row_backward(
        grad_attn_full, mixed_rows, w_out_full, a_out_sel, b_rows_sel[:, 0]
    )
    grad_heads = head_pull(grad_mixed.reshape(seqs, length, heads_here, VALUE_DIM))[0].astype(
        jnp.bfloat16
    )
    grad_query_rot, grad_key_rot, grad_values = jax.vmap(
        attend_back, in_axes=(0, 0, 0, 0, None, 0, 0)
    )(query_in, key_in, value_in, allowed, lambda_here, log_total, grad_heads)
    grad_query = query_pull(grad_query_rot.reshape(seqs, length, qw_here))[0].astype(jnp.bfloat16)
    grad_key = key_pull(grad_key_rot.reshape(seqs, length, qw_here))[0].astype(jnp.bfloat16)
    grad_attn_rows, attn_grad_lows, attn_grads_up = column_backward(
        normed_full,
        (
            (grad_query, w_qkv_full[0], a_in_sel[:, 0], b_qkv_sel[:, 0], proj_low[0]),
            (grad_key, w_qkv_full[1], a_in_sel[:, 1], b_qkv_sel[:, 1], proj_low[1]),
            (grad_values.reshape(seqs, length, qw_here), w_qkv_full[2], a_in_sel[:, 2], b_qkv_sel[:, 2], proj_low[2]),
        ),
    )
    grad_tokens = grad_hidden + norm_attn_pull(grad_attn_rows)[0]

    grad_lows = tok_sum(jnp.stack(attn_grad_lows + ffn_grad_lows))
    grad_a_in_all = jnp.concatenate(
        [
            hp_dot(normed_full.astype(jnp.float32), grad_lows[:3], "std,pstr->psdr"),
            hp_dot(ffn_full.astype(jnp.float32), grad_lows[3:], "std,pstr->psdr"),
        ]
    )
    grad_a_in_part = mine_of(grad_a_in_all, 2)
    grad_b_rows_all = adapter_scale * jnp.stack(
        [
            hp_dot(row_lows[0], grad_attn_full.astype(jnp.float32), "str,std->srd"),
            hp_dot(row_lows[1], grad_ffn_full.astype(jnp.float32), "str,std->srd"),
        ]
    )
    grad_b_rows_part = mine_of(grad_b_rows_all, 3)

    def place(part, axis, total):
        shape = list(part.shape[1:])
        shape[axis] = total
        dense = jnp.zeros(shape, jnp.float32)
        for s in range(seqs):
            current = lax.dynamic_slice_in_dim(dense, offsets[s], RANK, axis)
            dense = lax.dynamic_update_slice_in_dim(dense, current + part[s], offsets[s], axis)
        return dense

    dense_a_in = place(jnp.moveaxis(grad_a_in_part, 1, 0), 3, COLS)
    dense_b_rows = place(jnp.moveaxis(grad_b_rows_part, 1, 0), 1, COLS)
    wide = jnp.concatenate(
        [
            jnp.moveaxis(dense_a_in, 1, 0).reshape(fsdp_count, -1),
            jnp.moveaxis(dense_b_rows, 2, 0).reshape(fsdp_count, -1),
        ],
        axis=1,
    )
    wide_sum = lax.all_to_all(wide, "fsdp", 0, 0, tiled=False).sum(0)
    a_in_block = wide_sum[: 5 * 16 * COLS].reshape(5, 16, COLS)
    b_rows_block = wide_sum[5 * 16 * COLS :].reshape(2, COLS, 16)

    dense_b_qkv = place(jnp.stack(attn_grads_up, 1), 1, COLS)
    dense_b_gateup = place(jnp.stack(ffn_grads_up, 1), 1, COLS)
    dense_a_out = place(grad_a_out, 1, COLS)
    dense_a_down = place(grad_a_down, 1, COLS)
    per = COLS // fsdp_count
    narrow = jnp.concatenate(
        [
            jnp.moveaxis(dense_b_qkv.reshape(3, fsdp_count, per, qw_here), 1, 0).reshape(fsdp_count, -1),
            jnp.moveaxis(dense_b_gateup.reshape(2, fsdp_count, per, ff_here), 1, 0).reshape(fsdp_count, -1),
            jnp.moveaxis(dense_a_out.reshape(qw_here, fsdp_count, per), 1, 0).reshape(fsdp_count, -1),
            jnp.moveaxis(dense_a_down.reshape(ff_here, fsdp_count, per), 1, 0).reshape(fsdp_count, -1),
        ],
        axis=1,
    ).astype(jnp.bfloat16)
    narrow_sum = lax.all_to_all(narrow, "fsdp", 0, 0, tiled=False).astype(jnp.float32).sum(0)
    sizes = [3 * per * qw_here, 2 * per * ff_here, qw_here * per, ff_here * per]
    cuts = [0]
    for size in sizes:
        cuts.append(cuts[-1] + size)
    b_qkv_block = narrow_sum[cuts[0] : cuts[1]].reshape(3, per, qw_here)
    b_gateup_block = narrow_sum[cuts[1] : cuts[2]].reshape(2, per, ff_here)
    a_out_block = narrow_sum[cuts[2] : cuts[3]].reshape(qw_here, per)
    a_down_block = narrow_sum[cuts[3] : cuts[4]].reshape(ff_here, per)

    return (
        output,
        grad_tokens,
        a_in_block,
        b_qkv_block,
        b_gateup_block,
        a_out_block,
        a_down_block,
        b_rows_block,
    )


def solution(mesh):
    return jax.shard_map(
        per_device,
        mesh=mesh,
        in_specs=(
            P("fsdp", "tok", None),
            P("fsdp", "tok", None),
            P("fsdp", None),
            P("fsdp"),
            P(None, "fsdp", "tok"),
            P("tok", "fsdp"),
            P(None, "fsdp", "tok"),
            P("tok", "fsdp"),
            P(),
            P(),
            P(),
            P(),
            P(None, ("fsdp", "tok"), None),
            P(None, "fsdp", "tok"),
            P(None, "fsdp", "tok"),
            P("tok", "fsdp"),
            P("tok", "fsdp"),
            P(None, None, ("fsdp", "tok")),
        ),
        out_specs=(
            P("fsdp", "tok", None),
            P("fsdp", "tok", None),
            P(None, ("fsdp", "tok"), None),
            P(None, "fsdp", "tok"),
            P(None, "fsdp", "tok"),
            P("tok", "fsdp"),
            P("tok", "fsdp"),
            P(None, None, ("fsdp", "tok")),
        ),
        check_vma=False,
    )
```

```python
from functools import partial

import jax
import jax.numpy as jnp
from jax import lax
from jax.sharding import PartitionSpec as P

D = 2048
HEAD_DIM = 128
VALUE_DIM = 256
RANK = 16
COLS = 128


highest = lax.Precision.HIGHEST
negative = -1e30
adapter_scale = 2.0
lambda_init = 0.2
rotary_base = 10000.0
row_epsilon = 1e-06
head_epsilon = 1e-05


def rows_norm(values, gain_vector):
    return (
        values
        * lax.rsqrt(jnp.mean(values * values, axis=-1, keepdims=True) + row_epsilon)
        * gain_vector
    )


def head_norm(values, gain_vector):
    scaled = values * lax.rsqrt(jnp.mean(values * values, axis=-1, keepdims=True) + head_epsilon)
    return scaled * gain_vector * (1.0 - lambda_init)


def rotary_heads(values, positions, head_dim):
    lead = values.shape[:-1]
    groups = values.reshape(lead + (-1, head_dim))
    half_dim = head_dim // 2
    frequency = rotary_base ** (-jnp.arange(half_dim, dtype=jnp.float32) / half_dim)
    angles = positions.astype(jnp.float32)[:, None] * frequency[None, :]
    cosine = jnp.cos(angles)[:, None, :]
    sine_part = jnp.sin(angles)[:, None, :]
    first_half = groups[..., :half_dim]
    second = groups[..., half_dim:]
    turned = jnp.concatenate(
        [first_half * cosine - second * sine_part, second * cosine + first_half * sine_part],
        axis=-1,
    )
    return turned.reshape(values.shape)


def swiglu(gate_rows, up_rows):
    return gate_rows * jax.nn.sigmoid(gate_rows) * up_rows


def attention_scores(query_in, key_in, allowed):
    raw_scores = jnp.einsum(
        "qhmd,khmd->hmqk", query_in, key_in, preferred_element_type=jnp.float32
    ) * query_in.shape[-1] ** (-0.5)
    return jnp.where(allowed[None, None], raw_scores, negative)


def attend(query_in, key_in, value_in, allowed, lambda_here):
    scores = attention_scores(query_in, key_in, allowed)
    row_max = jnp.max(scores, axis=-1, keepdims=True)
    log_total = row_max + jnp.log(jnp.sum(jnp.exp(scores - row_max), axis=-1, keepdims=True))
    soft_max = jnp.exp(scores - log_total)
    differ = (soft_max[:, 0] - lambda_here[:, None, None] * soft_max[:, 1]).astype(jnp.bfloat16)
    heads_out = jnp.einsum("hqk,khd->qhd", differ, value_in, preferred_element_type=jnp.float32)
    return (heads_out, log_total)


def attend_back(query_in, key_in, value_in, allowed, lambda_here, log_total, grad_heads):
    scale = query_in.shape[-1] ** (-0.5)
    scores = attention_scores(query_in, key_in, allowed)
    soft_max = jnp.exp(scores - log_total)
    differ = (soft_max[:, 0] - lambda_here[:, None, None] * soft_max[:, 1]).astype(jnp.bfloat16)
    grad_values = jnp.einsum("hqk,qhd->khd", differ, grad_heads, preferred_element_type=jnp.float32)
    grad_differ = jnp.einsum(
        "qhd,khd->hqk", grad_heads, value_in, preferred_element_type=jnp.float32
    )
    grad_soft = jnp.stack([grad_differ, -lambda_here[:, None, None] * grad_differ], axis=1)
    grad_scores = (
        soft_max * (grad_soft - jnp.sum(grad_soft * soft_max, axis=-1, keepdims=True))
    ).astype(jnp.bfloat16)
    grad_query = (
        jnp.einsum("hmqk,khmd->qhmd", grad_scores, key_in, preferred_element_type=jnp.float32)
        * scale
    )
    grad_key = (
        jnp.einsum("hmqk,qhmd->khmd", grad_scores, query_in, preferred_element_type=jnp.float32)
        * scale
    )
    return (grad_query, grad_key, grad_values.astype(jnp.bfloat16))


def xor_pairs(count, bit):
    return [(i, i ^ bit) for i in range(count)]


def tok_gather(values, axis=0):
    count = lax.axis_size("tok")
    me = lax.axis_index("tok")
    far = lax.ppermute(values, "tok", xor_pairs(count, 2))
    pair = jnp.where(
        (me & 2) == 0, jnp.stack([values, far], axis), jnp.stack([far, values], axis)
    )
    near = lax.ppermute(pair, "tok", xor_pairs(count, 1))
    full = jnp.where(
        (me & 1) == 0, jnp.stack([pair, near], axis + 1), jnp.stack([near, pair], axis + 1)
    )
    return full.reshape(values.shape[:axis] + (count,) + values.shape[axis:])


def tok_scatter(blocks, axis=0):
    count = lax.axis_size("tok")
    me = lax.axis_index("tok")
    core = me & 1
    half = (me >> 1) & 1
    split = blocks.reshape(blocks.shape[:axis] + (2, 2) + blocks.shape[axis + 1 :])
    mine = lax.dynamic_index_in_dim(split, core, axis + 1, keepdims=False)
    theirs = lax.dynamic_index_in_dim(split, 1 - core, axis + 1, keepdims=False)
    chip_sum = mine + lax.ppermute(theirs, "tok", xor_pairs(count, 1))
    keep = lax.dynamic_index_in_dim(chip_sum, half, axis, keepdims=False)
    send = lax.dynamic_index_in_dim(chip_sum, 1 - half, axis, keepdims=False)
    return keep + lax.ppermute(send, "tok", xor_pairs(count, 2))


def tok_sum(values):
    count = lax.axis_size("tok")
    chip_sum = values + lax.ppermute(values, "tok", xor_pairs(count, 1))
    return chip_sum + lax.ppermute(chip_sum, "tok", xor_pairs(count, 2))


def hp_dot(left, right, spec):
    return jnp.einsum(spec, left, right, precision=highest, preferred_element_type=jnp.float32)


def per_device(
    tokens,
    cotangent,
    segments,
    adapter_id,
    w_qkv,
    w_out,
    w_gateup,
    w_down,
    gain_attn,
    gain_ffn,
    gain_sub,
    lambda_head,
    a_in,
    b_qkv,
    b_gateup,
    a_out,
    a_down,
    b_rows,
):
    tok_count = lax.axis_size("tok")
    fsdp_count = lax.axis_size("fsdp")
    me_tok = lax.axis_index("tok")
    seqs, local_len, _ = tokens.shape
    length = local_len * tok_count
    qw_here = w_qkv.shape[2]
    ff_here = w_gateup.shape[2]
    heads_here = qw_here // VALUE_DIM
    lambda_here = lax.dynamic_slice_in_dim(lambda_head, me_tok * heads_here, heads_here)
    positions = jnp.arange(length)
    offsets = adapter_id * RANK
    fsdp_rows = w_qkv.shape[1]
    groups_per_adapter = RANK // b_qkv.shape[1]

    def fsdp_gather(values, axis):
        tiled_in = jnp.broadcast_to(values[None], (fsdp_count,) + values.shape)
        tiled_in = tiled_in.reshape((fsdp_count * values.shape[0],) + values.shape[1:])
        return lax.all_to_all(tiled_in, "fsdp", 0, axis, tiled=True)

    def packed_gather(small, axes):
        count = 1
        for name in axes:
            count *= lax.axis_size(name)
        flat = jnp.concatenate([p.reshape(-1, COLS) for p in small], axis=0)
        tiled_in = jnp.broadcast_to(flat[None], (count,) + flat.shape).reshape(-1, COLS)
        got = lax.all_to_all(tiled_in, axes, 0, 0, tiled=True).reshape((count,) + flat.shape)
        out = []
        start = 0
        for p in small:
            rows = p.size // COLS
            out.append(got[:, start : start + rows].reshape((count,) + p.shape))
            start += rows
        return out

    w_qkv_full = fsdp_gather(w_qkv, 1)
    w_qkv_full, a_in, b_rows = lax.optimization_barrier((w_qkv_full, a_in, b_rows))
    g_ain, g_brows = packed_gather([a_in, b_rows], ("fsdp", "tok"))
    g_ain, b_qkv, b_gateup, a_out, a_down = lax.optimization_barrier((g_ain, b_qkv, b_gateup, a_out, a_down))
    g_bqkv, g_bgateup, g_aout, g_adown = packed_gather([b_qkv, b_gateup, a_out, a_down], ("fsdp",))
    g_bqkv, w_out = lax.optimization_barrier((g_bqkv, w_out))
    w_out_full = fsdp_gather(w_out, 1)
    w_out_full, w_gateup = lax.optimization_barrier((w_out_full, w_gateup))
    w_gateup_full = fsdp_gather(w_gateup, 1)
    w_gateup_full, w_down = lax.optimization_barrier((w_gateup_full, w_down))
    w_down_full = fsdp_gather(w_down, 1)
    a_in_full = jnp.moveaxis(g_ain, 0, 1).reshape(5, D, COLS)
    b_rows_full = jnp.moveaxis(g_brows, 0, 2).reshape(2, COLS, D)

    def pick_cols(values, axis):
        return jnp.stack(
            [lax.dynamic_slice_in_dim(values, offsets[s], RANK, axis) for s in range(seqs)]
        )

    def pick_groups(values):
        return jnp.stack(
            [
                lax.dynamic_slice_in_dim(values, adapter_id[s] * groups_per_adapter, groups_per_adapter, 0)
                for s in range(seqs)
            ]
        )

    a_in_sel = pick_cols(a_in_full, 2)
    b_rows_sel = pick_cols(b_rows_full, 1)
    b_qkv_sel = jnp.moveaxis(pick_groups(g_bqkv), 1, 2).reshape(seqs, 3, RANK, qw_here)
    b_gateup_sel = jnp.moveaxis(pick_groups(g_bgateup), 1, 2).reshape(seqs, 2, RANK, ff_here)
    a_out_sel = jnp.moveaxis(pick_groups(g_aout), 1, 2).reshape(seqs, qw_here, RANK)
    a_down_sel = jnp.moveaxis(pick_groups(g_adown), 1, 2).reshape(seqs, ff_here, RANK)

    def gather_rows(values):
        full = tok_gather(values, 1)
        return full.reshape(seqs, length, values.shape[-1])

    def scatter_rows(values):
        return tok_scatter(values.reshape(seqs, tok_count, local_len, values.shape[-1]), 1)

    def column_forward(rows_full, weight, down_sel, up_sel):
        lowrank = jnp.einsum("std,sdr->str", rows_full, down_sel, preferred_element_type=jnp.float32)
        linear = jnp.einsum("std,de->ste", rows_full, weight, preferred_element_type=jnp.float32)
        return linear + adapter_scale * hp_dot(lowrank, up_sel.astype(jnp.float32), "str,sre->ste"), lowrank

    def row_forward(rows_here, weight, down_sel, up_sel):
        lowrank = jnp.einsum("std,sdr->str", rows_here, down_sel, preferred_element_type=jnp.float32)
        main_part = jnp.einsum("std,de->ste", rows_here, weight, preferred_element_type=jnp.float32)
        total = main_part + adapter_scale * hp_dot(lowrank, up_sel.astype(jnp.float32), "str,sre->ste")
        return scatter_rows(total), lowrank

    inputs_rows = tokens.astype(jnp.float32)
    allowed = (segments[:, :, None] == segments[:, None, :]) & (
        positions[:, None] >= positions[None, :]
    )[None]
    grad_ffn_full = gather_rows(cotangent)
    normed_rows, norm_attn_pull = jax.vjp(partial(rows_norm, gain_vector=gain_attn), inputs_rows)
    normed_full = gather_rows(normed_rows.astype(jnp.bfloat16))
    proj_lin = []
    proj_low = []
    for p in range(3):
        lin, lowr = column_forward(normed_full, w_qkv_full[p], a_in_sel[:, p], b_qkv_sel[:, p])
        proj_lin.append(lin)
        proj_low.append(lowr)
    rotate = partial(rotary_heads, positions=positions, head_dim=HEAD_DIM)
    query_rot, query_pull = jax.vjp(rotate, proj_lin[0])
    key_rot, key_pull = jax.vjp(rotate, proj_lin[1])
    query_in = query_rot.astype(jnp.bfloat16).reshape(seqs, length, heads_here, 2, HEAD_DIM)
    key_in = key_rot.astype(jnp.bfloat16).reshape(seqs, length, heads_here, 2, HEAD_DIM)
    value_in = proj_lin[2].astype(jnp.bfloat16).reshape(seqs, length, heads_here, VALUE_DIM)
    heads_out, log_total = jax.vmap(attend, in_axes=(0, 0, 0, 0, None))(
        query_in, key_in, value_in, allowed, lambda_here
    )
    mixed_float, head_pull = jax.vjp(partial(head_norm, gain_vector=gain_sub), heads_out)
    mixed_rows = mixed_float.reshape(seqs, length, qw_here).astype(jnp.bfloat16)
    attn_rows, out_low = row_forward(mixed_rows, w_out_full, a_out_sel, b_rows_sel[:, 0])
    hidden = inputs_rows + attn_rows
    normed_ffn, norm_ffn_pull = jax.vjp(partial(rows_norm, gain_vector=gain_ffn), hidden)
    ffn_full = gather_rows(normed_ffn.astype(jnp.bfloat16))
    gate_lin, gate_low = column_forward(ffn_full, w_gateup_full[0], a_in_sel[:, 3], b_gateup_sel[:, 0])
    up_lin, up_low = column_forward(ffn_full, w_gateup_full[1], a_in_sel[:, 4], b_gateup_sel[:, 1])
    product_float, swiglu_pull = jax.vjp(swiglu, gate_lin, up_lin)
    product = product_float.astype(jnp.bfloat16)
    ffn_rows, down_low = row_forward(product, w_down_full, a_down_sel, b_rows_sel[:, 1])
    output = (hidden + ffn_rows).astype(jnp.bfloat16)
    row_lows = tok_sum(jnp.stack([out_low, down_low]))

    tangent = cotangent.astype(jnp.float32)

    def row_backward(grad_full, rows_here, weight, down_sel, up_sel):
        grad_float = grad_full.astype(jnp.float32)
        grad_low = adapter_scale * hp_dot(grad_float, up_sel.astype(jnp.float32), "ste,sre->str")
        grad_down = hp_dot(rows_here.astype(jnp.float32), grad_low, "std,str->sdr")
        grad_inputs = jnp.einsum(
            "ste,de->std", grad_full, weight, preferred_element_type=jnp.float32
        ) + hp_dot(grad_low, down_sel.astype(jnp.float32), "str,sdr->std")
        return grad_inputs, grad_down

    def column_backward(rows_full, entries):
        running = None
        grad_lows = []
        grads_up = []
        for grad_rows, weight, down_sel, up_sel, lowrank in entries:
            grad_float = grad_rows.astype(jnp.float32)
            grad_low = adapter_scale * hp_dot(grad_float, up_sel.astype(jnp.float32), "ste,sre->str")
            grads_up.append(adapter_scale * hp_dot(lowrank, grad_float, "str,ste->sre"))
            grad_lows.append(grad_low)
            term = jnp.einsum(
                "ste,de->std", grad_rows, weight, preferred_element_type=jnp.float32
            ) + hp_dot(grad_low, down_sel.astype(jnp.float32), "str,sdr->std")
            running = term if running is None else running + term
        return scatter_rows(running), grad_lows, grads_up

    def mine_of(values, axis):
        shape = values.shape
        split = values.reshape(
            shape[:axis] + (fsdp_count, tok_count, D // (fsdp_count * tok_count)) + shape[axis + 1 :]
        )
        return lax.dynamic_index_in_dim(split, me_tok, axis + 1, keepdims=False)

    grad_product, grad_a_down = row_backward(
        grad_ffn_full, product, w_down_full, a_down_sel, b_rows_sel[:, 1]
    )
    grad_gate, grad_up = swiglu_pull(grad_product)
    grad_ffn_rows, ffn_grad_lows, ffn_grads_up = column_backward(
        ffn_full,
        (
            (grad_gate.astype(jnp.bfloat16), w_gateup_full[0], a_in_sel[:, 3], b_gateup_sel[:, 0], gate_low),
            (grad_up.astype(jnp.bfloat16), w_gateup_full[1], a_in_sel[:, 4], b_gateup_sel[:, 1], up_low),
        ),
    )
    grad_hidden = tangent + norm_ffn_pull(grad_ffn_rows)[0]
    grad_attn_full = gather_rows(grad_hidden.astype(jnp.bfloat16))
    grad_mixed, grad_a_out = row_backward(
        grad_attn_full, mixed_rows, w_out_full, a_out_sel, b_rows_sel[:, 0]
    )
    grad_heads = head_pull(grad_mixed.reshape(seqs, length, heads_here, VALUE_DIM))[0].astype(
        jnp.bfloat16
    )
    grad_query_rot, grad_key_rot, grad_values = jax.vmap(
        attend_back, in_axes=(0, 0, 0, 0, None, 0, 0)
    )(query_in, key_in, value_in, allowed, lambda_here, log_total, grad_heads)
    grad_query = query_pull(grad_query_rot.reshape(seqs, length, qw_here))[0].astype(jnp.bfloat16)
    grad_key = key_pull(grad_key_rot.reshape(seqs, length, qw_here))[0].astype(jnp.bfloat16)
    grad_attn_rows, attn_grad_lows, attn_grads_up = column_backward(
        normed_full,
        (
            (grad_query, w_qkv_full[0], a_in_sel[:, 0], b_qkv_sel[:, 0], proj_low[0]),
            (grad_key, w_qkv_full[1], a_in_sel[:, 1], b_qkv_sel[:, 1], proj_low[1]),
            (grad_values.reshape(seqs, length, qw_here), w_qkv_full[2], a_in_sel[:, 2], b_qkv_sel[:, 2], proj_low[2]),
        ),
    )
    grad_tokens = grad_hidden + norm_attn_pull(grad_attn_rows)[0]

    grad_lows = tok_sum(jnp.stack(attn_grad_lows + ffn_grad_lows))
    grad_a_in_all = jnp.concatenate(
        [
            hp_dot(normed_full.astype(jnp.float32), grad_lows[:3], "std,pstr->psdr"),
            hp_dot(ffn_full.astype(jnp.float32), grad_lows[3:], "std,pstr->psdr"),
        ]
    )
    grad_a_in_part = mine_of(grad_a_in_all, 2)
    grad_b_rows_all = adapter_scale * jnp.stack(
        [
            hp_dot(row_lows[0], grad_attn_full.astype(jnp.float32), "str,std->srd"),
            hp_dot(row_lows[1], grad_ffn_full.astype(jnp.float32), "str,std->srd"),
        ]
    )
    grad_b_rows_part = mine_of(grad_b_rows_all, 3)

    def place(part, axis, total):
        shape = list(part.shape[1:])
        shape[axis] = total
        dense = jnp.zeros(shape, jnp.float32)
        for s in range(seqs):
            current = lax.dynamic_slice_in_dim(dense, offsets[s], RANK, axis)
            dense = lax.dynamic_update_slice_in_dim(dense, current + part[s], offsets[s], axis)
        return dense

    dense_a_in = place(jnp.moveaxis(grad_a_in_part, 1, 0), 3, COLS)
    dense_b_rows = place(jnp.moveaxis(grad_b_rows_part, 1, 0), 1, COLS)
    wide = jnp.concatenate(
        [
            jnp.moveaxis(dense_a_in, 1, 0).reshape(fsdp_count, -1),
            jnp.moveaxis(dense_b_rows, 2, 0).reshape(fsdp_count, -1),
        ],
        axis=1,
    )
    wide_sum = lax.all_to_all(wide, "fsdp", 0, 0, tiled=False).sum(0)
    a_in_block = wide_sum[: 5 * 16 * COLS].reshape(5, 16, COLS)
    b_rows_block = wide_sum[5 * 16 * COLS :].reshape(2, COLS, 16)

    dense_b_qkv = place(jnp.stack(attn_grads_up, 1), 1, COLS)
    dense_b_gateup = place(jnp.stack(ffn_grads_up, 1), 1, COLS)
    dense_a_out = place(grad_a_out, 1, COLS)
    dense_a_down = place(grad_a_down, 1, COLS)
    per = COLS // fsdp_count
    narrow = jnp.concatenate(
        [
            jnp.moveaxis(dense_b_qkv.reshape(3, fsdp_count, per, qw_here), 1, 0).reshape(fsdp_count, -1),
            jnp.moveaxis(dense_b_gateup.reshape(2, fsdp_count, per, ff_here), 1, 0).reshape(fsdp_count, -1),
            jnp.moveaxis(dense_a_out.reshape(qw_here, fsdp_count, per), 1, 0).reshape(fsdp_count, -1),
            jnp.moveaxis(dense_a_down.reshape(ff_here, fsdp_count, per), 1, 0).reshape(fsdp_count, -1),
        ],
        axis=1,
    ).astype(jnp.bfloat16)
    narrow_sum = lax.all_to_all(narrow, "fsdp", 0, 0, tiled=False).astype(jnp.float32).sum(0)
    sizes = [3 * per * qw_here, 2 * per * ff_here, qw_here * per, ff_here * per]
    cuts = [0]
    for size in sizes:
        cuts.append(cuts[-1] + size)
    b_qkv_block = narrow_sum[cuts[0] : cuts[1]].reshape(3, per, qw_here)
    b_gateup_block = narrow_sum[cuts[1] : cuts[2]].reshape(2, per, ff_here)
    a_out_block = narrow_sum[cuts[2] : cuts[3]].reshape(qw_here, per)
    a_down_block = narrow_sum[cuts[3] : cuts[4]].reshape(ff_here, per)

    return (
        output,
        grad_tokens,
        a_in_block,
        b_qkv_block,
        b_gateup_block,
        a_out_block,
        a_down_block,
        b_rows_block,
    )


def solution(mesh):
    return jax.shard_map(
        per_device,
        mesh=mesh,
        in_specs=(
            P("fsdp", "tok", None),
            P("fsdp", "tok", None),
            P("fsdp", None),
            P("fsdp"),
            P(None, "fsdp", "tok"),
            P("tok", "fsdp"),
            P(None, "fsdp", "tok"),
            P("tok", "fsdp"),
            P(),
            P(),
            P(),
            P(),
            P(None, ("fsdp", "tok"), None),
            P(None, "fsdp", "tok"),
            P(None, "fsdp", "tok"),
            P("tok", "fsdp"),
            P("tok", "fsdp"),
            P(None, None, ("fsdp", "tok")),
        ),
        out_specs=(
            P("fsdp", "tok", None),
            P("fsdp", "tok", None),
            P(None, ("fsdp", "tok"), None),
            P(None, "fsdp", "tok"),
            P(None, "fsdp", "tok"),
            P("tok", "fsdp"),
            P("tok", "fsdp"),
            P(None, None, ("fsdp", "tok")),
        ),
        check_vma=False,
    )
```

```python
from functools import partial

import jax
import jax.numpy as jnp
from jax import lax
from jax.experimental import pallas as pl
from jax.experimental.pallas import tpu as pltpu
from jax.sharding import PartitionSpec as P

D = 2048
HEAD_DIM = 128
VALUE_DIM = 256
RANK = 16
COLS = 128


highest = lax.Precision.HIGHEST
negative = -1e30
adapter_scale = 2.0
lambda_init = 0.2
rotary_base = 10000.0
row_epsilon = 1e-06
head_epsilon = 1e-05


def rows_norm(values, gain_vector):
    return (
        values
        * lax.rsqrt(jnp.mean(values * values, axis=-1, keepdims=True) + row_epsilon)
        * gain_vector
    )


def head_norm(values, gain_vector):
    scaled = values * lax.rsqrt(jnp.mean(values * values, axis=-1, keepdims=True) + head_epsilon)
    return scaled * gain_vector * (1.0 - lambda_init)


def rotary_heads(values, positions, head_dim):
    lead = values.shape[:-1]
    groups = values.reshape(lead + (-1, head_dim))
    half_dim = head_dim // 2
    frequency = rotary_base ** (-jnp.arange(half_dim, dtype=jnp.float32) / half_dim)
    angles = positions.astype(jnp.float32)[:, None] * frequency[None, :]
    cosine = jnp.cos(angles)[:, None, :]
    sine_part = jnp.sin(angles)[:, None, :]
    first_half = groups[..., :half_dim]
    second = groups[..., half_dim:]
    turned = jnp.concatenate(
        [first_half * cosine - second * sine_part, second * cosine + first_half * sine_part],
        axis=-1,
    )
    return turned.reshape(values.shape)


def swiglu(gate_rows, up_rows):
    return gate_rows * jax.nn.sigmoid(gate_rows) * up_rows


def attention_scores(query_in, key_in, allowed):
    raw_scores = jnp.einsum(
        "qhmd,khmd->hmqk", query_in, key_in, preferred_element_type=jnp.float32
    ) * query_in.shape[-1] ** (-0.5)
    return jnp.where(allowed[None, None], raw_scores, negative)


def attend(query_in, key_in, value_in, allowed, lambda_here):
    scores = attention_scores(query_in, key_in, allowed)
    row_max = jnp.max(scores, axis=-1, keepdims=True)
    log_total = row_max + jnp.log(jnp.sum(jnp.exp(scores - row_max), axis=-1, keepdims=True))
    soft_max = jnp.exp(scores - log_total)
    differ = (soft_max[:, 0] - lambda_here[:, None, None] * soft_max[:, 1]).astype(jnp.bfloat16)
    heads_out = jnp.einsum("hqk,khd->qhd", differ, value_in, preferred_element_type=jnp.float32)
    return (heads_out, log_total)


def attend_back(query_in, key_in, value_in, allowed, lambda_here, log_total, grad_heads):
    scale = query_in.shape[-1] ** (-0.5)
    scores = attention_scores(query_in, key_in, allowed)
    soft_max = jnp.exp(scores - log_total)
    differ = (soft_max[:, 0] - lambda_here[:, None, None] * soft_max[:, 1]).astype(jnp.bfloat16)
    grad_values = jnp.einsum("hqk,qhd->khd", differ, grad_heads, preferred_element_type=jnp.float32)
    grad_differ = jnp.einsum(
        "qhd,khd->hqk", grad_heads, value_in, preferred_element_type=jnp.float32
    )
    grad_soft = jnp.stack([grad_differ, -lambda_here[:, None, None] * grad_differ], axis=1)
    grad_scores = (
        soft_max * (grad_soft - jnp.sum(grad_soft * soft_max, axis=-1, keepdims=True))
    ).astype(jnp.bfloat16)
    grad_query = (
        jnp.einsum("hmqk,khmd->qhmd", grad_scores, key_in, preferred_element_type=jnp.float32)
        * scale
    )
    grad_key = (
        jnp.einsum("hmqk,qhmd->khmd", grad_scores, query_in, preferred_element_type=jnp.float32)
        * scale
    )
    return (grad_query, grad_key, grad_values.astype(jnp.bfloat16))


def _colgrad_kernel(e_ref, w_ref, el_ref, at_ref, o_ref, acc_ref):
    p = pl.program_id(2)

    @pl.when(p == 0)
    def _():
        acc_ref[...] = jnp.zeros_like(acc_ref)

    acc_ref[...] += lax.dot_general(
        e_ref[...], w_ref[...], (((1,), (1,)), ((), ())), preferred_element_type=jnp.float32
    )
    acc_ref[...] += jnp.dot(
        el_ref[...], at_ref[...].astype(jnp.float32),
        precision=lax.Precision.HIGHEST, preferred_element_type=jnp.float32,
    )

    @pl.when(p == pl.num_programs(2) - 1)
    def _():
        o_ref[...] = acc_ref[...]

def column_input_grad(e_all, w_all, el_all, at_all, tile=512):
    projs, seqs, length, width = e_all.shape
    model = w_all.shape[1]
    rank = el_all.shape[-1]
    return pl.pallas_call(
        _colgrad_kernel,
        out_shape=jax.ShapeDtypeStruct((seqs, length, model), jnp.float32),
        grid=(seqs, model // tile, projs),
        in_specs=[
            pl.BlockSpec((None, None, length, width), lambda s, j, p: (p, s, 0, 0)),
            pl.BlockSpec((None, tile, width), lambda s, j, p: (p, j, 0)),
            pl.BlockSpec((None, None, length, rank), lambda s, j, p: (p, s, 0, 0)),
            pl.BlockSpec((None, None, rank, tile), lambda s, j, p: (p, s, 0, j)),
        ],
        out_specs=pl.BlockSpec((None, length, tile), lambda s, j, p: (s, 0, j)),
        scratch_shapes=[pltpu.VMEM((length, tile), jnp.float32)],
        compiler_params=pltpu.CompilerParams(
            dimension_semantics=("parallel", "parallel", "arbitrary")
        ),
        cost_estimate=pl.CostEstimate(
            flops=2 * projs * seqs * length * model * (width + rank),
            transcendentals=0,
            bytes_accessed=2 * (e_all.size + seqs * w_all.size) + 4 * seqs * length * model,
        ),
    )(e_all, w_all, el_all, at_all)


def xor_pairs(count, bit):
    return [(i, i ^ bit) for i in range(count)]


def tok_gather(values, axis=0):
    count = lax.axis_size("tok")
    me = lax.axis_index("tok")
    far = lax.ppermute(values, "tok", xor_pairs(count, 2))
    pair = jnp.where(
        (me & 2) == 0, jnp.stack([values, far], axis), jnp.stack([far, values], axis)
    )
    near = lax.ppermute(pair, "tok", xor_pairs(count, 1))
    full = jnp.where(
        (me & 1) == 0, jnp.stack([pair, near], axis + 1), jnp.stack([near, pair], axis + 1)
    )
    return full.reshape(values.shape[:axis] + (count,) + values.shape[axis:])


def tok_scatter(blocks, axis=0):
    count = lax.axis_size("tok")
    me = lax.axis_index("tok")
    core = me & 1
    half = (me >> 1) & 1
    split = blocks.reshape(blocks.shape[:axis] + (2, 2) + blocks.shape[axis + 1 :])
    mine = lax.dynamic_index_in_dim(split, core, axis + 1, keepdims=False)
    theirs = lax.dynamic_index_in_dim(split, 1 - core, axis + 1, keepdims=False)
    chip_sum = mine + lax.ppermute(theirs, "tok", xor_pairs(count, 1))
    keep = lax.dynamic_index_in_dim(chip_sum, half, axis, keepdims=False)
    send = lax.dynamic_index_in_dim(chip_sum, 1 - half, axis, keepdims=False)
    return keep + lax.ppermute(send, "tok", xor_pairs(count, 2))


def tok_sum(values):
    count = lax.axis_size("tok")
    chip_sum = values + lax.ppermute(values, "tok", xor_pairs(count, 1))
    return chip_sum + lax.ppermute(chip_sum, "tok", xor_pairs(count, 2))


def hp_dot(left, right, spec):
    return jnp.einsum(spec, left, right, precision=highest, preferred_element_type=jnp.float32)


def per_device(
    tokens,
    cotangent,
    segments,
    adapter_id,
    w_qkv,
    w_out,
    w_gateup,
    w_down,
    gain_attn,
    gain_ffn,
    gain_sub,
    lambda_head,
    a_in,
    b_qkv,
    b_gateup,
    a_out,
    a_down,
    b_rows,
):
    tok_count = lax.axis_size("tok")
    fsdp_count = lax.axis_size("fsdp")
    me_tok = lax.axis_index("tok")
    seqs, local_len, _ = tokens.shape
    length = local_len * tok_count
    qw_here = w_qkv.shape[2]
    ff_here = w_gateup.shape[2]
    heads_here = qw_here // VALUE_DIM
    lambda_here = lax.dynamic_slice_in_dim(lambda_head, me_tok * heads_here, heads_here)
    positions = jnp.arange(length)
    offsets = adapter_id * RANK
    fsdp_rows = w_qkv.shape[1]
    groups_per_adapter = RANK // b_qkv.shape[1]

    def fsdp_gather(values, axis):
        tiled_in = jnp.broadcast_to(values[None], (fsdp_count,) + values.shape)
        tiled_in = tiled_in.reshape((fsdp_count * values.shape[0],) + values.shape[1:])
        return lax.all_to_all(tiled_in, "fsdp", 0, axis, tiled=True)

    def packed_gather(small, axes):
        count = 1
        for name in axes:
            count *= lax.axis_size(name)
        flat = jnp.concatenate([p.reshape(-1, COLS) for p in small], axis=0)
        tiled_in = jnp.broadcast_to(flat[None], (count,) + flat.shape).reshape(-1, COLS)
        got = lax.all_to_all(tiled_in, axes, 0, 0, tiled=True).reshape((count,) + flat.shape)
        out = []
        start = 0
        for p in small:
            rows = p.size // COLS
            out.append(got[:, start : start + rows].reshape((count,) + p.shape))
            start += rows
        return out

    w_qkv_full = fsdp_gather(w_qkv, 1)
    w_qkv_full, a_in, b_rows = lax.optimization_barrier((w_qkv_full, a_in, b_rows))
    g_ain, g_brows = packed_gather([a_in, b_rows], ("fsdp", "tok"))
    g_ain, b_qkv, b_gateup, a_out, a_down = lax.optimization_barrier((g_ain, b_qkv, b_gateup, a_out, a_down))
    g_bqkv, g_bgateup, g_aout, g_adown = packed_gather([b_qkv, b_gateup, a_out, a_down], ("fsdp",))
    g_bqkv, w_out = lax.optimization_barrier((g_bqkv, w_out))
    w_out_full = fsdp_gather(w_out, 1)
    w_out_full, w_gateup = lax.optimization_barrier((w_out_full, w_gateup))
    w_gateup_full = fsdp_gather(w_gateup, 1)
    w_gateup_full, w_down = lax.optimization_barrier((w_gateup_full, w_down))
    w_down_full = fsdp_gather(w_down, 1)
    a_in_full = jnp.moveaxis(g_ain, 0, 1).reshape(5, D, COLS)
    b_rows_full = jnp.moveaxis(g_brows, 0, 2).reshape(2, COLS, D)

    def pick_cols(values, axis):
        return jnp.stack(
            [lax.dynamic_slice_in_dim(values, offsets[s], RANK, axis) for s in range(seqs)]
        )

    def pick_groups(values):
        return jnp.stack(
            [
                lax.dynamic_slice_in_dim(values, adapter_id[s] * groups_per_adapter, groups_per_adapter, 0)
                for s in range(seqs)
            ]
        )

    a_in_sel = pick_cols(a_in_full, 2)
    b_rows_sel = pick_cols(b_rows_full, 1)
    b_qkv_sel = jnp.moveaxis(pick_groups(g_bqkv), 1, 2).reshape(seqs, 3, RANK, qw_here)
    b_gateup_sel = jnp.moveaxis(pick_groups(g_bgateup), 1, 2).reshape(seqs, 2, RANK, ff_here)
    a_out_sel = jnp.moveaxis(pick_groups(g_aout), 1, 2).reshape(seqs, qw_here, RANK)
    a_down_sel = jnp.moveaxis(pick_groups(g_adown), 1, 2).reshape(seqs, ff_here, RANK)

    def gather_rows(values):
        full = tok_gather(values, 1)
        return full.reshape(seqs, length, values.shape[-1])

    def scatter_rows(values):
        return tok_scatter(values.reshape(seqs, tok_count, local_len, values.shape[-1]), 1)

    def column_forward(rows_full, weight, down_sel, up_sel):
        lowrank = jnp.einsum("std,sdr->str", rows_full, down_sel, preferred_element_type=jnp.float32)
        linear = jnp.einsum("std,de->ste", rows_full, weight, preferred_element_type=jnp.float32)
        return linear + adapter_scale * hp_dot(lowrank, up_sel.astype(jnp.float32), "str,sre->ste"), lowrank

    def row_forward(rows_here, weight, down_sel, up_sel):
        lowrank = jnp.einsum("std,sdr->str", rows_here, down_sel, preferred_element_type=jnp.float32)
        main_part = jnp.einsum("std,de->ste", rows_here, weight, preferred_element_type=jnp.float32)
        total = main_part + adapter_scale * hp_dot(lowrank, up_sel.astype(jnp.float32), "str,sre->ste")
        return scatter_rows(total), lowrank

    inputs_rows = tokens.astype(jnp.float32)
    allowed = (segments[:, :, None] == segments[:, None, :]) & (
        positions[:, None] >= positions[None, :]
    )[None]
    grad_ffn_full = gather_rows(cotangent)
    normed_rows, norm_attn_pull = jax.vjp(partial(rows_norm, gain_vector=gain_attn), inputs_rows)
    normed_full = gather_rows(normed_rows.astype(jnp.bfloat16))
    proj_lin = []
    proj_low = []
    for p in range(3):
        lin, lowr = column_forward(normed_full, w_qkv_full[p], a_in_sel[:, p], b_qkv_sel[:, p])
        proj_lin.append(lin)
        proj_low.append(lowr)
    rotate = partial(rotary_heads, positions=positions, head_dim=HEAD_DIM)
    query_rot, query_pull = jax.vjp(rotate, proj_lin[0])
    key_rot, key_pull = jax.vjp(rotate, proj_lin[1])
    query_in = query_rot.astype(jnp.bfloat16).reshape(seqs, length, heads_here, 2, HEAD_DIM)
    key_in = key_rot.astype(jnp.bfloat16).reshape(seqs, length, heads_here, 2, HEAD_DIM)
    value_in = proj_lin[2].astype(jnp.bfloat16).reshape(seqs, length, heads_here, VALUE_DIM)
    heads_out, log_total = jax.vmap(attend, in_axes=(0, 0, 0, 0, None))(
        query_in, key_in, value_in, allowed, lambda_here
    )
    mixed_float, head_pull = jax.vjp(partial(head_norm, gain_vector=gain_sub), heads_out)
    mixed_rows = mixed_float.reshape(seqs, length, qw_here).astype(jnp.bfloat16)
    attn_rows, out_low = row_forward(mixed_rows, w_out_full, a_out_sel, b_rows_sel[:, 0])
    hidden = inputs_rows + attn_rows
    normed_ffn, norm_ffn_pull = jax.vjp(partial(rows_norm, gain_vector=gain_ffn), hidden)
    ffn_full = gather_rows(normed_ffn.astype(jnp.bfloat16))
    gate_lin, gate_low = column_forward(ffn_full, w_gateup_full[0], a_in_sel[:, 3], b_gateup_sel[:, 0])
    up_lin, up_low = column_forward(ffn_full, w_gateup_full[1], a_in_sel[:, 4], b_gateup_sel[:, 1])
    product_float, swiglu_pull = jax.vjp(swiglu, gate_lin, up_lin)
    product = product_float.astype(jnp.bfloat16)
    ffn_rows, down_low = row_forward(product, w_down_full, a_down_sel, b_rows_sel[:, 1])
    output = (hidden + ffn_rows).astype(jnp.bfloat16)
    row_lows = tok_sum(jnp.stack([out_low, down_low]))

    tangent = cotangent.astype(jnp.float32)

    def row_backward(grad_full, rows_here, weight, down_sel, up_sel):
        grad_float = grad_full.astype(jnp.float32)
        grad_low = adapter_scale * hp_dot(grad_float, up_sel.astype(jnp.float32), "ste,sre->str")
        grad_down = hp_dot(rows_here.astype(jnp.float32), grad_low, "std,str->sdr")
        grad_inputs = jnp.einsum(
            "ste,de->std", grad_full, weight, preferred_element_type=jnp.float32
        ) + hp_dot(grad_low, down_sel.astype(jnp.float32), "str,sdr->std")
        return grad_inputs, grad_down

    def column_backward(weights, downs_t, entries):
        grad_lows = []
        grads_up = []
        for grad_rows, up_sel, lowrank in entries:
            grad_float = grad_rows.astype(jnp.float32)
            grad_lows.append(
                adapter_scale * hp_dot(grad_float, up_sel.astype(jnp.float32), "ste,sre->str")
            )
            grads_up.append(adapter_scale * hp_dot(lowrank, grad_float, "str,ste->sre"))
        running = column_input_grad(
            jnp.stack([entry[0] for entry in entries]), weights, jnp.stack(grad_lows), downs_t
        )
        return scatter_rows(running), grad_lows, grads_up

    def mine_of(values, axis):
        shape = values.shape
        split = values.reshape(
            shape[:axis] + (fsdp_count, tok_count, D // (fsdp_count * tok_count)) + shape[axis + 1 :]
        )
        return lax.dynamic_index_in_dim(split, me_tok, axis + 1, keepdims=False)

    grad_product, grad_a_down = row_backward(
        grad_ffn_full, product, w_down_full, a_down_sel, b_rows_sel[:, 1]
    )
    grad_gate, grad_up = swiglu_pull(grad_product)
    grad_ffn_rows, ffn_grad_lows, ffn_grads_up = column_backward(
        w_gateup_full,
        jnp.transpose(a_in_sel[:, 3:5], (1, 0, 3, 2)),
        (
            (grad_gate.astype(jnp.bfloat16), b_gateup_sel[:, 0], gate_low),
            (grad_up.astype(jnp.bfloat16), b_gateup_sel[:, 1], up_low),
        ),
    )
    grad_hidden = tangent + norm_ffn_pull(grad_ffn_rows)[0]
    grad_attn_full = gather_rows(grad_hidden.astype(jnp.bfloat16))
    grad_mixed, grad_a_out = row_backward(
        grad_attn_full, mixed_rows, w_out_full, a_out_sel, b_rows_sel[:, 0]
    )
    grad_heads = head_pull(grad_mixed.reshape(seqs, length, heads_here, VALUE_DIM))[0].astype(
        jnp.bfloat16
    )
    grad_query_rot, grad_key_rot, grad_values = jax.vmap(
        attend_back, in_axes=(0, 0, 0, 0, None, 0, 0)
    )(query_in, key_in, value_in, allowed, lambda_here, log_total, grad_heads)
    grad_query = query_pull(grad_query_rot.reshape(seqs, length, qw_here))[0].astype(jnp.bfloat16)
    grad_key = key_pull(grad_key_rot.reshape(seqs, length, qw_here))[0].astype(jnp.bfloat16)
    grad_attn_rows, attn_grad_lows, attn_grads_up = column_backward(
        w_qkv_full,
        jnp.transpose(a_in_sel[:, 0:3], (1, 0, 3, 2)),
        (
            (grad_query, b_qkv_sel[:, 0], proj_low[0]),
            (grad_key, b_qkv_sel[:, 1], proj_low[1]),
            (grad_values.reshape(seqs, length, qw_here), b_qkv_sel[:, 2], proj_low[2]),
        ),
    )
    grad_tokens = grad_hidden + norm_attn_pull(grad_attn_rows)[0]

    grad_lows = tok_sum(jnp.stack(attn_grad_lows + ffn_grad_lows))
    grad_a_in_all = jnp.concatenate(
        [
            hp_dot(normed_full.astype(jnp.float32), grad_lows[:3], "std,pstr->psdr"),
            hp_dot(ffn_full.astype(jnp.float32), grad_lows[3:], "std,pstr->psdr"),
        ]
    )
    grad_a_in_part = mine_of(grad_a_in_all, 2)
    grad_b_rows_all = adapter_scale * jnp.stack(
        [
            hp_dot(row_lows[0], grad_attn_full.astype(jnp.float32), "str,std->srd"),
            hp_dot(row_lows[1], grad_ffn_full.astype(jnp.float32), "str,std->srd"),
        ]
    )
    grad_b_rows_part = mine_of(grad_b_rows_all, 3)

    def place(part, axis, total):
        shape = list(part.shape[1:])
        shape[axis] = total
        dense = jnp.zeros(shape, jnp.float32)
        for s in range(seqs):
            current = lax.dynamic_slice_in_dim(dense, offsets[s], RANK, axis)
            dense = lax.dynamic_update_slice_in_dim(dense, current + part[s], offsets[s], axis)
        return dense

    dense_a_in = place(jnp.moveaxis(grad_a_in_part, 1, 0), 3, COLS)
    dense_b_rows = place(jnp.moveaxis(grad_b_rows_part, 1, 0), 1, COLS)
    wide = jnp.concatenate(
        [
            jnp.moveaxis(dense_a_in, 1, 0).reshape(fsdp_count, -1),
            jnp.moveaxis(dense_b_rows, 2, 0).reshape(fsdp_count, -1),
        ],
        axis=1,
    )
    wide_sum = lax.all_to_all(wide, "fsdp", 0, 0, tiled=False).sum(0)
    a_in_block = wide_sum[: 5 * 16 * COLS].reshape(5, 16, COLS)
    b_rows_block = wide_sum[5 * 16 * COLS :].reshape(2, COLS, 16)

    dense_b_qkv = place(jnp.stack(attn_grads_up, 1), 1, COLS)
    dense_b_gateup = place(jnp.stack(ffn_grads_up, 1), 1, COLS)
    dense_a_out = place(grad_a_out, 1, COLS)
    dense_a_down = place(grad_a_down, 1, COLS)
    per = COLS // fsdp_count
    narrow = jnp.concatenate(
        [
            jnp.moveaxis(dense_b_qkv.reshape(3, fsdp_count, per, qw_here), 1, 0).reshape(fsdp_count, -1),
            jnp.moveaxis(dense_b_gateup.reshape(2, fsdp_count, per, ff_here), 1, 0).reshape(fsdp_count, -1),
            jnp.moveaxis(dense_a_out.reshape(qw_here, fsdp_count, per), 1, 0).reshape(fsdp_count, -1),
            jnp.moveaxis(dense_a_down.reshape(ff_here, fsdp_count, per), 1, 0).reshape(fsdp_count, -1),
        ],
        axis=1,
    ).astype(jnp.bfloat16)
    narrow_sum = lax.all_to_all(narrow, "fsdp", 0, 0, tiled=False).astype(jnp.float32).sum(0)
    sizes = [3 * per * qw_here, 2 * per * ff_here, qw_here * per, ff_here * per]
    cuts = [0]
    for size in sizes:
        cuts.append(cuts[-1] + size)
    b_qkv_block = narrow_sum[cuts[0] : cuts[1]].reshape(3, per, qw_here)
    b_gateup_block = narrow_sum[cuts[1] : cuts[2]].reshape(2, per, ff_here)
    a_out_block = narrow_sum[cuts[2] : cuts[3]].reshape(qw_here, per)
    a_down_block = narrow_sum[cuts[3] : cuts[4]].reshape(ff_here, per)

    return (
        output,
        grad_tokens,
        a_in_block,
        b_qkv_block,
        b_gateup_block,
        a_out_block,
        a_down_block,
        b_rows_block,
    )


def solution(mesh):
    return jax.shard_map(
        per_device,
        mesh=mesh,
        in_specs=(
            P("fsdp", "tok", None),
            P("fsdp", "tok", None),
            P("fsdp", None),
            P("fsdp"),
            P(None, "fsdp", "tok"),
            P("tok", "fsdp"),
            P(None, "fsdp", "tok"),
            P("tok", "fsdp"),
            P(),
            P(),
            P(),
            P(),
            P(None, ("fsdp", "tok"), None),
            P(None, "fsdp", "tok"),
            P(None, "fsdp", "tok"),
            P("tok", "fsdp"),
            P("tok", "fsdp"),
            P(None, None, ("fsdp", "tok")),
        ),
        out_specs=(
            P("fsdp", "tok", None),
            P("fsdp", "tok", None),
            P(None, ("fsdp", "tok"), None),
            P(None, "fsdp", "tok"),
            P(None, "fsdp", "tok"),
            P("tok", "fsdp"),
            P("tok", "fsdp"),
            P(None, None, ("fsdp", "tok")),
        ),
        check_vma=False,
    )
```

```python
from functools import partial

import jax
import jax.numpy as jnp
from jax import lax
from jax.sharding import PartitionSpec as P

D = 2048
HEAD_DIM = 128
VALUE_DIM = 256
RANK = 16
COLS = 128


highest = lax.Precision.HIGHEST
negative = -1e30
adapter_scale = 2.0
lambda_init = 0.2
rotary_base = 10000.0
row_epsilon = 1e-06
head_epsilon = 1e-05


def rows_norm(values, gain_vector):
    return (
        values
        * lax.rsqrt(jnp.mean(values * values, axis=-1, keepdims=True) + row_epsilon)
        * gain_vector
    )


def head_norm(values, gain_vector):
    scaled = values * lax.rsqrt(jnp.mean(values * values, axis=-1, keepdims=True) + head_epsilon)
    return scaled * gain_vector * (1.0 - lambda_init)


def rotary_heads(values, positions, head_dim):
    lead = values.shape[:-1]
    groups = values.reshape(lead + (-1, head_dim))
    half_dim = head_dim // 2
    frequency = rotary_base ** (-jnp.arange(half_dim, dtype=jnp.float32) / half_dim)
    angles = positions.astype(jnp.float32)[:, None] * frequency[None, :]
    cosine = jnp.cos(angles)[:, None, :]
    sine_part = jnp.sin(angles)[:, None, :]
    first_half = groups[..., :half_dim]
    second = groups[..., half_dim:]
    turned = jnp.concatenate(
        [first_half * cosine - second * sine_part, second * cosine + first_half * sine_part],
        axis=-1,
    )
    return turned.reshape(values.shape)


def swiglu(gate_rows, up_rows):
    return gate_rows * jax.nn.sigmoid(gate_rows) * up_rows


def attention_scores(query_in, key_in, allowed):
    raw_scores = jnp.einsum(
        "qhmd,khmd->hmqk", query_in, key_in, preferred_element_type=jnp.float32
    ) * query_in.shape[-1] ** (-0.5)
    return jnp.where(allowed[None, None], raw_scores, negative)


def attend(query_in, key_in, value_in, allowed, lambda_here):
    scores = attention_scores(query_in, key_in, allowed)
    row_max = jnp.max(scores, axis=-1, keepdims=True)
    log_total = row_max + jnp.log(jnp.sum(jnp.exp(scores - row_max), axis=-1, keepdims=True))
    soft_max = jnp.exp(scores - log_total)
    differ = (soft_max[:, 0] - lambda_here[:, None, None] * soft_max[:, 1]).astype(jnp.bfloat16)
    heads_out = jnp.einsum("hqk,khd->qhd", differ, value_in, preferred_element_type=jnp.float32)
    return (heads_out, log_total)


def attend_back(query_in, key_in, value_in, allowed, lambda_here, log_total, grad_heads):
    scale = query_in.shape[-1] ** (-0.5)
    scores = attention_scores(query_in, key_in, allowed)
    soft_max = jnp.exp(scores - log_total)
    differ = (soft_max[:, 0] - lambda_here[:, None, None] * soft_max[:, 1]).astype(jnp.bfloat16)
    grad_values = jnp.einsum("hqk,qhd->khd", differ, grad_heads, preferred_element_type=jnp.float32)
    grad_differ = jnp.einsum(
        "qhd,khd->hqk", grad_heads, value_in, preferred_element_type=jnp.float32
    )
    grad_soft = jnp.stack([grad_differ, -lambda_here[:, None, None] * grad_differ], axis=1)
    grad_scores = (
        soft_max * (grad_soft - jnp.sum(grad_soft * soft_max, axis=-1, keepdims=True))
    ).astype(jnp.bfloat16)
    grad_query = (
        jnp.einsum("hmqk,khmd->qhmd", grad_scores, key_in, preferred_element_type=jnp.float32)
        * scale
    )
    grad_key = (
        jnp.einsum("hmqk,qhmd->khmd", grad_scores, query_in, preferred_element_type=jnp.float32)
        * scale
    )
    return (grad_query, grad_key, grad_values.astype(jnp.bfloat16))


def xor_pairs(count, bit):
    return [(i, i ^ bit) for i in range(count)]


def tok_gather(values, axis=0):
    count = lax.axis_size("tok")
    me = lax.axis_index("tok")
    far = lax.ppermute(values, "tok", xor_pairs(count, 2))
    pair = jnp.where(
        (me & 2) == 0, jnp.stack([values, far], axis), jnp.stack([far, values], axis)
    )
    near = lax.ppermute(pair, "tok", xor_pairs(count, 1))
    full = jnp.where(
        (me & 1) == 0, jnp.stack([pair, near], axis + 1), jnp.stack([near, pair], axis + 1)
    )
    return full.reshape(values.shape[:axis] + (count,) + values.shape[axis:])


def tok_scatter(blocks, axis=0):
    count = lax.axis_size("tok")
    me = lax.axis_index("tok")
    core = me & 1
    half = (me >> 1) & 1
    split = blocks.reshape(blocks.shape[:axis] + (2, 2) + blocks.shape[axis + 1 :])
    mine = lax.dynamic_index_in_dim(split, core, axis + 1, keepdims=False)
    theirs = lax.dynamic_index_in_dim(split, 1 - core, axis + 1, keepdims=False)
    chip_sum = mine + lax.ppermute(theirs, "tok", xor_pairs(count, 1))
    keep = lax.dynamic_index_in_dim(chip_sum, half, axis, keepdims=False)
    send = lax.dynamic_index_in_dim(chip_sum, 1 - half, axis, keepdims=False)
    got = lax.ppermute(send.astype(jnp.bfloat16), "tok", xor_pairs(count, 2))
    return keep + got.astype(keep.dtype)


def tok_sum(values):
    count = lax.axis_size("tok")
    chip_sum = values + lax.ppermute(values, "tok", xor_pairs(count, 1))
    return chip_sum + lax.ppermute(chip_sum, "tok", xor_pairs(count, 2))


def hp_dot(left, right, spec):
    return jnp.einsum(spec, left, right, precision=highest, preferred_element_type=jnp.float32)


def per_device(
    tokens,
    cotangent,
    segments,
    adapter_id,
    w_qkv,
    w_out,
    w_gateup,
    w_down,
    gain_attn,
    gain_ffn,
    gain_sub,
    lambda_head,
    a_in,
    b_qkv,
    b_gateup,
    a_out,
    a_down,
    b_rows,
):
    tok_count = lax.axis_size("tok")
    fsdp_count = lax.axis_size("fsdp")
    me_tok = lax.axis_index("tok")
    seqs, local_len, _ = tokens.shape
    length = local_len * tok_count
    qw_here = w_qkv.shape[2]
    ff_here = w_gateup.shape[2]
    heads_here = qw_here // VALUE_DIM
    lambda_here = lax.dynamic_slice_in_dim(lambda_head, me_tok * heads_here, heads_here)
    positions = jnp.arange(length)
    offsets = adapter_id * RANK
    fsdp_rows = w_qkv.shape[1]
    groups_per_adapter = RANK // b_qkv.shape[1]

    def fsdp_gather(values, axis):
        tiled_in = jnp.broadcast_to(values[None], (fsdp_count,) + values.shape)
        tiled_in = tiled_in.reshape((fsdp_count * values.shape[0],) + values.shape[1:])
        return lax.all_to_all(tiled_in, "fsdp", 0, axis, tiled=True)

    def packed_gather(small, axes):
        count = 1
        for name in axes:
            count *= lax.axis_size(name)
        flat = jnp.concatenate([p.reshape(-1, COLS) for p in small], axis=0)
        tiled_in = jnp.broadcast_to(flat[None], (count,) + flat.shape).reshape(-1, COLS)
        got = lax.all_to_all(tiled_in, axes, 0, 0, tiled=True).reshape((count,) + flat.shape)
        out = []
        start = 0
        for p in small:
            rows = p.size // COLS
            out.append(got[:, start : start + rows].reshape((count,) + p.shape))
            start += rows
        return out

    w_qkv_full = fsdp_gather(w_qkv, 1)
    w_qkv_full, a_in, b_rows = lax.optimization_barrier((w_qkv_full, a_in, b_rows))
    g_ain, g_brows = packed_gather([a_in, b_rows], ("fsdp", "tok"))
    g_ain, b_qkv, b_gateup, a_out, a_down = lax.optimization_barrier((g_ain, b_qkv, b_gateup, a_out, a_down))
    g_bqkv, g_bgateup, g_aout, g_adown = packed_gather([b_qkv, b_gateup, a_out, a_down], ("fsdp",))
    g_bqkv, w_out = lax.optimization_barrier((g_bqkv, w_out))
    w_out_full = fsdp_gather(w_out, 1)
    w_out_full, w_gateup = lax.optimization_barrier((w_out_full, w_gateup))
    w_gateup_full = fsdp_gather(w_gateup, 1)
    w_gateup_full, w_down = lax.optimization_barrier((w_gateup_full, w_down))
    w_down_full = fsdp_gather(w_down, 1)
    a_in_full = jnp.moveaxis(g_ain, 0, 1).reshape(5, D, COLS)
    b_rows_full = jnp.moveaxis(g_brows, 0, 2).reshape(2, COLS, D)

    def pick_cols(values, axis):
        return jnp.stack(
            [lax.dynamic_slice_in_dim(values, offsets[s], RANK, axis) for s in range(seqs)]
        )

    def pick_groups(values):
        return jnp.stack(
            [
                lax.dynamic_slice_in_dim(values, adapter_id[s] * groups_per_adapter, groups_per_adapter, 0)
                for s in range(seqs)
            ]
        )

    a_in_sel = pick_cols(a_in_full, 2)
    b_rows_sel = pick_cols(b_rows_full, 1)
    b_qkv_sel = jnp.moveaxis(pick_groups(g_bqkv), 1, 2).reshape(seqs, 3, RANK, qw_here)
    b_gateup_sel = jnp.moveaxis(pick_groups(g_bgateup), 1, 2).reshape(seqs, 2, RANK, ff_here)
    a_out_sel = jnp.moveaxis(pick_groups(g_aout), 1, 2).reshape(seqs, qw_here, RANK)
    a_down_sel = jnp.moveaxis(pick_groups(g_adown), 1, 2).reshape(seqs, ff_here, RANK)

    def gather_rows(values):
        full = tok_gather(values, 1)
        return full.reshape(seqs, length, values.shape[-1])

    def scatter_rows(values):
        return tok_scatter(values.reshape(seqs, tok_count, local_len, values.shape[-1]), 1)

    def column_forward(rows_full, weight, down_sel, up_sel):
        lowrank = jnp.einsum("std,sdr->str", rows_full, down_sel, preferred_element_type=jnp.float32)
        linear = jnp.einsum("std,de->ste", rows_full, weight, preferred_element_type=jnp.float32)
        return linear + adapter_scale * hp_dot(lowrank, up_sel.astype(jnp.float32), "str,sre->ste"), lowrank

    def row_forward(rows_here, weight, down_sel, up_sel):
        lowrank = jnp.einsum("std,sdr->str", rows_here, down_sel, preferred_element_type=jnp.float32)
        main_part = jnp.einsum("std,de->ste", rows_here, weight, preferred_element_type=jnp.float32)
        total = main_part + adapter_scale * hp_dot(lowrank, up_sel.astype(jnp.float32), "str,sre->ste")
        return scatter_rows(total), lowrank

    inputs_rows = tokens.astype(jnp.float32)
    allowed = (segments[:, :, None] == segments[:, None, :]) & (
        positions[:, None] >= positions[None, :]
    )[None]
    grad_ffn_full = gather_rows(cotangent)
    normed_rows, norm_attn_pull = jax.vjp(partial(rows_norm, gain_vector=gain_attn), inputs_rows)
    normed_full = gather_rows(normed_rows.astype(jnp.bfloat16))
    proj_lin = []
    proj_low = []
    for p in range(3):
        lin, lowr = column_forward(normed_full, w_qkv_full[p], a_in_sel[:, p], b_qkv_sel[:, p])
        proj_lin.append(lin)
        proj_low.append(lowr)
    rotate = partial(rotary_heads, positions=positions, head_dim=HEAD_DIM)
    query_rot, query_pull = jax.vjp(rotate, proj_lin[0])
    key_rot, key_pull = jax.vjp(rotate, proj_lin[1])
    query_in = query_rot.astype(jnp.bfloat16).reshape(seqs, length, heads_here, 2, HEAD_DIM)
    key_in = key_rot.astype(jnp.bfloat16).reshape(seqs, length, heads_here, 2, HEAD_DIM)
    value_in = proj_lin[2].astype(jnp.bfloat16).reshape(seqs, length, heads_here, VALUE_DIM)
    heads_out, log_total = jax.vmap(attend, in_axes=(0, 0, 0, 0, None))(
        query_in, key_in, value_in, allowed, lambda_here
    )
    mixed_float, head_pull = jax.vjp(partial(head_norm, gain_vector=gain_sub), heads_out)
    mixed_rows = mixed_float.reshape(seqs, length, qw_here).astype(jnp.bfloat16)
    attn_rows, out_low = row_forward(mixed_rows, w_out_full, a_out_sel, b_rows_sel[:, 0])
    hidden = inputs_rows + attn_rows
    normed_ffn, norm_ffn_pull = jax.vjp(partial(rows_norm, gain_vector=gain_ffn), hidden)
    ffn_full = gather_rows(normed_ffn.astype(jnp.bfloat16))
    gate_lin, gate_low = column_forward(ffn_full, w_gateup_full[0], a_in_sel[:, 3], b_gateup_sel[:, 0])
    up_lin, up_low = column_forward(ffn_full, w_gateup_full[1], a_in_sel[:, 4], b_gateup_sel[:, 1])
    product_float, swiglu_pull = jax.vjp(swiglu, gate_lin, up_lin)
    product = product_float.astype(jnp.bfloat16)
    ffn_rows, down_low = row_forward(product, w_down_full, a_down_sel, b_rows_sel[:, 1])
    output = (hidden + ffn_rows).astype(jnp.bfloat16)
    row_lows = tok_sum(jnp.stack([out_low, down_low]))

    tangent = cotangent.astype(jnp.float32)

    def row_backward(grad_full, rows_here, weight, down_sel, up_sel):
        grad_float = grad_full.astype(jnp.float32)
        grad_low = adapter_scale * hp_dot(grad_float, up_sel.astype(jnp.float32), "ste,sre->str")
        grad_down = hp_dot(rows_here.astype(jnp.float32), grad_low, "std,str->sdr")
        grad_inputs = jnp.einsum(
            "ste,de->std", grad_full, weight, preferred_element_type=jnp.float32
        ) + hp_dot(grad_low, down_sel.astype(jnp.float32), "str,sdr->std")
        return grad_inputs, grad_down

    def column_backward(rows_full, entries):
        running = None
        grad_lows = []
        grads_up = []
        for grad_rows, weight, down_sel, up_sel, lowrank in entries:
            grad_float = grad_rows.astype(jnp.float32)
            grad_low = adapter_scale * hp_dot(grad_float, up_sel.astype(jnp.float32), "ste,sre->str")
            grads_up.append(adapter_scale * hp_dot(lowrank, grad_float, "str,ste->sre"))
            grad_lows.append(grad_low)
            term = jnp.einsum(
                "ste,de->std", grad_rows, weight, preferred_element_type=jnp.float32
            ) + hp_dot(grad_low, down_sel.astype(jnp.float32), "str,sdr->std")
            running = term if running is None else running + term
        return scatter_rows(running), grad_lows, grads_up

    def mine_of(values, axis):
        shape = values.shape
        split = values.reshape(
            shape[:axis] + (fsdp_count, tok_count, D // (fsdp_count * tok_count)) + shape[axis + 1 :]
        )
        return lax.dynamic_index_in_dim(split, me_tok, axis + 1, keepdims=False)

    grad_product, grad_a_down = row_backward(
        grad_ffn_full, product, w_down_full, a_down_sel, b_rows_sel[:, 1]
    )
    grad_gate, grad_up = swiglu_pull(grad_product)
    grad_ffn_rows, ffn_grad_lows, ffn_grads_up = column_backward(
        ffn_full,
        (
            (grad_gate.astype(jnp.bfloat16), w_gateup_full[0], a_in_sel[:, 3], b_gateup_sel[:, 0], gate_low),
            (grad_up.astype(jnp.bfloat16), w_gateup_full[1], a_in_sel[:, 4], b_gateup_sel[:, 1], up_low),
        ),
    )
    grad_hidden = tangent + norm_ffn_pull(grad_ffn_rows)[0]
    grad_attn_full = gather_rows(grad_hidden.astype(jnp.bfloat16))
    grad_mixed, grad_a_out = row_backward(
        grad_attn_full, mixed_rows, w_out_full, a_out_sel, b_rows_sel[:, 0]
    )
    grad_heads = head_pull(grad_mixed.reshape(seqs, length, heads_here, VALUE_DIM))[0].astype(
        jnp.bfloat16
    )
    grad_query_rot, grad_key_rot, grad_values = jax.vmap(
        attend_back, in_axes=(0, 0, 0, 0, None, 0, 0)
    )(query_in, key_in, value_in, allowed, lambda_here, log_total, grad_heads)
    grad_query = query_pull(grad_query_rot.reshape(seqs, length, qw_here))[0].astype(jnp.bfloat16)
    grad_key = key_pull(grad_key_rot.reshape(seqs, length, qw_here))[0].astype(jnp.bfloat16)
    grad_attn_rows, attn_grad_lows, attn_grads_up = column_backward(
        normed_full,
        (
            (grad_query, w_qkv_full[0], a_in_sel[:, 0], b_qkv_sel[:, 0], proj_low[0]),
            (grad_key, w_qkv_full[1], a_in_sel[:, 1], b_qkv_sel[:, 1], proj_low[1]),
            (grad_values.reshape(seqs, length, qw_here), w_qkv_full[2], a_in_sel[:, 2], b_qkv_sel[:, 2], proj_low[2]),
        ),
    )
    grad_tokens = grad_hidden + norm_attn_pull(grad_attn_rows)[0]

    grad_lows = tok_sum(jnp.stack(attn_grad_lows + ffn_grad_lows))
    grad_a_in_all = jnp.concatenate(
        [
            hp_dot(normed_full.astype(jnp.float32), grad_lows[:3], "std,pstr->psdr"),
            hp_dot(ffn_full.astype(jnp.float32), grad_lows[3:], "std,pstr->psdr"),
        ]
    )
    grad_a_in_part = mine_of(grad_a_in_all, 2)
    grad_b_rows_all = adapter_scale * jnp.stack(
        [
            hp_dot(row_lows[0], grad_attn_full.astype(jnp.float32), "str,std->srd"),
            hp_dot(row_lows[1], grad_ffn_full.astype(jnp.float32), "str,std->srd"),
        ]
    )
    grad_b_rows_part = mine_of(grad_b_rows_all, 3)

    def place(part, axis, total):
        shape = list(part.shape[1:])
        shape[axis] = total
        dense = jnp.zeros(shape, jnp.float32)
        for s in range(seqs):
            current = lax.dynamic_slice_in_dim(dense, offsets[s], RANK, axis)
            dense = lax.dynamic_update_slice_in_dim(dense, current + part[s], offsets[s], axis)
        return dense

    dense_a_in = place(jnp.moveaxis(grad_a_in_part, 1, 0), 3, COLS)
    dense_b_rows = place(jnp.moveaxis(grad_b_rows_part, 1, 0), 1, COLS)
    wide = jnp.concatenate(
        [
            jnp.moveaxis(dense_a_in, 1, 0).reshape(fsdp_count, -1),
            jnp.moveaxis(dense_b_rows, 2, 0).reshape(fsdp_count, -1),
        ],
        axis=1,
    )
    wide_sum = lax.all_to_all(wide, "fsdp", 0, 0, tiled=False).sum(0)
    a_in_block = wide_sum[: 5 * 16 * COLS].reshape(5, 16, COLS)
    b_rows_block = wide_sum[5 * 16 * COLS :].reshape(2, COLS, 16)

    dense_b_qkv = place(jnp.stack(attn_grads_up, 1), 1, COLS)
    dense_b_gateup = place(jnp.stack(ffn_grads_up, 1), 1, COLS)
    dense_a_out = place(grad_a_out, 1, COLS)
    dense_a_down = place(grad_a_down, 1, COLS)
    per = COLS // fsdp_count
    narrow = jnp.concatenate(
        [
            jnp.moveaxis(dense_b_qkv.reshape(3, fsdp_count, per, qw_here), 1, 0).reshape(fsdp_count, -1),
            jnp.moveaxis(dense_b_gateup.reshape(2, fsdp_count, per, ff_here), 1, 0).reshape(fsdp_count, -1),
            jnp.moveaxis(dense_a_out.reshape(qw_here, fsdp_count, per), 1, 0).reshape(fsdp_count, -1),
            jnp.moveaxis(dense_a_down.reshape(ff_here, fsdp_count, per), 1, 0).reshape(fsdp_count, -1),
        ],
        axis=1,
    ).astype(jnp.bfloat16)
    narrow_sum = lax.all_to_all(narrow, "fsdp", 0, 0, tiled=False).astype(jnp.float32).sum(0)
    sizes = [3 * per * qw_here, 2 * per * ff_here, qw_here * per, ff_here * per]
    cuts = [0]
    for size in sizes:
        cuts.append(cuts[-1] + size)
    b_qkv_block = narrow_sum[cuts[0] : cuts[1]].reshape(3, per, qw_here)
    b_gateup_block = narrow_sum[cuts[1] : cuts[2]].reshape(2, per, ff_here)
    a_out_block = narrow_sum[cuts[2] : cuts[3]].reshape(qw_here, per)
    a_down_block = narrow_sum[cuts[3] : cuts[4]].reshape(ff_here, per)

    return (
        output,
        grad_tokens,
        a_in_block,
        b_qkv_block,
        b_gateup_block,
        a_out_block,
        a_down_block,
        b_rows_block,
    )


def solution(mesh):
    return jax.shard_map(
        per_device,
        mesh=mesh,
        in_specs=(
            P("fsdp", "tok", None),
            P("fsdp", "tok", None),
            P("fsdp", None),
            P("fsdp"),
            P(None, "fsdp", "tok"),
            P("tok", "fsdp"),
            P(None, "fsdp", "tok"),
            P("tok", "fsdp"),
            P(),
            P(),
            P(),
            P(),
            P(None, ("fsdp", "tok"), None),
            P(None, "fsdp", "tok"),
            P(None, "fsdp", "tok"),
            P("tok", "fsdp"),
            P("tok", "fsdp"),
            P(None, None, ("fsdp", "tok")),
        ),
        out_specs=(
            P("fsdp", "tok", None),
            P("fsdp", "tok", None),
            P(None, ("fsdp", "tok"), None),
            P(None, "fsdp", "tok"),
            P(None, "fsdp", "tok"),
            P("tok", "fsdp"),
            P("tok", "fsdp"),
            P(None, None, ("fsdp", "tok")),
        ),
        check_vma=False,
    )
```

```python
from functools import partial

import jax
import jax.numpy as jnp
from jax import lax
from jax.sharding import PartitionSpec as P

D = 2048
HEAD_DIM = 128
VALUE_DIM = 256
RANK = 16
COLS = 128


highest = lax.Precision.HIGHEST
negative = -1e30
adapter_scale = 2.0
lambda_init = 0.2
rotary_base = 10000.0
row_epsilon = 1e-06
head_epsilon = 1e-05


def rows_norm(values, gain_vector):
    return (
        values
        * lax.rsqrt(jnp.mean(values * values, axis=-1, keepdims=True) + row_epsilon)
        * gain_vector
    )


def head_norm(values, gain_vector):
    scaled = values * lax.rsqrt(jnp.mean(values * values, axis=-1, keepdims=True) + head_epsilon)
    return scaled * gain_vector * (1.0 - lambda_init)


def rotary_heads(values, positions, head_dim):
    lead = values.shape[:-1]
    groups = values.reshape(lead + (-1, head_dim))
    half_dim = head_dim // 2
    frequency = rotary_base ** (-jnp.arange(half_dim, dtype=jnp.float32) / half_dim)
    angles = positions.astype(jnp.float32)[:, None] * frequency[None, :]
    cosine = jnp.cos(angles)[:, None, :]
    sine_part = jnp.sin(angles)[:, None, :]
    first_half = groups[..., :half_dim]
    second = groups[..., half_dim:]
    turned = jnp.concatenate(
        [first_half * cosine - second * sine_part, second * cosine + first_half * sine_part],
        axis=-1,
    )
    return turned.reshape(values.shape)


def swiglu(gate_rows, up_rows):
    return gate_rows * jax.nn.sigmoid(gate_rows) * up_rows


def attention_scores(query_in, key_in, allowed):
    raw_scores = jnp.einsum(
        "qhmd,khmd->hmqk", query_in, key_in, preferred_element_type=jnp.float32
    ) * query_in.shape[-1] ** (-0.5)
    return jnp.where(allowed[None, None], raw_scores, negative)


def attend(query_in, key_in, value_in, allowed, lambda_here):
    scores = attention_scores(query_in, key_in, allowed)
    row_max = jnp.max(scores, axis=-1, keepdims=True)
    log_total = row_max + jnp.log(jnp.sum(jnp.exp(scores - row_max), axis=-1, keepdims=True))
    soft_max = jnp.exp(scores - log_total)
    differ = (soft_max[:, 0] - lambda_here[:, None, None] * soft_max[:, 1]).astype(jnp.bfloat16)
    heads_out = jnp.einsum("hqk,khd->qhd", differ, value_in, preferred_element_type=jnp.float32)
    return (heads_out, log_total)


def attend_back(query_in, key_in, value_in, allowed, lambda_here, log_total, grad_heads):
    scale = query_in.shape[-1] ** (-0.5)
    scores = attention_scores(query_in, key_in, allowed)
    soft_max = jnp.exp(scores - log_total)
    differ = (soft_max[:, 0] - lambda_here[:, None, None] * soft_max[:, 1]).astype(jnp.bfloat16)
    grad_values = jnp.einsum("hqk,qhd->khd", differ, grad_heads, preferred_element_type=jnp.float32)
    grad_differ = jnp.einsum(
        "qhd,khd->hqk", grad_heads, value_in, preferred_element_type=jnp.float32
    )
    grad_soft = jnp.stack([grad_differ, -lambda_here[:, None, None] * grad_differ], axis=1)
    grad_scores = (
        soft_max * (grad_soft - jnp.sum(grad_soft * soft_max, axis=-1, keepdims=True))
    ).astype(jnp.bfloat16)
    grad_query = (
        jnp.einsum("hmqk,khmd->qhmd", grad_scores, key_in, preferred_element_type=jnp.float32)
        * scale
    )
    grad_key = (
        jnp.einsum("hmqk,qhmd->khmd", grad_scores, query_in, preferred_element_type=jnp.float32)
        * scale
    )
    return (grad_query, grad_key, grad_values.astype(jnp.bfloat16))


def xor_pairs(count, bit):
    return [(i, i ^ bit) for i in range(count)]


def tok_gather(values, axis=0):
    count = lax.axis_size("tok")
    me = lax.axis_index("tok")
    far = lax.ppermute(values, "tok", xor_pairs(count, 2))
    pair = jnp.where(
        (me & 2) == 0, jnp.stack([values, far], axis), jnp.stack([far, values], axis)
    )
    near = lax.ppermute(pair, "tok", xor_pairs(count, 1))
    full = jnp.where(
        (me & 1) == 0, jnp.stack([pair, near], axis + 1), jnp.stack([near, pair], axis + 1)
    )
    return full.reshape(values.shape[:axis] + (count,) + values.shape[axis:])


def tok_scatter(blocks, axis=0):
    count = lax.axis_size("tok")
    me = lax.axis_index("tok")
    core = me & 1
    half = (me >> 1) & 1
    split = blocks.reshape(blocks.shape[:axis] + (2, 2) + blocks.shape[axis + 1 :])
    mine = lax.dynamic_index_in_dim(split, core, axis + 1, keepdims=False)
    theirs = lax.dynamic_index_in_dim(split, 1 - core, axis + 1, keepdims=False)
    chip_sum = mine + lax.ppermute(theirs, "tok", xor_pairs(count, 1))
    keep = lax.dynamic_index_in_dim(chip_sum, half, axis, keepdims=False)
    send = lax.dynamic_index_in_dim(chip_sum, 1 - half, axis, keepdims=False)
    got = lax.ppermute(send.astype(jnp.bfloat16), "tok", xor_pairs(count, 2))
    return keep + got.astype(keep.dtype)


def tok_sum(values):
    count = lax.axis_size("tok")
    chip_sum = values + lax.ppermute(values, "tok", xor_pairs(count, 1))
    return chip_sum + lax.ppermute(chip_sum, "tok", xor_pairs(count, 2))


def fsdp_coords():
    me = lax.axis_index("fsdp")
    return {"x": me // 8, "z": (me // 4) % 2, "y": me % 4}


def fsdp_pairs(kind, step):
    pairs = []
    for x in range(4):
        for z in range(2):
            for y in range(4):
                if kind == "z":
                    target = (x * 2 + 1 - z) * 4 + y
                elif kind == "x":
                    target = (((x + step) % 4) * 2 + z) * 4 + y
                else:
                    target = (x * 2 + z) * 4 + (y + step) % 4
                pairs.append(((x * 2 + z) * 4 + y, target))
    return pairs


def place(buffer, piece, position, inner=0):
    start = (position, inner) + (0,) * (piece.ndim - 1)
    return lax.dynamic_update_slice(buffer, piece[None], start)


def ring_stage(stack, kind, coord):
    count = stack.shape[0]
    from_left = lax.ppermute(stack, "fsdp", fsdp_pairs(kind, 1))
    from_right = lax.ppermute(stack, "fsdp", fsdp_pairs(kind, -1))
    far_left = lax.ppermute(from_left[: count // 2], "fsdp", fsdp_pairs(kind, 1))
    far_right = lax.ppermute(from_right[count // 2 :], "fsdp", fsdp_pairs(kind, -1))
    out = jnp.zeros((4,) + stack.shape, stack.dtype)
    out = place(out, stack, coord)
    out = place(out, from_right, (coord + 1) % 4)
    out = place(out, from_left, (coord + 3) % 4)
    out = place(out, far_left, (coord + 2) % 4)
    return place(out, far_right, (coord + 2) % 4, count // 2)


def torus_gather(part_a, part_b):
    coord = fsdp_coords()
    other_a, other_b = lax.ppermute((part_a, part_b), "fsdp", fsdp_pairs("z", 1))
    stacks = []
    for mine, other in ((part_a, other_a), (part_b, other_b)):
        pair = jnp.zeros((2,) + mine.shape, mine.dtype)
        pair = place(pair, mine, coord["z"])
        stacks.append(place(pair, other, 1 - coord["z"]))
    stack_a = ring_stage(ring_stage(stacks[0], "x", coord["x"]), "y", coord["y"])
    stack_b = ring_stage(ring_stage(stacks[1], "y", coord["y"]), "x", coord["x"])
    return stack_a, stack_b


def hp_dot(left, right, spec):
    return jnp.einsum(spec, left, right, precision=highest, preferred_element_type=jnp.float32)


def per_device(
    tokens,
    cotangent,
    segments,
    adapter_id,
    w_qkv,
    w_out,
    w_gateup,
    w_down,
    gain_attn,
    gain_ffn,
    gain_sub,
    lambda_head,
    a_in,
    b_qkv,
    b_gateup,
    a_out,
    a_down,
    b_rows,
):
    tok_count = lax.axis_size("tok")
    fsdp_count = lax.axis_size("fsdp")
    me_tok = lax.axis_index("tok")
    seqs, local_len, _ = tokens.shape
    length = local_len * tok_count
    qw_here = w_qkv.shape[2]
    ff_here = w_gateup.shape[2]
    heads_here = qw_here // VALUE_DIM
    lambda_here = lax.dynamic_slice_in_dim(lambda_head, me_tok * heads_here, heads_here)
    positions = jnp.arange(length)
    offsets = adapter_id * RANK
    fsdp_rows = w_qkv.shape[1]
    groups_per_adapter = RANK // b_qkv.shape[1]

    a_in_tok = tok_gather(a_in)
    b_rows_tok = tok_gather(b_rows)
    leaves_a = [w_qkv, w_down, a_in_tok, b_rows_tok]
    leaves_b = [w_gateup, w_out, b_qkv, b_gateup, a_out, a_down]
    stack_a, stack_b = torus_gather(
        jnp.concatenate([p.reshape(-1, COLS) for p in leaves_a]),
        jnp.concatenate([p.reshape(-1, COLS) for p in leaves_b]),
    )

    def rows_of(stack, leaves):
        out = []
        start = 0
        for p in leaves:
            rows = p.size // COLS
            out.append(stack[:, :, :, start : start + rows].reshape(stack.shape[:3] + p.shape))
            start += rows
        return out

    s_qkv, s_down, s_ain, s_brows = rows_of(stack_a, leaves_a)
    s_gateup, s_out, s_bqkv, s_bgateup, s_aout, s_adown = rows_of(stack_b, leaves_b)
    w_qkv_full = jnp.transpose(s_qkv, (3, 1, 2, 0, 4, 5)).reshape(3, D, qw_here)
    w_down_full = jnp.transpose(s_down, (3, 1, 2, 0, 4)).reshape(ff_here, D)
    a_in_full = jnp.transpose(s_ain, (4, 1, 2, 0, 3, 5, 6)).reshape(5, D, COLS)
    b_rows_full = jnp.transpose(s_brows, (4, 5, 1, 2, 0, 3, 6)).reshape(2, COLS, D)
    w_gateup_full = jnp.transpose(s_gateup, (3, 0, 2, 1, 4, 5)).reshape(2, D, ff_here)
    w_out_full = jnp.transpose(s_out, (3, 0, 2, 1, 4)).reshape(qw_here, D)

    def fsdp_first(values):
        return jnp.transpose(values, (0, 2, 1) + tuple(range(3, values.ndim))).reshape(
            (fsdp_count,) + values.shape[3:]
        )

    g_bqkv = fsdp_first(s_bqkv)
    g_bgateup = fsdp_first(s_bgateup)
    g_aout = fsdp_first(s_aout)
    g_adown = fsdp_first(s_adown)

    def pick_cols(values, axis):
        return jnp.stack(
            [lax.dynamic_slice_in_dim(values, offsets[s], RANK, axis) for s in range(seqs)]
        )

    def pick_groups(values):
        return jnp.stack(
            [
                lax.dynamic_slice_in_dim(values, adapter_id[s] * groups_per_adapter, groups_per_adapter, 0)
                for s in range(seqs)
            ]
        )

    a_in_sel = pick_cols(a_in_full, 2)
    b_rows_sel = pick_cols(b_rows_full, 1)
    b_qkv_sel = jnp.moveaxis(pick_groups(g_bqkv), 1, 2).reshape(seqs, 3, RANK, qw_here)
    b_gateup_sel = jnp.moveaxis(pick_groups(g_bgateup), 1, 2).reshape(seqs, 2, RANK, ff_here)
    a_out_sel = jnp.moveaxis(pick_groups(g_aout), 1, 2).reshape(seqs, qw_here, RANK)
    a_down_sel = jnp.moveaxis(pick_groups(g_adown), 1, 2).reshape(seqs, ff_here, RANK)

    def gather_rows(values):
        full = tok_gather(values, 1)
        return full.reshape(seqs, length, values.shape[-1])

    def scatter_rows(values):
        return tok_scatter(values.reshape(seqs, tok_count, local_len, values.shape[-1]), 1)

    def column_forward(rows_full, weight, down_sel, up_sel):
        lowrank = jnp.einsum("std,sdr->str", rows_full, down_sel, preferred_element_type=jnp.float32)
        linear = jnp.einsum("std,de->ste", rows_full, weight, preferred_element_type=jnp.float32)
        return linear + adapter_scale * hp_dot(lowrank, up_sel.astype(jnp.float32), "str,sre->ste"), lowrank

    def row_forward(rows_here, weight, down_sel, up_sel):
        lowrank = jnp.einsum("std,sdr->str", rows_here, down_sel, preferred_element_type=jnp.float32)
        main_part = jnp.einsum("std,de->ste", rows_here, weight, preferred_element_type=jnp.float32)
        total = main_part + adapter_scale * hp_dot(lowrank, up_sel.astype(jnp.float32), "str,sre->ste")
        return scatter_rows(total), lowrank

    inputs_rows = tokens.astype(jnp.float32)
    allowed = (segments[:, :, None] == segments[:, None, :]) & (
        positions[:, None] >= positions[None, :]
    )[None]
    grad_ffn_full = gather_rows(cotangent)
    normed_rows, norm_attn_pull = jax.vjp(partial(rows_norm, gain_vector=gain_attn), inputs_rows)
    normed_full = gather_rows(normed_rows.astype(jnp.bfloat16))
    proj_lin = []
    proj_low = []
    for p in range(3):
        lin, lowr = column_forward(normed_full, w_qkv_full[p], a_in_sel[:, p], b_qkv_sel[:, p])
        proj_lin.append(lin)
        proj_low.append(lowr)
    rotate = partial(rotary_heads, positions=positions, head_dim=HEAD_DIM)
    query_rot, query_pull = jax.vjp(rotate, proj_lin[0])
    key_rot, key_pull = jax.vjp(rotate, proj_lin[1])
    query_in = query_rot.astype(jnp.bfloat16).reshape(seqs, length, heads_here, 2, HEAD_DIM)
    key_in = key_rot.astype(jnp.bfloat16).reshape(seqs, length, heads_here, 2, HEAD_DIM)
    value_in = proj_lin[2].astype(jnp.bfloat16).reshape(seqs, length, heads_here, VALUE_DIM)
    heads_out, log_total = jax.vmap(attend, in_axes=(0, 0, 0, 0, None))(
        query_in, key_in, value_in, allowed, lambda_here
    )
    mixed_float, head_pull = jax.vjp(partial(head_norm, gain_vector=gain_sub), heads_out)
    mixed_rows = mixed_float.reshape(seqs, length, qw_here).astype(jnp.bfloat16)
    attn_rows, out_low = row_forward(mixed_rows, w_out_full, a_out_sel, b_rows_sel[:, 0])
    hidden = inputs_rows + attn_rows
    normed_ffn, norm_ffn_pull = jax.vjp(partial(rows_norm, gain_vector=gain_ffn), hidden)
    ffn_full = gather_rows(normed_ffn.astype(jnp.bfloat16))
    gate_lin, gate_low = column_forward(ffn_full, w_gateup_full[0], a_in_sel[:, 3], b_gateup_sel[:, 0])
    up_lin, up_low = column_forward(ffn_full, w_gateup_full[1], a_in_sel[:, 4], b_gateup_sel[:, 1])
    product_float, swiglu_pull = jax.vjp(swiglu, gate_lin, up_lin)
    product = product_float.astype(jnp.bfloat16)
    ffn_rows, down_low = row_forward(product, w_down_full, a_down_sel, b_rows_sel[:, 1])
    output = (hidden + ffn_rows).astype(jnp.bfloat16)
    row_lows = tok_sum(jnp.stack([out_low, down_low]))

    tangent = cotangent.astype(jnp.float32)

    def row_backward(grad_full, rows_here, weight, down_sel, up_sel):
        grad_float = grad_full.astype(jnp.float32)
        grad_low = adapter_scale * hp_dot(grad_float, up_sel.astype(jnp.float32), "ste,sre->str")
        grad_down = hp_dot(rows_here.astype(jnp.float32), grad_low, "std,str->sdr")
        grad_inputs = jnp.einsum(
            "ste,de->std", grad_full, weight, preferred_element_type=jnp.float32
        ) + hp_dot(grad_low, down_sel.astype(jnp.float32), "str,sdr->std")
        return grad_inputs, grad_down

    def column_backward(rows_full, entries):
        running = None
        grad_lows = []
        grads_up = []
        for grad_rows, weight, down_sel, up_sel, lowrank in entries:
            grad_float = grad_rows.astype(jnp.float32)
            grad_low = adapter_scale * hp_dot(grad_float, up_sel.astype(jnp.float32), "ste,sre->str")
            grads_up.append(adapter_scale * hp_dot(lowrank, grad_float, "str,ste->sre"))
            grad_lows.append(grad_low)
            term = jnp.einsum(
                "ste,de->std", grad_rows, weight, preferred_element_type=jnp.float32
            ) + hp_dot(grad_low, down_sel.astype(jnp.float32), "str,sdr->std")
            running = term if running is None else running + term
        return scatter_rows(running), grad_lows, grads_up

    def mine_of(values, axis):
        shape = values.shape
        split = values.reshape(
            shape[:axis] + (fsdp_count, tok_count, D // (fsdp_count * tok_count)) + shape[axis + 1 :]
        )
        return lax.dynamic_index_in_dim(split, me_tok, axis + 1, keepdims=False)

    grad_product, grad_a_down = row_backward(
        grad_ffn_full, product, w_down_full, a_down_sel, b_rows_sel[:, 1]
    )
    grad_gate, grad_up = swiglu_pull(grad_product)
    grad_ffn_rows, ffn_grad_lows, ffn_grads_up = column_backward(
        ffn_full,
        (
            (grad_gate.astype(jnp.bfloat16), w_gateup_full[0], a_in_sel[:, 3], b_gateup_sel[:, 0], gate_low),
            (grad_up.astype(jnp.bfloat16), w_gateup_full[1], a_in_sel[:, 4], b_gateup_sel[:, 1], up_low),
        ),
    )
    grad_hidden = tangent + norm_ffn_pull(grad_ffn_rows)[0]
    grad_attn_full = gather_rows(grad_hidden.astype(jnp.bfloat16))
    grad_mixed, grad_a_out = row_backward(
        grad_attn_full, mixed_rows, w_out_full, a_out_sel, b_rows_sel[:, 0]
    )
    grad_heads = head_pull(grad_mixed.reshape(seqs, length, heads_here, VALUE_DIM))[0].astype(
        jnp.bfloat16
    )
    grad_query_rot, grad_key_rot, grad_values = jax.vmap(
        attend_back, in_axes=(0, 0, 0, 0, None, 0, 0)
    )(query_in, key_in, value_in, allowed, lambda_here, log_total, grad_heads)
    grad_query = query_pull(grad_query_rot.reshape(seqs, length, qw_here))[0].astype(jnp.bfloat16)
    grad_key = key_pull(grad_key_rot.reshape(seqs, length, qw_here))[0].astype(jnp.bfloat16)
    grad_attn_rows, attn_grad_lows, attn_grads_up = column_backward(
        normed_full,
        (
            (grad_query, w_qkv_full[0], a_in_sel[:, 0], b_qkv_sel[:, 0], proj_low[0]),
            (grad_key, w_qkv_full[1], a_in_sel[:, 1], b_qkv_sel[:, 1], proj_low[1]),
            (grad_values.reshape(seqs, length, qw_here), w_qkv_full[2], a_in_sel[:, 2], b_qkv_sel[:, 2], proj_low[2]),
        ),
    )
    grad_tokens = grad_hidden + norm_attn_pull(grad_attn_rows)[0]

    grad_lows = tok_sum(jnp.stack(attn_grad_lows + ffn_grad_lows))
    grad_a_in_all = jnp.concatenate(
        [
            hp_dot(normed_full.astype(jnp.float32), grad_lows[:3], "std,pstr->psdr"),
            hp_dot(ffn_full.astype(jnp.float32), grad_lows[3:], "std,pstr->psdr"),
        ]
    )
    grad_a_in_part = mine_of(grad_a_in_all, 2)
    grad_b_rows_all = adapter_scale * jnp.stack(
        [
            hp_dot(row_lows[0], grad_attn_full.astype(jnp.float32), "str,std->srd"),
            hp_dot(row_lows[1], grad_ffn_full.astype(jnp.float32), "str,std->srd"),
        ]
    )
    grad_b_rows_part = mine_of(grad_b_rows_all, 3)

    def place(part, axis, total):
        shape = list(part.shape[1:])
        shape[axis] = total
        dense = jnp.zeros(shape, jnp.float32)
        for s in range(seqs):
            current = lax.dynamic_slice_in_dim(dense, offsets[s], RANK, axis)
            dense = lax.dynamic_update_slice_in_dim(dense, current + part[s], offsets[s], axis)
        return dense

    dense_a_in = place(jnp.moveaxis(grad_a_in_part, 1, 0), 3, COLS)
    dense_b_rows = place(jnp.moveaxis(grad_b_rows_part, 1, 0), 1, COLS)
    wide = jnp.concatenate(
        [
            jnp.moveaxis(dense_a_in, 1, 0).reshape(fsdp_count, -1),
            jnp.moveaxis(dense_b_rows, 2, 0).reshape(fsdp_count, -1),
        ],
        axis=1,
    )
    wide_sum = lax.all_to_all(wide, "fsdp", 0, 0, tiled=False).sum(0)
    a_in_block = wide_sum[: 5 * 16 * COLS].reshape(5, 16, COLS)
    b_rows_block = wide_sum[5 * 16 * COLS :].reshape(2, COLS, 16)

    dense_b_qkv = place(jnp.stack(attn_grads_up, 1), 1, COLS)
    dense_b_gateup = place(jnp.stack(ffn_grads_up, 1), 1, COLS)
    dense_a_out = place(grad_a_out, 1, COLS)
    dense_a_down = place(grad_a_down, 1, COLS)
    per = COLS // fsdp_count
    narrow = jnp.concatenate(
        [
            jnp.moveaxis(dense_b_qkv.reshape(3, fsdp_count, per, qw_here), 1, 0).reshape(fsdp_count, -1),
            jnp.moveaxis(dense_b_gateup.reshape(2, fsdp_count, per, ff_here), 1, 0).reshape(fsdp_count, -1),
            jnp.moveaxis(dense_a_out.reshape(qw_here, fsdp_count, per), 1, 0).reshape(fsdp_count, -1),
            jnp.moveaxis(dense_a_down.reshape(ff_here, fsdp_count, per), 1, 0).reshape(fsdp_count, -1),
        ],
        axis=1,
    ).astype(jnp.bfloat16)
    narrow_sum = lax.all_to_all(narrow, "fsdp", 0, 0, tiled=False).astype(jnp.float32).sum(0)
    sizes = [3 * per * qw_here, 2 * per * ff_here, qw_here * per, ff_here * per]
    cuts = [0]
    for size in sizes:
        cuts.append(cuts[-1] + size)
    b_qkv_block = narrow_sum[cuts[0] : cuts[1]].reshape(3, per, qw_here)
    b_gateup_block = narrow_sum[cuts[1] : cuts[2]].reshape(2, per, ff_here)
    a_out_block = narrow_sum[cuts[2] : cuts[3]].reshape(qw_here, per)
    a_down_block = narrow_sum[cuts[3] : cuts[4]].reshape(ff_here, per)

    return (
        output,
        grad_tokens,
        a_in_block,
        b_qkv_block,
        b_gateup_block,
        a_out_block,
        a_down_block,
        b_rows_block,
    )


def solution(mesh):
    return jax.shard_map(
        per_device,
        mesh=mesh,
        in_specs=(
            P("fsdp", "tok", None),
            P("fsdp", "tok", None),
            P("fsdp", None),
            P("fsdp"),
            P(None, "fsdp", "tok"),
            P("tok", "fsdp"),
            P(None, "fsdp", "tok"),
            P("tok", "fsdp"),
            P(),
            P(),
            P(),
            P(),
            P(None, ("fsdp", "tok"), None),
            P(None, "fsdp", "tok"),
            P(None, "fsdp", "tok"),
            P("tok", "fsdp"),
            P("tok", "fsdp"),
            P(None, None, ("fsdp", "tok")),
        ),
        out_specs=(
            P("fsdp", "tok", None),
            P("fsdp", "tok", None),
            P(None, ("fsdp", "tok"), None),
            P(None, "fsdp", "tok"),
            P(None, "fsdp", "tok"),
            P("tok", "fsdp"),
            P("tok", "fsdp"),
            P(None, None, ("fsdp", "tok")),
        ),
        check_vma=False,
    )
```

```python
from functools import partial

import jax
import jax.numpy as jnp
from jax import lax
from jax.sharding import PartitionSpec as P

D = 2048
HEAD_DIM = 128
VALUE_DIM = 256
RANK = 16
COLS = 128


highest = lax.Precision.HIGHEST
negative = -1e30
adapter_scale = 2.0
lambda_init = 0.2
rotary_base = 10000.0
row_epsilon = 1e-06
head_epsilon = 1e-05


def rows_norm(values, gain_vector):
    return (
        values
        * lax.rsqrt(jnp.mean(values * values, axis=-1, keepdims=True) + row_epsilon)
        * gain_vector
    )


def head_norm(values, gain_vector):
    scaled = values * lax.rsqrt(jnp.mean(values * values, axis=-1, keepdims=True) + head_epsilon)
    return scaled * gain_vector * (1.0 - lambda_init)


def rotary_heads(values, positions, head_dim):
    lead = values.shape[:-1]
    groups = values.reshape(lead + (-1, head_dim))
    half_dim = head_dim // 2
    frequency = rotary_base ** (-jnp.arange(half_dim, dtype=jnp.float32) / half_dim)
    angles = positions.astype(jnp.float32)[:, None] * frequency[None, :]
    cosine = jnp.cos(angles)[:, None, :]
    sine_part = jnp.sin(angles)[:, None, :]
    first_half = groups[..., :half_dim]
    second = groups[..., half_dim:]
    turned = jnp.concatenate(
        [first_half * cosine - second * sine_part, second * cosine + first_half * sine_part],
        axis=-1,
    )
    return turned.reshape(values.shape)


def swiglu(gate_rows, up_rows):
    return gate_rows * jax.nn.sigmoid(gate_rows) * up_rows


def attention_scores(query_in, key_in, allowed):
    raw_scores = jnp.einsum(
        "qhmd,khmd->hmqk", query_in, key_in, preferred_element_type=jnp.float32
    ) * query_in.shape[-1] ** (-0.5)
    return jnp.where(allowed[None, None], raw_scores, negative)


def attend(query_in, key_in, value_in, allowed, lambda_here):
    scores = attention_scores(query_in, key_in, allowed)
    row_max = jnp.max(scores, axis=-1, keepdims=True)
    log_total = row_max + jnp.log(jnp.sum(jnp.exp(scores - row_max), axis=-1, keepdims=True))
    soft_max = jnp.exp(scores - log_total)
    differ = (soft_max[:, 0] - lambda_here[:, None, None] * soft_max[:, 1]).astype(jnp.bfloat16)
    heads_out = jnp.einsum("hqk,khd->qhd", differ, value_in, preferred_element_type=jnp.float32)
    return (heads_out, log_total)


def attend_back(query_in, key_in, value_in, allowed, lambda_here, log_total, grad_heads):
    scale = query_in.shape[-1] ** (-0.5)
    scores = attention_scores(query_in, key_in, allowed)
    soft_max = jnp.exp(scores - log_total)
    differ = (soft_max[:, 0] - lambda_here[:, None, None] * soft_max[:, 1]).astype(jnp.bfloat16)
    grad_values = jnp.einsum("hqk,qhd->khd", differ, grad_heads, preferred_element_type=jnp.float32)
    grad_differ = jnp.einsum(
        "qhd,khd->hqk", grad_heads, value_in, preferred_element_type=jnp.float32
    )
    grad_soft = jnp.stack([grad_differ, -lambda_here[:, None, None] * grad_differ], axis=1)
    grad_scores = (
        soft_max * (grad_soft - jnp.sum(grad_soft * soft_max, axis=-1, keepdims=True))
    ).astype(jnp.bfloat16)
    grad_query = (
        jnp.einsum("hmqk,khmd->qhmd", grad_scores, key_in, preferred_element_type=jnp.float32)
        * scale
    )
    grad_key = (
        jnp.einsum("hmqk,qhmd->khmd", grad_scores, query_in, preferred_element_type=jnp.float32)
        * scale
    )
    return (grad_query, grad_key, grad_values.astype(jnp.bfloat16))


def xor_pairs(count, bit):
    return [(i, i ^ bit) for i in range(count)]


def tok_gather(values, axis=0):
    count = lax.axis_size("tok")
    me = lax.axis_index("tok")
    far = lax.ppermute(values, "tok", xor_pairs(count, 2))
    pair = jnp.where(
        (me & 2) == 0, jnp.stack([values, far], axis), jnp.stack([far, values], axis)
    )
    near = lax.ppermute(pair, "tok", xor_pairs(count, 1))
    full = jnp.where(
        (me & 1) == 0, jnp.stack([pair, near], axis + 1), jnp.stack([near, pair], axis + 1)
    )
    return full.reshape(values.shape[:axis] + (count,) + values.shape[axis:])


def tok_scatter(blocks, axis=0):
    count = lax.axis_size("tok")
    me = lax.axis_index("tok")
    core = me & 1
    half = (me >> 1) & 1
    split = blocks.reshape(blocks.shape[:axis] + (2, 2) + blocks.shape[axis + 1 :])
    mine = lax.dynamic_index_in_dim(split, core, axis + 1, keepdims=False)
    theirs = lax.dynamic_index_in_dim(split, 1 - core, axis + 1, keepdims=False)
    chip_sum = mine + lax.ppermute(theirs, "tok", xor_pairs(count, 1))
    keep = lax.dynamic_index_in_dim(chip_sum, half, axis, keepdims=False)
    send = lax.dynamic_index_in_dim(chip_sum, 1 - half, axis, keepdims=False)
    got = lax.ppermute(send.astype(jnp.bfloat16), "tok", xor_pairs(count, 2))
    return keep + got.astype(keep.dtype)


def tok_sum(values):
    count = lax.axis_size("tok")
    chip_sum = values + lax.ppermute(values, "tok", xor_pairs(count, 1))
    return chip_sum + lax.ppermute(chip_sum, "tok", xor_pairs(count, 2))


def fsdp_coords():
    me = lax.axis_index("fsdp")
    return {"x": me // 8, "z": (me // 4) % 2, "y": me % 4}


def fsdp_pairs(kind, step):
    pairs = []
    for x in range(4):
        for z in range(2):
            for y in range(4):
                if kind == "z":
                    target = (x * 2 + 1 - z) * 4 + y
                elif kind == "x":
                    target = (((x + step) % 4) * 2 + z) * 4 + y
                else:
                    target = (x * 2 + z) * 4 + (y + step) % 4
                pairs.append(((x * 2 + z) * 4 + y, target))
    return pairs


def put(buffer, piece, axis, offset):
    start = [0] * buffer.ndim
    start[axis] = offset
    return lax.dynamic_update_slice(buffer, piece, start)


def grow(pieces, axes, factor):
    return [
        jnp.zeros(p.shape[:ax] + (p.shape[ax] * factor,) + p.shape[ax + 1 :], p.dtype)
        for p, ax in zip(pieces, axes)
    ]


def halves(pieces, axes, second):
    out = []
    for p, ax in zip(pieces, axes):
        n = p.shape[ax] // 2
        out.append(lax.slice_in_dim(p, n if second else 0, 2 * n if second else n, axis=ax))
    return out


def pair_stage(stacks, axes, coord):
    other = lax.ppermute(stacks, "fsdp", fsdp_pairs("z", 1))
    outs = []
    for mine, theirs, buffer, ax in zip(stacks, other, grow(stacks, axes, 2), axes):
        n = mine.shape[ax]
        buffer = put(buffer, mine, ax, coord * n)
        outs.append(put(buffer, theirs, ax, (1 - coord) * n))
    return outs


def ring_stage(stacks, axes, kind, coord):
    from_left = lax.ppermute(stacks, "fsdp", fsdp_pairs(kind, 1))
    from_right = lax.ppermute(stacks, "fsdp", fsdp_pairs(kind, -1))
    split = stacks[0].shape[axes[0]] > 1
    if split:
        far_left = lax.ppermute(halves(from_left, axes, False), "fsdp", fsdp_pairs(kind, 1))
        far_right = lax.ppermute(halves(from_right, axes, True), "fsdp", fsdp_pairs(kind, -1))
    else:
        far_left = lax.ppermute(from_left, "fsdp", fsdp_pairs(kind, 1))
    outs = []
    for i, (buffer, ax) in enumerate(zip(grow(stacks, axes, 4), axes)):
        n = stacks[i].shape[ax]
        buffer = put(buffer, stacks[i], ax, coord * n)
        buffer = put(buffer, from_right[i], ax, ((coord + 1) % 4) * n)
        buffer = put(buffer, from_left[i], ax, ((coord + 3) % 4) * n)
        buffer = put(buffer, far_left[i], ax, ((coord + 2) % 4) * n)
        if split:
            buffer = put(buffer, far_right[i], ax, ((coord + 2) % 4) * n + n // 2)
        outs.append(buffer)
    return outs


def torus_gather(route_a, axes_a, route_b, axes_b):
    coord = fsdp_coords()
    route_a = ring_stage(route_a, axes_a, "y", coord["y"])
    route_b = ring_stage(route_b, axes_b, "x", coord["x"])
    both = pair_stage(route_a + route_b, axes_a + axes_b, coord["z"])
    route_a, route_b = both[: len(route_a)], both[len(route_a) :]
    return ring_stage(route_a, axes_a, "x", coord["x"]), ring_stage(route_b, axes_b, "y", coord["y"])


def hp_dot(left, right, spec):
    return jnp.einsum(spec, left, right, precision=highest, preferred_element_type=jnp.float32)


def per_device(
    tokens,
    cotangent,
    segments,
    adapter_id,
    w_qkv,
    w_out,
    w_gateup,
    w_down,
    gain_attn,
    gain_ffn,
    gain_sub,
    lambda_head,
    a_in,
    b_qkv,
    b_gateup,
    a_out,
    a_down,
    b_rows,
):
    tok_count = lax.axis_size("tok")
    fsdp_count = lax.axis_size("fsdp")
    me_tok = lax.axis_index("tok")
    seqs, local_len, _ = tokens.shape
    length = local_len * tok_count
    qw_here = w_qkv.shape[2]
    ff_here = w_gateup.shape[2]
    heads_here = qw_here // VALUE_DIM
    lambda_here = lax.dynamic_slice_in_dim(lambda_head, me_tok * heads_here, heads_here)
    positions = jnp.arange(length)
    offsets = adapter_id * RANK
    fsdp_rows = w_qkv.shape[1]
    groups_per_adapter = RANK // b_qkv.shape[1]

    a_in_tok = tok_gather(a_in)
    b_rows_tok = tok_gather(b_rows)
    small = [a_in_tok, b_rows_tok, b_qkv, b_gateup, a_out, a_down]
    small_flat = jnp.concatenate([p.reshape(-1, COLS) for p in small])
    (g_qkv, g_out, g_down, g_small), (g_gateup,) = torus_gather(
        [w_qkv[:, None], w_out[None], w_down[None], small_flat[None]],
        [1, 0, 0, 0],
        [w_gateup[:, None]],
        [1],
    )
    w_qkv_full = g_qkv.reshape(3, D, qw_here)
    w_out_full = jnp.moveaxis(g_out, 0, 1).reshape(qw_here, D)
    w_down_full = jnp.moveaxis(g_down, 0, 1).reshape(ff_here, D)
    w_gateup_perm = g_gateup.reshape(2, D, ff_here)
    unpacked = []
    start = 0
    for p in small:
        rows = p.size // COLS
        unpacked.append(g_small[:, start : start + rows].reshape((fsdp_count,) + p.shape))
        start += rows
    (g_ain, g_brows, g_bqkv, g_bgateup, g_aout, g_adown) = unpacked
    a_in_full = jnp.transpose(g_ain, (2, 0, 1, 3, 4)).reshape(5, D, COLS)
    b_rows_full = jnp.transpose(g_brows, (2, 3, 0, 1, 4)).reshape(2, COLS, D)

    def to_yzx(values):
        lead = values.shape[:-1]
        split = values.reshape(lead + (4, 2, 4, D // fsdp_count))
        n = len(lead)
        order = tuple(range(n)) + (n + 2, n + 1, n, n + 3)
        return jnp.transpose(split, order).reshape(values.shape)

    def from_yzx(values):
        lead = values.shape[:-1]
        split = values.reshape(lead + (4, 2, 4, D // fsdp_count))
        n = len(lead)
        order = tuple(range(n)) + (n + 2, n + 1, n, n + 3)
        return jnp.transpose(split, order).reshape(values.shape)

    def pick_cols(values, axis):
        return jnp.stack(
            [lax.dynamic_slice_in_dim(values, offsets[s], RANK, axis) for s in range(seqs)]
        )

    def pick_groups(values):
        return jnp.stack(
            [
                lax.dynamic_slice_in_dim(values, adapter_id[s] * groups_per_adapter, groups_per_adapter, 0)
                for s in range(seqs)
            ]
        )

    a_in_sel = pick_cols(a_in_full, 2)
    b_rows_sel = pick_cols(b_rows_full, 1)
    b_qkv_sel = jnp.moveaxis(pick_groups(g_bqkv), 1, 2).reshape(seqs, 3, RANK, qw_here)
    b_gateup_sel = jnp.moveaxis(pick_groups(g_bgateup), 1, 2).reshape(seqs, 2, RANK, ff_here)
    a_out_sel = jnp.moveaxis(pick_groups(g_aout), 1, 2).reshape(seqs, qw_here, RANK)
    a_down_sel = jnp.moveaxis(pick_groups(g_adown), 1, 2).reshape(seqs, ff_here, RANK)

    def gather_rows(values):
        full = tok_gather(values, 1)
        return full.reshape(seqs, length, values.shape[-1])

    def scatter_rows(values):
        return tok_scatter(values.reshape(seqs, tok_count, local_len, values.shape[-1]), 1)

    def column_forward(rows_full, weight, down_sel, up_sel, rows_for_weight=None):
        if rows_for_weight is None:
            rows_for_weight = rows_full
        lowrank = jnp.einsum("std,sdr->str", rows_full, down_sel, preferred_element_type=jnp.float32)
        linear = jnp.einsum("std,de->ste", rows_for_weight, weight, preferred_element_type=jnp.float32)
        return linear + adapter_scale * hp_dot(lowrank, up_sel.astype(jnp.float32), "str,sre->ste"), lowrank

    def row_forward(rows_here, weight, down_sel, up_sel):
        lowrank = jnp.einsum("std,sdr->str", rows_here, down_sel, preferred_element_type=jnp.float32)
        main_part = jnp.einsum("std,de->ste", rows_here, weight, preferred_element_type=jnp.float32)
        total = main_part + adapter_scale * hp_dot(lowrank, up_sel.astype(jnp.float32), "str,sre->ste")
        return scatter_rows(total), lowrank

    inputs_rows = tokens.astype(jnp.float32)
    allowed = (segments[:, :, None] == segments[:, None, :]) & (
        positions[:, None] >= positions[None, :]
    )[None]
    grad_ffn_full = gather_rows(cotangent)
    normed_rows, norm_attn_pull = jax.vjp(partial(rows_norm, gain_vector=gain_attn), inputs_rows)
    normed_full = gather_rows(normed_rows.astype(jnp.bfloat16))
    proj_lin = []
    proj_low = []
    for p in range(3):
        lin, lowr = column_forward(normed_full, w_qkv_full[p], a_in_sel[:, p], b_qkv_sel[:, p])
        proj_lin.append(lin)
        proj_low.append(lowr)
    rotate = partial(rotary_heads, positions=positions, head_dim=HEAD_DIM)
    query_rot, query_pull = jax.vjp(rotate, proj_lin[0])
    key_rot, key_pull = jax.vjp(rotate, proj_lin[1])
    query_in = query_rot.astype(jnp.bfloat16).reshape(seqs, length, heads_here, 2, HEAD_DIM)
    key_in = key_rot.astype(jnp.bfloat16).reshape(seqs, length, heads_here, 2, HEAD_DIM)
    value_in = proj_lin[2].astype(jnp.bfloat16).reshape(seqs, length, heads_here, VALUE_DIM)
    heads_out, log_total = jax.vmap(attend, in_axes=(0, 0, 0, 0, None))(
        query_in, key_in, value_in, allowed, lambda_here
    )
    mixed_float, head_pull = jax.vjp(partial(head_norm, gain_vector=gain_sub), heads_out)
    mixed_rows = mixed_float.reshape(seqs, length, qw_here).astype(jnp.bfloat16)
    attn_rows, out_low = row_forward(mixed_rows, w_out_full, a_out_sel, b_rows_sel[:, 0])
    hidden = inputs_rows + attn_rows
    normed_ffn, norm_ffn_pull = jax.vjp(partial(rows_norm, gain_vector=gain_ffn), hidden)
    ffn_full = gather_rows(normed_ffn.astype(jnp.bfloat16))
    ffn_perm = to_yzx(ffn_full)
    gate_lin, gate_low = column_forward(ffn_full, w_gateup_perm[0], a_in_sel[:, 3], b_gateup_sel[:, 0], ffn_perm)
    up_lin, up_low = column_forward(ffn_full, w_gateup_perm[1], a_in_sel[:, 4], b_gateup_sel[:, 1], ffn_perm)
    product_float, swiglu_pull = jax.vjp(swiglu, gate_lin, up_lin)
    product = product_float.astype(jnp.bfloat16)
    ffn_rows, down_low = row_forward(product, w_down_full, a_down_sel, b_rows_sel[:, 1])
    output = (hidden + ffn_rows).astype(jnp.bfloat16)
    row_lows = tok_sum(jnp.stack([out_low, down_low]))

    tangent = cotangent.astype(jnp.float32)

    def row_backward(grad_full, rows_here, weight, down_sel, up_sel):
        grad_float = grad_full.astype(jnp.float32)
        grad_low = adapter_scale * hp_dot(grad_float, up_sel.astype(jnp.float32), "ste,sre->str")
        grad_down = hp_dot(rows_here.astype(jnp.float32), grad_low, "std,str->sdr")
        grad_inputs = jnp.einsum(
            "ste,de->std", grad_full, weight, preferred_element_type=jnp.float32
        ) + hp_dot(grad_low, down_sel.astype(jnp.float32), "str,sdr->std")
        return grad_inputs, grad_down

    def column_backward(rows_full, entries, weight_order=None):
        running = None
        grad_lows = []
        grads_up = []
        for grad_rows, weight, down_sel, up_sel, lowrank in entries:
            grad_float = grad_rows.astype(jnp.float32)
            grad_low = adapter_scale * hp_dot(grad_float, up_sel.astype(jnp.float32), "ste,sre->str")
            grads_up.append(adapter_scale * hp_dot(lowrank, grad_float, "str,ste->sre"))
            grad_lows.append(grad_low)
            main_term = jnp.einsum("ste,de->std", grad_rows, weight, preferred_element_type=jnp.float32)
            if weight_order is not None:
                main_term = weight_order(main_term)
            term = main_term + hp_dot(grad_low, down_sel.astype(jnp.float32), "str,sdr->std")
            running = term if running is None else running + term
        return scatter_rows(running), grad_lows, grads_up

    def mine_of(values, axis):
        shape = values.shape
        split = values.reshape(
            shape[:axis] + (fsdp_count, tok_count, D // (fsdp_count * tok_count)) + shape[axis + 1 :]
        )
        return lax.dynamic_index_in_dim(split, me_tok, axis + 1, keepdims=False)

    grad_product, grad_a_down = row_backward(
        grad_ffn_full, product, w_down_full, a_down_sel, b_rows_sel[:, 1]
    )
    grad_gate, grad_up = swiglu_pull(grad_product)
    grad_ffn_rows, ffn_grad_lows, ffn_grads_up = column_backward(
        ffn_full,
        (
            (grad_gate.astype(jnp.bfloat16), w_gateup_perm[0], a_in_sel[:, 3], b_gateup_sel[:, 0], gate_low),
            (grad_up.astype(jnp.bfloat16), w_gateup_perm[1], a_in_sel[:, 4], b_gateup_sel[:, 1], up_low),
        ),
        from_yzx,
    )
    grad_hidden = tangent + norm_ffn_pull(grad_ffn_rows)[0]
    grad_attn_full = gather_rows(grad_hidden.astype(jnp.bfloat16))
    grad_mixed, grad_a_out = row_backward(
        grad_attn_full, mixed_rows, w_out_full, a_out_sel, b_rows_sel[:, 0]
    )
    grad_heads = head_pull(grad_mixed.reshape(seqs, length, heads_here, VALUE_DIM))[0].astype(
        jnp.bfloat16
    )
    grad_query_rot, grad_key_rot, grad_values = jax.vmap(
        attend_back, in_axes=(0, 0, 0, 0, None, 0, 0)
    )(query_in, key_in, value_in, allowed, lambda_here, log_total, grad_heads)
    grad_query = query_pull(grad_query_rot.reshape(seqs, length, qw_here))[0].astype(jnp.bfloat16)
    grad_key = key_pull(grad_key_rot.reshape(seqs, length, qw_here))[0].astype(jnp.bfloat16)
    grad_attn_rows, attn_grad_lows, attn_grads_up = column_backward(
        normed_full,
        (
            (grad_query, w_qkv_full[0], a_in_sel[:, 0], b_qkv_sel[:, 0], proj_low[0]),
            (grad_key, w_qkv_full[1], a_in_sel[:, 1], b_qkv_sel[:, 1], proj_low[1]),
            (grad_values.reshape(seqs, length, qw_here), w_qkv_full[2], a_in_sel[:, 2], b_qkv_sel[:, 2], proj_low[2]),
        ),
    )
    grad_tokens = grad_hidden + norm_attn_pull(grad_attn_rows)[0]

    grad_lows = tok_sum(jnp.stack(attn_grad_lows + ffn_grad_lows))
    grad_a_in_all = jnp.concatenate(
        [
            hp_dot(normed_full.astype(jnp.float32), grad_lows[:3], "std,pstr->psdr"),
            hp_dot(ffn_full.astype(jnp.float32), grad_lows[3:], "std,pstr->psdr"),
        ]
    )
    grad_a_in_part = mine_of(grad_a_in_all, 2)
    grad_b_rows_all = adapter_scale * jnp.stack(
        [
            hp_dot(row_lows[0], grad_attn_full.astype(jnp.float32), "str,std->srd"),
            hp_dot(row_lows[1], grad_ffn_full.astype(jnp.float32), "str,std->srd"),
        ]
    )
    grad_b_rows_part = mine_of(grad_b_rows_all, 3)

    def place(part, axis, total):
        shape = list(part.shape[1:])
        shape[axis] = total
        dense = jnp.zeros(shape, jnp.float32)
        for s in range(seqs):
            current = lax.dynamic_slice_in_dim(dense, offsets[s], RANK, axis)
            dense = lax.dynamic_update_slice_in_dim(dense, current + part[s], offsets[s], axis)
        return dense

    dense_a_in = place(jnp.moveaxis(grad_a_in_part, 1, 0), 3, COLS)
    dense_b_rows = place(jnp.moveaxis(grad_b_rows_part, 1, 0), 1, COLS)
    wide = jnp.concatenate(
        [
            jnp.moveaxis(dense_a_in, 1, 0).reshape(fsdp_count, -1),
            jnp.moveaxis(dense_b_rows, 2, 0).reshape(fsdp_count, -1),
        ],
        axis=1,
    )
    wide_sum = lax.all_to_all(wide, "fsdp", 0, 0, tiled=False).sum(0)
    a_in_block = wide_sum[: 5 * 16 * COLS].reshape(5, 16, COLS)
    b_rows_block = wide_sum[5 * 16 * COLS :].reshape(2, COLS, 16)

    dense_b_qkv = place(jnp.stack(attn_grads_up, 1), 1, COLS)
    dense_b_gateup = place(jnp.stack(ffn_grads_up, 1), 1, COLS)
    dense_a_out = place(grad_a_out, 1, COLS)
    dense_a_down = place(grad_a_down, 1, COLS)
    per = COLS // fsdp_count
    narrow = jnp.concatenate(
        [
            jnp.moveaxis(dense_b_qkv.reshape(3, fsdp_count, per, qw_here), 1, 0).reshape(fsdp_count, -1),
            jnp.moveaxis(dense_b_gateup.reshape(2, fsdp_count, per, ff_here), 1, 0).reshape(fsdp_count, -1),
            jnp.moveaxis(dense_a_out.reshape(qw_here, fsdp_count, per), 1, 0).reshape(fsdp_count, -1),
            jnp.moveaxis(dense_a_down.reshape(ff_here, fsdp_count, per), 1, 0).reshape(fsdp_count, -1),
        ],
        axis=1,
    ).astype(jnp.bfloat16)
    narrow_sum = lax.all_to_all(narrow, "fsdp", 0, 0, tiled=False).astype(jnp.float32).sum(0)
    sizes = [3 * per * qw_here, 2 * per * ff_here, qw_here * per, ff_here * per]
    cuts = [0]
    for size in sizes:
        cuts.append(cuts[-1] + size)
    b_qkv_block = narrow_sum[cuts[0] : cuts[1]].reshape(3, per, qw_here)
    b_gateup_block = narrow_sum[cuts[1] : cuts[2]].reshape(2, per, ff_here)
    a_out_block = narrow_sum[cuts[2] : cuts[3]].reshape(qw_here, per)
    a_down_block = narrow_sum[cuts[3] : cuts[4]].reshape(ff_here, per)

    return (
        output,
        grad_tokens,
        a_in_block,
        b_qkv_block,
        b_gateup_block,
        a_out_block,
        a_down_block,
        b_rows_block,
    )


def solution(mesh):
    return jax.shard_map(
        per_device,
        mesh=mesh,
        in_specs=(
            P("fsdp", "tok", None),
            P("fsdp", "tok", None),
            P("fsdp", None),
            P("fsdp"),
            P(None, "fsdp", "tok"),
            P("tok", "fsdp"),
            P(None, "fsdp", "tok"),
            P("tok", "fsdp"),
            P(),
            P(),
            P(),
            P(),
            P(None, ("fsdp", "tok"), None),
            P(None, "fsdp", "tok"),
            P(None, "fsdp", "tok"),
            P("tok", "fsdp"),
            P("tok", "fsdp"),
            P(None, None, ("fsdp", "tok")),
        ),
        out_specs=(
            P("fsdp", "tok", None),
            P("fsdp", "tok", None),
            P(None, ("fsdp", "tok"), None),
            P(None, "fsdp", "tok"),
            P(None, "fsdp", "tok"),
            P("tok", "fsdp"),
            P("tok", "fsdp"),
            P(None, None, ("fsdp", "tok")),
        ),
        check_vma=False,
    )
```

```python
from functools import partial

import jax
import jax.numpy as jnp
from jax import lax
from jax.sharding import PartitionSpec as P

D = 2048
HEAD_DIM = 128
VALUE_DIM = 256
RANK = 16
COLS = 128


highest = lax.Precision.HIGHEST
negative = -1e30
adapter_scale = 2.0
lambda_init = 0.2
rotary_base = 10000.0
row_epsilon = 1e-06
head_epsilon = 1e-05


def rows_norm(values, gain_vector):
    return (
        values
        * lax.rsqrt(jnp.mean(values * values, axis=-1, keepdims=True) + row_epsilon)
        * gain_vector
    )


def head_norm(values, gain_vector):
    scaled = values * lax.rsqrt(jnp.mean(values * values, axis=-1, keepdims=True) + head_epsilon)
    return scaled * gain_vector * (1.0 - lambda_init)


def rotary_heads(values, positions, head_dim):
    lead = values.shape[:-1]
    groups = values.reshape(lead + (-1, head_dim))
    half_dim = head_dim // 2
    frequency = rotary_base ** (-jnp.arange(half_dim, dtype=jnp.float32) / half_dim)
    angles = positions.astype(jnp.float32)[:, None] * frequency[None, :]
    cosine = jnp.cos(angles)[:, None, :]
    sine_part = jnp.sin(angles)[:, None, :]
    first_half = groups[..., :half_dim]
    second = groups[..., half_dim:]
    turned = jnp.concatenate(
        [first_half * cosine - second * sine_part, second * cosine + first_half * sine_part],
        axis=-1,
    )
    return turned.reshape(values.shape)


def swiglu(gate_rows, up_rows):
    return gate_rows * jax.nn.sigmoid(gate_rows) * up_rows


def attention_scores(query_in, key_in, allowed):
    raw_scores = jnp.einsum(
        "qhmd,khmd->hmqk", query_in, key_in, preferred_element_type=jnp.float32
    ) * query_in.shape[-1] ** (-0.5)
    return jnp.where(allowed[None, None], raw_scores, negative)


def attend(query_in, key_in, value_in, allowed, lambda_here):
    scores = attention_scores(query_in, key_in, allowed)
    row_max = jnp.max(scores, axis=-1, keepdims=True)
    log_total = row_max + jnp.log(jnp.sum(jnp.exp(scores - row_max), axis=-1, keepdims=True))
    soft_max = jnp.exp(scores - log_total)
    differ = (soft_max[:, 0] - lambda_here[:, None, None] * soft_max[:, 1]).astype(jnp.bfloat16)
    heads_out = jnp.einsum("hqk,khd->qhd", differ, value_in, preferred_element_type=jnp.float32)
    return (heads_out, log_total)


def attend_back(query_in, key_in, value_in, allowed, lambda_here, log_total, grad_heads):
    scale = query_in.shape[-1] ** (-0.5)
    scores = attention_scores(query_in, key_in, allowed)
    soft_max = jnp.exp(scores - log_total)
    differ = (soft_max[:, 0] - lambda_here[:, None, None] * soft_max[:, 1]).astype(jnp.bfloat16)
    grad_values = jnp.einsum("hqk,qhd->khd", differ, grad_heads, preferred_element_type=jnp.float32)
    grad_differ = jnp.einsum(
        "qhd,khd->hqk", grad_heads, value_in, preferred_element_type=jnp.float32
    )
    grad_soft = jnp.stack([grad_differ, -lambda_here[:, None, None] * grad_differ], axis=1)
    grad_scores = (
        soft_max * (grad_soft - jnp.sum(grad_soft * soft_max, axis=-1, keepdims=True))
    ).astype(jnp.bfloat16)
    grad_query = (
        jnp.einsum("hmqk,khmd->qhmd", grad_scores, key_in, preferred_element_type=jnp.float32)
        * scale
    )
    grad_key = (
        jnp.einsum("hmqk,qhmd->khmd", grad_scores, query_in, preferred_element_type=jnp.float32)
        * scale
    )
    return (grad_query, grad_key, grad_values.astype(jnp.bfloat16))


def xor_pairs(count, bit):
    return [(i, i ^ bit) for i in range(count)]


def tok_gather(values, axis=0):
    count = lax.axis_size("tok")
    me = lax.axis_index("tok")
    far = lax.ppermute(values, "tok", xor_pairs(count, 2))
    pair = jnp.where(
        (me & 2) == 0, jnp.stack([values, far], axis), jnp.stack([far, values], axis)
    )
    near = lax.ppermute(pair, "tok", xor_pairs(count, 1))
    full = jnp.where(
        (me & 1) == 0, jnp.stack([pair, near], axis + 1), jnp.stack([near, pair], axis + 1)
    )
    return full.reshape(values.shape[:axis] + (count,) + values.shape[axis:])


def tok_scatter(blocks, axis=0):
    count = lax.axis_size("tok")
    me = lax.axis_index("tok")
    core = me & 1
    half = (me >> 1) & 1
    split = blocks.reshape(blocks.shape[:axis] + (2, 2) + blocks.shape[axis + 1 :])
    mine = lax.dynamic_index_in_dim(split, core, axis + 1, keepdims=False)
    theirs = lax.dynamic_index_in_dim(split, 1 - core, axis + 1, keepdims=False)
    chip_sum = mine + lax.ppermute(theirs, "tok", xor_pairs(count, 1))
    keep = lax.dynamic_index_in_dim(chip_sum, half, axis, keepdims=False)
    send = lax.dynamic_index_in_dim(chip_sum, 1 - half, axis, keepdims=False)
    got = lax.ppermute(send.astype(jnp.bfloat16), "tok", xor_pairs(count, 2))
    return keep + got.astype(keep.dtype)


def tok_sum(values):
    count = lax.axis_size("tok")
    chip_sum = values + lax.ppermute(values, "tok", xor_pairs(count, 1))
    return chip_sum + lax.ppermute(chip_sum, "tok", xor_pairs(count, 2))


def fsdp_coords():
    me = lax.axis_index("fsdp")
    return {"x": me // 8, "z": (me // 4) % 2, "y": me % 4}


def fsdp_pairs(kind, step):
    pairs = []
    for x in range(4):
        for z in range(2):
            for y in range(4):
                if kind == "z":
                    target = (x * 2 + 1 - z) * 4 + y
                elif kind == "x":
                    target = (((x + step) % 4) * 2 + z) * 4 + y
                else:
                    target = (x * 2 + z) * 4 + (y + step) % 4
                pairs.append(((x * 2 + z) * 4 + y, target))
    return pairs


def put(buffer, piece, axis, offset):
    start = [0] * buffer.ndim
    start[axis] = offset
    return lax.dynamic_update_slice(buffer, piece, start)


def grow(pieces, axes, factor):
    return [
        jnp.zeros(p.shape[:ax] + (p.shape[ax] * factor,) + p.shape[ax + 1 :], p.dtype)
        for p, ax in zip(pieces, axes)
    ]


def halves(pieces, axes, second):
    out = []
    for p, ax in zip(pieces, axes):
        n = p.shape[ax] // 2
        out.append(lax.slice_in_dim(p, n if second else 0, 2 * n if second else n, axis=ax))
    return out


def pair_stage(stacks, axes, coord):
    other = lax.ppermute(stacks, "fsdp", fsdp_pairs("z", 1))
    outs = []
    for mine, theirs, buffer, ax in zip(stacks, other, grow(stacks, axes, 2), axes):
        n = mine.shape[ax]
        buffer = put(buffer, mine, ax, coord * n)
        outs.append(put(buffer, theirs, ax, (1 - coord) * n))
    return outs


def ring_stage(stacks, axes, kind, coord):
    from_left = lax.ppermute(stacks, "fsdp", fsdp_pairs(kind, 1))
    from_right = lax.ppermute(stacks, "fsdp", fsdp_pairs(kind, -1))
    split = stacks[0].shape[axes[0]] > 1
    if split:
        far_left = lax.ppermute(halves(from_left, axes, False), "fsdp", fsdp_pairs(kind, 1))
        far_right = lax.ppermute(halves(from_right, axes, True), "fsdp", fsdp_pairs(kind, -1))
    else:
        far_left = lax.ppermute(from_left, "fsdp", fsdp_pairs(kind, 1))
    outs = []
    for i, (buffer, ax) in enumerate(zip(grow(stacks, axes, 4), axes)):
        n = stacks[i].shape[ax]
        buffer = put(buffer, stacks[i], ax, coord * n)
        buffer = put(buffer, from_right[i], ax, ((coord + 1) % 4) * n)
        buffer = put(buffer, from_left[i], ax, ((coord + 3) % 4) * n)
        buffer = put(buffer, far_left[i], ax, ((coord + 2) % 4) * n)
        if split:
            buffer = put(buffer, far_right[i], ax, ((coord + 2) % 4) * n + n // 2)
        outs.append(buffer)
    return outs


def torus_gather(route_a, axes_a, route_b, axes_b):
    coord = fsdp_coords()
    route_a = ring_stage(route_a, axes_a, "y", coord["y"])
    route_b = ring_stage(route_b, axes_b, "x", coord["x"])
    both = pair_stage(route_a + route_b, axes_a + axes_b, coord["z"])
    route_a, route_b = both[: len(route_a)], both[len(route_a) :]
    return ring_stage(route_a, axes_a, "x", coord["x"]), ring_stage(route_b, axes_b, "y", coord["y"])


def hp_dot(left, right, spec):
    return jnp.einsum(spec, left, right, precision=highest, preferred_element_type=jnp.float32)


def per_device(
    tokens,
    cotangent,
    segments,
    adapter_id,
    w_qkv,
    w_out,
    w_gateup,
    w_down,
    gain_attn,
    gain_ffn,
    gain_sub,
    lambda_head,
    a_in,
    b_qkv,
    b_gateup,
    a_out,
    a_down,
    b_rows,
):
    tok_count = lax.axis_size("tok")
    fsdp_count = lax.axis_size("fsdp")
    me_tok = lax.axis_index("tok")
    seqs, local_len, _ = tokens.shape
    length = local_len * tok_count
    qw_here = w_qkv.shape[2]
    ff_here = w_gateup.shape[2]
    heads_here = qw_here // VALUE_DIM
    lambda_here = lax.dynamic_slice_in_dim(lambda_head, me_tok * heads_here, heads_here)
    positions = jnp.arange(length)
    offsets = adapter_id * RANK
    fsdp_rows = w_qkv.shape[1]
    groups_per_adapter = RANK // b_qkv.shape[1]

    a_in_tok = tok_gather(a_in)
    b_rows_tok = tok_gather(b_rows)
    small = [a_in_tok, b_rows_tok, b_qkv, b_gateup, a_out, a_down]
    small_flat = jnp.concatenate([p.reshape(-1, COLS) for p in small])
    (g_qkv, g_out, g_down, g_small), (g_gateup,) = torus_gather(
        [w_qkv[:, None], w_out[None], w_down[None], small_flat[None]],
        [1, 0, 0, 0],
        [w_gateup[:, None]],
        [1],
    )
    w_qkv_full = g_qkv.reshape(3, D, qw_here)
    w_out_full = jnp.moveaxis(g_out, 0, 1).reshape(qw_here, D)
    w_down_full = jnp.moveaxis(g_down, 0, 1).reshape(ff_here, D)
    w_gateup_perm = g_gateup.reshape(2, D, ff_here)
    unpacked = []
    start = 0
    for p in small:
        rows = p.size // COLS
        unpacked.append(g_small[:, start : start + rows].reshape((fsdp_count,) + p.shape))
        start += rows
    (g_ain, g_brows, g_bqkv, g_bgateup, g_aout, g_adown) = unpacked
    a_in_full = jnp.transpose(g_ain, (2, 0, 1, 3, 4)).reshape(5, D, COLS)
    b_rows_full = jnp.transpose(g_brows, (2, 3, 0, 1, 4)).reshape(2, COLS, D)

    def to_yzx(values):
        lead = values.shape[:-1]
        split = values.reshape(lead + (4, 2, 4, D // fsdp_count))
        n = len(lead)
        order = tuple(range(n)) + (n + 2, n + 1, n, n + 3)
        return jnp.transpose(split, order).reshape(values.shape)

    def from_yzx(values):
        lead = values.shape[:-1]
        split = values.reshape(lead + (4, 2, 4, D // fsdp_count))
        n = len(lead)
        order = tuple(range(n)) + (n + 2, n + 1, n, n + 3)
        return jnp.transpose(split, order).reshape(values.shape)

    def pick_cols(values, axis):
        return jnp.stack(
            [lax.dynamic_slice_in_dim(values, offsets[s], RANK, axis) for s in range(seqs)]
        )

    def pick_groups(values):
        return jnp.stack(
            [
                lax.dynamic_slice_in_dim(values, adapter_id[s] * groups_per_adapter, groups_per_adapter, 0)
                for s in range(seqs)
            ]
        )

    a_in_sel = pick_cols(a_in_full, 2)
    b_rows_sel = pick_cols(b_rows_full, 1)
    b_qkv_sel = jnp.moveaxis(pick_groups(g_bqkv), 1, 2).reshape(seqs, 3, RANK, qw_here)
    b_gateup_sel = jnp.moveaxis(pick_groups(g_bgateup), 1, 2).reshape(seqs, 2, RANK, ff_here)
    a_out_sel = jnp.moveaxis(pick_groups(g_aout), 1, 2).reshape(seqs, qw_here, RANK)
    a_down_sel = jnp.moveaxis(pick_groups(g_adown), 1, 2).reshape(seqs, ff_here, RANK)

    def gather_rows(values):
        full = tok_gather(values, 1)
        return full.reshape(seqs, length, values.shape[-1])

    def scatter_rows(values):
        return tok_scatter(values.reshape(seqs, tok_count, local_len, values.shape[-1]), 1)

    def column_forward(rows_full, weight, down_sel, up_sel, rows_for_weight=None):
        if rows_for_weight is None:
            rows_for_weight = rows_full
        lowrank = jnp.einsum("std,sdr->str", rows_full, down_sel, preferred_element_type=jnp.float32)
        linear = jnp.einsum("std,de->ste", rows_for_weight, weight, preferred_element_type=jnp.float32)
        return linear + adapter_scale * hp_dot(lowrank, up_sel.astype(jnp.float32), "str,sre->ste"), lowrank

    def row_forward(rows_here, weight, down_sel, up_sel):
        lowrank = jnp.einsum("std,sdr->str", rows_here, down_sel, preferred_element_type=jnp.float32)
        main_part = jnp.einsum("std,de->ste", rows_here, weight, preferred_element_type=jnp.float32)
        total = main_part + adapter_scale * hp_dot(lowrank, up_sel.astype(jnp.float32), "str,sre->ste")
        return scatter_rows(total), lowrank

    inputs_rows = tokens.astype(jnp.float32)
    allowed = (segments[:, :, None] == segments[:, None, :]) & (
        positions[:, None] >= positions[None, :]
    )[None]
    grad_ffn_full = gather_rows(cotangent)
    normed_rows, norm_attn_pull = jax.vjp(partial(rows_norm, gain_vector=gain_attn), inputs_rows)
    normed_full = gather_rows(normed_rows.astype(jnp.bfloat16))
    proj_lin = []
    proj_low = []
    for p in range(3):
        lin, lowr = column_forward(normed_full, w_qkv_full[p], a_in_sel[:, p], b_qkv_sel[:, p])
        proj_lin.append(lin)
        proj_low.append(lowr)
    rotate = partial(rotary_heads, positions=positions, head_dim=HEAD_DIM)
    query_rot, query_pull = jax.vjp(rotate, proj_lin[0])
    key_rot, key_pull = jax.vjp(rotate, proj_lin[1])
    query_in = query_rot.astype(jnp.bfloat16).reshape(seqs, length, heads_here, 2, HEAD_DIM)
    key_in = key_rot.astype(jnp.bfloat16).reshape(seqs, length, heads_here, 2, HEAD_DIM)
    value_in = proj_lin[2].astype(jnp.bfloat16).reshape(seqs, length, heads_here, VALUE_DIM)
    heads_out, log_total = jax.vmap(attend, in_axes=(0, 0, 0, 0, None))(
        query_in, key_in, value_in, allowed, lambda_here
    )
    mixed_float, head_pull = jax.vjp(partial(head_norm, gain_vector=gain_sub), heads_out)
    mixed_rows = mixed_float.reshape(seqs, length, qw_here).astype(jnp.bfloat16)
    attn_rows, out_low = row_forward(mixed_rows, w_out_full, a_out_sel, b_rows_sel[:, 0])
    hidden = inputs_rows + attn_rows
    normed_ffn, norm_ffn_pull = jax.vjp(partial(rows_norm, gain_vector=gain_ffn), hidden)
    ffn_full = gather_rows(normed_ffn.astype(jnp.bfloat16))
    ffn_perm = to_yzx(ffn_full)
    gate_lin, gate_low = column_forward(ffn_full, w_gateup_perm[0], a_in_sel[:, 3], b_gateup_sel[:, 0], ffn_perm)
    up_lin, up_low = column_forward(ffn_full, w_gateup_perm[1], a_in_sel[:, 4], b_gateup_sel[:, 1], ffn_perm)
    product_float, swiglu_pull = jax.vjp(swiglu, gate_lin, up_lin)
    product = product_float.astype(jnp.bfloat16)
    ffn_rows, down_low = row_forward(product, w_down_full, a_down_sel, b_rows_sel[:, 1])
    output = (hidden + ffn_rows).astype(jnp.bfloat16)
    row_lows = tok_sum(jnp.stack([out_low, down_low]))

    tangent = cotangent.astype(jnp.float32)

    def row_backward(grad_full, rows_here, weight, down_sel, up_sel):
        grad_float = grad_full.astype(jnp.float32)
        grad_low = adapter_scale * hp_dot(grad_float, up_sel.astype(jnp.float32), "ste,sre->str")
        grad_down = hp_dot(rows_here.astype(jnp.float32), grad_low, "std,str->sdr")
        grad_inputs = jnp.einsum(
            "ste,de->std", grad_full, weight, preferred_element_type=jnp.float32
        ) + hp_dot(grad_low, down_sel.astype(jnp.float32), "str,sdr->std")
        return grad_inputs, grad_down

    def column_backward(rows_full, entries, weight_order=None):
        running = None
        grad_lows = []
        grads_up = []
        for grad_rows, weight, down_sel, up_sel, lowrank in entries:
            grad_float = grad_rows.astype(jnp.float32)
            grad_low = adapter_scale * hp_dot(grad_float, up_sel.astype(jnp.float32), "ste,sre->str")
            grads_up.append(adapter_scale * hp_dot(lowrank, grad_float, "str,ste->sre"))
            grad_lows.append(grad_low)
            main_term = jnp.einsum("ste,de->std", grad_rows, weight, preferred_element_type=jnp.float32)
            if weight_order is not None:
                main_term = weight_order(main_term)
            term = main_term + hp_dot(grad_low, down_sel.astype(jnp.float32), "str,sdr->std")
            running = term if running is None else running + term
        return scatter_rows(running), grad_lows, grads_up

    def mine_of(values, axis):
        shape = values.shape
        split = values.reshape(
            shape[:axis] + (fsdp_count, tok_count, D // (fsdp_count * tok_count)) + shape[axis + 1 :]
        )
        return lax.dynamic_index_in_dim(split, me_tok, axis + 1, keepdims=False)

    grad_product, grad_a_down = row_backward(
        grad_ffn_full, product, w_down_full, a_down_sel, b_rows_sel[:, 1]
    )
    grad_gate, grad_up = swiglu_pull(grad_product)
    grad_ffn_rows, ffn_grad_lows, ffn_grads_up = column_backward(
        ffn_full,
        (
            (grad_gate.astype(jnp.bfloat16), w_gateup_perm[0], a_in_sel[:, 3], b_gateup_sel[:, 0], gate_low),
            (grad_up.astype(jnp.bfloat16), w_gateup_perm[1], a_in_sel[:, 4], b_gateup_sel[:, 1], up_low),
        ),
        from_yzx,
    )
    grad_hidden = tangent + norm_ffn_pull(grad_ffn_rows)[0]
    grad_attn_full = gather_rows(grad_hidden.astype(jnp.bfloat16))
    grad_mixed, grad_a_out = row_backward(
        grad_attn_full, mixed_rows, w_out_full, a_out_sel, b_rows_sel[:, 0]
    )
    grad_heads = head_pull(grad_mixed.reshape(seqs, length, heads_here, VALUE_DIM))[0].astype(
        jnp.bfloat16
    )
    grad_query_rot, grad_key_rot, grad_values = jax.vmap(
        attend_back, in_axes=(0, 0, 0, 0, None, 0, 0)
    )(query_in, key_in, value_in, allowed, lambda_here, log_total, grad_heads)
    grad_query = query_pull(grad_query_rot.reshape(seqs, length, qw_here))[0].astype(jnp.bfloat16)
    grad_key = key_pull(grad_key_rot.reshape(seqs, length, qw_here))[0].astype(jnp.bfloat16)
    grad_attn_rows, attn_grad_lows, attn_grads_up = column_backward(
        normed_full,
        (
            (grad_query, w_qkv_full[0], a_in_sel[:, 0], b_qkv_sel[:, 0], proj_low[0]),
            (grad_key, w_qkv_full[1], a_in_sel[:, 1], b_qkv_sel[:, 1], proj_low[1]),
            (grad_values.reshape(seqs, length, qw_here), w_qkv_full[2], a_in_sel[:, 2], b_qkv_sel[:, 2], proj_low[2]),
        ),
    )
    grad_tokens = grad_hidden + norm_attn_pull(grad_attn_rows)[0]

    grad_lows = tok_sum(jnp.stack(attn_grad_lows + ffn_grad_lows))
    onehot = (
        jnp.arange(COLS)[None, None, :] == offsets[:, None, None] + jnp.arange(RANK)[None, :, None]
    ).astype(jnp.float32)
    wide_lows = hp_dot(grad_lows, onehot, "pstr,src->pstc")
    dense_a_in = jnp.concatenate(
        [
            hp_dot(normed_full.astype(jnp.float32), wide_lows[:3], "std,pstc->pdc"),
            hp_dot(ffn_full.astype(jnp.float32), wide_lows[3:], "std,pstc->pdc"),
        ]
    )
    a_in_mine = lax.dynamic_index_in_dim(
        dense_a_in.reshape(5, fsdp_count, tok_count, RANK, COLS), me_tok, 2, keepdims=False
    )
    wide_row_lows = hp_dot(row_lows, onehot, "qstr,src->qstc")
    dense_b_rows = adapter_scale * hp_dot(
        wide_row_lows,
        jnp.stack([grad_attn_full, grad_ffn_full]).astype(jnp.float32),
        "qstc,qstd->qcd",
    )
    b_rows_mine = lax.dynamic_index_in_dim(
        dense_b_rows.reshape(2, COLS, fsdp_count, tok_count, RANK), me_tok, 3, keepdims=False
    )
    wide = jnp.concatenate(
        [
            jnp.moveaxis(a_in_mine, 1, 0).reshape(fsdp_count, -1),
            jnp.moveaxis(b_rows_mine, 2, 0).reshape(fsdp_count, -1),
        ],
        axis=1,
    )
    wide_sum = lax.all_to_all(wide, "fsdp", 0, 0, tiled=False).sum(0)
    a_in_block = wide_sum[: 5 * 16 * COLS].reshape(5, 16, COLS)
    b_rows_block = wide_sum[5 * 16 * COLS :].reshape(2, COLS, 16)

    dense_b_qkv = hp_dot(onehot, jnp.stack(attn_grads_up, 1), "src,spre->pce")
    dense_b_gateup = hp_dot(onehot, jnp.stack(ffn_grads_up, 1), "src,spre->pce")
    dense_a_out = hp_dot(grad_a_out, onehot, "sdr,src->dc")
    dense_a_down = hp_dot(grad_a_down, onehot, "sdr,src->dc")
    per = COLS // fsdp_count
    narrow = jnp.concatenate(
        [
            jnp.moveaxis(dense_b_qkv.reshape(3, fsdp_count, per, qw_here), 1, 0).reshape(fsdp_count, -1),
            jnp.moveaxis(dense_b_gateup.reshape(2, fsdp_count, per, ff_here), 1, 0).reshape(fsdp_count, -1),
            jnp.moveaxis(dense_a_out.reshape(qw_here, fsdp_count, per), 1, 0).reshape(fsdp_count, -1),
            jnp.moveaxis(dense_a_down.reshape(ff_here, fsdp_count, per), 1, 0).reshape(fsdp_count, -1),
        ],
        axis=1,
    ).astype(jnp.bfloat16)
    narrow_sum = lax.all_to_all(narrow, "fsdp", 0, 0, tiled=False).astype(jnp.float32).sum(0)
    sizes = [3 * per * qw_here, 2 * per * ff_here, qw_here * per, ff_here * per]
    cuts = [0]
    for size in sizes:
        cuts.append(cuts[-1] + size)
    b_qkv_block = narrow_sum[cuts[0] : cuts[1]].reshape(3, per, qw_here)
    b_gateup_block = narrow_sum[cuts[1] : cuts[2]].reshape(2, per, ff_here)
    a_out_block = narrow_sum[cuts[2] : cuts[3]].reshape(qw_here, per)
    a_down_block = narrow_sum[cuts[3] : cuts[4]].reshape(ff_here, per)

    return (
        output,
        grad_tokens,
        a_in_block,
        b_qkv_block,
        b_gateup_block,
        a_out_block,
        a_down_block,
        b_rows_block,
    )


def solution(mesh):
    return jax.shard_map(
        per_device,
        mesh=mesh,
        in_specs=(
            P("fsdp", "tok", None),
            P("fsdp", "tok", None),
            P("fsdp", None),
            P("fsdp"),
            P(None, "fsdp", "tok"),
            P("tok", "fsdp"),
            P(None, "fsdp", "tok"),
            P("tok", "fsdp"),
            P(),
            P(),
            P(),
            P(),
            P(None, ("fsdp", "tok"), None),
            P(None, "fsdp", "tok"),
            P(None, "fsdp", "tok"),
            P("tok", "fsdp"),
            P("tok", "fsdp"),
            P(None, None, ("fsdp", "tok")),
        ),
        out_specs=(
            P("fsdp", "tok", None),
            P("fsdp", "tok", None),
            P(None, ("fsdp", "tok"), None),
            P(None, "fsdp", "tok"),
            P(None, "fsdp", "tok"),
            P("tok", "fsdp"),
            P("tok", "fsdp"),
            P(None, None, ("fsdp", "tok")),
        ),
        check_vma=False,
    )
```

```python
from functools import partial

import jax
import jax.numpy as jnp
from jax import lax
from jax.sharding import PartitionSpec as P

D = 2048
HEAD_DIM = 128
VALUE_DIM = 256
RANK = 16
COLS = 128


highest = lax.Precision.HIGHEST
negative = -1e30
adapter_scale = 2.0
lambda_init = 0.2
rotary_base = 10000.0
row_epsilon = 1e-06
head_epsilon = 1e-05


def rows_norm(values, gain_vector):
    return (
        values
        * lax.rsqrt(jnp.mean(values * values, axis=-1, keepdims=True) + row_epsilon)
        * gain_vector
    )


def head_norm(values, gain_vector):
    scaled = values * lax.rsqrt(jnp.mean(values * values, axis=-1, keepdims=True) + head_epsilon)
    return scaled * gain_vector * (1.0 - lambda_init)


def rotary_heads(values, positions, head_dim):
    lead = values.shape[:-1]
    groups = values.reshape(lead + (-1, head_dim))
    half_dim = head_dim // 2
    frequency = rotary_base ** (-jnp.arange(half_dim, dtype=jnp.float32) / half_dim)
    angles = positions.astype(jnp.float32)[:, None] * frequency[None, :]
    cosine = jnp.cos(angles)[:, None, :]
    sine_part = jnp.sin(angles)[:, None, :]
    first_half = groups[..., :half_dim]
    second = groups[..., half_dim:]
    turned = jnp.concatenate(
        [first_half * cosine - second * sine_part, second * cosine + first_half * sine_part],
        axis=-1,
    )
    return turned.reshape(values.shape)


def swiglu(gate_rows, up_rows):
    return gate_rows * jax.nn.sigmoid(gate_rows) * up_rows


def attention_scores(query_in, key_in, allowed):
    raw_scores = jnp.einsum(
        "qhmd,khmd->hmqk", query_in, key_in, preferred_element_type=jnp.float32
    ) * query_in.shape[-1] ** (-0.5)
    return jnp.where(allowed[None, None], raw_scores, negative)


def attend(query_in, key_in, value_in, allowed, lambda_here):
    scores = attention_scores(query_in, key_in, allowed)
    row_max = jnp.max(scores, axis=-1, keepdims=True)
    log_total = row_max + jnp.log(jnp.sum(jnp.exp(scores - row_max), axis=-1, keepdims=True))
    soft_max = jnp.exp(scores - log_total)
    differ = (soft_max[:, 0] - lambda_here[:, None, None] * soft_max[:, 1]).astype(jnp.bfloat16)
    heads_out = jnp.einsum("hqk,khd->qhd", differ, value_in, preferred_element_type=jnp.float32)
    return (heads_out, log_total)


def attend_back(query_in, key_in, value_in, allowed, lambda_here, log_total, grad_heads):
    scale = query_in.shape[-1] ** (-0.5)
    scores = attention_scores(query_in, key_in, allowed)
    soft_max = jnp.exp(scores - log_total)
    differ = (soft_max[:, 0] - lambda_here[:, None, None] * soft_max[:, 1]).astype(jnp.bfloat16)
    grad_values = jnp.einsum("hqk,qhd->khd", differ, grad_heads, preferred_element_type=jnp.float32)
    grad_differ = jnp.einsum(
        "qhd,khd->hqk", grad_heads, value_in, preferred_element_type=jnp.float32
    )
    grad_soft = jnp.stack([grad_differ, -lambda_here[:, None, None] * grad_differ], axis=1)
    grad_scores = (
        soft_max * (grad_soft - jnp.sum(grad_soft * soft_max, axis=-1, keepdims=True))
    ).astype(jnp.bfloat16)
    grad_query = (
        jnp.einsum("hmqk,khmd->qhmd", grad_scores, key_in, preferred_element_type=jnp.float32)
        * scale
    )
    grad_key = (
        jnp.einsum("hmqk,qhmd->khmd", grad_scores, query_in, preferred_element_type=jnp.float32)
        * scale
    )
    return (grad_query, grad_key, grad_values.astype(jnp.bfloat16))


def xor_pairs(count, bit):
    return [(i, i ^ bit) for i in range(count)]


def tok_gather(values, axis=0):
    count = lax.axis_size("tok")
    me = lax.axis_index("tok")
    far = lax.ppermute(values, "tok", xor_pairs(count, 2))
    pair = jnp.where(
        (me & 2) == 0, jnp.stack([values, far], axis), jnp.stack([far, values], axis)
    )
    near = lax.ppermute(pair, "tok", xor_pairs(count, 1))
    full = jnp.where(
        (me & 1) == 0, jnp.stack([pair, near], axis + 1), jnp.stack([near, pair], axis + 1)
    )
    return full.reshape(values.shape[:axis] + (count,) + values.shape[axis:])


def tok_scatter(blocks, axis=0):
    count = lax.axis_size("tok")
    me = lax.axis_index("tok")
    core = me & 1
    half = (me >> 1) & 1
    split = blocks.reshape(blocks.shape[:axis] + (2, 2) + blocks.shape[axis + 1 :])
    mine = lax.dynamic_index_in_dim(split, core, axis + 1, keepdims=False)
    theirs = lax.dynamic_index_in_dim(split, 1 - core, axis + 1, keepdims=False)
    chip_sum = mine + lax.ppermute(theirs, "tok", xor_pairs(count, 1))
    keep = lax.dynamic_index_in_dim(chip_sum, half, axis, keepdims=False)
    send = lax.dynamic_index_in_dim(chip_sum, 1 - half, axis, keepdims=False)
    got = lax.ppermute(send.astype(jnp.bfloat16), "tok", xor_pairs(count, 2))
    return keep + got.astype(keep.dtype)


def tok_gather_rel(values, axis):
    count = lax.axis_size("tok")
    far = lax.ppermute(values, "tok", xor_pairs(count, 2))
    pair = jnp.stack([values, far], axis)
    near = lax.ppermute(pair, "tok", xor_pairs(count, 1))
    full = jnp.stack([pair, near], axis + 1)
    return full.reshape(values.shape[:axis] + (count,) + values.shape[axis:])


def tok_scatter_rel(blocks, axis):
    count = lax.axis_size("tok")
    split = blocks.reshape(blocks.shape[:axis] + (2, 2) + blocks.shape[axis + 1 :])
    mine = lax.index_in_dim(split, 0, axis + 1, keepdims=False)
    theirs = lax.index_in_dim(split, 1, axis + 1, keepdims=False)
    chip_sum = mine + lax.ppermute(theirs, "tok", xor_pairs(count, 1))
    keep = lax.index_in_dim(chip_sum, 0, axis, keepdims=False)
    send = lax.index_in_dim(chip_sum, 1, axis, keepdims=False)
    got = lax.ppermute(send.astype(jnp.bfloat16), "tok", xor_pairs(count, 2))
    return keep + got.astype(keep.dtype)


def tok_sum_rows(values, axis):
    count = lax.axis_size("tok")
    shape = values.shape
    split_shape = shape[:axis] + (2, 2, shape[axis] // 4) + shape[axis + 1 :]

    def swapped(other, block_axis):
        return jnp.flip(other.reshape(split_shape), axis + block_axis).reshape(shape)

    chip_sum = values + swapped(lax.ppermute(values, "tok", xor_pairs(count, 1)), 1)
    return chip_sum + swapped(lax.ppermute(chip_sum, "tok", xor_pairs(count, 2)), 0)


def tok_sum(values):
    count = lax.axis_size("tok")
    chip_sum = values + lax.ppermute(values, "tok", xor_pairs(count, 1))
    return chip_sum + lax.ppermute(chip_sum, "tok", xor_pairs(count, 2))


def fsdp_coords():
    me = lax.axis_index("fsdp")
    return {"x": me // 8, "z": (me // 4) % 2, "y": me % 4}


def fsdp_pairs(kind, step):
    pairs = []
    for x in range(4):
        for z in range(2):
            for y in range(4):
                if kind == "z":
                    target = (x * 2 + 1 - z) * 4 + y
                elif kind == "x":
                    target = (((x + step) % 4) * 2 + z) * 4 + y
                else:
                    target = (x * 2 + z) * 4 + (y + step) % 4
                pairs.append(((x * 2 + z) * 4 + y, target))
    return pairs


def put(buffer, piece, axis, offset):
    start = [0] * buffer.ndim
    start[axis] = offset
    return lax.dynamic_update_slice(buffer, piece, start)


def grow(pieces, axes, factor):
    return [
        jnp.zeros(p.shape[:ax] + (p.shape[ax] * factor,) + p.shape[ax + 1 :], p.dtype)
        for p, ax in zip(pieces, axes)
    ]


def halves(pieces, axes, second):
    out = []
    for p, ax in zip(pieces, axes):
        n = p.shape[ax] // 2
        out.append(lax.slice_in_dim(p, n if second else 0, 2 * n if second else n, axis=ax))
    return out


def pair_stage(stacks, axes, coord):
    other = lax.ppermute(stacks, "fsdp", fsdp_pairs("z", 1))
    outs = []
    for mine, theirs, buffer, ax in zip(stacks, other, grow(stacks, axes, 2), axes):
        n = mine.shape[ax]
        buffer = put(buffer, mine, ax, coord * n)
        outs.append(put(buffer, theirs, ax, (1 - coord) * n))
    return outs


def ring_stage(stacks, axes, kind, coord):
    from_left = lax.ppermute(stacks, "fsdp", fsdp_pairs(kind, 1))
    from_right = lax.ppermute(stacks, "fsdp", fsdp_pairs(kind, -1))
    split = stacks[0].shape[axes[0]] > 1
    if split:
        far_left = lax.ppermute(halves(from_left, axes, False), "fsdp", fsdp_pairs(kind, 1))
        far_right = lax.ppermute(halves(from_right, axes, True), "fsdp", fsdp_pairs(kind, -1))
    else:
        far_left = lax.ppermute(from_left, "fsdp", fsdp_pairs(kind, 1))
    outs = []
    for i, (buffer, ax) in enumerate(zip(grow(stacks, axes, 4), axes)):
        n = stacks[i].shape[ax]
        buffer = put(buffer, stacks[i], ax, coord * n)
        buffer = put(buffer, from_right[i], ax, ((coord + 1) % 4) * n)
        buffer = put(buffer, from_left[i], ax, ((coord + 3) % 4) * n)
        buffer = put(buffer, far_left[i], ax, ((coord + 2) % 4) * n)
        if split:
            buffer = put(buffer, far_right[i], ax, ((coord + 2) % 4) * n + n // 2)
        outs.append(buffer)
    return outs


def torus_gather(route_a, axes_a, route_b, axes_b):
    coord = fsdp_coords()
    route_a = ring_stage(route_a, axes_a, "y", coord["y"])
    route_b = ring_stage(route_b, axes_b, "x", coord["x"])
    both = pair_stage(route_a + route_b, axes_a + axes_b, coord["z"])
    route_a, route_b = both[: len(route_a)], both[len(route_a) :]
    return ring_stage(route_a, axes_a, "x", coord["x"]), ring_stage(route_b, axes_b, "y", coord["y"])


def hp_dot(left, right, spec):
    return jnp.einsum(spec, left, right, precision=highest, preferred_element_type=jnp.float32)


def per_device(
    tokens,
    cotangent,
    segments,
    adapter_id,
    w_qkv,
    w_out,
    w_gateup,
    w_down,
    gain_attn,
    gain_ffn,
    gain_sub,
    lambda_head,
    a_in,
    b_qkv,
    b_gateup,
    a_out,
    a_down,
    b_rows,
):
    tok_count = lax.axis_size("tok")
    fsdp_count = lax.axis_size("fsdp")
    me_tok = lax.axis_index("tok")
    seqs, local_len, _ = tokens.shape
    length = local_len * tok_count
    qw_here = w_qkv.shape[2]
    ff_here = w_gateup.shape[2]
    heads_here = qw_here // VALUE_DIM
    lambda_here = lax.dynamic_slice_in_dim(lambda_head, me_tok * heads_here, heads_here)
    rows_at = jnp.arange(length)
    positions = (me_tok ^ (rows_at // local_len)) * local_len + rows_at % local_len
    offsets = adapter_id * RANK
    fsdp_rows = w_qkv.shape[1]
    groups_per_adapter = RANK // b_qkv.shape[1]

    a_in_tok = tok_gather(a_in)
    b_rows_tok = tok_gather(b_rows)
    small = [a_in_tok, b_rows_tok, b_qkv, b_gateup, a_out, a_down]
    small_flat = jnp.concatenate([p.reshape(-1, COLS) for p in small])
    (g_qkv, g_out, g_down, g_small), (g_gateup,) = torus_gather(
        [w_qkv[:, None], w_out[None], w_down[None], small_flat[None]],
        [1, 0, 0, 0],
        [w_gateup[:, None]],
        [1],
    )
    w_qkv_full = g_qkv.reshape(3, D, qw_here)
    w_out_full = jnp.moveaxis(g_out, 0, 1).reshape(qw_here, D)
    w_down_full = jnp.moveaxis(g_down, 0, 1).reshape(ff_here, D)
    w_gateup_perm = g_gateup.reshape(2, D, ff_here)
    unpacked = []
    start = 0
    for p in small:
        rows = p.size // COLS
        unpacked.append(g_small[:, start : start + rows].reshape((fsdp_count,) + p.shape))
        start += rows
    (g_ain, g_brows, g_bqkv, g_bgateup, g_aout, g_adown) = unpacked
    a_in_full = jnp.transpose(g_ain, (2, 0, 1, 3, 4)).reshape(5, D, COLS)
    b_rows_full = jnp.transpose(g_brows, (2, 3, 0, 1, 4)).reshape(2, COLS, D)

    def to_yzx(values):
        lead = values.shape[:-1]
        split = values.reshape(lead + (4, 2, 4, D // fsdp_count))
        n = len(lead)
        order = tuple(range(n)) + (n + 2, n + 1, n, n + 3)
        return jnp.transpose(split, order).reshape(values.shape)

    def from_yzx(values):
        lead = values.shape[:-1]
        split = values.reshape(lead + (4, 2, 4, D // fsdp_count))
        n = len(lead)
        order = tuple(range(n)) + (n + 2, n + 1, n, n + 3)
        return jnp.transpose(split, order).reshape(values.shape)

    def pick_cols(values, axis):
        return jnp.stack(
            [lax.dynamic_slice_in_dim(values, offsets[s], RANK, axis) for s in range(seqs)]
        )

    def pick_groups(values):
        return jnp.stack(
            [
                lax.dynamic_slice_in_dim(values, adapter_id[s] * groups_per_adapter, groups_per_adapter, 0)
                for s in range(seqs)
            ]
        )

    a_in_sel = pick_cols(a_in_full, 2)
    b_rows_sel = pick_cols(b_rows_full, 1)
    b_qkv_sel = jnp.moveaxis(pick_groups(g_bqkv), 1, 2).reshape(seqs, 3, RANK, qw_here)
    b_gateup_sel = jnp.moveaxis(pick_groups(g_bgateup), 1, 2).reshape(seqs, 2, RANK, ff_here)
    a_out_sel = jnp.moveaxis(pick_groups(g_aout), 1, 2).reshape(seqs, qw_here, RANK)
    a_down_sel = jnp.moveaxis(pick_groups(g_adown), 1, 2).reshape(seqs, ff_here, RANK)

    def gather_rows(values):
        full = tok_gather_rel(values, 1)
        return full.reshape(seqs, length, values.shape[-1])

    def scatter_rows(values):
        return tok_scatter_rel(values.reshape(seqs, tok_count, local_len, values.shape[-1]), 1)

    def column_forward(rows_full, weight, down_sel, up_sel, rows_for_weight=None):
        if rows_for_weight is None:
            rows_for_weight = rows_full
        lowrank = jnp.einsum("std,sdr->str", rows_full, down_sel, preferred_element_type=jnp.float32)
        linear = jnp.einsum("std,de->ste", rows_for_weight, weight, preferred_element_type=jnp.float32)
        return linear + adapter_scale * hp_dot(lowrank, up_sel.astype(jnp.float32), "str,sre->ste"), lowrank

    def row_forward(rows_here, weight, down_sel, up_sel):
        lowrank = jnp.einsum("std,sdr->str", rows_here, down_sel, preferred_element_type=jnp.float32)
        main_part = jnp.einsum("std,de->ste", rows_here, weight, preferred_element_type=jnp.float32)
        total = main_part + adapter_scale * hp_dot(lowrank, up_sel.astype(jnp.float32), "str,sre->ste")
        return scatter_rows(total), lowrank

    inputs_rows = tokens.astype(jnp.float32)
    segments = jnp.take(segments, positions, axis=1)
    allowed = (segments[:, :, None] == segments[:, None, :]) & (
        positions[:, None] >= positions[None, :]
    )[None]
    grad_ffn_full = gather_rows(cotangent)
    normed_rows, norm_attn_pull = jax.vjp(partial(rows_norm, gain_vector=gain_attn), inputs_rows)
    normed_full = gather_rows(normed_rows.astype(jnp.bfloat16))
    proj_lin = []
    proj_low = []
    for p in range(3):
        lin, lowr = column_forward(normed_full, w_qkv_full[p], a_in_sel[:, p], b_qkv_sel[:, p])
        proj_lin.append(lin)
        proj_low.append(lowr)
    rotate = partial(rotary_heads, positions=positions, head_dim=HEAD_DIM)
    query_rot, query_pull = jax.vjp(rotate, proj_lin[0])
    key_rot, key_pull = jax.vjp(rotate, proj_lin[1])
    query_in = query_rot.astype(jnp.bfloat16).reshape(seqs, length, heads_here, 2, HEAD_DIM)
    key_in = key_rot.astype(jnp.bfloat16).reshape(seqs, length, heads_here, 2, HEAD_DIM)
    value_in = proj_lin[2].astype(jnp.bfloat16).reshape(seqs, length, heads_here, VALUE_DIM)
    heads_out, log_total = jax.vmap(attend, in_axes=(0, 0, 0, 0, None))(
        query_in, key_in, value_in, allowed, lambda_here
    )
    mixed_float, head_pull = jax.vjp(partial(head_norm, gain_vector=gain_sub), heads_out)
    mixed_rows = mixed_float.reshape(seqs, length, qw_here).astype(jnp.bfloat16)
    attn_rows, out_low = row_forward(mixed_rows, w_out_full, a_out_sel, b_rows_sel[:, 0])
    hidden = inputs_rows + attn_rows
    normed_ffn, norm_ffn_pull = jax.vjp(partial(rows_norm, gain_vector=gain_ffn), hidden)
    ffn_full = gather_rows(normed_ffn.astype(jnp.bfloat16))
    ffn_perm = to_yzx(ffn_full)
    gate_lin, gate_low = column_forward(ffn_full, w_gateup_perm[0], a_in_sel[:, 3], b_gateup_sel[:, 0], ffn_perm)
    up_lin, up_low = column_forward(ffn_full, w_gateup_perm[1], a_in_sel[:, 4], b_gateup_sel[:, 1], ffn_perm)
    product_float, swiglu_pull = jax.vjp(swiglu, gate_lin, up_lin)
    product = product_float.astype(jnp.bfloat16)
    ffn_rows, down_low = row_forward(product, w_down_full, a_down_sel, b_rows_sel[:, 1])
    output = (hidden + ffn_rows).astype(jnp.bfloat16)
    row_lows = tok_sum_rows(jnp.stack([out_low, down_low]), 2)

    tangent = cotangent.astype(jnp.float32)

    def row_backward(grad_full, rows_here, weight, down_sel, up_sel):
        grad_float = grad_full.astype(jnp.float32)
        grad_low = adapter_scale * hp_dot(grad_float, up_sel.astype(jnp.float32), "ste,sre->str")
        grad_down = hp_dot(rows_here.astype(jnp.float32), grad_low, "std,str->sdr")
        grad_inputs = jnp.einsum(
            "ste,de->std", grad_full, weight, preferred_element_type=jnp.float32
        ) + hp_dot(grad_low, down_sel.astype(jnp.float32), "str,sdr->std")
        return grad_inputs, grad_down

    def column_backward(rows_full, entries, weight_order=None):
        running = None
        grad_lows = []
        grads_up = []
        for grad_rows, weight, down_sel, up_sel, lowrank in entries:
            grad_float = grad_rows.astype(jnp.float32)
            grad_low = adapter_scale * hp_dot(grad_float, up_sel.astype(jnp.float32), "ste,sre->str")
            grads_up.append(adapter_scale * hp_dot(lowrank, grad_float, "str,ste->sre"))
            grad_lows.append(grad_low)
            main_term = jnp.einsum("ste,de->std", grad_rows, weight, preferred_element_type=jnp.float32)
            if weight_order is not None:
                main_term = weight_order(main_term)
            term = main_term + hp_dot(grad_low, down_sel.astype(jnp.float32), "str,sdr->std")
            running = term if running is None else running + term
        return scatter_rows(running), grad_lows, grads_up

    def mine_of(values, axis):
        shape = values.shape
        split = values.reshape(
            shape[:axis] + (fsdp_count, tok_count, D // (fsdp_count * tok_count)) + shape[axis + 1 :]
        )
        return lax.dynamic_index_in_dim(split, me_tok, axis + 1, keepdims=False)

    grad_product, grad_a_down = row_backward(
        grad_ffn_full, product, w_down_full, a_down_sel, b_rows_sel[:, 1]
    )
    grad_gate, grad_up = swiglu_pull(grad_product)
    grad_ffn_rows, ffn_grad_lows, ffn_grads_up = column_backward(
        ffn_full,
        (
            (grad_gate.astype(jnp.bfloat16), w_gateup_perm[0], a_in_sel[:, 3], b_gateup_sel[:, 0], gate_low),
            (grad_up.astype(jnp.bfloat16), w_gateup_perm[1], a_in_sel[:, 4], b_gateup_sel[:, 1], up_low),
        ),
        from_yzx,
    )
    grad_hidden = tangent + norm_ffn_pull(grad_ffn_rows)[0]
    grad_attn_full = gather_rows(grad_hidden.astype(jnp.bfloat16))
    grad_mixed, grad_a_out = row_backward(
        grad_attn_full, mixed_rows, w_out_full, a_out_sel, b_rows_sel[:, 0]
    )
    grad_heads = head_pull(grad_mixed.reshape(seqs, length, heads_here, VALUE_DIM))[0].astype(
        jnp.bfloat16
    )
    grad_query_rot, grad_key_rot, grad_values = jax.vmap(
        attend_back, in_axes=(0, 0, 0, 0, None, 0, 0)
    )(query_in, key_in, value_in, allowed, lambda_here, log_total, grad_heads)
    grad_query = query_pull(grad_query_rot.reshape(seqs, length, qw_here))[0].astype(jnp.bfloat16)
    grad_key = key_pull(grad_key_rot.reshape(seqs, length, qw_here))[0].astype(jnp.bfloat16)
    grad_attn_rows, attn_grad_lows, attn_grads_up = column_backward(
        normed_full,
        (
            (grad_query, w_qkv_full[0], a_in_sel[:, 0], b_qkv_sel[:, 0], proj_low[0]),
            (grad_key, w_qkv_full[1], a_in_sel[:, 1], b_qkv_sel[:, 1], proj_low[1]),
            (grad_values.reshape(seqs, length, qw_here), w_qkv_full[2], a_in_sel[:, 2], b_qkv_sel[:, 2], proj_low[2]),
        ),
    )
    grad_tokens = grad_hidden + norm_attn_pull(grad_attn_rows)[0]

    grad_lows = tok_sum_rows(jnp.stack(attn_grad_lows + ffn_grad_lows), 2)
    onehot = (
        jnp.arange(COLS)[None, None, :] == offsets[:, None, None] + jnp.arange(RANK)[None, :, None]
    ).astype(jnp.float32)
    wide_lows = hp_dot(grad_lows, onehot, "pstr,src->pstc")
    dense_a_in = jnp.concatenate(
        [
            hp_dot(normed_full.astype(jnp.float32), wide_lows[:3], "std,pstc->pdc"),
            hp_dot(ffn_full.astype(jnp.float32), wide_lows[3:], "std,pstc->pdc"),
        ]
    )
    a_in_mine = lax.dynamic_index_in_dim(
        dense_a_in.reshape(5, fsdp_count, tok_count, RANK, COLS), me_tok, 2, keepdims=False
    )
    wide_row_lows = hp_dot(row_lows, onehot, "qstr,src->qstc")
    dense_b_rows = adapter_scale * hp_dot(
        wide_row_lows,
        jnp.stack([grad_attn_full, grad_ffn_full]).astype(jnp.float32),
        "qstc,qstd->qcd",
    )
    b_rows_mine = lax.dynamic_index_in_dim(
        dense_b_rows.reshape(2, COLS, fsdp_count, tok_count, RANK), me_tok, 3, keepdims=False
    )
    wide = jnp.concatenate(
        [
            jnp.moveaxis(a_in_mine, 1, 0).reshape(fsdp_count, -1),
            jnp.moveaxis(b_rows_mine, 2, 0).reshape(fsdp_count, -1),
        ],
        axis=1,
    )
    wide_sum = lax.all_to_all(wide, "fsdp", 0, 0, tiled=False).sum(0)
    a_in_block = wide_sum[: 5 * 16 * COLS].reshape(5, 16, COLS)
    b_rows_block = wide_sum[5 * 16 * COLS :].reshape(2, COLS, 16)

    dense_b_qkv = hp_dot(onehot, jnp.stack(attn_grads_up, 1), "src,spre->pce")
    dense_b_gateup = hp_dot(onehot, jnp.stack(ffn_grads_up, 1), "src,spre->pce")
    dense_a_out = hp_dot(grad_a_out, onehot, "sdr,src->dc")
    dense_a_down = hp_dot(grad_a_down, onehot, "sdr,src->dc")
    per = COLS // fsdp_count
    narrow = jnp.concatenate(
        [
            jnp.moveaxis(dense_b_qkv.reshape(3, fsdp_count, per, qw_here), 1, 0).reshape(fsdp_count, -1),
            jnp.moveaxis(dense_b_gateup.reshape(2, fsdp_count, per, ff_here), 1, 0).reshape(fsdp_count, -1),
            jnp.moveaxis(dense_a_out.reshape(qw_here, fsdp_count, per), 1, 0).reshape(fsdp_count, -1),
            jnp.moveaxis(dense_a_down.reshape(ff_here, fsdp_count, per), 1, 0).reshape(fsdp_count, -1),
        ],
        axis=1,
    ).astype(jnp.bfloat16)
    narrow_sum = lax.all_to_all(narrow, "fsdp", 0, 0, tiled=False).astype(jnp.float32).sum(0)
    sizes = [3 * per * qw_here, 2 * per * ff_here, qw_here * per, ff_here * per]
    cuts = [0]
    for size in sizes:
        cuts.append(cuts[-1] + size)
    b_qkv_block = narrow_sum[cuts[0] : cuts[1]].reshape(3, per, qw_here)
    b_gateup_block = narrow_sum[cuts[1] : cuts[2]].reshape(2, per, ff_here)
    a_out_block = narrow_sum[cuts[2] : cuts[3]].reshape(qw_here, per)
    a_down_block = narrow_sum[cuts[3] : cuts[4]].reshape(ff_here, per)

    return (
        output,
        grad_tokens,
        a_in_block,
        b_qkv_block,
        b_gateup_block,
        a_out_block,
        a_down_block,
        b_rows_block,
    )


def solution(mesh):
    return jax.shard_map(
        per_device,
        mesh=mesh,
        in_specs=(
            P("fsdp", "tok", None),
            P("fsdp", "tok", None),
            P("fsdp", None),
            P("fsdp"),
            P(None, "fsdp", "tok"),
            P("tok", "fsdp"),
            P(None, "fsdp", "tok"),
            P("tok", "fsdp"),
            P(),
            P(),
            P(),
            P(),
            P(None, ("fsdp", "tok"), None),
            P(None, "fsdp", "tok"),
            P(None, "fsdp", "tok"),
            P("tok", "fsdp"),
            P("tok", "fsdp"),
            P(None, None, ("fsdp", "tok")),
        ),
        out_specs=(
            P("fsdp", "tok", None),
            P("fsdp", "tok", None),
            P(None, ("fsdp", "tok"), None),
            P(None, "fsdp", "tok"),
            P(None, "fsdp", "tok"),
            P("tok", "fsdp"),
            P("tok", "fsdp"),
            P(None, None, ("fsdp", "tok")),
        ),
        check_vma=False,
    )
```

```python
from functools import partial

import jax
import jax.numpy as jnp
from jax import lax
from jax.sharding import PartitionSpec as P

D = 2048
HEAD_DIM = 128
VALUE_DIM = 256
RANK = 16
COLS = 128


highest = lax.Precision.HIGHEST
negative = -1e30
adapter_scale = 2.0
lambda_init = 0.2
rotary_base = 10000.0
row_epsilon = 1e-06
head_epsilon = 1e-05


def rows_norm(values, gain_vector):
    return (
        values
        * lax.rsqrt(jnp.mean(values * values, axis=-1, keepdims=True) + row_epsilon)
        * gain_vector
    )


def head_norm(values, gain_vector):
    scaled = values * lax.rsqrt(jnp.mean(values * values, axis=-1, keepdims=True) + head_epsilon)
    return scaled * gain_vector * (1.0 - lambda_init)


def rotary_heads(values, positions, head_dim):
    lead = values.shape[:-1]
    groups = values.reshape(lead + (-1, head_dim))
    half_dim = head_dim // 2
    frequency = rotary_base ** (-jnp.arange(half_dim, dtype=jnp.float32) / half_dim)
    angles = positions.astype(jnp.float32)[:, None] * frequency[None, :]
    cosine = jnp.cos(angles)[:, None, :]
    sine_part = jnp.sin(angles)[:, None, :]
    first_half = groups[..., :half_dim]
    second = groups[..., half_dim:]
    turned = jnp.concatenate(
        [first_half * cosine - second * sine_part, second * cosine + first_half * sine_part],
        axis=-1,
    )
    return turned.reshape(values.shape)


def swiglu(gate_rows, up_rows):
    return gate_rows * jax.nn.sigmoid(gate_rows) * up_rows


def attention_scores(query_in, key_in, allowed):
    raw_scores = jnp.einsum(
        "qhmd,khmd->hmqk", query_in, key_in, preferred_element_type=jnp.float32
    ) * query_in.shape[-1] ** (-0.5)
    return jnp.where(allowed[None, None], raw_scores, negative)


def attend(query_in, key_in, value_in, allowed, lambda_here):
    scores = attention_scores(query_in, key_in, allowed)
    row_max = jnp.max(scores, axis=-1, keepdims=True)
    log_total = row_max + jnp.log(jnp.sum(jnp.exp(scores - row_max), axis=-1, keepdims=True))
    soft_max = jnp.exp(scores - log_total)
    differ = (soft_max[:, 0] - lambda_here[:, None, None] * soft_max[:, 1]).astype(jnp.bfloat16)
    heads_out = jnp.einsum("hqk,khd->qhd", differ, value_in, preferred_element_type=jnp.float32)
    return (heads_out, log_total)


def attend_back(query_in, key_in, value_in, allowed, lambda_here, log_total, grad_heads):
    scale = query_in.shape[-1] ** (-0.5)
    scores = attention_scores(query_in, key_in, allowed)
    soft_max = jnp.exp(scores - log_total)
    differ = (soft_max[:, 0] - lambda_here[:, None, None] * soft_max[:, 1]).astype(jnp.bfloat16)
    grad_values = jnp.einsum("hqk,qhd->khd", differ, grad_heads, preferred_element_type=jnp.float32)
    grad_differ = jnp.einsum(
        "qhd,khd->hqk", grad_heads, value_in, preferred_element_type=jnp.float32
    )
    grad_soft = jnp.stack([grad_differ, -lambda_here[:, None, None] * grad_differ], axis=1)
    grad_scores = (
        soft_max * (grad_soft - jnp.sum(grad_soft * soft_max, axis=-1, keepdims=True))
    ).astype(jnp.bfloat16)
    grad_query = (
        jnp.einsum("hmqk,khmd->qhmd", grad_scores, key_in, preferred_element_type=jnp.float32)
        * scale
    )
    grad_key = (
        jnp.einsum("hmqk,qhmd->khmd", grad_scores, query_in, preferred_element_type=jnp.float32)
        * scale
    )
    return (grad_query, grad_key, grad_values.astype(jnp.bfloat16))


def xor_pairs(count, bit):
    return [(i, i ^ bit) for i in range(count)]


def tok_gather(values, axis=0):
    count = lax.axis_size("tok")
    me = lax.axis_index("tok")
    far = lax.ppermute(values, "tok", xor_pairs(count, 2))
    pair = jnp.where(
        (me & 2) == 0, jnp.stack([values, far], axis), jnp.stack([far, values], axis)
    )
    near = lax.ppermute(pair, "tok", xor_pairs(count, 1))
    full = jnp.where(
        (me & 1) == 0, jnp.stack([pair, near], axis + 1), jnp.stack([near, pair], axis + 1)
    )
    return full.reshape(values.shape[:axis] + (count,) + values.shape[axis:])


def tok_scatter(blocks, axis=0):
    count = lax.axis_size("tok")
    me = lax.axis_index("tok")
    core = me & 1
    half = (me >> 1) & 1
    split = blocks.reshape(blocks.shape[:axis] + (2, 2) + blocks.shape[axis + 1 :])
    mine = lax.dynamic_index_in_dim(split, core, axis + 1, keepdims=False)
    theirs = lax.dynamic_index_in_dim(split, 1 - core, axis + 1, keepdims=False)
    chip_sum = mine + lax.ppermute(theirs, "tok", xor_pairs(count, 1))
    keep = lax.dynamic_index_in_dim(chip_sum, half, axis, keepdims=False)
    send = lax.dynamic_index_in_dim(chip_sum, 1 - half, axis, keepdims=False)
    got = lax.ppermute(send.astype(jnp.bfloat16), "tok", xor_pairs(count, 2))
    return keep + got.astype(keep.dtype)


def tok_sum(values):
    count = lax.axis_size("tok")
    chip_sum = values + lax.ppermute(values, "tok", xor_pairs(count, 1))
    return chip_sum + lax.ppermute(chip_sum, "tok", xor_pairs(count, 2))


def fsdp_coords():
    me = lax.axis_index("fsdp")
    return {"x": me // 8, "z": (me // 4) % 2, "y": me % 4}


def fsdp_pairs(kind, step):
    pairs = []
    for x in range(4):
        for z in range(2):
            for y in range(4):
                if kind == "z":
                    target = (x * 2 + 1 - z) * 4 + y
                elif kind == "x":
                    target = (((x + step) % 4) * 2 + z) * 4 + y
                else:
                    target = (x * 2 + z) * 4 + (y + step) % 4
                pairs.append(((x * 2 + z) * 4 + y, target))
    return pairs


def put(buffer, piece, axis, offset):
    start = [0] * buffer.ndim
    start[axis] = offset
    return lax.dynamic_update_slice(buffer, piece, start)


def grow(pieces, axes, factor):
    return [
        jnp.zeros(p.shape[:ax] + (p.shape[ax] * factor,) + p.shape[ax + 1 :], p.dtype)
        for p, ax in zip(pieces, axes)
    ]


def halves(pieces, axes, second):
    out = []
    for p, ax in zip(pieces, axes):
        n = p.shape[ax] // 2
        out.append(lax.slice_in_dim(p, n if second else 0, 2 * n if second else n, axis=ax))
    return out


def pair_stage(stacks, axes, coord):
    other = lax.ppermute(stacks, "fsdp", fsdp_pairs("z", 1))
    outs = []
    for mine, theirs, buffer, ax in zip(stacks, other, grow(stacks, axes, 2), axes):
        n = mine.shape[ax]
        buffer = put(buffer, mine, ax, coord * n)
        outs.append(put(buffer, theirs, ax, (1 - coord) * n))
    return outs


def ring_stage(stacks, axes, kind, coord):
    from_left = lax.ppermute(stacks, "fsdp", fsdp_pairs(kind, 1))
    from_right = lax.ppermute(stacks, "fsdp", fsdp_pairs(kind, -1))
    split = stacks[0].shape[axes[0]] > 1
    if split:
        far_left = lax.ppermute(halves(from_left, axes, False), "fsdp", fsdp_pairs(kind, 1))
        far_right = lax.ppermute(halves(from_right, axes, True), "fsdp", fsdp_pairs(kind, -1))
    else:
        far_left = lax.ppermute(from_left, "fsdp", fsdp_pairs(kind, 1))
    outs = []
    for i, (buffer, ax) in enumerate(zip(grow(stacks, axes, 4), axes)):
        n = stacks[i].shape[ax]
        buffer = put(buffer, stacks[i], ax, coord * n)
        buffer = put(buffer, from_right[i], ax, ((coord + 1) % 4) * n)
        buffer = put(buffer, from_left[i], ax, ((coord + 3) % 4) * n)
        buffer = put(buffer, far_left[i], ax, ((coord + 2) % 4) * n)
        if split:
            buffer = put(buffer, far_right[i], ax, ((coord + 2) % 4) * n + n // 2)
        outs.append(buffer)
    return outs


def torus_gather(route_a, axes_a, route_b, axes_b):
    coord = fsdp_coords()
    route_a = ring_stage(route_a, axes_a, "y", coord["y"])
    route_b = ring_stage(route_b, axes_b, "x", coord["x"])
    both = pair_stage(route_a + route_b, axes_a + axes_b, coord["z"])
    route_a, route_b = both[: len(route_a)], both[len(route_a) :]
    return ring_stage(route_a, axes_a, "x", coord["x"]), ring_stage(route_b, axes_b, "y", coord["y"])


def hp_dot(left, right, spec):
    return jnp.einsum(spec, left, right, precision=highest, preferred_element_type=jnp.float32)


def per_device(
    tokens,
    cotangent,
    segments,
    adapter_id,
    w_qkv,
    w_out,
    w_gateup,
    w_down,
    gain_attn,
    gain_ffn,
    gain_sub,
    lambda_head,
    a_in,
    b_qkv,
    b_gateup,
    a_out,
    a_down,
    b_rows,
):
    tok_count = lax.axis_size("tok")
    fsdp_count = lax.axis_size("fsdp")
    me_tok = lax.axis_index("tok")
    seqs, local_len, _ = tokens.shape
    length = local_len * tok_count
    qw_here = w_qkv.shape[2]
    ff_here = w_gateup.shape[2]
    heads_here = qw_here // VALUE_DIM
    lambda_here = lax.dynamic_slice_in_dim(lambda_head, me_tok * heads_here, heads_here)
    positions = jnp.arange(length)
    offsets = adapter_id * RANK
    fsdp_rows = w_qkv.shape[1]
    groups_per_adapter = RANK // b_qkv.shape[1]

    a_in_tok = tok_gather(a_in)
    b_rows_tok = tok_gather(b_rows)
    small = [a_in_tok, b_rows_tok, b_qkv, b_gateup, a_out, a_down]
    small_flat = jnp.concatenate([p.reshape(-1, COLS) for p in small])
    (g_qkv, g_out, g_down, g_small), (g_gateup,) = torus_gather(
        [w_qkv[:, None], w_out[None], w_down[None], small_flat[None]],
        [1, 0, 0, 0],
        [w_gateup[:, None]],
        [1],
    )
    w_qkv_full = g_qkv.reshape(3, D, qw_here)
    w_out_full = jnp.moveaxis(g_out, 0, 1).reshape(qw_here, D)
    w_down_full = jnp.moveaxis(g_down, 0, 1).reshape(ff_here, D)
    w_gateup_perm = g_gateup.reshape(2, D, ff_here)
    unpacked = []
    start = 0
    for p in small:
        rows = p.size // COLS
        unpacked.append(g_small[:, start : start + rows].reshape((fsdp_count,) + p.shape))
        start += rows
    (g_ain, g_brows, g_bqkv, g_bgateup, g_aout, g_adown) = unpacked
    pick = (
        jnp.arange(COLS)[None, None, :] == offsets[:, None, None] + jnp.arange(RANK)[None, :, None]
    ).astype(jnp.bfloat16)
    a_in_pick = jnp.einsum("ftpic,src->spftir", g_ain, pick, preferred_element_type=jnp.float32)
    a_in_pick = a_in_pick.astype(jnp.bfloat16).reshape(seqs, 5, D, RANK)
    b_rows_pick = jnp.einsum("src,ftqcj->sqrftj", pick, g_brows, preferred_element_type=jnp.float32)
    b_rows_pick = b_rows_pick.astype(jnp.bfloat16).reshape(seqs, 2, RANK, D)

    def to_yzx(values):
        lead = values.shape[:-1]
        split = values.reshape(lead + (4, 2, 4, D // fsdp_count))
        n = len(lead)
        order = tuple(range(n)) + (n + 2, n + 1, n, n + 3)
        return jnp.transpose(split, order).reshape(values.shape)

    def from_yzx(values):
        lead = values.shape[:-1]
        split = values.reshape(lead + (4, 2, 4, D // fsdp_count))
        n = len(lead)
        order = tuple(range(n)) + (n + 2, n + 1, n, n + 3)
        return jnp.transpose(split, order).reshape(values.shape)

    def pick_cols(values, axis):
        return jnp.stack(
            [lax.dynamic_slice_in_dim(values, offsets[s], RANK, axis) for s in range(seqs)]
        )

    def pick_groups(values):
        return jnp.stack(
            [
                lax.dynamic_slice_in_dim(values, adapter_id[s] * groups_per_adapter, groups_per_adapter, 0)
                for s in range(seqs)
            ]
        )

    a_in_sel = a_in_pick
    b_rows_sel = b_rows_pick
    b_qkv_sel = jnp.moveaxis(pick_groups(g_bqkv), 1, 2).reshape(seqs, 3, RANK, qw_here)
    b_gateup_sel = jnp.moveaxis(pick_groups(g_bgateup), 1, 2).reshape(seqs, 2, RANK, ff_here)
    a_out_sel = jnp.moveaxis(pick_groups(g_aout), 1, 2).reshape(seqs, qw_here, RANK)
    a_down_sel = jnp.moveaxis(pick_groups(g_adown), 1, 2).reshape(seqs, ff_here, RANK)

    def gather_rows(values):
        full = tok_gather(values, 1)
        return full.reshape(seqs, length, values.shape[-1])

    def scatter_rows(values):
        return tok_scatter(values.reshape(seqs, tok_count, local_len, values.shape[-1]), 1)

    def column_forward(rows_full, weight, down_sel, up_sel, rows_for_weight=None):
        if rows_for_weight is None:
            rows_for_weight = rows_full
        lowrank = jnp.einsum("std,sdr->str", rows_full, down_sel, preferred_element_type=jnp.float32)
        linear = jnp.einsum("std,de->ste", rows_for_weight, weight, preferred_element_type=jnp.float32)
        return linear + adapter_scale * hp_dot(lowrank, up_sel.astype(jnp.float32), "str,sre->ste"), lowrank

    def row_forward(rows_here, weight, down_sel, up_sel):
        lowrank = jnp.einsum("std,sdr->str", rows_here, down_sel, preferred_element_type=jnp.float32)
        main_part = jnp.einsum("std,de->ste", rows_here, weight, preferred_element_type=jnp.float32)
        total = main_part + adapter_scale * hp_dot(lowrank, up_sel.astype(jnp.float32), "str,sre->ste")
        return scatter_rows(total), lowrank

    inputs_rows = tokens.astype(jnp.float32)
    allowed = (segments[:, :, None] == segments[:, None, :]) & (
        positions[:, None] >= positions[None, :]
    )[None]
    grad_ffn_full = gather_rows(cotangent)
    normed_rows, norm_attn_pull = jax.vjp(partial(rows_norm, gain_vector=gain_attn), inputs_rows)
    normed_full = gather_rows(normed_rows.astype(jnp.bfloat16))
    proj_lin = []
    proj_low = []
    for p in range(3):
        lin, lowr = column_forward(normed_full, w_qkv_full[p], a_in_sel[:, p], b_qkv_sel[:, p])
        proj_lin.append(lin)
        proj_low.append(lowr)
    rotate = partial(rotary_heads, positions=positions, head_dim=HEAD_DIM)
    query_rot, query_pull = jax.vjp(rotate, proj_lin[0])
    key_rot, key_pull = jax.vjp(rotate, proj_lin[1])
    query_in = query_rot.astype(jnp.bfloat16).reshape(seqs, length, heads_here, 2, HEAD_DIM)
    key_in = key_rot.astype(jnp.bfloat16).reshape(seqs, length, heads_here, 2, HEAD_DIM)
    value_in = proj_lin[2].astype(jnp.bfloat16).reshape(seqs, length, heads_here, VALUE_DIM)
    heads_out, log_total = jax.vmap(attend, in_axes=(0, 0, 0, 0, None))(
        query_in, key_in, value_in, allowed, lambda_here
    )
    mixed_float, head_pull = jax.vjp(partial(head_norm, gain_vector=gain_sub), heads_out)
    mixed_rows = mixed_float.reshape(seqs, length, qw_here).astype(jnp.bfloat16)
    attn_rows, out_low = row_forward(mixed_rows, w_out_full, a_out_sel, b_rows_sel[:, 0])
    hidden = inputs_rows + attn_rows
    normed_ffn, norm_ffn_pull = jax.vjp(partial(rows_norm, gain_vector=gain_ffn), hidden)
    ffn_full = gather_rows(normed_ffn.astype(jnp.bfloat16))
    ffn_perm = to_yzx(ffn_full)
    gate_lin, gate_low = column_forward(ffn_full, w_gateup_perm[0], a_in_sel[:, 3], b_gateup_sel[:, 0], ffn_perm)
    up_lin, up_low = column_forward(ffn_full, w_gateup_perm[1], a_in_sel[:, 4], b_gateup_sel[:, 1], ffn_perm)
    product_float, swiglu_pull = jax.vjp(swiglu, gate_lin, up_lin)
    product = product_float.astype(jnp.bfloat16)
    ffn_rows, down_low = row_forward(product, w_down_full, a_down_sel, b_rows_sel[:, 1])
    output = (hidden + ffn_rows).astype(jnp.bfloat16)
    row_lows = tok_sum(jnp.stack([out_low, down_low]))

    tangent = cotangent.astype(jnp.float32)

    def row_backward(grad_full, rows_here, weight, down_sel, up_sel):
        grad_float = grad_full.astype(jnp.float32)
        grad_low = adapter_scale * hp_dot(grad_float, up_sel.astype(jnp.float32), "ste,sre->str")
        grad_down = hp_dot(rows_here.astype(jnp.float32), grad_low, "std,str->sdr")
        grad_inputs = jnp.einsum(
            "ste,de->std", grad_full, weight, preferred_element_type=jnp.float32
        ) + hp_dot(grad_low, down_sel.astype(jnp.float32), "str,sdr->std")
        return grad_inputs, grad_down

    def column_backward(rows_full, entries, weight_order=None):
        running = None
        grad_lows = []
        grads_up = []
        for grad_rows, weight, down_sel, up_sel, lowrank in entries:
            grad_float = grad_rows.astype(jnp.float32)
            grad_low = adapter_scale * hp_dot(grad_float, up_sel.astype(jnp.float32), "ste,sre->str")
            grads_up.append(adapter_scale * hp_dot(lowrank, grad_float, "str,ste->sre"))
            grad_lows.append(grad_low)
            main_term = jnp.einsum("ste,de->std", grad_rows, weight, preferred_element_type=jnp.float32)
            if weight_order is not None:
                main_term = weight_order(main_term)
            term = main_term + hp_dot(grad_low, down_sel.astype(jnp.float32), "str,sdr->std")
            running = term if running is None else running + term
        return scatter_rows(running), grad_lows, grads_up

    def mine_of(values, axis):
        shape = values.shape
        split = values.reshape(
            shape[:axis] + (fsdp_count, tok_count, D // (fsdp_count * tok_count)) + shape[axis + 1 :]
        )
        return lax.dynamic_index_in_dim(split, me_tok, axis + 1, keepdims=False)

    grad_product, grad_a_down = row_backward(
        grad_ffn_full, product, w_down_full, a_down_sel, b_rows_sel[:, 1]
    )
    grad_gate, grad_up = swiglu_pull(grad_product)
    grad_ffn_rows, ffn_grad_lows, ffn_grads_up = column_backward(
        ffn_full,
        (
            (grad_gate.astype(jnp.bfloat16), w_gateup_perm[0], a_in_sel[:, 3], b_gateup_sel[:, 0], gate_low),
            (grad_up.astype(jnp.bfloat16), w_gateup_perm[1], a_in_sel[:, 4], b_gateup_sel[:, 1], up_low),
        ),
        from_yzx,
    )
    grad_hidden = tangent + norm_ffn_pull(grad_ffn_rows)[0]
    grad_attn_full = gather_rows(grad_hidden.astype(jnp.bfloat16))
    grad_mixed, grad_a_out = row_backward(
        grad_attn_full, mixed_rows, w_out_full, a_out_sel, b_rows_sel[:, 0]
    )
    grad_heads = head_pull(grad_mixed.reshape(seqs, length, heads_here, VALUE_DIM))[0].astype(
        jnp.bfloat16
    )
    grad_query_rot, grad_key_rot, grad_values = jax.vmap(
        attend_back, in_axes=(0, 0, 0, 0, None, 0, 0)
    )(query_in, key_in, value_in, allowed, lambda_here, log_total, grad_heads)
    grad_query = query_pull(grad_query_rot.reshape(seqs, length, qw_here))[0].astype(jnp.bfloat16)
    grad_key = key_pull(grad_key_rot.reshape(seqs, length, qw_here))[0].astype(jnp.bfloat16)
    grad_attn_rows, attn_grad_lows, attn_grads_up = column_backward(
        normed_full,
        (
            (grad_query, w_qkv_full[0], a_in_sel[:, 0], b_qkv_sel[:, 0], proj_low[0]),
            (grad_key, w_qkv_full[1], a_in_sel[:, 1], b_qkv_sel[:, 1], proj_low[1]),
            (grad_values.reshape(seqs, length, qw_here), w_qkv_full[2], a_in_sel[:, 2], b_qkv_sel[:, 2], proj_low[2]),
        ),
    )
    grad_tokens = grad_hidden + norm_attn_pull(grad_attn_rows)[0]

    grad_lows = tok_sum(jnp.stack(attn_grad_lows + ffn_grad_lows))
    onehot = (
        jnp.arange(COLS)[None, None, :] == offsets[:, None, None] + jnp.arange(RANK)[None, :, None]
    ).astype(jnp.float32)
    wide_lows = hp_dot(grad_lows, onehot, "pstr,src->pstc")
    dense_a_in = jnp.concatenate(
        [
            hp_dot(normed_full.astype(jnp.float32), wide_lows[:3], "std,pstc->pdc"),
            hp_dot(ffn_full.astype(jnp.float32), wide_lows[3:], "std,pstc->pdc"),
        ]
    )
    a_in_mine = lax.dynamic_index_in_dim(
        dense_a_in.reshape(5, fsdp_count, tok_count, RANK, COLS), me_tok, 2, keepdims=False
    )
    wide_row_lows = hp_dot(row_lows, onehot, "qstr,src->qstc")
    dense_b_rows = adapter_scale * hp_dot(
        wide_row_lows,
        jnp.stack([grad_attn_full, grad_ffn_full]).astype(jnp.float32),
        "qstc,qstd->qcd",
    )
    b_rows_mine = lax.dynamic_index_in_dim(
        dense_b_rows.reshape(2, COLS, fsdp_count, tok_count, RANK), me_tok, 3, keepdims=False
    )
    wide = jnp.concatenate(
        [
            jnp.moveaxis(a_in_mine, 1, 0).reshape(fsdp_count, -1),
            jnp.moveaxis(b_rows_mine, 2, 0).reshape(fsdp_count, -1),
        ],
        axis=1,
    )
    wide_sum = lax.all_to_all(wide, "fsdp", 0, 0, tiled=False).sum(0)
    a_in_block = wide_sum[: 5 * 16 * COLS].reshape(5, 16, COLS)
    b_rows_block = wide_sum[5 * 16 * COLS :].reshape(2, COLS, 16)

    dense_b_qkv = hp_dot(onehot, jnp.stack(attn_grads_up, 1), "src,spre->pce")
    dense_b_gateup = hp_dot(onehot, jnp.stack(ffn_grads_up, 1), "src,spre->pce")
    dense_a_out = hp_dot(grad_a_out, onehot, "sdr,src->dc")
    dense_a_down = hp_dot(grad_a_down, onehot, "sdr,src->dc")
    per = COLS // fsdp_count
    narrow = jnp.concatenate(
        [
            jnp.moveaxis(dense_b_qkv.reshape(3, fsdp_count, per, qw_here), 1, 0).reshape(fsdp_count, -1),
            jnp.moveaxis(dense_b_gateup.reshape(2, fsdp_count, per, ff_here), 1, 0).reshape(fsdp_count, -1),
            jnp.moveaxis(dense_a_out.reshape(qw_here, fsdp_count, per), 1, 0).reshape(fsdp_count, -1),
            jnp.moveaxis(dense_a_down.reshape(ff_here, fsdp_count, per), 1, 0).reshape(fsdp_count, -1),
        ],
        axis=1,
    ).astype(jnp.bfloat16)
    narrow_sum = lax.all_to_all(narrow, "fsdp", 0, 0, tiled=False).astype(jnp.float32).sum(0)
    sizes = [3 * per * qw_here, 2 * per * ff_here, qw_here * per, ff_here * per]
    cuts = [0]
    for size in sizes:
        cuts.append(cuts[-1] + size)
    b_qkv_block = narrow_sum[cuts[0] : cuts[1]].reshape(3, per, qw_here)
    b_gateup_block = narrow_sum[cuts[1] : cuts[2]].reshape(2, per, ff_here)
    a_out_block = narrow_sum[cuts[2] : cuts[3]].reshape(qw_here, per)
    a_down_block = narrow_sum[cuts[3] : cuts[4]].reshape(ff_here, per)

    return (
        output,
        grad_tokens,
        a_in_block,
        b_qkv_block,
        b_gateup_block,
        a_out_block,
        a_down_block,
        b_rows_block,
    )


def solution(mesh):
    return jax.shard_map(
        per_device,
        mesh=mesh,
        in_specs=(
            P("fsdp", "tok", None),
            P("fsdp", "tok", None),
            P("fsdp", None),
            P("fsdp"),
            P(None, "fsdp", "tok"),
            P("tok", "fsdp"),
            P(None, "fsdp", "tok"),
            P("tok", "fsdp"),
            P(),
            P(),
            P(),
            P(),
            P(None, ("fsdp", "tok"), None),
            P(None, "fsdp", "tok"),
            P(None, "fsdp", "tok"),
            P("tok", "fsdp"),
            P("tok", "fsdp"),
            P(None, None, ("fsdp", "tok")),
        ),
        out_specs=(
            P("fsdp", "tok", None),
            P("fsdp", "tok", None),
            P(None, ("fsdp", "tok"), None),
            P(None, "fsdp", "tok"),
            P(None, "fsdp", "tok"),
            P("tok", "fsdp"),
            P("tok", "fsdp"),
            P(None, None, ("fsdp", "tok")),
        ),
        check_vma=False,
    )
```

```python
from functools import partial

import jax
import jax.numpy as jnp
from jax import lax
from jax.sharding import PartitionSpec as P

D = 2048
HEAD_DIM = 128
VALUE_DIM = 256
RANK = 16
COLS = 128


highest = lax.Precision.HIGHEST
negative = -1e30
adapter_scale = 2.0
lambda_init = 0.2
rotary_base = 10000.0
row_epsilon = 1e-06
head_epsilon = 1e-05


def rows_norm(values, gain_vector):
    return (
        values
        * lax.rsqrt(jnp.mean(values * values, axis=-1, keepdims=True) + row_epsilon)
        * gain_vector
    )


def head_norm(values, gain_vector):
    scaled = values * lax.rsqrt(jnp.mean(values * values, axis=-1, keepdims=True) + head_epsilon)
    return scaled * gain_vector * (1.0 - lambda_init)


def rotary_heads(values, positions, head_dim):
    lead = values.shape[:-1]
    groups = values.reshape(lead + (-1, head_dim))
    half_dim = head_dim // 2
    frequency = rotary_base ** (-jnp.arange(half_dim, dtype=jnp.float32) / half_dim)
    angles = positions.astype(jnp.float32)[:, None] * frequency[None, :]
    cosine = jnp.cos(angles)[:, None, :]
    sine_part = jnp.sin(angles)[:, None, :]
    first_half = groups[..., :half_dim]
    second = groups[..., half_dim:]
    turned = jnp.concatenate(
        [first_half * cosine - second * sine_part, second * cosine + first_half * sine_part],
        axis=-1,
    )
    return turned.reshape(values.shape)


def swiglu(gate_rows, up_rows):
    return gate_rows * jax.nn.sigmoid(gate_rows) * up_rows


def attention_scores(query_in, key_in, allowed):
    raw_scores = jnp.einsum(
        "qhmd,khmd->hmqk", query_in, key_in, preferred_element_type=jnp.float32
    ) * query_in.shape[-1] ** (-0.5)
    return jnp.where(allowed[None, None], raw_scores, negative)


def attend(query_in, key_in, value_in, allowed, lambda_here):
    scores = attention_scores(query_in, key_in, allowed)
    row_max = jnp.max(scores, axis=-1, keepdims=True)
    log_total = row_max + jnp.log(jnp.sum(jnp.exp(scores - row_max), axis=-1, keepdims=True))
    soft_max = jnp.exp(scores - log_total)
    differ = (soft_max[:, 0] - lambda_here[:, None, None] * soft_max[:, 1]).astype(jnp.bfloat16)
    heads_out = jnp.einsum("hqk,khd->qhd", differ, value_in, preferred_element_type=jnp.float32)
    return (heads_out, log_total)


def attend_back(query_in, key_in, value_in, allowed, lambda_here, log_total, grad_heads):
    scale = query_in.shape[-1] ** (-0.5)
    scores = attention_scores(query_in, key_in, allowed)
    soft_max = jnp.exp(scores - log_total)
    differ = (soft_max[:, 0] - lambda_here[:, None, None] * soft_max[:, 1]).astype(jnp.bfloat16)
    grad_values = jnp.einsum("hqk,qhd->khd", differ, grad_heads, preferred_element_type=jnp.float32)
    grad_differ = jnp.einsum(
        "qhd,khd->hqk", grad_heads, value_in, preferred_element_type=jnp.float32
    )
    grad_soft = jnp.stack([grad_differ, -lambda_here[:, None, None] * grad_differ], axis=1)
    grad_scores = (
        soft_max * (grad_soft - jnp.sum(grad_soft * soft_max, axis=-1, keepdims=True))
    ).astype(jnp.bfloat16)
    grad_query = (
        jnp.einsum("hmqk,khmd->qhmd", grad_scores, key_in, preferred_element_type=jnp.float32)
        * scale
    )
    grad_key = (
        jnp.einsum("hmqk,qhmd->khmd", grad_scores, query_in, preferred_element_type=jnp.float32)
        * scale
    )
    return (grad_query, grad_key, grad_values.astype(jnp.bfloat16))


def xor_pairs(count, bit):
    return [(i, i ^ bit) for i in range(count)]


def tok_gather(values, axis=0):
    count = lax.axis_size("tok")
    me = lax.axis_index("tok")
    far = lax.ppermute(values, "tok", xor_pairs(count, 2))
    pair = jnp.where(
        (me & 2) == 0, jnp.stack([values, far], axis), jnp.stack([far, values], axis)
    )
    near = lax.ppermute(pair, "tok", xor_pairs(count, 1))
    full = jnp.where(
        (me & 1) == 0, jnp.stack([pair, near], axis + 1), jnp.stack([near, pair], axis + 1)
    )
    return full.reshape(values.shape[:axis] + (count,) + values.shape[axis:])


def tok_scatter(blocks, axis=0):
    count = lax.axis_size("tok")
    me = lax.axis_index("tok")
    core = me & 1
    half = (me >> 1) & 1
    split = blocks.reshape(blocks.shape[:axis] + (2, 2) + blocks.shape[axis + 1 :])
    mine = lax.dynamic_index_in_dim(split, core, axis + 1, keepdims=False)
    theirs = lax.dynamic_index_in_dim(split, 1 - core, axis + 1, keepdims=False)
    chip_sum = mine + lax.ppermute(theirs, "tok", xor_pairs(count, 1))
    keep = lax.dynamic_index_in_dim(chip_sum, half, axis, keepdims=False)
    send = lax.dynamic_index_in_dim(chip_sum, 1 - half, axis, keepdims=False)
    got = lax.ppermute(send.astype(jnp.bfloat16), "tok", xor_pairs(count, 2))
    return keep + got.astype(keep.dtype)


def tok_sum(values):
    count = lax.axis_size("tok")
    chip_sum = values + lax.ppermute(values, "tok", xor_pairs(count, 1))
    return chip_sum + lax.ppermute(chip_sum, "tok", xor_pairs(count, 2))


def fsdp_coords():
    me = lax.axis_index("fsdp")
    return {"x": me // 8, "z": (me // 4) % 2, "y": me % 4}


def fsdp_pairs(kind, step):
    pairs = []
    for x in range(4):
        for z in range(2):
            for y in range(4):
                if kind == "z":
                    target = (x * 2 + 1 - z) * 4 + y
                elif kind == "x":
                    target = (((x + step) % 4) * 2 + z) * 4 + y
                else:
                    target = (x * 2 + z) * 4 + (y + step) % 4
                pairs.append(((x * 2 + z) * 4 + y, target))
    return pairs


def put(buffer, piece, axis, offset):
    start = [0] * buffer.ndim
    start[axis] = offset
    return lax.dynamic_update_slice(buffer, piece, start)


def grow(pieces, axes, factor):
    return [
        jnp.zeros(p.shape[:ax] + (p.shape[ax] * factor,) + p.shape[ax + 1 :], p.dtype)
        for p, ax in zip(pieces, axes)
    ]


def halves(pieces, axes, second):
    out = []
    for p, ax in zip(pieces, axes):
        n = p.shape[ax] // 2
        out.append(lax.slice_in_dim(p, n if second else 0, 2 * n if second else n, axis=ax))
    return out


def pair_stage(stacks, axes, coord):
    other = lax.ppermute(stacks, "fsdp", fsdp_pairs("z", 1))
    outs = []
    for mine, theirs, buffer, ax in zip(stacks, other, grow(stacks, axes, 2), axes):
        n = mine.shape[ax]
        buffer = put(buffer, mine, ax, coord * n)
        outs.append(put(buffer, theirs, ax, (1 - coord) * n))
    return outs


def ring_stage(stacks, axes, kind, coord):
    from_left = lax.ppermute(stacks, "fsdp", fsdp_pairs(kind, 1))
    from_right = lax.ppermute(stacks, "fsdp", fsdp_pairs(kind, -1))
    split = stacks[0].shape[axes[0]] > 1
    if split:
        far_left = lax.ppermute(halves(from_left, axes, False), "fsdp", fsdp_pairs(kind, 1))
        far_right = lax.ppermute(halves(from_right, axes, True), "fsdp", fsdp_pairs(kind, -1))
    else:
        far_left = lax.ppermute(from_left, "fsdp", fsdp_pairs(kind, 1))
    outs = []
    for i, (buffer, ax) in enumerate(zip(grow(stacks, axes, 4), axes)):
        n = stacks[i].shape[ax]
        buffer = put(buffer, stacks[i], ax, coord * n)
        buffer = put(buffer, from_right[i], ax, ((coord + 1) % 4) * n)
        buffer = put(buffer, from_left[i], ax, ((coord + 3) % 4) * n)
        buffer = put(buffer, far_left[i], ax, ((coord + 2) % 4) * n)
        if split:
            buffer = put(buffer, far_right[i], ax, ((coord + 2) % 4) * n + n // 2)
        outs.append(buffer)
    return outs


def torus_gather(route_a, axes_a, route_b, axes_b):
    coord = fsdp_coords()
    route_a = ring_stage(route_a, axes_a, "y", coord["y"])
    route_b = ring_stage(route_b, axes_b, "x", coord["x"])
    both = pair_stage(route_a + route_b, axes_a + axes_b, coord["z"])
    route_a, route_b = both[: len(route_a)], both[len(route_a) :]
    return ring_stage(route_a, axes_a, "x", coord["x"]), ring_stage(route_b, axes_b, "y", coord["y"])


def hp_dot(left, right, spec):
    return jnp.einsum(spec, left, right, precision=highest, preferred_element_type=jnp.float32)


def per_device(
    tokens,
    cotangent,
    segments,
    adapter_id,
    w_qkv,
    w_out,
    w_gateup,
    w_down,
    gain_attn,
    gain_ffn,
    gain_sub,
    lambda_head,
    a_in,
    b_qkv,
    b_gateup,
    a_out,
    a_down,
    b_rows,
):
    tok_count = lax.axis_size("tok")
    fsdp_count = lax.axis_size("fsdp")
    me_tok = lax.axis_index("tok")
    seqs, local_len, _ = tokens.shape
    length = local_len * tok_count
    qw_here = w_qkv.shape[2]
    ff_here = w_gateup.shape[2]
    heads_here = qw_here // VALUE_DIM
    lambda_here = lax.dynamic_slice_in_dim(lambda_head, me_tok * heads_here, heads_here)
    positions = jnp.arange(length)
    offsets = adapter_id * RANK
    fsdp_rows = w_qkv.shape[1]
    groups_per_adapter = RANK // b_qkv.shape[1]

    a_in_tok = tok_gather(a_in)
    b_rows_tok = tok_gather(b_rows)
    small = [a_in_tok, b_rows_tok, b_qkv, b_gateup, a_out, a_down]
    small_flat = jnp.concatenate([p.reshape(-1, COLS) for p in small])
    (g_qkv, g_out, g_down, g_small), (g_gateup,) = torus_gather(
        [w_qkv[:, None], w_out[None], w_down[None], small_flat[None]],
        [1, 0, 0, 0],
        [w_gateup[:, None]],
        [1],
    )
    w_qkv_full = g_qkv.reshape(3, D, qw_here)
    w_out_full = jnp.moveaxis(g_out, 0, 1).reshape(qw_here, D)
    w_down_full = jnp.moveaxis(g_down, 0, 1).reshape(ff_here, D)
    w_gateup_perm = g_gateup.reshape(2, D, ff_here)
    unpacked = []
    start = 0
    for p in small:
        rows = p.size // COLS
        unpacked.append(g_small[:, start : start + rows].reshape((fsdp_count,) + p.shape))
        start += rows
    (g_ain, g_brows, g_bqkv, g_bgateup, g_aout, g_adown) = unpacked
    a_in_full = jnp.transpose(g_ain, (2, 0, 1, 3, 4)).reshape(5, D, COLS)
    b_rows_full = jnp.transpose(g_brows, (2, 3, 0, 1, 4)).reshape(2, COLS, D)

    def to_yzx(values):
        lead = values.shape[:-1]
        split = values.reshape(lead + (4, 2, 4, D // fsdp_count))
        n = len(lead)
        order = tuple(range(n)) + (n + 2, n + 1, n, n + 3)
        return jnp.transpose(split, order).reshape(values.shape)

    def from_yzx(values):
        lead = values.shape[:-1]
        split = values.reshape(lead + (4, 2, 4, D // fsdp_count))
        n = len(lead)
        order = tuple(range(n)) + (n + 2, n + 1, n, n + 3)
        return jnp.transpose(split, order).reshape(values.shape)

    def pick_cols(values, axis):
        return jnp.stack(
            [lax.dynamic_slice_in_dim(values, offsets[s], RANK, axis) for s in range(seqs)]
        )

    def pick_groups(values):
        return jnp.stack(
            [
                lax.dynamic_slice_in_dim(values, adapter_id[s] * groups_per_adapter, groups_per_adapter, 0)
                for s in range(seqs)
            ]
        )

    a_in_sel = pick_cols(a_in_full, 2)
    b_rows_sel = pick_cols(b_rows_full, 1)
    b_qkv_sel = jnp.moveaxis(pick_groups(g_bqkv), 1, 2).reshape(seqs, 3, RANK, qw_here)
    b_gateup_sel = jnp.moveaxis(pick_groups(g_bgateup), 1, 2).reshape(seqs, 2, RANK, ff_here)
    a_out_sel = jnp.moveaxis(pick_groups(g_aout), 1, 2).reshape(seqs, qw_here, RANK)
    a_down_sel = jnp.moveaxis(pick_groups(g_adown), 1, 2).reshape(seqs, ff_here, RANK)

    def gather_rows(values):
        full = tok_gather(values, 1)
        return full.reshape(seqs, length, values.shape[-1])

    def scatter_rows(values):
        return tok_scatter(values.reshape(seqs, tok_count, local_len, values.shape[-1]), 1)

    def column_forward(rows_full, weight, down_sel, up_sel, rows_for_weight=None):
        if rows_for_weight is None:
            rows_for_weight = rows_full
        lowrank = jnp.einsum("std,sdr->str", rows_full, down_sel, preferred_element_type=jnp.float32)
        linear = jnp.einsum("std,de->ste", rows_for_weight, weight, preferred_element_type=jnp.float32)
        return linear + adapter_scale * hp_dot(lowrank, up_sel.astype(jnp.float32), "str,sre->ste"), lowrank

    def row_forward(rows_here, weight, down_sel, up_sel):
        lowrank = jnp.einsum("std,sdr->str", rows_here, down_sel, preferred_element_type=jnp.float32)
        main_part = jnp.einsum("std,de->ste", rows_here, weight, preferred_element_type=jnp.float32)
        total = main_part + adapter_scale * hp_dot(lowrank, up_sel.astype(jnp.float32), "str,sre->ste")
        return scatter_rows(total), lowrank

    inputs_rows = tokens.astype(jnp.float32)
    allowed = (segments[:, :, None] == segments[:, None, :]) & (
        positions[:, None] >= positions[None, :]
    )[None]
    grad_ffn_full = gather_rows(cotangent)
    normed_rows, norm_attn_pull = jax.vjp(partial(rows_norm, gain_vector=gain_attn), inputs_rows)
    normed_full = gather_rows(normed_rows.astype(jnp.bfloat16))
    proj_lin = []
    proj_low = []
    for p in range(3):
        lin, lowr = column_forward(normed_full, w_qkv_full[p], a_in_sel[:, p], b_qkv_sel[:, p])
        proj_lin.append(lin)
        proj_low.append(lowr)
    rotate = partial(rotary_heads, positions=positions, head_dim=HEAD_DIM)
    query_rot, query_pull = jax.vjp(rotate, proj_lin[0])
    key_rot, key_pull = jax.vjp(rotate, proj_lin[1])
    query_in = query_rot.astype(jnp.bfloat16).reshape(seqs, length, heads_here, 2, HEAD_DIM)
    key_in = key_rot.astype(jnp.bfloat16).reshape(seqs, length, heads_here, 2, HEAD_DIM)
    value_in = proj_lin[2].astype(jnp.bfloat16).reshape(seqs, length, heads_here, VALUE_DIM)
    heads_out, log_total = jax.vmap(attend, in_axes=(0, 0, 0, 0, None))(
        query_in, key_in, value_in, allowed, lambda_here
    )
    mixed_float, head_pull = jax.vjp(partial(head_norm, gain_vector=gain_sub), heads_out)
    mixed_rows = mixed_float.reshape(seqs, length, qw_here).astype(jnp.bfloat16)
    attn_rows, out_low = row_forward(mixed_rows, w_out_full, a_out_sel, b_rows_sel[:, 0])
    hidden = inputs_rows + attn_rows
    normed_ffn, norm_ffn_pull = jax.vjp(partial(rows_norm, gain_vector=gain_ffn), hidden)
    ffn_full = gather_rows(normed_ffn.astype(jnp.bfloat16))
    ffn_perm = to_yzx(ffn_full)
    gate_lin, gate_low = column_forward(ffn_full, w_gateup_perm[0], a_in_sel[:, 3], b_gateup_sel[:, 0], ffn_perm)
    up_lin, up_low = column_forward(ffn_full, w_gateup_perm[1], a_in_sel[:, 4], b_gateup_sel[:, 1], ffn_perm)
    product_float, swiglu_pull = jax.vjp(swiglu, gate_lin, up_lin)
    product = product_float.astype(jnp.bfloat16)
    ffn_rows, down_low = row_forward(product, w_down_full, a_down_sel, b_rows_sel[:, 1])
    output = (hidden + ffn_rows).astype(jnp.bfloat16)
    row_lows = tok_sum(jnp.stack([out_low, down_low]))

    tangent = cotangent.astype(jnp.float32)

    def row_backward(grad_full, rows_here, weight, down_sel, up_sel):
        grad_float = grad_full.astype(jnp.float32)
        grad_low = adapter_scale * hp_dot(grad_float, up_sel.astype(jnp.float32), "ste,sre->str")
        grad_down = hp_dot(rows_here.astype(jnp.float32), grad_low, "std,str->sdr")
        grad_inputs = jnp.einsum(
            "ste,de->std", grad_full, weight, preferred_element_type=jnp.float32
        ) + hp_dot(grad_low, down_sel.astype(jnp.float32), "str,sdr->std")
        return grad_inputs, grad_down

    def column_backward(rows_full, entries, weight_order=None):
        running = None
        grad_lows = []
        grads_up = []
        for grad_rows, weight, down_sel, up_sel, lowrank in entries:
            grad_float = grad_rows.astype(jnp.float32)
            grad_low = adapter_scale * hp_dot(grad_float, up_sel.astype(jnp.float32), "ste,sre->str")
            grads_up.append(adapter_scale * hp_dot(lowrank, grad_float, "str,ste->sre"))
            grad_lows.append(grad_low)
            main_term = jnp.einsum("ste,de->std", grad_rows, weight, preferred_element_type=jnp.float32)
            if weight_order is not None:
                main_term = weight_order(main_term)
            term = main_term + hp_dot(grad_low, down_sel.astype(jnp.float32), "str,sdr->std")
            running = term if running is None else running + term
        return scatter_rows(running), grad_lows, grads_up

    def mine_of(values, axis):
        shape = values.shape
        split = values.reshape(
            shape[:axis] + (fsdp_count, tok_count, D // (fsdp_count * tok_count)) + shape[axis + 1 :]
        )
        return lax.dynamic_index_in_dim(split, me_tok, axis + 1, keepdims=False)

    grad_product, grad_a_down = row_backward(
        grad_ffn_full, product, w_down_full, a_down_sel, b_rows_sel[:, 1]
    )
    grad_gate, grad_up = swiglu_pull(grad_product)
    grad_ffn_rows, ffn_grad_lows, ffn_grads_up = column_backward(
        ffn_full,
        (
            (grad_gate.astype(jnp.bfloat16), w_gateup_perm[0], a_in_sel[:, 3], b_gateup_sel[:, 0], gate_low),
            (grad_up.astype(jnp.bfloat16), w_gateup_perm[1], a_in_sel[:, 4], b_gateup_sel[:, 1], up_low),
        ),
        from_yzx,
    )
    grad_hidden = tangent + norm_ffn_pull(grad_ffn_rows)[0]
    grad_attn_full = gather_rows(grad_hidden.astype(jnp.bfloat16))
    grad_mixed, grad_a_out = row_backward(
        grad_attn_full, mixed_rows, w_out_full, a_out_sel, b_rows_sel[:, 0]
    )
    grad_heads = head_pull(grad_mixed.reshape(seqs, length, heads_here, VALUE_DIM))[0].astype(
        jnp.bfloat16
    )
    grad_query_rot, grad_key_rot, grad_values = jax.vmap(
        attend_back, in_axes=(0, 0, 0, 0, None, 0, 0)
    )(query_in, key_in, value_in, allowed, lambda_here, log_total, grad_heads)
    grad_query = query_pull(grad_query_rot.reshape(seqs, length, qw_here))[0].astype(jnp.bfloat16)
    grad_key = key_pull(grad_key_rot.reshape(seqs, length, qw_here))[0].astype(jnp.bfloat16)
    grad_attn_rows, attn_grad_lows, attn_grads_up = column_backward(
        normed_full,
        (
            (grad_query, w_qkv_full[0], a_in_sel[:, 0], b_qkv_sel[:, 0], proj_low[0]),
            (grad_key, w_qkv_full[1], a_in_sel[:, 1], b_qkv_sel[:, 1], proj_low[1]),
            (grad_values.reshape(seqs, length, qw_here), w_qkv_full[2], a_in_sel[:, 2], b_qkv_sel[:, 2], proj_low[2]),
        ),
    )
    grad_tokens = grad_hidden + norm_attn_pull(grad_attn_rows)[0]

    grad_lows = tok_sum(jnp.stack(attn_grad_lows + ffn_grad_lows))
    onehot = (
        jnp.arange(COLS)[None, None, :] == offsets[:, None, None] + jnp.arange(RANK)[None, :, None]
    ).astype(jnp.float32)
    wide_lows = hp_dot(grad_lows, onehot, "pstr,src->pstc")
    dense_a_in = jnp.concatenate(
        [
            hp_dot(normed_full.astype(jnp.float32), wide_lows[:3], "std,pstc->pdc"),
            hp_dot(ffn_full.astype(jnp.float32), wide_lows[3:], "std,pstc->pdc"),
        ]
    )
    a_in_mine = lax.dynamic_index_in_dim(
        dense_a_in.reshape(5, fsdp_count, tok_count, RANK, COLS), me_tok, 2, keepdims=False
    )
    wide_row_lows = hp_dot(row_lows, onehot, "qstr,src->qstc")
    dense_b_rows = adapter_scale * hp_dot(
        wide_row_lows,
        jnp.stack([grad_attn_full, grad_ffn_full]).astype(jnp.float32),
        "qstc,qstd->qcd",
    )
    b_rows_mine = lax.dynamic_index_in_dim(
        dense_b_rows.reshape(2, COLS, fsdp_count, tok_count, RANK), me_tok, 3, keepdims=False
    )
    def reduce_to_owners(parts, kind):
        rows = [p.size // (fsdp_count * COLS) for p in parts]
        packed = jnp.concatenate(
            [p.reshape(fsdp_count, r, COLS) for p, r in zip(parts, rows)], axis=1
        ).astype(kind)
        total = lax.all_to_all(packed, "fsdp", 0, 0, tiled=False).astype(jnp.float32).sum(0)
        out = []
        start = 0
        for p, r in zip(parts, rows):
            out.append(total[start : start + r].reshape(p.shape[1:]))
            start += r
        return out

    per = COLS // fsdp_count
    dense_b_gateup = hp_dot(onehot, jnp.stack(ffn_grads_up, 1), "src,spre->pce")
    dense_a_down = hp_dot(grad_a_down, onehot, "sdr,src->dc")
    b_gateup_block, a_down_block = reduce_to_owners(
        [
            jnp.moveaxis(dense_b_gateup.reshape(2, fsdp_count, per, ff_here), 1, 0),
            jnp.moveaxis(dense_a_down.reshape(ff_here, fsdp_count, per), 1, 0),
        ],
        jnp.bfloat16,
    )
    dense_b_qkv = hp_dot(onehot, jnp.stack(attn_grads_up, 1), "src,spre->pce")
    dense_a_out = hp_dot(grad_a_out, onehot, "sdr,src->dc")
    b_qkv_block, a_out_block = reduce_to_owners(
        [
            jnp.moveaxis(dense_b_qkv.reshape(3, fsdp_count, per, qw_here), 1, 0),
            jnp.moveaxis(dense_a_out.reshape(qw_here, fsdp_count, per), 1, 0),
        ],
        jnp.bfloat16,
    )
    a_in_block, b_rows_block = reduce_to_owners(
        [jnp.moveaxis(a_in_mine, 1, 0), jnp.moveaxis(b_rows_mine, 2, 0)], jnp.float32
    )

    return (
        output,
        grad_tokens,
        a_in_block,
        b_qkv_block,
        b_gateup_block,
        a_out_block,
        a_down_block,
        b_rows_block,
    )


def solution(mesh):
    return jax.shard_map(
        per_device,
        mesh=mesh,
        in_specs=(
            P("fsdp", "tok", None),
            P("fsdp", "tok", None),
            P("fsdp", None),
            P("fsdp"),
            P(None, "fsdp", "tok"),
            P("tok", "fsdp"),
            P(None, "fsdp", "tok"),
            P("tok", "fsdp"),
            P(),
            P(),
            P(),
            P(),
            P(None, ("fsdp", "tok"), None),
            P(None, "fsdp", "tok"),
            P(None, "fsdp", "tok"),
            P("tok", "fsdp"),
            P("tok", "fsdp"),
            P(None, None, ("fsdp", "tok")),
        ),
        out_specs=(
            P("fsdp", "tok", None),
            P("fsdp", "tok", None),
            P(None, ("fsdp", "tok"), None),
            P(None, "fsdp", "tok"),
            P(None, "fsdp", "tok"),
            P("tok", "fsdp"),
            P("tok", "fsdp"),
            P(None, None, ("fsdp", "tok")),
        ),
        check_vma=False,
    )
```

```python
from functools import partial

import jax
import jax.numpy as jnp
from jax import lax
from jax.sharding import PartitionSpec as P

D = 2048
HEAD_DIM = 128
VALUE_DIM = 256
RANK = 16
COLS = 128


highest = lax.Precision.HIGHEST
negative = -1e30
adapter_scale = 2.0
lambda_init = 0.2
rotary_base = 10000.0
row_epsilon = 1e-06
head_epsilon = 1e-05


def rows_norm(values, gain_vector):
    return (
        values
        * lax.rsqrt(jnp.mean(values * values, axis=-1, keepdims=True) + row_epsilon)
        * gain_vector
    )


def head_norm(values, gain_vector):
    scaled = values * lax.rsqrt(jnp.mean(values * values, axis=-1, keepdims=True) + head_epsilon)
    return scaled * gain_vector * (1.0 - lambda_init)


def rotary_heads(values, positions, head_dim):
    lead = values.shape[:-1]
    groups = values.reshape(lead + (-1, head_dim))
    half_dim = head_dim // 2
    frequency = rotary_base ** (-jnp.arange(half_dim, dtype=jnp.float32) / half_dim)
    angles = positions.astype(jnp.float32)[:, None] * frequency[None, :]
    cosine = jnp.cos(angles)[:, None, :]
    sine_part = jnp.sin(angles)[:, None, :]
    first_half = groups[..., :half_dim]
    second = groups[..., half_dim:]
    turned = jnp.concatenate(
        [first_half * cosine - second * sine_part, second * cosine + first_half * sine_part],
        axis=-1,
    )
    return turned.reshape(values.shape)


def swiglu(gate_rows, up_rows):
    return gate_rows * jax.nn.sigmoid(gate_rows) * up_rows


def attention_scores(query_in, key_in, allowed):
    raw_scores = jnp.einsum(
        "qhmd,khmd->hmqk", query_in, key_in, preferred_element_type=jnp.float32
    ) * query_in.shape[-1] ** (-0.5)
    return jnp.where(allowed[None, None], raw_scores, negative)


def attend(query_in, key_in, value_in, allowed, lambda_here):
    scores = attention_scores(query_in, key_in, allowed)
    row_max = jnp.max(scores, axis=-1, keepdims=True)
    log_total = row_max + jnp.log(jnp.sum(jnp.exp(scores - row_max), axis=-1, keepdims=True))
    soft_max = jnp.exp(scores - log_total)
    differ = (soft_max[:, 0] - lambda_here[:, None, None] * soft_max[:, 1]).astype(jnp.bfloat16)
    heads_out = jnp.einsum("hqk,khd->qhd", differ, value_in, preferred_element_type=jnp.float32)
    return (heads_out, log_total)


def attend_back(query_in, key_in, value_in, allowed, lambda_here, log_total, grad_heads):
    scale = query_in.shape[-1] ** (-0.5)
    scores = attention_scores(query_in, key_in, allowed)
    soft_max = jnp.exp(scores - log_total)
    differ = (soft_max[:, 0] - lambda_here[:, None, None] * soft_max[:, 1]).astype(jnp.bfloat16)
    grad_values = jnp.einsum("hqk,qhd->khd", differ, grad_heads, preferred_element_type=jnp.float32)
    grad_differ = jnp.einsum(
        "qhd,khd->hqk", grad_heads, value_in, preferred_element_type=jnp.float32
    )
    grad_soft = jnp.stack([grad_differ, -lambda_here[:, None, None] * grad_differ], axis=1)
    grad_scores = (
        soft_max * (grad_soft - jnp.sum(grad_soft * soft_max, axis=-1, keepdims=True))
    ).astype(jnp.bfloat16)
    grad_query = (
        jnp.einsum("hmqk,khmd->qhmd", grad_scores, key_in, preferred_element_type=jnp.float32)
        * scale
    )
    grad_key = (
        jnp.einsum("hmqk,qhmd->khmd", grad_scores, query_in, preferred_element_type=jnp.float32)
        * scale
    )
    return (grad_query, grad_key, grad_values.astype(jnp.bfloat16))


def xor_pairs(count, bit):
    return [(i, i ^ bit) for i in range(count)]


def tok_gather(values, axis=0):
    count = lax.axis_size("tok")
    me = lax.axis_index("tok")
    far = lax.ppermute(values, "tok", xor_pairs(count, 2))
    pair = jnp.where(
        (me & 2) == 0, jnp.stack([values, far], axis), jnp.stack([far, values], axis)
    )
    near = lax.ppermute(pair, "tok", xor_pairs(count, 1))
    full = jnp.where(
        (me & 1) == 0, jnp.stack([pair, near], axis + 1), jnp.stack([near, pair], axis + 1)
    )
    return full.reshape(values.shape[:axis] + (count,) + values.shape[axis:])


def tok_scatter(blocks, axis=0):
    count = lax.axis_size("tok")
    me = lax.axis_index("tok")
    core = me & 1
    half = (me >> 1) & 1
    split = blocks.reshape(blocks.shape[:axis] + (2, 2) + blocks.shape[axis + 1 :])
    mine = lax.dynamic_index_in_dim(split, core, axis + 1, keepdims=False)
    theirs = lax.dynamic_index_in_dim(split, 1 - core, axis + 1, keepdims=False)
    chip_sum = mine + lax.ppermute(theirs, "tok", xor_pairs(count, 1))
    keep = lax.dynamic_index_in_dim(chip_sum, half, axis, keepdims=False)
    send = lax.dynamic_index_in_dim(chip_sum, 1 - half, axis, keepdims=False)
    got = lax.ppermute(send.astype(jnp.bfloat16), "tok", xor_pairs(count, 2))
    return keep + got.astype(keep.dtype)


def tok_sum(values):
    count = lax.axis_size("tok")
    chip_sum = values + lax.ppermute(values, "tok", xor_pairs(count, 1))
    return chip_sum + lax.ppermute(chip_sum, "tok", xor_pairs(count, 2))


def fsdp_coords():
    me = lax.axis_index("fsdp")
    return {"x": me // 8, "z": (me // 4) % 2, "y": me % 4}


def fsdp_pairs(kind, step):
    pairs = []
    for x in range(4):
        for z in range(2):
            for y in range(4):
                if kind == "z":
                    target = (x * 2 + 1 - z) * 4 + y
                elif kind == "x":
                    target = (((x + step) % 4) * 2 + z) * 4 + y
                else:
                    target = (x * 2 + z) * 4 + (y + step) % 4
                pairs.append(((x * 2 + z) * 4 + y, target))
    return pairs


def put(buffer, piece, axis, offset):
    start = [0] * buffer.ndim
    start[axis] = offset
    return lax.dynamic_update_slice(buffer, piece, start)


def grow(pieces, axes, factor):
    return [
        jnp.zeros(p.shape[:ax] + (p.shape[ax] * factor,) + p.shape[ax + 1 :], p.dtype)
        for p, ax in zip(pieces, axes)
    ]


def halves(pieces, axes, second):
    out = []
    for p, ax in zip(pieces, axes):
        n = p.shape[ax] // 2
        out.append(lax.slice_in_dim(p, n if second else 0, 2 * n if second else n, axis=ax))
    return out


def pair_stage(stacks, axes, coord):
    other = lax.ppermute(stacks, "fsdp", fsdp_pairs("z", 1))
    outs = []
    for mine, theirs, buffer, ax in zip(stacks, other, grow(stacks, axes, 2), axes):
        n = mine.shape[ax]
        buffer = put(buffer, mine, ax, coord * n)
        outs.append(put(buffer, theirs, ax, (1 - coord) * n))
    return outs


def ring_stage(stacks, axes, kind, coord):
    from_left = lax.ppermute(stacks, "fsdp", fsdp_pairs(kind, 1))
    from_right = lax.ppermute(stacks, "fsdp", fsdp_pairs(kind, -1))
    split = stacks[0].shape[axes[0]] > 1
    if split:
        far_left = lax.ppermute(halves(from_left, axes, False), "fsdp", fsdp_pairs(kind, 1))
        far_right = lax.ppermute(halves(from_right, axes, True), "fsdp", fsdp_pairs(kind, -1))
    else:
        far_left = lax.ppermute(from_left, "fsdp", fsdp_pairs(kind, 1))
    outs = []
    for i, (buffer, ax) in enumerate(zip(grow(stacks, axes, 4), axes)):
        n = stacks[i].shape[ax]
        buffer = put(buffer, stacks[i], ax, coord * n)
        buffer = put(buffer, from_right[i], ax, ((coord + 1) % 4) * n)
        buffer = put(buffer, from_left[i], ax, ((coord + 3) % 4) * n)
        buffer = put(buffer, far_left[i], ax, ((coord + 2) % 4) * n)
        if split:
            buffer = put(buffer, far_right[i], ax, ((coord + 2) % 4) * n + n // 2)
        outs.append(buffer)
    return outs


def torus_gather(route_a, axes_a, route_b, axes_b):
    coord = fsdp_coords()
    route_a = ring_stage(route_a, axes_a, "y", coord["y"])
    route_b = ring_stage(route_b, axes_b, "x", coord["x"])
    both = pair_stage(route_a + route_b, axes_a + axes_b, coord["z"])
    route_a, route_b = both[: len(route_a)], both[len(route_a) :]
    return ring_stage(route_a, axes_a, "x", coord["x"]), ring_stage(route_b, axes_b, "y", coord["y"])


def hp_dot(left, right, spec):
    return jnp.einsum(spec, left, right, precision=highest, preferred_element_type=jnp.float32)


def per_device(
    tokens,
    cotangent,
    segments,
    adapter_id,
    w_qkv,
    w_out,
    w_gateup,
    w_down,
    gain_attn,
    gain_ffn,
    gain_sub,
    lambda_head,
    a_in,
    b_qkv,
    b_gateup,
    a_out,
    a_down,
    b_rows,
):
    tok_count = lax.axis_size("tok")
    fsdp_count = lax.axis_size("fsdp")
    me_tok = lax.axis_index("tok")
    seqs, local_len, _ = tokens.shape
    length = local_len * tok_count
    qw_here = w_qkv.shape[2]
    ff_here = w_gateup.shape[2]
    heads_here = qw_here // VALUE_DIM
    lambda_here = lax.dynamic_slice_in_dim(lambda_head, me_tok * heads_here, heads_here)
    positions = jnp.arange(length)
    offsets = adapter_id * RANK
    fsdp_rows = w_qkv.shape[1]
    groups_per_adapter = RANK // b_qkv.shape[1]

    a_in_tok = tok_gather(a_in)
    b_rows_tok = tok_gather(b_rows)
    small = [a_in_tok, b_rows_tok, b_qkv, b_gateup, a_out, a_down]
    small_flat = jnp.concatenate([p.reshape(-1, COLS) for p in small])
    (g_qkv, g_out, g_down, g_small), (g_gateup,) = torus_gather(
        [w_qkv[:, None], w_out[None], w_down[None], small_flat[None]],
        [1, 0, 0, 0],
        [w_gateup[:, None]],
        [1],
    )
    w_qkv_full = g_qkv.reshape(3, D, qw_here)
    w_out_full = jnp.moveaxis(g_out, 0, 1).reshape(qw_here, D)
    w_down_full = jnp.moveaxis(g_down, 0, 1).reshape(ff_here, D)
    w_gateup_perm = jnp.transpose(
        g_gateup.reshape(2, 4, 2, 4, D // fsdp_count, ff_here), (0, 3, 2, 1, 4, 5)
    ).reshape(2, D, ff_here)
    unpacked = []
    start = 0
    for p in small:
        rows = p.size // COLS
        unpacked.append(g_small[:, start : start + rows].reshape((fsdp_count,) + p.shape))
        start += rows
    (g_ain, g_brows, g_bqkv, g_bgateup, g_aout, g_adown) = unpacked
    a_in_full = jnp.transpose(g_ain, (2, 0, 1, 3, 4)).reshape(5, D, COLS)
    b_rows_full = jnp.transpose(g_brows, (2, 3, 0, 1, 4)).reshape(2, COLS, D)

    def to_yzx(values):
        lead = values.shape[:-1]
        split = values.reshape(lead + (4, 2, 4, D // fsdp_count))
        n = len(lead)
        order = tuple(range(n)) + (n + 2, n + 1, n, n + 3)
        return jnp.transpose(split, order).reshape(values.shape)

    def from_yzx(values):
        lead = values.shape[:-1]
        split = values.reshape(lead + (4, 2, 4, D // fsdp_count))
        n = len(lead)
        order = tuple(range(n)) + (n + 2, n + 1, n, n + 3)
        return jnp.transpose(split, order).reshape(values.shape)

    def pick_cols(values, axis):
        return jnp.stack(
            [lax.dynamic_slice_in_dim(values, offsets[s], RANK, axis) for s in range(seqs)]
        )

    def pick_groups(values):
        return jnp.stack(
            [
                lax.dynamic_slice_in_dim(values, adapter_id[s] * groups_per_adapter, groups_per_adapter, 0)
                for s in range(seqs)
            ]
        )

    a_in_sel = pick_cols(a_in_full, 2)
    b_rows_sel = pick_cols(b_rows_full, 1)
    b_qkv_sel = jnp.moveaxis(pick_groups(g_bqkv), 1, 2).reshape(seqs, 3, RANK, qw_here)
    b_gateup_sel = jnp.moveaxis(pick_groups(g_bgateup), 1, 2).reshape(seqs, 2, RANK, ff_here)
    a_out_sel = jnp.moveaxis(pick_groups(g_aout), 1, 2).reshape(seqs, qw_here, RANK)
    a_down_sel = jnp.moveaxis(pick_groups(g_adown), 1, 2).reshape(seqs, ff_here, RANK)

    def gather_rows(values):
        full = tok_gather(values, 1)
        return full.reshape(seqs, length, values.shape[-1])

    def scatter_rows(values):
        return tok_scatter(values.reshape(seqs, tok_count, local_len, values.shape[-1]), 1)

    def column_forward(rows_full, weight, down_sel, up_sel, rows_for_weight=None):
        if rows_for_weight is None:
            rows_for_weight = rows_full
        lowrank = jnp.einsum("std,sdr->str", rows_full, down_sel, preferred_element_type=jnp.float32)
        linear = jnp.einsum("std,de->ste", rows_for_weight, weight, preferred_element_type=jnp.float32)
        return linear + adapter_scale * hp_dot(lowrank, up_sel.astype(jnp.float32), "str,sre->ste"), lowrank

    def row_forward(rows_here, weight, down_sel, up_sel):
        lowrank = jnp.einsum("std,sdr->str", rows_here, down_sel, preferred_element_type=jnp.float32)
        main_part = jnp.einsum("std,de->ste", rows_here, weight, preferred_element_type=jnp.float32)
        total = main_part + adapter_scale * hp_dot(lowrank, up_sel.astype(jnp.float32), "str,sre->ste")
        return scatter_rows(total), lowrank

    inputs_rows = tokens.astype(jnp.float32)
    allowed = (segments[:, :, None] == segments[:, None, :]) & (
        positions[:, None] >= positions[None, :]
    )[None]
    grad_ffn_full = gather_rows(cotangent)
    normed_rows, norm_attn_pull = jax.vjp(partial(rows_norm, gain_vector=gain_attn), inputs_rows)
    normed_full = gather_rows(normed_rows.astype(jnp.bfloat16))
    proj_lin = []
    proj_low = []
    for p in range(3):
        lin, lowr = column_forward(normed_full, w_qkv_full[p], a_in_sel[:, p], b_qkv_sel[:, p])
        proj_lin.append(lin)
        proj_low.append(lowr)
    rotate = partial(rotary_heads, positions=positions, head_dim=HEAD_DIM)
    query_rot, query_pull = jax.vjp(rotate, proj_lin[0])
    key_rot, key_pull = jax.vjp(rotate, proj_lin[1])
    query_in = query_rot.astype(jnp.bfloat16).reshape(seqs, length, heads_here, 2, HEAD_DIM)
    key_in = key_rot.astype(jnp.bfloat16).reshape(seqs, length, heads_here, 2, HEAD_DIM)
    value_in = proj_lin[2].astype(jnp.bfloat16).reshape(seqs, length, heads_here, VALUE_DIM)
    heads_out, log_total = jax.vmap(attend, in_axes=(0, 0, 0, 0, None))(
        query_in, key_in, value_in, allowed, lambda_here
    )
    mixed_float, head_pull = jax.vjp(partial(head_norm, gain_vector=gain_sub), heads_out)
    mixed_rows = mixed_float.reshape(seqs, length, qw_here).astype(jnp.bfloat16)
    attn_rows, out_low = row_forward(mixed_rows, w_out_full, a_out_sel, b_rows_sel[:, 0])
    hidden = inputs_rows + attn_rows
    normed_ffn, norm_ffn_pull = jax.vjp(partial(rows_norm, gain_vector=gain_ffn), hidden)
    ffn_full = gather_rows(normed_ffn.astype(jnp.bfloat16))
    gate_lin, gate_low = column_forward(ffn_full, w_gateup_perm[0], a_in_sel[:, 3], b_gateup_sel[:, 0])
    up_lin, up_low = column_forward(ffn_full, w_gateup_perm[1], a_in_sel[:, 4], b_gateup_sel[:, 1])
    product_float, swiglu_pull = jax.vjp(swiglu, gate_lin, up_lin)
    product = product_float.astype(jnp.bfloat16)
    ffn_rows, down_low = row_forward(product, w_down_full, a_down_sel, b_rows_sel[:, 1])
    output = (hidden + ffn_rows).astype(jnp.bfloat16)
    row_lows = tok_sum(jnp.stack([out_low, down_low]))

    tangent = cotangent.astype(jnp.float32)

    def row_backward(grad_full, rows_here, weight, down_sel, up_sel):
        grad_float = grad_full.astype(jnp.float32)
        grad_low = adapter_scale * hp_dot(grad_float, up_sel.astype(jnp.float32), "ste,sre->str")
        grad_down = hp_dot(rows_here.astype(jnp.float32), grad_low, "std,str->sdr")
        grad_inputs = jnp.einsum(
            "ste,de->std", grad_full, weight, preferred_element_type=jnp.float32
        ) + hp_dot(grad_low, down_sel.astype(jnp.float32), "str,sdr->std")
        return grad_inputs, grad_down

    def column_backward(rows_full, entries, weight_order=None):
        running = None
        grad_lows = []
        grads_up = []
        for grad_rows, weight, down_sel, up_sel, lowrank in entries:
            grad_float = grad_rows.astype(jnp.float32)
            grad_low = adapter_scale * hp_dot(grad_float, up_sel.astype(jnp.float32), "ste,sre->str")
            grads_up.append(adapter_scale * hp_dot(lowrank, grad_float, "str,ste->sre"))
            grad_lows.append(grad_low)
            main_term = jnp.einsum("ste,de->std", grad_rows, weight, preferred_element_type=jnp.float32)
            if weight_order is not None:
                main_term = weight_order(main_term)
            term = main_term + hp_dot(grad_low, down_sel.astype(jnp.float32), "str,sdr->std")
            running = term if running is None else running + term
        return scatter_rows(running), grad_lows, grads_up

    def mine_of(values, axis):
        shape = values.shape
        split = values.reshape(
            shape[:axis] + (fsdp_count, tok_count, D // (fsdp_count * tok_count)) + shape[axis + 1 :]
        )
        return lax.dynamic_index_in_dim(split, me_tok, axis + 1, keepdims=False)

    grad_product, grad_a_down = row_backward(
        grad_ffn_full, product, w_down_full, a_down_sel, b_rows_sel[:, 1]
    )
    grad_gate, grad_up = swiglu_pull(grad_product)
    grad_ffn_rows, ffn_grad_lows, ffn_grads_up = column_backward(
        ffn_full,
        (
            (grad_gate.astype(jnp.bfloat16), w_gateup_perm[0], a_in_sel[:, 3], b_gateup_sel[:, 0], gate_low),
            (grad_up.astype(jnp.bfloat16), w_gateup_perm[1], a_in_sel[:, 4], b_gateup_sel[:, 1], up_low),
        ),
    )
    grad_hidden = tangent + norm_ffn_pull(grad_ffn_rows)[0]
    grad_attn_full = gather_rows(grad_hidden.astype(jnp.bfloat16))
    grad_mixed, grad_a_out = row_backward(
        grad_attn_full, mixed_rows, w_out_full, a_out_sel, b_rows_sel[:, 0]
    )
    grad_heads = head_pull(grad_mixed.reshape(seqs, length, heads_here, VALUE_DIM))[0].astype(
        jnp.bfloat16
    )
    grad_query_rot, grad_key_rot, grad_values = jax.vmap(
        attend_back, in_axes=(0, 0, 0, 0, None, 0, 0)
    )(query_in, key_in, value_in, allowed, lambda_here, log_total, grad_heads)
    grad_query = query_pull(grad_query_rot.reshape(seqs, length, qw_here))[0].astype(jnp.bfloat16)
    grad_key = key_pull(grad_key_rot.reshape(seqs, length, qw_here))[0].astype(jnp.bfloat16)
    grad_attn_rows, attn_grad_lows, attn_grads_up = column_backward(
        normed_full,
        (
            (grad_query, w_qkv_full[0], a_in_sel[:, 0], b_qkv_sel[:, 0], proj_low[0]),
            (grad_key, w_qkv_full[1], a_in_sel[:, 1], b_qkv_sel[:, 1], proj_low[1]),
            (grad_values.reshape(seqs, length, qw_here), w_qkv_full[2], a_in_sel[:, 2], b_qkv_sel[:, 2], proj_low[2]),
        ),
    )
    grad_tokens = grad_hidden + norm_attn_pull(grad_attn_rows)[0]

    grad_lows = tok_sum(jnp.stack(attn_grad_lows + ffn_grad_lows))
    onehot = (
        jnp.arange(COLS)[None, None, :] == offsets[:, None, None] + jnp.arange(RANK)[None, :, None]
    ).astype(jnp.float32)
    wide_lows = hp_dot(grad_lows, onehot, "pstr,src->pstc")
    dense_a_in = jnp.concatenate(
        [
            hp_dot(normed_full.astype(jnp.float32), wide_lows[:3], "std,pstc->pdc"),
            hp_dot(ffn_full.astype(jnp.float32), wide_lows[3:], "std,pstc->pdc"),
        ]
    )
    a_in_mine = lax.dynamic_index_in_dim(
        dense_a_in.reshape(5, fsdp_count, tok_count, RANK, COLS), me_tok, 2, keepdims=False
    )
    wide_row_lows = hp_dot(row_lows, onehot, "qstr,src->qstc")
    dense_b_rows = adapter_scale * hp_dot(
        wide_row_lows,
        jnp.stack([grad_attn_full, grad_ffn_full]).astype(jnp.float32),
        "qstc,qstd->qcd",
    )
    b_rows_mine = lax.dynamic_index_in_dim(
        dense_b_rows.reshape(2, COLS, fsdp_count, tok_count, RANK), me_tok, 3, keepdims=False
    )
    def reduce_to_owners(parts, kind):
        rows = [p.size // (fsdp_count * COLS) for p in parts]
        packed = jnp.concatenate(
            [p.reshape(fsdp_count, r, COLS) for p, r in zip(parts, rows)], axis=1
        ).astype(kind)
        total = lax.all_to_all(packed, "fsdp", 0, 0, tiled=False).astype(jnp.float32).sum(0)
        out = []
        start = 0
        for p, r in zip(parts, rows):
            out.append(total[start : start + r].reshape(p.shape[1:]))
            start += r
        return out

    per = COLS // fsdp_count
    dense_b_gateup = hp_dot(onehot, jnp.stack(ffn_grads_up, 1), "src,spre->pce")
    dense_a_down = hp_dot(grad_a_down, onehot, "sdr,src->dc")
    b_gateup_block, a_down_block = reduce_to_owners(
        [
            jnp.moveaxis(dense_b_gateup.reshape(2, fsdp_count, per, ff_here), 1, 0),
            jnp.moveaxis(dense_a_down.reshape(ff_here, fsdp_count, per), 1, 0),
        ],
        jnp.bfloat16,
    )
    dense_b_qkv = hp_dot(onehot, jnp.stack(attn_grads_up, 1), "src,spre->pce")
    dense_a_out = hp_dot(grad_a_out, onehot, "sdr,src->dc")
    b_qkv_block, a_out_block = reduce_to_owners(
        [
            jnp.moveaxis(dense_b_qkv.reshape(3, fsdp_count, per, qw_here), 1, 0),
            jnp.moveaxis(dense_a_out.reshape(qw_here, fsdp_count, per), 1, 0),
        ],
        jnp.bfloat16,
    )
    a_in_block, b_rows_block = reduce_to_owners(
        [jnp.moveaxis(a_in_mine, 1, 0), jnp.moveaxis(b_rows_mine, 2, 0)], jnp.float32
    )

    return (
        output,
        grad_tokens,
        a_in_block,
        b_qkv_block,
        b_gateup_block,
        a_out_block,
        a_down_block,
        b_rows_block,
    )


def solution(mesh):
    return jax.shard_map(
        per_device,
        mesh=mesh,
        in_specs=(
            P("fsdp", "tok", None),
            P("fsdp", "tok", None),
            P("fsdp", None),
            P("fsdp"),
            P(None, "fsdp", "tok"),
            P("tok", "fsdp"),
            P(None, "fsdp", "tok"),
            P("tok", "fsdp"),
            P(),
            P(),
            P(),
            P(),
            P(None, ("fsdp", "tok"), None),
            P(None, "fsdp", "tok"),
            P(None, "fsdp", "tok"),
            P("tok", "fsdp"),
            P("tok", "fsdp"),
            P(None, None, ("fsdp", "tok")),
        ),
        out_specs=(
            P("fsdp", "tok", None),
            P("fsdp", "tok", None),
            P(None, ("fsdp", "tok"), None),
            P(None, "fsdp", "tok"),
            P(None, "fsdp", "tok"),
            P("tok", "fsdp"),
            P("tok", "fsdp"),
            P(None, None, ("fsdp", "tok")),
        ),
        check_vma=False,
    )
```

```python
from functools import partial

import jax
import jax.numpy as jnp
from jax import lax
from jax.sharding import PartitionSpec as P

D = 2048
HEAD_DIM = 128
VALUE_DIM = 256
RANK = 16
COLS = 128


highest = lax.Precision.HIGHEST
negative = -1e30
adapter_scale = 2.0
lambda_init = 0.2
rotary_base = 10000.0
row_epsilon = 1e-06
head_epsilon = 1e-05


def rows_norm(values, gain_vector):
    return (
        values
        * lax.rsqrt(jnp.mean(values * values, axis=-1, keepdims=True) + row_epsilon)
        * gain_vector
    )


def head_norm(values, gain_vector):
    scaled = values * lax.rsqrt(jnp.mean(values * values, axis=-1, keepdims=True) + head_epsilon)
    return scaled * gain_vector * (1.0 - lambda_init)


def rotary_heads(values, positions, head_dim):
    lead = values.shape[:-1]
    groups = values.reshape(lead + (-1, head_dim))
    half_dim = head_dim // 2
    frequency = rotary_base ** (-jnp.arange(half_dim, dtype=jnp.float32) / half_dim)
    angles = positions.astype(jnp.float32)[:, None] * frequency[None, :]
    cosine = jnp.cos(angles)[:, None, :]
    sine_part = jnp.sin(angles)[:, None, :]
    first_half = groups[..., :half_dim]
    second = groups[..., half_dim:]
    turned = jnp.concatenate(
        [first_half * cosine - second * sine_part, second * cosine + first_half * sine_part],
        axis=-1,
    )
    return turned.reshape(values.shape)


def swiglu(gate_rows, up_rows):
    return gate_rows * jax.nn.sigmoid(gate_rows) * up_rows


def attention_scores(query_in, key_in, allowed):
    raw_scores = jnp.einsum(
        "qhmd,khmd->hmqk", query_in, key_in, preferred_element_type=jnp.float32
    ) * query_in.shape[-1] ** (-0.5)
    return jnp.where(allowed[None, None], raw_scores, negative)


def attend(query_in, key_in, value_in, allowed, lambda_here):
    scores = attention_scores(query_in, key_in, allowed)
    row_max = jnp.max(scores, axis=-1, keepdims=True)
    log_total = row_max + jnp.log(jnp.sum(jnp.exp(scores - row_max), axis=-1, keepdims=True))
    soft_max = jnp.exp(scores - log_total)
    differ = (soft_max[:, 0] - lambda_here[:, None, None] * soft_max[:, 1]).astype(jnp.bfloat16)
    heads_out = jnp.einsum("hqk,khd->qhd", differ, value_in, preferred_element_type=jnp.float32)
    return (heads_out, log_total)


def attend_back(query_in, key_in, value_in, allowed, lambda_here, log_total, grad_heads):
    scale = query_in.shape[-1] ** (-0.5)
    scores = attention_scores(query_in, key_in, allowed)
    soft_max = jnp.exp(scores - log_total)
    differ = (soft_max[:, 0] - lambda_here[:, None, None] * soft_max[:, 1]).astype(jnp.bfloat16)
    grad_values = jnp.einsum("hqk,qhd->khd", differ, grad_heads, preferred_element_type=jnp.float32)
    grad_differ = jnp.einsum(
        "qhd,khd->hqk", grad_heads, value_in, preferred_element_type=jnp.float32
    )
    grad_soft = jnp.stack([grad_differ, -lambda_here[:, None, None] * grad_differ], axis=1)
    grad_scores = (
        soft_max * (grad_soft - jnp.sum(grad_soft * soft_max, axis=-1, keepdims=True))
    ).astype(jnp.bfloat16)
    grad_query = (
        jnp.einsum("hmqk,khmd->qhmd", grad_scores, key_in, preferred_element_type=jnp.float32)
        * scale
    )
    grad_key = (
        jnp.einsum("hmqk,qhmd->khmd", grad_scores, query_in, preferred_element_type=jnp.float32)
        * scale
    )
    return (grad_query, grad_key, grad_values.astype(jnp.bfloat16))


def xor_pairs(count, bit):
    return [(i, i ^ bit) for i in range(count)]


def tok_gather(values, axis=0):
    count = lax.axis_size("tok")
    me = lax.axis_index("tok")
    far = lax.ppermute(values, "tok", xor_pairs(count, 2))
    pair = jnp.where(
        (me & 2) == 0, jnp.stack([values, far], axis), jnp.stack([far, values], axis)
    )
    near = lax.ppermute(pair, "tok", xor_pairs(count, 1))
    full = jnp.where(
        (me & 1) == 0, jnp.stack([pair, near], axis + 1), jnp.stack([near, pair], axis + 1)
    )
    return full.reshape(values.shape[:axis] + (count,) + values.shape[axis:])


def tok_scatter(blocks, axis=0):
    count = lax.axis_size("tok")
    me = lax.axis_index("tok")
    core = me & 1
    half = (me >> 1) & 1
    split = blocks.reshape(blocks.shape[:axis] + (2, 2) + blocks.shape[axis + 1 :])
    mine = lax.dynamic_index_in_dim(split, core, axis + 1, keepdims=False)
    theirs = lax.dynamic_index_in_dim(split, 1 - core, axis + 1, keepdims=False)
    chip_sum = mine + lax.ppermute(theirs, "tok", xor_pairs(count, 1))
    keep = lax.dynamic_index_in_dim(chip_sum, half, axis, keepdims=False)
    send = lax.dynamic_index_in_dim(chip_sum, 1 - half, axis, keepdims=False)
    got = lax.ppermute(send.astype(jnp.bfloat16), "tok", xor_pairs(count, 2))
    return keep + got.astype(keep.dtype)


def tok_sum(values):
    count = lax.axis_size("tok")
    chip_sum = values + lax.ppermute(values, "tok", xor_pairs(count, 1))
    return chip_sum + lax.ppermute(chip_sum, "tok", xor_pairs(count, 2))


def fsdp_coords():
    me = lax.axis_index("fsdp")
    return {"x": me // 8, "z": (me // 4) % 2, "y": me % 4}


def fsdp_pairs(kind, step):
    pairs = []
    for x in range(4):
        for z in range(2):
            for y in range(4):
                if kind == "z":
                    target = (x * 2 + 1 - z) * 4 + y
                elif kind == "x":
                    target = (((x + step) % 4) * 2 + z) * 4 + y
                else:
                    target = (x * 2 + z) * 4 + (y + step) % 4
                pairs.append(((x * 2 + z) * 4 + y, target))
    return pairs


def put(buffer, piece, axis, offset):
    start = [0] * buffer.ndim
    start[axis] = offset
    return lax.dynamic_update_slice(buffer, piece, start)


def grow(pieces, axes, factor):
    return [
        jnp.zeros(p.shape[:ax] + (p.shape[ax] * factor,) + p.shape[ax + 1 :], p.dtype)
        for p, ax in zip(pieces, axes)
    ]


def halves(pieces, axes, second):
    out = []
    for p, ax in zip(pieces, axes):
        n = p.shape[ax] // 2
        out.append(lax.slice_in_dim(p, n if second else 0, 2 * n if second else n, axis=ax))
    return out


def pair_stage(stacks, axes, coord):
    other = lax.ppermute(stacks, "fsdp", fsdp_pairs("z", 1))
    outs = []
    for mine, theirs, buffer, ax in zip(stacks, other, grow(stacks, axes, 2), axes):
        n = mine.shape[ax]
        buffer = put(buffer, mine, ax, coord * n)
        outs.append(put(buffer, theirs, ax, (1 - coord) * n))
    return outs


def ring_stage(stacks, axes, kind, coord):
    from_left = lax.ppermute(stacks, "fsdp", fsdp_pairs(kind, 1))
    from_right = lax.ppermute(stacks, "fsdp", fsdp_pairs(kind, -1))
    split = stacks[0].shape[axes[0]] > 1
    if split:
        far_left = lax.ppermute(halves(from_left, axes, False), "fsdp", fsdp_pairs(kind, 1))
        far_right = lax.ppermute(halves(from_right, axes, True), "fsdp", fsdp_pairs(kind, -1))
    else:
        far_left = lax.ppermute(from_left, "fsdp", fsdp_pairs(kind, 1))
    outs = []
    for i, (buffer, ax) in enumerate(zip(grow(stacks, axes, 4), axes)):
        n = stacks[i].shape[ax]
        buffer = put(buffer, stacks[i], ax, coord * n)
        buffer = put(buffer, from_right[i], ax, ((coord + 1) % 4) * n)
        buffer = put(buffer, from_left[i], ax, ((coord + 3) % 4) * n)
        buffer = put(buffer, far_left[i], ax, ((coord + 2) % 4) * n)
        if split:
            buffer = put(buffer, far_right[i], ax, ((coord + 2) % 4) * n + n // 2)
        outs.append(buffer)
    return outs


def torus_gather(route_a, axes_a, route_b, axes_b):
    coord = fsdp_coords()
    route_a = ring_stage(route_a, axes_a, "y", coord["y"])
    route_b = ring_stage(route_b, axes_b, "x", coord["x"])
    both = pair_stage(route_a + route_b, axes_a + axes_b, coord["z"])
    route_a, route_b = both[: len(route_a)], both[len(route_a) :]
    return ring_stage(route_a, axes_a, "x", coord["x"]), ring_stage(route_b, axes_b, "y", coord["y"])


def hp_dot(left, right, spec):
    return jnp.einsum(spec, left, right, precision=highest, preferred_element_type=jnp.float32)


def per_device(
    tokens,
    cotangent,
    segments,
    adapter_id,
    w_qkv,
    w_out,
    w_gateup,
    w_down,
    gain_attn,
    gain_ffn,
    gain_sub,
    lambda_head,
    a_in,
    b_qkv,
    b_gateup,
    a_out,
    a_down,
    b_rows,
):
    tok_count = lax.axis_size("tok")
    fsdp_count = lax.axis_size("fsdp")
    me_tok = lax.axis_index("tok")
    seqs, local_len, _ = tokens.shape
    length = local_len * tok_count
    qw_here = w_qkv.shape[2]
    ff_here = w_gateup.shape[2]
    heads_here = qw_here // VALUE_DIM
    lambda_here = lax.dynamic_slice_in_dim(lambda_head, me_tok * heads_here, heads_here)
    positions = jnp.arange(length)
    offsets = adapter_id * RANK
    fsdp_rows = w_qkv.shape[1]
    groups_per_adapter = RANK // b_qkv.shape[1]

    a_in_tok = tok_gather(a_in)
    b_rows_tok = tok_gather(b_rows)
    small = [a_in_tok, b_rows_tok, b_qkv, b_gateup, a_out, a_down]
    small_flat = jnp.concatenate([p.reshape(-1, COLS) for p in small])
    (g_qkv, g_out, g_down, g_small), (g_gateup,) = torus_gather(
        [w_qkv[:, None], w_out[None], w_down[None], small_flat[None]],
        [1, 0, 0, 0],
        [w_gateup[:, None]],
        [1],
    )
    w_qkv_full = g_qkv.reshape(3, D, qw_here)
    w_out_full = jnp.moveaxis(g_out, 0, 1).reshape(qw_here, D)
    w_down_full = jnp.moveaxis(g_down, 0, 1).reshape(ff_here, D)
    w_gateup_perm = jnp.transpose(
        g_gateup.reshape(2, 4, 2, 4, D // fsdp_count, ff_here), (0, 3, 2, 1, 4, 5)
    ).reshape(2, D, ff_here)
    unpacked = []
    start = 0
    for p in small:
        rows = p.size // COLS
        unpacked.append(g_small[:, start : start + rows].reshape((fsdp_count,) + p.shape))
        start += rows
    (g_ain, g_brows, g_bqkv, g_bgateup, g_aout, g_adown) = unpacked
    a_in_full = jnp.transpose(g_ain, (2, 0, 1, 3, 4)).reshape(5, D, COLS)

    def to_yzx(values):
        lead = values.shape[:-1]
        split = values.reshape(lead + (4, 2, 4, D // fsdp_count))
        n = len(lead)
        order = tuple(range(n)) + (n + 2, n + 1, n, n + 3)
        return jnp.transpose(split, order).reshape(values.shape)

    def from_yzx(values):
        lead = values.shape[:-1]
        split = values.reshape(lead + (4, 2, 4, D // fsdp_count))
        n = len(lead)
        order = tuple(range(n)) + (n + 2, n + 1, n, n + 3)
        return jnp.transpose(split, order).reshape(values.shape)

    def pick_cols(values, axis):
        return jnp.stack(
            [lax.dynamic_slice_in_dim(values, offsets[s], RANK, axis) for s in range(seqs)]
        )

    def pick_groups(values):
        return jnp.stack(
            [
                lax.dynamic_slice_in_dim(values, adapter_id[s] * groups_per_adapter, groups_per_adapter, 0)
                for s in range(seqs)
            ]
        )

    a_in_sel = pick_cols(a_in_full, 2)
    b_rows_sel = jnp.stack(
        [
            jnp.transpose(
                lax.dynamic_slice_in_dim(g_brows, offsets[s], RANK, 3), (2, 3, 0, 1, 4)
            ).reshape(2, RANK, D)
            for s in range(seqs)
        ]
    )
    b_qkv_sel = jnp.moveaxis(pick_groups(g_bqkv), 1, 2).reshape(seqs, 3, RANK, qw_here)
    b_gateup_sel = jnp.moveaxis(pick_groups(g_bgateup), 1, 2).reshape(seqs, 2, RANK, ff_here)
    a_out_sel = jnp.moveaxis(pick_groups(g_aout), 1, 2).reshape(seqs, qw_here, RANK)
    a_down_sel = jnp.moveaxis(pick_groups(g_adown), 1, 2).reshape(seqs, ff_here, RANK)

    def gather_rows(values):
        full = tok_gather(values, 1)
        return full.reshape(seqs, length, values.shape[-1])

    def scatter_rows(values):
        return tok_scatter(values.reshape(seqs, tok_count, local_len, values.shape[-1]), 1)

    def column_forward(rows_full, weight, down_sel, up_sel, rows_for_weight=None):
        if rows_for_weight is None:
            rows_for_weight = rows_full
        lowrank = jnp.einsum("std,sdr->str", rows_full, down_sel, preferred_element_type=jnp.float32)
        linear = jnp.einsum("std,de->ste", rows_for_weight, weight, preferred_element_type=jnp.float32)
        return linear + adapter_scale * hp_dot(lowrank, up_sel.astype(jnp.float32), "str,sre->ste"), lowrank

    def row_forward(rows_here, weight, down_sel, up_sel):
        lowrank = jnp.einsum("std,sdr->str", rows_here, down_sel, preferred_element_type=jnp.float32)
        main_part = jnp.einsum("std,de->ste", rows_here, weight, preferred_element_type=jnp.float32)
        total = main_part + adapter_scale * hp_dot(lowrank, up_sel.astype(jnp.float32), "str,sre->ste")
        return scatter_rows(total), lowrank

    inputs_rows = tokens.astype(jnp.float32)
    allowed = (segments[:, :, None] == segments[:, None, :]) & (
        positions[:, None] >= positions[None, :]
    )[None]
    grad_ffn_full = gather_rows(cotangent)
    normed_rows, norm_attn_pull = jax.vjp(partial(rows_norm, gain_vector=gain_attn), inputs_rows)
    normed_full = gather_rows(normed_rows.astype(jnp.bfloat16))
    proj_lin = []
    proj_low = []
    for p in range(3):
        lin, lowr = column_forward(normed_full, w_qkv_full[p], a_in_sel[:, p], b_qkv_sel[:, p])
        proj_lin.append(lin)
        proj_low.append(lowr)
    rotate = partial(rotary_heads, positions=positions, head_dim=HEAD_DIM)
    query_rot, query_pull = jax.vjp(rotate, proj_lin[0])
    key_rot, key_pull = jax.vjp(rotate, proj_lin[1])
    query_in = query_rot.astype(jnp.bfloat16).reshape(seqs, length, heads_here, 2, HEAD_DIM)
    key_in = key_rot.astype(jnp.bfloat16).reshape(seqs, length, heads_here, 2, HEAD_DIM)
    value_in = proj_lin[2].astype(jnp.bfloat16).reshape(seqs, length, heads_here, VALUE_DIM)
    heads_out, log_total = jax.vmap(attend, in_axes=(0, 0, 0, 0, None))(
        query_in, key_in, value_in, allowed, lambda_here
    )
    mixed_float, head_pull = jax.vjp(partial(head_norm, gain_vector=gain_sub), heads_out)
    mixed_rows = mixed_float.reshape(seqs, length, qw_here).astype(jnp.bfloat16)
    attn_rows, out_low = row_forward(mixed_rows, w_out_full, a_out_sel, b_rows_sel[:, 0])
    hidden = inputs_rows + attn_rows
    normed_ffn, norm_ffn_pull = jax.vjp(partial(rows_norm, gain_vector=gain_ffn), hidden)
    ffn_full = gather_rows(normed_ffn.astype(jnp.bfloat16))
    gate_lin, gate_low = column_forward(ffn_full, w_gateup_perm[0], a_in_sel[:, 3], b_gateup_sel[:, 0])
    up_lin, up_low = column_forward(ffn_full, w_gateup_perm[1], a_in_sel[:, 4], b_gateup_sel[:, 1])
    product_float, swiglu_pull = jax.vjp(swiglu, gate_lin, up_lin)
    product = product_float.astype(jnp.bfloat16)
    ffn_rows, down_low = row_forward(product, w_down_full, a_down_sel, b_rows_sel[:, 1])
    output = (hidden + ffn_rows).astype(jnp.bfloat16)
    row_lows = tok_sum(jnp.stack([out_low, down_low]))

    tangent = cotangent.astype(jnp.float32)

    def row_backward(grad_full, rows_here, weight, down_sel, up_sel):
        grad_float = grad_full.astype(jnp.float32)
        grad_low = adapter_scale * hp_dot(grad_float, up_sel.astype(jnp.float32), "ste,sre->str")
        grad_down = hp_dot(rows_here.astype(jnp.float32), grad_low, "std,str->sdr")
        grad_inputs = jnp.einsum(
            "ste,de->std", grad_full, weight, preferred_element_type=jnp.float32
        ) + hp_dot(grad_low, down_sel.astype(jnp.float32), "str,sdr->std")
        return grad_inputs, grad_down

    def column_backward(rows_full, entries, weight_order=None):
        running = None
        grad_lows = []
        grads_up = []
        for grad_rows, weight, down_sel, up_sel, lowrank in entries:
            grad_float = grad_rows.astype(jnp.float32)
            grad_low = adapter_scale * hp_dot(grad_float, up_sel.astype(jnp.float32), "ste,sre->str")
            grads_up.append(adapter_scale * hp_dot(lowrank, grad_float, "str,ste->sre"))
            grad_lows.append(grad_low)
            main_term = jnp.einsum("ste,de->std", grad_rows, weight, preferred_element_type=jnp.float32)
            if weight_order is not None:
                main_term = weight_order(main_term)
            term = main_term + hp_dot(grad_low, down_sel.astype(jnp.float32), "str,sdr->std")
            running = term if running is None else running + term
        return scatter_rows(running), grad_lows, grads_up

    def mine_of(values, axis):
        shape = values.shape
        split = values.reshape(
            shape[:axis] + (fsdp_count, tok_count, D // (fsdp_count * tok_count)) + shape[axis + 1 :]
        )
        return lax.dynamic_index_in_dim(split, me_tok, axis + 1, keepdims=False)

    grad_product, grad_a_down = row_backward(
        grad_ffn_full, product, w_down_full, a_down_sel, b_rows_sel[:, 1]
    )
    grad_gate, grad_up = swiglu_pull(grad_product)
    grad_ffn_rows, ffn_grad_lows, ffn_grads_up = column_backward(
        ffn_full,
        (
            (grad_gate.astype(jnp.bfloat16), w_gateup_perm[0], a_in_sel[:, 3], b_gateup_sel[:, 0], gate_low),
            (grad_up.astype(jnp.bfloat16), w_gateup_perm[1], a_in_sel[:, 4], b_gateup_sel[:, 1], up_low),
        ),
    )
    grad_hidden = tangent + norm_ffn_pull(grad_ffn_rows)[0]
    grad_attn_full = gather_rows(grad_hidden.astype(jnp.bfloat16))
    grad_mixed, grad_a_out = row_backward(
        grad_attn_full, mixed_rows, w_out_full, a_out_sel, b_rows_sel[:, 0]
    )
    grad_heads = head_pull(grad_mixed.reshape(seqs, length, heads_here, VALUE_DIM))[0].astype(
        jnp.bfloat16
    )
    grad_query_rot, grad_key_rot, grad_values = jax.vmap(
        attend_back, in_axes=(0, 0, 0, 0, None, 0, 0)
    )(query_in, key_in, value_in, allowed, lambda_here, log_total, grad_heads)
    grad_query = query_pull(grad_query_rot.reshape(seqs, length, qw_here))[0].astype(jnp.bfloat16)
    grad_key = key_pull(grad_key_rot.reshape(seqs, length, qw_here))[0].astype(jnp.bfloat16)
    grad_attn_rows, attn_grad_lows, attn_grads_up = column_backward(
        normed_full,
        (
            (grad_query, w_qkv_full[0], a_in_sel[:, 0], b_qkv_sel[:, 0], proj_low[0]),
            (grad_key, w_qkv_full[1], a_in_sel[:, 1], b_qkv_sel[:, 1], proj_low[1]),
            (grad_values.reshape(seqs, length, qw_here), w_qkv_full[2], a_in_sel[:, 2], b_qkv_sel[:, 2], proj_low[2]),
        ),
    )
    grad_tokens = grad_hidden + norm_attn_pull(grad_attn_rows)[0]

    grad_lows = tok_sum(jnp.stack(attn_grad_lows + ffn_grad_lows))
    onehot = (
        jnp.arange(COLS)[None, None, :] == offsets[:, None, None] + jnp.arange(RANK)[None, :, None]
    ).astype(jnp.float32)
    wide_lows = hp_dot(grad_lows, onehot, "pstr,src->pstc")
    def a_in_rows_mine(dense):
        split = dense.reshape(dense.shape[0], fsdp_count, tok_count, RANK, COLS)
        return lax.dynamic_index_in_dim(split, me_tok, 2, keepdims=False)

    a_in_mine = jnp.concatenate(
        [
            a_in_rows_mine(hp_dot(normed_full.astype(jnp.float32), wide_lows[:3], "std,pstc->pdc")),
            a_in_rows_mine(hp_dot(ffn_full.astype(jnp.float32), wide_lows[3:], "std,pstc->pdc")),
        ]
    )
    wide_row_lows = hp_dot(row_lows, onehot, "qstr,src->qstc")
    dense_b_rows = adapter_scale * hp_dot(
        wide_row_lows,
        jnp.stack([grad_attn_full, grad_ffn_full]).astype(jnp.float32),
        "qstc,qstd->qcd",
    )
    b_rows_mine = lax.dynamic_index_in_dim(
        dense_b_rows.reshape(2, COLS, fsdp_count, tok_count, RANK), me_tok, 3, keepdims=False
    )
    def reduce_to_owners(parts, kind):
        rows = [p.size // (fsdp_count * COLS) for p in parts]
        packed = jnp.concatenate(
            [p.reshape(fsdp_count, r, COLS) for p, r in zip(parts, rows)], axis=1
        ).astype(kind)
        total = lax.all_to_all(packed, "fsdp", 0, 0, tiled=False).astype(jnp.float32).sum(0)
        out = []
        start = 0
        for p, r in zip(parts, rows):
            out.append(total[start : start + r].reshape(p.shape[1:]))
            start += r
        return out

    per = COLS // fsdp_count
    dense_b_gateup = hp_dot(onehot, jnp.stack(ffn_grads_up, 1), "src,spre->pce")
    dense_a_down = hp_dot(grad_a_down, onehot, "sdr,src->dc")
    b_gateup_block, a_down_block = reduce_to_owners(
        [
            jnp.moveaxis(dense_b_gateup.reshape(2, fsdp_count, per, ff_here), 1, 0),
            jnp.moveaxis(dense_a_down.reshape(ff_here, fsdp_count, per), 1, 0),
        ],
        jnp.bfloat16,
    )
    dense_b_qkv = hp_dot(onehot, jnp.stack(attn_grads_up, 1), "src,spre->pce")
    dense_a_out = hp_dot(grad_a_out, onehot, "sdr,src->dc")
    b_qkv_block, a_out_block = reduce_to_owners(
        [
            jnp.moveaxis(dense_b_qkv.reshape(3, fsdp_count, per, qw_here), 1, 0),
            jnp.moveaxis(dense_a_out.reshape(qw_here, fsdp_count, per), 1, 0),
        ],
        jnp.bfloat16,
    )
    a_in_block, b_rows_block = reduce_to_owners(
        [jnp.moveaxis(a_in_mine, 1, 0), jnp.moveaxis(b_rows_mine, 2, 0)], jnp.float32
    )

    return (
        output,
        grad_tokens,
        a_in_block,
        b_qkv_block,
        b_gateup_block,
        a_out_block,
        a_down_block,
        b_rows_block,
    )


def solution(mesh):
    return jax.shard_map(
        per_device,
        mesh=mesh,
        in_specs=(
            P("fsdp", "tok", None),
            P("fsdp", "tok", None),
            P("fsdp", None),
            P("fsdp"),
            P(None, "fsdp", "tok"),
            P("tok", "fsdp"),
            P(None, "fsdp", "tok"),
            P("tok", "fsdp"),
            P(),
            P(),
            P(),
            P(),
            P(None, ("fsdp", "tok"), None),
            P(None, "fsdp", "tok"),
            P(None, "fsdp", "tok"),
            P("tok", "fsdp"),
            P("tok", "fsdp"),
            P(None, None, ("fsdp", "tok")),
        ),
        out_specs=(
            P("fsdp", "tok", None),
            P("fsdp", "tok", None),
            P(None, ("fsdp", "tok"), None),
            P(None, "fsdp", "tok"),
            P(None, "fsdp", "tok"),
            P("tok", "fsdp"),
            P("tok", "fsdp"),
            P(None, None, ("fsdp", "tok")),
        ),
        check_vma=False,
    )
```

```python
from functools import partial

import jax
import jax.numpy as jnp
from jax import lax
from jax.sharding import PartitionSpec as P

D = 2048
HEAD_DIM = 128
VALUE_DIM = 256
RANK = 16
COLS = 128


highest = lax.Precision.HIGHEST
negative = -1e30
adapter_scale = 2.0
lambda_init = 0.2
rotary_base = 10000.0
row_epsilon = 1e-06
head_epsilon = 1e-05


def rows_norm(values, gain_vector):
    return (
        values
        * lax.rsqrt(jnp.mean(values * values, axis=-1, keepdims=True) + row_epsilon)
        * gain_vector
    )


def head_norm(values, gain_vector):
    scaled = values * lax.rsqrt(jnp.mean(values * values, axis=-1, keepdims=True) + head_epsilon)
    return scaled * gain_vector * (1.0 - lambda_init)


def rotary_heads(values, positions, head_dim):
    lead = values.shape[:-1]
    groups = values.reshape(lead + (-1, head_dim))
    half_dim = head_dim // 2
    frequency = rotary_base ** (-jnp.arange(half_dim, dtype=jnp.float32) / half_dim)
    angles = positions.astype(jnp.float32)[:, None] * frequency[None, :]
    cosine = jnp.cos(angles)[:, None, :]
    sine_part = jnp.sin(angles)[:, None, :]
    first_half = groups[..., :half_dim]
    second = groups[..., half_dim:]
    turned = jnp.concatenate(
        [first_half * cosine - second * sine_part, second * cosine + first_half * sine_part],
        axis=-1,
    )
    return turned.reshape(values.shape)


def swiglu(gate_rows, up_rows):
    return gate_rows * jax.nn.sigmoid(gate_rows) * up_rows


def attention_scores(query_in, key_in, allowed):
    raw_scores = jnp.einsum(
        "qhmd,khmd->hmqk", query_in, key_in, preferred_element_type=jnp.float32
    ) * query_in.shape[-1] ** (-0.5)
    return jnp.where(allowed[None, None], raw_scores, negative)


def attend(query_in, key_in, value_in, allowed, lambda_here):
    scores = attention_scores(query_in, key_in, allowed)
    row_max = jnp.max(scores, axis=-1, keepdims=True)
    log_total = row_max + jnp.log(jnp.sum(jnp.exp(scores - row_max), axis=-1, keepdims=True))
    soft_max = jnp.exp(scores - log_total)
    differ = (soft_max[:, 0] - lambda_here[:, None, None] * soft_max[:, 1]).astype(jnp.bfloat16)
    heads_out = jnp.einsum("hqk,khd->qhd", differ, value_in, preferred_element_type=jnp.float32)
    return (heads_out, log_total)


def attend_back(query_in, key_in, value_in, allowed, lambda_here, log_total, grad_heads):
    scale = query_in.shape[-1] ** (-0.5)
    scores = attention_scores(query_in, key_in, allowed)
    soft_max = jnp.exp(scores - log_total)
    differ = (soft_max[:, 0] - lambda_here[:, None, None] * soft_max[:, 1]).astype(jnp.bfloat16)
    grad_values = jnp.einsum("hqk,qhd->khd", differ, grad_heads, preferred_element_type=jnp.float32)
    grad_differ = jnp.einsum(
        "qhd,khd->hqk", grad_heads, value_in, preferred_element_type=jnp.float32
    )
    grad_soft = jnp.stack([grad_differ, -lambda_here[:, None, None] * grad_differ], axis=1)
    grad_scores = (
        soft_max * (grad_soft - jnp.sum(grad_soft * soft_max, axis=-1, keepdims=True))
    ).astype(jnp.bfloat16)
    grad_query = (
        jnp.einsum("hmqk,khmd->qhmd", grad_scores, key_in, preferred_element_type=jnp.float32)
        * scale
    )
    grad_key = (
        jnp.einsum("hmqk,qhmd->khmd", grad_scores, query_in, preferred_element_type=jnp.float32)
        * scale
    )
    return (grad_query, grad_key, grad_values.astype(jnp.bfloat16))


def xor_pairs(count, bit):
    return [(i, i ^ bit) for i in range(count)]


def tok_gather(values, axis=0):
    count = lax.axis_size("tok")
    me = lax.axis_index("tok")
    far = lax.ppermute(values, "tok", xor_pairs(count, 2))
    pair = jnp.where(
        (me & 2) == 0, jnp.stack([values, far], axis), jnp.stack([far, values], axis)
    )
    near = lax.ppermute(pair, "tok", xor_pairs(count, 1))
    full = jnp.where(
        (me & 1) == 0, jnp.stack([pair, near], axis + 1), jnp.stack([near, pair], axis + 1)
    )
    return full.reshape(values.shape[:axis] + (count,) + values.shape[axis:])


def tok_scatter(blocks, axis=0):
    count = lax.axis_size("tok")
    me = lax.axis_index("tok")
    core = me & 1
    half = (me >> 1) & 1
    split = blocks.reshape(blocks.shape[:axis] + (2, 2) + blocks.shape[axis + 1 :])
    mine = lax.dynamic_index_in_dim(split, core, axis + 1, keepdims=False)
    theirs = lax.dynamic_index_in_dim(split, 1 - core, axis + 1, keepdims=False)
    chip_sum = mine + lax.ppermute(theirs, "tok", xor_pairs(count, 1))
    keep = lax.dynamic_index_in_dim(chip_sum, half, axis, keepdims=False)
    send = lax.dynamic_index_in_dim(chip_sum, 1 - half, axis, keepdims=False)
    got = lax.ppermute(send.astype(jnp.bfloat16), "tok", xor_pairs(count, 2))
    return keep + got.astype(keep.dtype)


def tok_sum(values):
    count = lax.axis_size("tok")
    chip_sum = values + lax.ppermute(values, "tok", xor_pairs(count, 1))
    return chip_sum + lax.ppermute(chip_sum, "tok", xor_pairs(count, 2))


def fsdp_coords():
    me = lax.axis_index("fsdp")
    return {"x": me // 8, "z": (me // 4) % 2, "y": me % 4}


def fsdp_pairs(kind, step):
    pairs = []
    for x in range(4):
        for z in range(2):
            for y in range(4):
                if kind == "z":
                    target = (x * 2 + 1 - z) * 4 + y
                elif kind == "x":
                    target = (((x + step) % 4) * 2 + z) * 4 + y
                else:
                    target = (x * 2 + z) * 4 + (y + step) % 4
                pairs.append(((x * 2 + z) * 4 + y, target))
    return pairs


def put(buffer, piece, axis, offset):
    start = [0] * buffer.ndim
    start[axis] = offset
    return lax.dynamic_update_slice(buffer, piece, start)


def grow(pieces, axes, factor):
    return [
        jnp.zeros(p.shape[:ax] + (p.shape[ax] * factor,) + p.shape[ax + 1 :], p.dtype)
        for p, ax in zip(pieces, axes)
    ]


def halves(pieces, axes, second):
    out = []
    for p, ax in zip(pieces, axes):
        n = p.shape[ax] // 2
        out.append(lax.slice_in_dim(p, n if second else 0, 2 * n if second else n, axis=ax))
    return out


def pair_stage(stacks, axes, coord):
    other = lax.ppermute(stacks, "fsdp", fsdp_pairs("z", 1))
    outs = []
    for mine, theirs, buffer, ax in zip(stacks, other, grow(stacks, axes, 2), axes):
        n = mine.shape[ax]
        buffer = put(buffer, mine, ax, coord * n)
        outs.append(put(buffer, theirs, ax, (1 - coord) * n))
    return outs


def ring_stage(stacks, axes, kind, coord):
    from_left = lax.ppermute(stacks, "fsdp", fsdp_pairs(kind, 1))
    from_right = lax.ppermute(stacks, "fsdp", fsdp_pairs(kind, -1))
    split = stacks[0].shape[axes[0]] > 1
    if split:
        far_left = lax.ppermute(halves(from_left, axes, False), "fsdp", fsdp_pairs(kind, 1))
        far_right = lax.ppermute(halves(from_right, axes, True), "fsdp", fsdp_pairs(kind, -1))
    else:
        far_left = lax.ppermute(from_left, "fsdp", fsdp_pairs(kind, 1))
    outs = []
    for i, (buffer, ax) in enumerate(zip(grow(stacks, axes, 4), axes)):
        n = stacks[i].shape[ax]
        buffer = put(buffer, stacks[i], ax, coord * n)
        buffer = put(buffer, from_right[i], ax, ((coord + 1) % 4) * n)
        buffer = put(buffer, from_left[i], ax, ((coord + 3) % 4) * n)
        buffer = put(buffer, far_left[i], ax, ((coord + 2) % 4) * n)
        if split:
            buffer = put(buffer, far_right[i], ax, ((coord + 2) % 4) * n + n // 2)
        outs.append(buffer)
    return outs


def torus_gather(route_a, axes_a, route_b, axes_b):
    coord = fsdp_coords()
    route_a = ring_stage(route_a, axes_a, "y", coord["y"])
    route_b = ring_stage(route_b, axes_b, "x", coord["x"])
    both = pair_stage(route_a + route_b, axes_a + axes_b, coord["z"])
    route_a, route_b = both[: len(route_a)], both[len(route_a) :]
    return ring_stage(route_a, axes_a, "x", coord["x"]), ring_stage(route_b, axes_b, "y", coord["y"])


def hp_dot(left, right, spec):
    return jnp.einsum(spec, left, right, precision=highest, preferred_element_type=jnp.float32)


def per_device(
    tokens,
    cotangent,
    segments,
    adapter_id,
    w_qkv,
    w_out,
    w_gateup,
    w_down,
    gain_attn,
    gain_ffn,
    gain_sub,
    lambda_head,
    a_in,
    b_qkv,
    b_gateup,
    a_out,
    a_down,
    b_rows,
):
    tok_count = lax.axis_size("tok")
    fsdp_count = lax.axis_size("fsdp")
    me_tok = lax.axis_index("tok")
    seqs, local_len, _ = tokens.shape
    length = local_len * tok_count
    qw_here = w_qkv.shape[2]
    ff_here = w_gateup.shape[2]
    heads_here = qw_here // VALUE_DIM
    lambda_here = lax.dynamic_slice_in_dim(lambda_head, me_tok * heads_here, heads_here)
    positions = jnp.arange(length)
    offsets = adapter_id * RANK
    fsdp_rows = w_qkv.shape[1]
    groups_per_adapter = RANK // b_qkv.shape[1]

    a_in_tok = tok_gather(a_in)
    b_rows_tok = tok_gather(b_rows)
    small = [a_in_tok, b_rows_tok, b_qkv, b_gateup, a_out, a_down]
    small_flat = jnp.concatenate([p.reshape(-1, COLS) for p in small])
    (g_qkv, g_down, g_small), (g_gateup, g_out) = torus_gather(
        [w_qkv[:, None], w_down[None], small_flat[None]],
        [1, 0, 0],
        [w_gateup[:, None], w_out[None]],
        [1, 0],
    )
    w_qkv_full = g_qkv.reshape(3, D, qw_here)
    w_out_full = jnp.transpose(
        g_out.reshape(4, 2, 4, qw_here, D // fsdp_count), (3, 2, 1, 0, 4)
    ).reshape(qw_here, D)
    w_down_full = jnp.moveaxis(g_down, 0, 1).reshape(ff_here, D)
    w_gateup_perm = jnp.transpose(
        g_gateup.reshape(2, 4, 2, 4, D // fsdp_count, ff_here), (0, 3, 2, 1, 4, 5)
    ).reshape(2, D, ff_here)
    unpacked = []
    start = 0
    for p in small:
        rows = p.size // COLS
        unpacked.append(g_small[:, start : start + rows].reshape((fsdp_count,) + p.shape))
        start += rows
    (g_ain, g_brows, g_bqkv, g_bgateup, g_aout, g_adown) = unpacked
    a_in_full = jnp.transpose(g_ain, (2, 0, 1, 3, 4)).reshape(5, D, COLS)
    b_rows_full = jnp.transpose(g_brows, (2, 3, 0, 1, 4)).reshape(2, COLS, D)

    def to_yzx(values):
        lead = values.shape[:-1]
        split = values.reshape(lead + (4, 2, 4, D // fsdp_count))
        n = len(lead)
        order = tuple(range(n)) + (n + 2, n + 1, n, n + 3)
        return jnp.transpose(split, order).reshape(values.shape)

    def from_yzx(values):
        lead = values.shape[:-1]
        split = values.reshape(lead + (4, 2, 4, D // fsdp_count))
        n = len(lead)
        order = tuple(range(n)) + (n + 2, n + 1, n, n + 3)
        return jnp.transpose(split, order).reshape(values.shape)

    def pick_cols(values, axis):
        return jnp.stack(
            [lax.dynamic_slice_in_dim(values, offsets[s], RANK, axis) for s in range(seqs)]
        )

    def pick_groups(values):
        return jnp.stack(
            [
                lax.dynamic_slice_in_dim(values, adapter_id[s] * groups_per_adapter, groups_per_adapter, 0)
                for s in range(seqs)
            ]
        )

    a_in_sel = pick_cols(a_in_full, 2)
    b_rows_sel = pick_cols(b_rows_full, 1)
    b_qkv_sel = jnp.moveaxis(pick_groups(g_bqkv), 1, 2).reshape(seqs, 3, RANK, qw_here)
    b_gateup_sel = jnp.moveaxis(pick_groups(g_bgateup), 1, 2).reshape(seqs, 2, RANK, ff_here)
    a_out_sel = jnp.moveaxis(pick_groups(g_aout), 1, 2).reshape(seqs, qw_here, RANK)
    a_down_sel = jnp.moveaxis(pick_groups(g_adown), 1, 2).reshape(seqs, ff_here, RANK)

    def gather_rows(values):
        full = tok_gather(values, 1)
        return full.reshape(seqs, length, values.shape[-1])

    def scatter_rows(values):
        return tok_scatter(values.reshape(seqs, tok_count, local_len, values.shape[-1]), 1)

    def column_forward(rows_full, weight, down_sel, up_sel, rows_for_weight=None):
        if rows_for_weight is None:
            rows_for_weight = rows_full
        lowrank = jnp.einsum("std,sdr->str", rows_full, down_sel, preferred_element_type=jnp.float32)
        linear = jnp.einsum("std,de->ste", rows_for_weight, weight, preferred_element_type=jnp.float32)
        return linear + adapter_scale * hp_dot(lowrank, up_sel.astype(jnp.float32), "str,sre->ste"), lowrank

    def row_forward(rows_here, weight, down_sel, up_sel):
        lowrank = jnp.einsum("std,sdr->str", rows_here, down_sel, preferred_element_type=jnp.float32)
        main_part = jnp.einsum("std,de->ste", rows_here, weight, preferred_element_type=jnp.float32)
        total = main_part + adapter_scale * hp_dot(lowrank, up_sel.astype(jnp.float32), "str,sre->ste")
        return scatter_rows(total), lowrank

    inputs_rows = tokens.astype(jnp.float32)
    allowed = (segments[:, :, None] == segments[:, None, :]) & (
        positions[:, None] >= positions[None, :]
    )[None]
    grad_ffn_full = gather_rows(cotangent)
    normed_rows, norm_attn_pull = jax.vjp(partial(rows_norm, gain_vector=gain_attn), inputs_rows)
    normed_full = gather_rows(normed_rows.astype(jnp.bfloat16))
    proj_lin = []
    proj_low = []
    for p in range(3):
        lin, lowr = column_forward(normed_full, w_qkv_full[p], a_in_sel[:, p], b_qkv_sel[:, p])
        proj_lin.append(lin)
        proj_low.append(lowr)
    rotate = partial(rotary_heads, positions=positions, head_dim=HEAD_DIM)
    query_rot, query_pull = jax.vjp(rotate, proj_lin[0])
    key_rot, key_pull = jax.vjp(rotate, proj_lin[1])
    query_in = query_rot.astype(jnp.bfloat16).reshape(seqs, length, heads_here, 2, HEAD_DIM)
    key_in = key_rot.astype(jnp.bfloat16).reshape(seqs, length, heads_here, 2, HEAD_DIM)
    value_in = proj_lin[2].astype(jnp.bfloat16).reshape(seqs, length, heads_here, VALUE_DIM)
    heads_out, log_total = jax.vmap(attend, in_axes=(0, 0, 0, 0, None))(
        query_in, key_in, value_in, allowed, lambda_here
    )
    mixed_float, head_pull = jax.vjp(partial(head_norm, gain_vector=gain_sub), heads_out)
    mixed_rows = mixed_float.reshape(seqs, length, qw_here).astype(jnp.bfloat16)
    attn_rows, out_low = row_forward(mixed_rows, w_out_full, a_out_sel, b_rows_sel[:, 0])
    hidden = inputs_rows + attn_rows
    normed_ffn, norm_ffn_pull = jax.vjp(partial(rows_norm, gain_vector=gain_ffn), hidden)
    ffn_full = gather_rows(normed_ffn.astype(jnp.bfloat16))
    gate_lin, gate_low = column_forward(ffn_full, w_gateup_perm[0], a_in_sel[:, 3], b_gateup_sel[:, 0])
    up_lin, up_low = column_forward(ffn_full, w_gateup_perm[1], a_in_sel[:, 4], b_gateup_sel[:, 1])
    product_float, swiglu_pull = jax.vjp(swiglu, gate_lin, up_lin)
    product = product_float.astype(jnp.bfloat16)
    ffn_rows, down_low = row_forward(product, w_down_full, a_down_sel, b_rows_sel[:, 1])
    output = (hidden + ffn_rows).astype(jnp.bfloat16)
    row_lows = tok_sum(jnp.stack([out_low, down_low]))

    tangent = cotangent.astype(jnp.float32)

    def row_backward(grad_full, rows_here, weight, down_sel, up_sel):
        grad_float = grad_full.astype(jnp.float32)
        grad_low = adapter_scale * hp_dot(grad_float, up_sel.astype(jnp.float32), "ste,sre->str")
        grad_down = hp_dot(rows_here.astype(jnp.float32), grad_low, "std,str->sdr")
        grad_inputs = jnp.einsum(
            "ste,de->std", grad_full, weight, preferred_element_type=jnp.float32
        ) + hp_dot(grad_low, down_sel.astype(jnp.float32), "str,sdr->std")
        return grad_inputs, grad_down

    def column_backward(rows_full, entries, weight_order=None):
        running = None
        grad_lows = []
        grads_up = []
        for grad_rows, weight, down_sel, up_sel, lowrank in entries:
            grad_float = grad_rows.astype(jnp.float32)
            grad_low = adapter_scale * hp_dot(grad_float, up_sel.astype(jnp.float32), "ste,sre->str")
            grads_up.append(adapter_scale * hp_dot(lowrank, grad_float, "str,ste->sre"))
            grad_lows.append(grad_low)
            main_term = jnp.einsum("ste,de->std", grad_rows, weight, preferred_element_type=jnp.float32)
            if weight_order is not None:
                main_term = weight_order(main_term)
            term = main_term + hp_dot(grad_low, down_sel.astype(jnp.float32), "str,sdr->std")
            running = term if running is None else running + term
        return scatter_rows(running), grad_lows, grads_up

    def mine_of(values, axis):
        shape = values.shape
        split = values.reshape(
            shape[:axis] + (fsdp_count, tok_count, D // (fsdp_count * tok_count)) + shape[axis + 1 :]
        )
        return lax.dynamic_index_in_dim(split, me_tok, axis + 1, keepdims=False)

    grad_product, grad_a_down = row_backward(
        grad_ffn_full, product, w_down_full, a_down_sel, b_rows_sel[:, 1]
    )
    grad_gate, grad_up = swiglu_pull(grad_product)
    grad_ffn_rows, ffn_grad_lows, ffn_grads_up = column_backward(
        ffn_full,
        (
            (grad_gate.astype(jnp.bfloat16), w_gateup_perm[0], a_in_sel[:, 3], b_gateup_sel[:, 0], gate_low),
            (grad_up.astype(jnp.bfloat16), w_gateup_perm[1], a_in_sel[:, 4], b_gateup_sel[:, 1], up_low),
        ),
    )
    grad_hidden = tangent + norm_ffn_pull(grad_ffn_rows)[0]
    grad_attn_full = gather_rows(grad_hidden.astype(jnp.bfloat16))
    grad_mixed, grad_a_out = row_backward(
        grad_attn_full, mixed_rows, w_out_full, a_out_sel, b_rows_sel[:, 0]
    )
    grad_heads = head_pull(grad_mixed.reshape(seqs, length, heads_here, VALUE_DIM))[0].astype(
        jnp.bfloat16
    )
    grad_query_rot, grad_key_rot, grad_values = jax.vmap(
        attend_back, in_axes=(0, 0, 0, 0, None, 0, 0)
    )(query_in, key_in, value_in, allowed, lambda_here, log_total, grad_heads)
    grad_query = query_pull(grad_query_rot.reshape(seqs, length, qw_here))[0].astype(jnp.bfloat16)
    grad_key = key_pull(grad_key_rot.reshape(seqs, length, qw_here))[0].astype(jnp.bfloat16)
    grad_attn_rows, attn_grad_lows, attn_grads_up = column_backward(
        normed_full,
        (
            (grad_query, w_qkv_full[0], a_in_sel[:, 0], b_qkv_sel[:, 0], proj_low[0]),
            (grad_key, w_qkv_full[1], a_in_sel[:, 1], b_qkv_sel[:, 1], proj_low[1]),
            (grad_values.reshape(seqs, length, qw_here), w_qkv_full[2], a_in_sel[:, 2], b_qkv_sel[:, 2], proj_low[2]),
        ),
    )
    grad_tokens = grad_hidden + norm_attn_pull(grad_attn_rows)[0]

    grad_lows = tok_sum(jnp.stack(attn_grad_lows + ffn_grad_lows))
    onehot = (
        jnp.arange(COLS)[None, None, :] == offsets[:, None, None] + jnp.arange(RANK)[None, :, None]
    ).astype(jnp.float32)
    wide_lows = hp_dot(grad_lows, onehot, "pstr,src->pstc")
    dense_a_in = jnp.concatenate(
        [
            hp_dot(normed_full.astype(jnp.float32), wide_lows[:3], "std,pstc->pdc"),
            hp_dot(ffn_full.astype(jnp.float32), wide_lows[3:], "std,pstc->pdc"),
        ]
    )
    a_in_mine = lax.dynamic_index_in_dim(
        dense_a_in.reshape(5, fsdp_count, tok_count, RANK, COLS), me_tok, 2, keepdims=False
    )
    wide_row_lows = hp_dot(row_lows, onehot, "qstr,src->qstc")
    dense_b_rows = adapter_scale * hp_dot(
        wide_row_lows,
        jnp.stack([grad_attn_full, grad_ffn_full]).astype(jnp.float32),
        "qstc,qstd->qcd",
    )
    b_rows_mine = lax.dynamic_index_in_dim(
        dense_b_rows.reshape(2, COLS, fsdp_count, tok_count, RANK), me_tok, 3, keepdims=False
    )
    def reduce_to_owners(parts, kind):
        rows = [p.size // (fsdp_count * COLS) for p in parts]
        packed = jnp.concatenate(
            [p.reshape(fsdp_count, r, COLS) for p, r in zip(parts, rows)], axis=1
        ).astype(kind)
        total = lax.all_to_all(packed, "fsdp", 0, 0, tiled=False).astype(jnp.float32).sum(0)
        out = []
        start = 0
        for p, r in zip(parts, rows):
            out.append(total[start : start + r].reshape(p.shape[1:]))
            start += r
        return out

    per = COLS // fsdp_count
    dense_b_gateup = hp_dot(onehot, jnp.stack(ffn_grads_up, 1), "src,spre->pce")
    dense_a_down = hp_dot(grad_a_down, onehot, "sdr,src->dc")
    b_gateup_block, a_down_block = reduce_to_owners(
        [
            jnp.moveaxis(dense_b_gateup.reshape(2, fsdp_count, per, ff_here), 1, 0),
            jnp.moveaxis(dense_a_down.reshape(ff_here, fsdp_count, per), 1, 0),
        ],
        jnp.bfloat16,
    )
    dense_b_qkv = hp_dot(onehot, jnp.stack(attn_grads_up, 1), "src,spre->pce")
    dense_a_out = hp_dot(grad_a_out, onehot, "sdr,src->dc")
    b_qkv_block, a_out_block = reduce_to_owners(
        [
            jnp.moveaxis(dense_b_qkv.reshape(3, fsdp_count, per, qw_here), 1, 0),
            jnp.moveaxis(dense_a_out.reshape(qw_here, fsdp_count, per), 1, 0),
        ],
        jnp.bfloat16,
    )
    a_in_block, b_rows_block = reduce_to_owners(
        [jnp.moveaxis(a_in_mine, 1, 0), jnp.moveaxis(b_rows_mine, 2, 0)], jnp.float32
    )

    return (
        output,
        grad_tokens,
        a_in_block,
        b_qkv_block,
        b_gateup_block,
        a_out_block,
        a_down_block,
        b_rows_block,
    )


def solution(mesh):
    return jax.shard_map(
        per_device,
        mesh=mesh,
        in_specs=(
            P("fsdp", "tok", None),
            P("fsdp", "tok", None),
            P("fsdp", None),
            P("fsdp"),
            P(None, "fsdp", "tok"),
            P("tok", "fsdp"),
            P(None, "fsdp", "tok"),
            P("tok", "fsdp"),
            P(),
            P(),
            P(),
            P(),
            P(None, ("fsdp", "tok"), None),
            P(None, "fsdp", "tok"),
            P(None, "fsdp", "tok"),
            P("tok", "fsdp"),
            P("tok", "fsdp"),
            P(None, None, ("fsdp", "tok")),
        ),
        out_specs=(
            P("fsdp", "tok", None),
            P("fsdp", "tok", None),
            P(None, ("fsdp", "tok"), None),
            P(None, "fsdp", "tok"),
            P(None, "fsdp", "tok"),
            P("tok", "fsdp"),
            P("tok", "fsdp"),
            P(None, None, ("fsdp", "tok")),
        ),
        check_vma=False,
    )
```

```python
from functools import partial

import jax
import jax.numpy as jnp
from jax import lax
from jax.sharding import PartitionSpec as P

D = 2048
HEAD_DIM = 128
VALUE_DIM = 256
RANK = 16
COLS = 128


highest = lax.Precision.HIGHEST
negative = -1e30
adapter_scale = 2.0
lambda_init = 0.2
rotary_base = 10000.0
row_epsilon = 1e-06
head_epsilon = 1e-05


def rows_norm(values, gain_vector):
    return (
        values
        * lax.rsqrt(jnp.mean(values * values, axis=-1, keepdims=True) + row_epsilon)
        * gain_vector
    )


def head_norm(values, gain_vector):
    scaled = values * lax.rsqrt(jnp.mean(values * values, axis=-1, keepdims=True) + head_epsilon)
    return scaled * gain_vector * (1.0 - lambda_init)


def rotary_heads(values, positions, head_dim):
    lead = values.shape[:-1]
    groups = values.reshape(lead + (-1, head_dim))
    half_dim = head_dim // 2
    frequency = rotary_base ** (-jnp.arange(half_dim, dtype=jnp.float32) / half_dim)
    angles = positions.astype(jnp.float32)[:, None] * frequency[None, :]
    cosine = jnp.cos(angles)[:, None, :]
    sine_part = jnp.sin(angles)[:, None, :]
    first_half = groups[..., :half_dim]
    second = groups[..., half_dim:]
    turned = jnp.concatenate(
        [first_half * cosine - second * sine_part, second * cosine + first_half * sine_part],
        axis=-1,
    )
    return turned.reshape(values.shape)


def swiglu(gate_rows, up_rows):
    return gate_rows * jax.nn.sigmoid(gate_rows) * up_rows


def attention_scores(query_in, key_in, allowed):
    raw_scores = jnp.einsum(
        "qhmd,khmd->hmqk", query_in, key_in, preferred_element_type=jnp.float32
    ) * query_in.shape[-1] ** (-0.5)
    return jnp.where(allowed[None, None], raw_scores, negative)


def attend(query_in, key_in, value_in, allowed, lambda_here):
    scores = attention_scores(query_in, key_in, allowed)
    row_max = jnp.max(scores, axis=-1, keepdims=True)
    log_total = row_max + jnp.log(jnp.sum(jnp.exp(scores - row_max), axis=-1, keepdims=True))
    soft_max = jnp.exp(scores - log_total)
    differ = (soft_max[:, 0] - lambda_here[:, None, None] * soft_max[:, 1]).astype(jnp.bfloat16)
    heads_out = jnp.einsum("hqk,khd->qhd", differ, value_in, preferred_element_type=jnp.float32)
    return (heads_out, log_total)


def attend_back(query_in, key_in, value_in, allowed, lambda_here, log_total, grad_heads):
    scale = query_in.shape[-1] ** (-0.5)
    scores = attention_scores(query_in, key_in, allowed)
    soft_max = jnp.exp(scores - log_total)
    differ = (soft_max[:, 0] - lambda_here[:, None, None] * soft_max[:, 1]).astype(jnp.bfloat16)
    grad_values = jnp.einsum("hqk,qhd->khd", differ, grad_heads, preferred_element_type=jnp.float32)
    grad_differ = jnp.einsum(
        "qhd,khd->hqk", grad_heads, value_in, preferred_element_type=jnp.float32
    )
    grad_soft = jnp.stack([grad_differ, -lambda_here[:, None, None] * grad_differ], axis=1)
    grad_scores = (
        soft_max * (grad_soft - jnp.sum(grad_soft * soft_max, axis=-1, keepdims=True))
    ).astype(jnp.bfloat16)
    grad_query = (
        jnp.einsum("hmqk,khmd->qhmd", grad_scores, key_in, preferred_element_type=jnp.float32)
        * scale
    )
    grad_key = (
        jnp.einsum("hmqk,qhmd->khmd", grad_scores, query_in, preferred_element_type=jnp.float32)
        * scale
    )
    return (grad_query, grad_key, grad_values.astype(jnp.bfloat16))


def xor_pairs(count, bit):
    return [(i, i ^ bit) for i in range(count)]


def tok_gather(values, axis=0):
    count = lax.axis_size("tok")
    me = lax.axis_index("tok")
    far = lax.ppermute(values, "tok", xor_pairs(count, 2))
    pair = jnp.where(
        (me & 2) == 0, jnp.stack([values, far], axis), jnp.stack([far, values], axis)
    )
    near = lax.ppermute(pair, "tok", xor_pairs(count, 1))
    full = jnp.where(
        (me & 1) == 0, jnp.stack([pair, near], axis + 1), jnp.stack([near, pair], axis + 1)
    )
    return full.reshape(values.shape[:axis] + (count,) + values.shape[axis:])


def tok_scatter(blocks, axis=0):
    count = lax.axis_size("tok")
    me = lax.axis_index("tok")
    core = me & 1
    half = (me >> 1) & 1
    split = blocks.reshape(blocks.shape[:axis] + (2, 2) + blocks.shape[axis + 1 :])
    mine = lax.dynamic_index_in_dim(split, core, axis + 1, keepdims=False)
    theirs = lax.dynamic_index_in_dim(split, 1 - core, axis + 1, keepdims=False)
    chip_sum = mine + lax.ppermute(theirs, "tok", xor_pairs(count, 1))
    keep = lax.dynamic_index_in_dim(chip_sum, half, axis, keepdims=False)
    send = lax.dynamic_index_in_dim(chip_sum, 1 - half, axis, keepdims=False)
    got = lax.ppermute(send.astype(jnp.bfloat16), "tok", xor_pairs(count, 2))
    return keep + got.astype(keep.dtype)


def tok_sum(values):
    count = lax.axis_size("tok")
    chip_sum = values + lax.ppermute(values, "tok", xor_pairs(count, 1))
    return chip_sum + lax.ppermute(chip_sum, "tok", xor_pairs(count, 2))


def fsdp_coords():
    me = lax.axis_index("fsdp")
    return {"x": me // 8, "z": (me // 4) % 2, "y": me % 4}


def fsdp_pairs(kind, step):
    pairs = []
    for x in range(4):
        for z in range(2):
            for y in range(4):
                if kind == "z":
                    target = (x * 2 + 1 - z) * 4 + y
                elif kind == "x":
                    target = (((x + step) % 4) * 2 + z) * 4 + y
                else:
                    target = (x * 2 + z) * 4 + (y + step) % 4
                pairs.append(((x * 2 + z) * 4 + y, target))
    return pairs


def put(buffer, piece, axis, offset):
    start = [0] * buffer.ndim
    start[axis] = offset
    return lax.dynamic_update_slice(buffer, piece, start)


def grow(pieces, axes, factor):
    return [
        jnp.zeros(p.shape[:ax] + (p.shape[ax] * factor,) + p.shape[ax + 1 :], p.dtype)
        for p, ax in zip(pieces, axes)
    ]


def halves(pieces, axes, second):
    out = []
    for p, ax in zip(pieces, axes):
        n = p.shape[ax] // 2
        out.append(lax.slice_in_dim(p, n if second else 0, 2 * n if second else n, axis=ax))
    return out


def pair_stage(stacks, axes, coord):
    other = lax.ppermute(stacks, "fsdp", fsdp_pairs("z", 1))
    outs = []
    for mine, theirs, buffer, ax in zip(stacks, other, grow(stacks, axes, 2), axes):
        n = mine.shape[ax]
        buffer = put(buffer, mine, ax, coord * n)
        outs.append(put(buffer, theirs, ax, (1 - coord) * n))
    return outs


def ring_stage(stacks, axes, kind, coord):
    from_left = lax.ppermute(stacks, "fsdp", fsdp_pairs(kind, 1))
    from_right = lax.ppermute(stacks, "fsdp", fsdp_pairs(kind, -1))
    split = stacks[0].shape[axes[0]] > 1
    if split:
        far_left = lax.ppermute(halves(from_left, axes, False), "fsdp", fsdp_pairs(kind, 1))
        far_right = lax.ppermute(halves(from_right, axes, True), "fsdp", fsdp_pairs(kind, -1))
    else:
        far_left = lax.ppermute(from_left, "fsdp", fsdp_pairs(kind, 1))
    outs = []
    for i, (buffer, ax) in enumerate(zip(grow(stacks, axes, 4), axes)):
        n = stacks[i].shape[ax]
        buffer = put(buffer, stacks[i], ax, coord * n)
        buffer = put(buffer, from_right[i], ax, ((coord + 1) % 4) * n)
        buffer = put(buffer, from_left[i], ax, ((coord + 3) % 4) * n)
        buffer = put(buffer, far_left[i], ax, ((coord + 2) % 4) * n)
        if split:
            buffer = put(buffer, far_right[i], ax, ((coord + 2) % 4) * n + n // 2)
        outs.append(buffer)
    return outs


def torus_gather(route_a, axes_a, route_b, axes_b):
    coord = fsdp_coords()
    route_a = ring_stage(route_a, axes_a, "y", coord["y"])
    route_b = ring_stage(route_b, axes_b, "x", coord["x"])
    both = pair_stage(route_a + route_b, axes_a + axes_b, coord["z"])
    route_a, route_b = both[: len(route_a)], both[len(route_a) :]
    return ring_stage(route_a, axes_a, "x", coord["x"]), ring_stage(route_b, axes_b, "y", coord["y"])


def hp_dot(left, right, spec):
    return jnp.einsum(spec, left, right, precision=highest, preferred_element_type=jnp.float32)


def per_device(
    tokens,
    cotangent,
    segments,
    adapter_id,
    w_qkv,
    w_out,
    w_gateup,
    w_down,
    gain_attn,
    gain_ffn,
    gain_sub,
    lambda_head,
    a_in,
    b_qkv,
    b_gateup,
    a_out,
    a_down,
    b_rows,
):
    tok_count = lax.axis_size("tok")
    fsdp_count = lax.axis_size("fsdp")
    me_tok = lax.axis_index("tok")
    seqs, local_len, _ = tokens.shape
    length = local_len * tok_count
    qw_here = w_qkv.shape[2]
    ff_here = w_gateup.shape[2]
    heads_here = qw_here // VALUE_DIM
    lambda_here = lax.dynamic_slice_in_dim(lambda_head, me_tok * heads_here, heads_here)
    positions = jnp.arange(length)
    offsets = adapter_id * RANK
    fsdp_rows = w_qkv.shape[1]
    groups_per_adapter = RANK // b_qkv.shape[1]

    a_in_tok = tok_gather(a_in)
    b_rows_tok = tok_gather(b_rows)
    small = [a_in_tok, b_rows_tok, b_qkv, b_gateup, a_out, a_down]
    small_flat = jnp.concatenate([p.reshape(-1, COLS) for p in small])
    (g_qkv, g_out, g_down, g_small), (g_gateup,) = torus_gather(
        [w_qkv[:, None], w_out[None], w_down[None], small_flat[None]],
        [1, 0, 0, 0],
        [w_gateup[:, None]],
        [1],
    )
    w_qkv_full = g_qkv.reshape(3, D, qw_here)
    w_out_full = jnp.moveaxis(g_out, 0, 1).reshape(qw_here, D)
    w_down_full = jnp.moveaxis(g_down, 0, 1).reshape(ff_here, D)
    w_gateup_perm = jnp.transpose(
        g_gateup.reshape(2, 4, 2, 4, D // fsdp_count, ff_here), (0, 3, 2, 1, 4, 5)
    ).reshape(2, D, ff_here)
    unpacked = []
    start = 0
    for p in small:
        rows = p.size // COLS
        unpacked.append(g_small[:, start : start + rows].reshape((fsdp_count,) + p.shape))
        start += rows
    (g_ain, g_brows, g_bqkv, g_bgateup, g_aout, g_adown) = unpacked
    a_in_full = jnp.transpose(g_ain, (2, 0, 1, 3, 4)).reshape(5, D, COLS)
    b_rows_full = jnp.transpose(g_brows, (2, 3, 0, 1, 4)).reshape(2, COLS, D)

    def to_yzx(values):
        lead = values.shape[:-1]
        split = values.reshape(lead + (4, 2, 4, D // fsdp_count))
        n = len(lead)
        order = tuple(range(n)) + (n + 2, n + 1, n, n + 3)
        return jnp.transpose(split, order).reshape(values.shape)

    def from_yzx(values):
        lead = values.shape[:-1]
        split = values.reshape(lead + (4, 2, 4, D // fsdp_count))
        n = len(lead)
        order = tuple(range(n)) + (n + 2, n + 1, n, n + 3)
        return jnp.transpose(split, order).reshape(values.shape)

    def pick_cols(values, axis):
        return jnp.stack(
            [lax.dynamic_slice_in_dim(values, offsets[s], RANK, axis) for s in range(seqs)]
        )

    def pick_groups(values):
        return jnp.stack(
            [
                lax.dynamic_slice_in_dim(values, adapter_id[s] * groups_per_adapter, groups_per_adapter, 0)
                for s in range(seqs)
            ]
        )

    a_in_sel = pick_cols(a_in_full, 2)
    b_rows_sel = pick_cols(b_rows_full, 1)
    b_qkv_sel = jnp.moveaxis(pick_groups(g_bqkv), 1, 2).reshape(seqs, 3, RANK, qw_here)
    b_gateup_sel = jnp.moveaxis(pick_groups(g_bgateup), 1, 2).reshape(seqs, 2, RANK, ff_here)
    a_out_sel = jnp.moveaxis(pick_groups(g_aout), 1, 2).reshape(seqs, qw_here, RANK)
    a_down_sel = jnp.moveaxis(pick_groups(g_adown), 1, 2).reshape(seqs, ff_here, RANK)

    def gather_rows(values):
        full = tok_gather(values, 1)
        return full.reshape(seqs, length, values.shape[-1])

    def scatter_rows(values):
        return tok_scatter(values.reshape(seqs, tok_count, local_len, values.shape[-1]), 1)

    def column_forward(rows_full, weight, down_sel, up_sel, rows_for_weight=None):
        if rows_for_weight is None:
            rows_for_weight = rows_full
        lowrank = jnp.einsum("std,sdr->str", rows_full, down_sel, preferred_element_type=jnp.float32)
        linear = jnp.einsum("std,de->ste", rows_for_weight, weight, preferred_element_type=jnp.float32)
        return linear + adapter_scale * hp_dot(lowrank, up_sel.astype(jnp.float32), "str,sre->ste"), lowrank

    def row_forward(rows_here, weight, down_sel, up_sel):
        lowrank = jnp.einsum("std,sdr->str", rows_here, down_sel, preferred_element_type=jnp.float32)
        main_part = jnp.einsum("std,de->ste", rows_here, weight, preferred_element_type=jnp.float32)
        total = main_part + adapter_scale * hp_dot(lowrank, up_sel.astype(jnp.float32), "str,sre->ste")
        return scatter_rows(total), lowrank

    inputs_rows = tokens.astype(jnp.float32)
    allowed = (segments[:, :, None] == segments[:, None, :]) & (
        positions[:, None] >= positions[None, :]
    )[None]
    grad_ffn_full = gather_rows(cotangent)
    normed_rows, norm_attn_pull = jax.vjp(partial(rows_norm, gain_vector=gain_attn), inputs_rows)
    normed_full = gather_rows(normed_rows.astype(jnp.bfloat16))
    proj_lin = []
    proj_low = []
    for p in range(3):
        lin, lowr = column_forward(normed_full, w_qkv_full[p], a_in_sel[:, p], b_qkv_sel[:, p])
        proj_lin.append(lin)
        proj_low.append(lowr)
    rotate = partial(rotary_heads, positions=positions, head_dim=HEAD_DIM)
    query_rot, query_pull = jax.vjp(rotate, proj_lin[0])
    key_rot, key_pull = jax.vjp(rotate, proj_lin[1])
    query_in = query_rot.astype(jnp.bfloat16).reshape(seqs, length, heads_here, 2, HEAD_DIM)
    key_in = key_rot.astype(jnp.bfloat16).reshape(seqs, length, heads_here, 2, HEAD_DIM)
    value_in = proj_lin[2].astype(jnp.bfloat16).reshape(seqs, length, heads_here, VALUE_DIM)
    heads_out, log_total = jax.vmap(attend, in_axes=(0, 0, 0, 0, None))(
        query_in, key_in, value_in, allowed, lambda_here
    )
    mixed_float, head_pull = jax.vjp(partial(head_norm, gain_vector=gain_sub), heads_out)
    mixed_rows = mixed_float.reshape(seqs, length, qw_here).astype(jnp.bfloat16)
    attn_rows, out_low = row_forward(mixed_rows, w_out_full, a_out_sel, b_rows_sel[:, 0])
    hidden = inputs_rows + attn_rows
    normed_ffn, norm_ffn_pull = jax.vjp(partial(rows_norm, gain_vector=gain_ffn), hidden)
    ffn_full = gather_rows(normed_ffn.astype(jnp.bfloat16))
    gate_lin, gate_low = column_forward(ffn_full, w_gateup_perm[0], a_in_sel[:, 3], b_gateup_sel[:, 0])
    up_lin, up_low = column_forward(ffn_full, w_gateup_perm[1], a_in_sel[:, 4], b_gateup_sel[:, 1])
    product_float, swiglu_pull = jax.vjp(swiglu, gate_lin, up_lin)
    product = product_float.astype(jnp.bfloat16)
    ffn_rows, down_low = row_forward(product, w_down_full, a_down_sel, b_rows_sel[:, 1])
    output = (hidden + ffn_rows).astype(jnp.bfloat16)
    row_lows = tok_sum(jnp.stack([out_low, down_low]))

    tangent = cotangent.astype(jnp.float32)

    def row_backward(grad_full, rows_here, weight, down_sel, up_sel):
        grad_float = grad_full.astype(jnp.float32)
        grad_low = adapter_scale * hp_dot(grad_float, up_sel.astype(jnp.float32), "ste,sre->str")
        grad_down = hp_dot(rows_here.astype(jnp.float32), grad_low, "std,str->sdr")
        grad_inputs = jnp.einsum(
            "ste,de->std", grad_full, weight, preferred_element_type=jnp.float32
        ) + hp_dot(grad_low, down_sel.astype(jnp.float32), "str,sdr->std")
        return grad_inputs, grad_down

    def column_backward(rows_full, entries, weight_order=None):
        running = None
        grad_lows = []
        grads_up = []
        for grad_rows, weight, down_sel, up_sel, lowrank in entries:
            grad_float = grad_rows.astype(jnp.float32)
            grad_low = adapter_scale * hp_dot(grad_float, up_sel.astype(jnp.float32), "ste,sre->str")
            grads_up.append(adapter_scale * hp_dot(lowrank, grad_float, "str,ste->sre"))
            grad_lows.append(grad_low)
            main_term = jnp.einsum("ste,de->std", grad_rows, weight, preferred_element_type=jnp.float32)
            if weight_order is not None:
                main_term = weight_order(main_term)
            term = main_term + hp_dot(grad_low, down_sel.astype(jnp.float32), "str,sdr->std")
            running = term if running is None else running + term
        return scatter_rows(running), grad_lows, grads_up

    def mine_of(values, axis):
        shape = values.shape
        split = values.reshape(
            shape[:axis] + (fsdp_count, tok_count, D // (fsdp_count * tok_count)) + shape[axis + 1 :]
        )
        return lax.dynamic_index_in_dim(split, me_tok, axis + 1, keepdims=False)

    grad_product, grad_a_down = row_backward(
        grad_ffn_full, product, w_down_full, a_down_sel, b_rows_sel[:, 1]
    )
    grad_gate, grad_up = swiglu_pull(grad_product)
    grad_ffn_rows, ffn_grad_lows, ffn_grads_up = column_backward(
        ffn_full,
        (
            (grad_gate.astype(jnp.bfloat16), w_gateup_perm[0], a_in_sel[:, 3], b_gateup_sel[:, 0], gate_low),
            (grad_up.astype(jnp.bfloat16), w_gateup_perm[1], a_in_sel[:, 4], b_gateup_sel[:, 1], up_low),
        ),
    )
    grad_hidden = tangent + norm_ffn_pull(grad_ffn_rows)[0]
    grad_attn_full = gather_rows(grad_hidden.astype(jnp.bfloat16))
    grad_mixed, grad_a_out = row_backward(
        grad_attn_full, mixed_rows, w_out_full, a_out_sel, b_rows_sel[:, 0]
    )
    grad_heads = head_pull(grad_mixed.reshape(seqs, length, heads_here, VALUE_DIM))[0].astype(
        jnp.bfloat16
    )
    grad_query_rot, grad_key_rot, grad_values = jax.vmap(
        attend_back, in_axes=(0, 0, 0, 0, None, 0, 0)
    )(query_in, key_in, value_in, allowed, lambda_here, log_total, grad_heads)
    grad_query = query_pull(grad_query_rot.reshape(seqs, length, qw_here))[0].astype(jnp.bfloat16)
    grad_key = key_pull(grad_key_rot.reshape(seqs, length, qw_here))[0].astype(jnp.bfloat16)
    grad_attn_rows, attn_grad_lows, attn_grads_up = column_backward(
        normed_full,
        (
            (grad_query, w_qkv_full[0], a_in_sel[:, 0], b_qkv_sel[:, 0], proj_low[0]),
            (grad_key, w_qkv_full[1], a_in_sel[:, 1], b_qkv_sel[:, 1], proj_low[1]),
            (grad_values.reshape(seqs, length, qw_here), w_qkv_full[2], a_in_sel[:, 2], b_qkv_sel[:, 2], proj_low[2]),
        ),
    )
    grad_tokens = grad_hidden + norm_attn_pull(grad_attn_rows)[0]

    grad_lows = tok_sum(jnp.stack(attn_grad_lows + ffn_grad_lows))
    onehot = (
        jnp.arange(COLS)[None, None, :] == offsets[:, None, None] + jnp.arange(RANK)[None, :, None]
    ).astype(jnp.float32)
    wide_lows = hp_dot(grad_lows, onehot, "pstr,src->pstc")
    dense_a_in = jnp.concatenate(
        [
            hp_dot(normed_full.astype(jnp.float32), wide_lows[:3], "std,pstc->pdc"),
            hp_dot(ffn_full.astype(jnp.float32), wide_lows[3:], "std,pstc->pdc"),
        ]
    )
    a_in_mine = lax.dynamic_index_in_dim(
        dense_a_in.reshape(5, fsdp_count, tok_count, RANK, COLS), me_tok, 2, keepdims=False
    )
    wide_row_lows = hp_dot(row_lows, onehot, "qstr,src->qstc")
    dense_b_rows = adapter_scale * hp_dot(
        wide_row_lows,
        jnp.stack([grad_attn_full, grad_ffn_full]).astype(jnp.float32),
        "qstc,qstd->qcd",
    )
    b_rows_mine = lax.dynamic_index_in_dim(
        dense_b_rows.reshape(2, COLS, fsdp_count, tok_count, RANK), me_tok, 3, keepdims=False
    )
    def reduce_to_owners(parts, kind):
        rows = [p.size // (fsdp_count * COLS) for p in parts]
        packed = jnp.concatenate(
            [p.reshape(fsdp_count, r, COLS) for p, r in zip(parts, rows)], axis=1
        ).astype(kind)
        total = lax.all_to_all(packed, "fsdp", 0, 0, tiled=False).astype(jnp.float32).sum(0)
        out = []
        start = 0
        for p, r in zip(parts, rows):
            out.append(total[start : start + r].reshape(p.shape[1:]))
            start += r
        return out

    per = COLS // fsdp_count
    dense_b_gateup = hp_dot(onehot, jnp.stack(ffn_grads_up, 1), "src,spre->pce")
    dense_a_down = hp_dot(grad_a_down, onehot, "sdr,src->dc")
    b_gateup_block, a_down_block = reduce_to_owners(
        [
            jnp.moveaxis(dense_b_gateup.reshape(2, fsdp_count, per, ff_here), 1, 0),
            jnp.moveaxis(dense_a_down.reshape(ff_here, fsdp_count, per), 1, 0),
        ],
        jnp.bfloat16,
    )
    dense_b_qkv = hp_dot(onehot, jnp.stack(attn_grads_up, 1), "src,spre->pce")
    dense_a_out = hp_dot(grad_a_out, onehot, "sdr,src->dc")
    b_qkv_block, a_out_block = reduce_to_owners(
        [
            jnp.moveaxis(dense_b_qkv.reshape(3, fsdp_count, per, qw_here), 1, 0),
            jnp.moveaxis(dense_a_out.reshape(qw_here, fsdp_count, per), 1, 0),
        ],
        jnp.bfloat16,
    )
    a_in_block, b_rows_block = reduce_to_owners(
        [jnp.moveaxis(a_in_mine, 1, 0), jnp.moveaxis(b_rows_mine, 2, 0)], jnp.bfloat16
    )

    return (
        output,
        grad_tokens,
        a_in_block,
        b_qkv_block,
        b_gateup_block,
        a_out_block,
        a_down_block,
        b_rows_block,
    )


def solution(mesh):
    return jax.shard_map(
        per_device,
        mesh=mesh,
        in_specs=(
            P("fsdp", "tok", None),
            P("fsdp", "tok", None),
            P("fsdp", None),
            P("fsdp"),
            P(None, "fsdp", "tok"),
            P("tok", "fsdp"),
            P(None, "fsdp", "tok"),
            P("tok", "fsdp"),
            P(),
            P(),
            P(),
            P(),
            P(None, ("fsdp", "tok"), None),
            P(None, "fsdp", "tok"),
            P(None, "fsdp", "tok"),
            P("tok", "fsdp"),
            P("tok", "fsdp"),
            P(None, None, ("fsdp", "tok")),
        ),
        out_specs=(
            P("fsdp", "tok", None),
            P("fsdp", "tok", None),
            P(None, ("fsdp", "tok"), None),
            P(None, "fsdp", "tok"),
            P(None, "fsdp", "tok"),
            P("tok", "fsdp"),
            P("tok", "fsdp"),
            P(None, None, ("fsdp", "tok")),
        ),
        check_vma=False,
    )
```

```python
from functools import partial

import jax
import jax.numpy as jnp
from jax import lax
from jax.sharding import PartitionSpec as P

D = 2048
HEAD_DIM = 128
VALUE_DIM = 256
RANK = 16
COLS = 128


highest = lax.Precision.HIGHEST
negative = -1e30
adapter_scale = 2.0
lambda_init = 0.2
rotary_base = 10000.0
row_epsilon = 1e-06
head_epsilon = 1e-05


def rows_norm(values, gain_vector):
    return (
        values
        * lax.rsqrt(jnp.mean(values * values, axis=-1, keepdims=True) + row_epsilon)
        * gain_vector
    )


def head_norm(values, gain_vector):
    scaled = values * lax.rsqrt(jnp.mean(values * values, axis=-1, keepdims=True) + head_epsilon)
    return scaled * gain_vector * (1.0 - lambda_init)


def rotary_heads(values, positions, head_dim):
    lead = values.shape[:-1]
    groups = values.reshape(lead + (-1, head_dim))
    half_dim = head_dim // 2
    frequency = rotary_base ** (-jnp.arange(half_dim, dtype=jnp.float32) / half_dim)
    angles = positions.astype(jnp.float32)[:, None] * frequency[None, :]
    cosine = jnp.cos(angles)[:, None, :]
    sine_part = jnp.sin(angles)[:, None, :]
    first_half = groups[..., :half_dim]
    second = groups[..., half_dim:]
    turned = jnp.concatenate(
        [first_half * cosine - second * sine_part, second * cosine + first_half * sine_part],
        axis=-1,
    )
    return turned.reshape(values.shape)


def swiglu(gate_rows, up_rows):
    return gate_rows * jax.nn.sigmoid(gate_rows) * up_rows


def attention_scores(query_in, key_in, allowed):
    raw_scores = jnp.einsum(
        "qhmd,khmd->hmqk", query_in, key_in, preferred_element_type=jnp.float32
    ) * query_in.shape[-1] ** (-0.5)
    return jnp.where(allowed[None, None], raw_scores, negative)


def attend(query_in, key_in, value_in, allowed, lambda_here):
    scores = attention_scores(query_in, key_in, allowed)
    row_max = jnp.max(scores, axis=-1, keepdims=True)
    log_total = row_max + jnp.log(jnp.sum(jnp.exp(scores - row_max), axis=-1, keepdims=True))
    soft_max = jnp.exp(scores - log_total)
    differ = (soft_max[:, 0] - lambda_here[:, None, None] * soft_max[:, 1]).astype(jnp.bfloat16)
    heads_out = jnp.einsum("hqk,khd->qhd", differ, value_in, preferred_element_type=jnp.float32)
    return (heads_out, log_total)


def attend_back(query_in, key_in, value_in, allowed, lambda_here, log_total, grad_heads):
    scale = query_in.shape[-1] ** (-0.5)
    scores = attention_scores(query_in, key_in, allowed)
    soft_max = jnp.exp(scores - log_total)
    differ = (soft_max[:, 0] - lambda_here[:, None, None] * soft_max[:, 1]).astype(jnp.bfloat16)
    grad_values = jnp.einsum("hqk,qhd->khd", differ, grad_heads, preferred_element_type=jnp.float32)
    grad_differ = jnp.einsum(
        "qhd,khd->hqk", grad_heads, value_in, preferred_element_type=jnp.float32
    )
    grad_soft = jnp.stack([grad_differ, -lambda_here[:, None, None] * grad_differ], axis=1)
    grad_scores = (
        soft_max * (grad_soft - jnp.sum(grad_soft * soft_max, axis=-1, keepdims=True))
    ).astype(jnp.bfloat16)
    grad_query = (
        jnp.einsum("hmqk,khmd->qhmd", grad_scores, key_in, preferred_element_type=jnp.float32)
        * scale
    )
    grad_key = (
        jnp.einsum("hmqk,qhmd->khmd", grad_scores, query_in, preferred_element_type=jnp.float32)
        * scale
    )
    return (grad_query, grad_key, grad_values.astype(jnp.bfloat16))


def xor_pairs(count, bit):
    return [(i, i ^ bit) for i in range(count)]


def tok_gather(values, axis=0):
    count = lax.axis_size("tok")
    me = lax.axis_index("tok")
    far = lax.ppermute(values, "tok", xor_pairs(count, 2))
    pair = jnp.where(
        (me & 2) == 0, jnp.stack([values, far], axis), jnp.stack([far, values], axis)
    )
    near = lax.ppermute(pair, "tok", xor_pairs(count, 1))
    full = jnp.where(
        (me & 1) == 0, jnp.stack([pair, near], axis + 1), jnp.stack([near, pair], axis + 1)
    )
    return full.reshape(values.shape[:axis] + (count,) + values.shape[axis:])


def tok_scatter(blocks, axis=0):
    count = lax.axis_size("tok")
    me = lax.axis_index("tok")
    core = me & 1
    half = (me >> 1) & 1
    split = blocks.reshape(blocks.shape[:axis] + (2, 2) + blocks.shape[axis + 1 :])
    mine = lax.dynamic_index_in_dim(split, core, axis + 1, keepdims=False)
    theirs = lax.dynamic_index_in_dim(split, 1 - core, axis + 1, keepdims=False)
    chip_sum = mine + lax.ppermute(theirs, "tok", xor_pairs(count, 1))
    keep = lax.dynamic_index_in_dim(chip_sum, half, axis, keepdims=False)
    send = lax.dynamic_index_in_dim(chip_sum, 1 - half, axis, keepdims=False)
    got = lax.ppermute(send.astype(jnp.bfloat16), "tok", xor_pairs(count, 2))
    return keep + got.astype(keep.dtype)


def tok_sum(values):
    count = lax.axis_size("tok")
    chip_sum = values + lax.ppermute(values, "tok", xor_pairs(count, 1))
    return chip_sum + lax.ppermute(chip_sum, "tok", xor_pairs(count, 2))


def fsdp_coords():
    me = lax.axis_index("fsdp")
    return {"x": me // 8, "z": (me // 4) % 2, "y": me % 4}


def fsdp_pairs(kind, step):
    pairs = []
    for x in range(4):
        for z in range(2):
            for y in range(4):
                if kind == "z":
                    target = (x * 2 + 1 - z) * 4 + y
                elif kind == "x":
                    target = (((x + step) % 4) * 2 + z) * 4 + y
                else:
                    target = (x * 2 + z) * 4 + (y + step) % 4
                pairs.append(((x * 2 + z) * 4 + y, target))
    return pairs


def put(buffer, piece, axis, offset):
    start = [0] * buffer.ndim
    start[axis] = offset
    return lax.dynamic_update_slice(buffer, piece, start)


def grow(pieces, axes, factor):
    return [
        jnp.zeros(p.shape[:ax] + (p.shape[ax] * factor,) + p.shape[ax + 1 :], p.dtype)
        for p, ax in zip(pieces, axes)
    ]


def halves(pieces, axes, second):
    out = []
    for p, ax in zip(pieces, axes):
        n = p.shape[ax] // 2
        out.append(lax.slice_in_dim(p, n if second else 0, 2 * n if second else n, axis=ax))
    return out


def pair_stage(stacks, axes, coord):
    other = lax.ppermute(stacks, "fsdp", fsdp_pairs("z", 1))
    outs = []
    for mine, theirs, buffer, ax in zip(stacks, other, grow(stacks, axes, 2), axes):
        n = mine.shape[ax]
        buffer = put(buffer, mine, ax, coord * n)
        outs.append(put(buffer, theirs, ax, (1 - coord) * n))
    return outs


def ring_stage(stacks, axes, kind, coord):
    from_left = lax.ppermute(stacks, "fsdp", fsdp_pairs(kind, 1))
    from_right = lax.ppermute(stacks, "fsdp", fsdp_pairs(kind, -1))
    split = stacks[0].shape[axes[0]] > 1
    if split:
        far_left = lax.ppermute(halves(from_left, axes, False), "fsdp", fsdp_pairs(kind, 1))
        far_right = lax.ppermute(halves(from_right, axes, True), "fsdp", fsdp_pairs(kind, -1))
    else:
        far_left = lax.ppermute(from_left, "fsdp", fsdp_pairs(kind, 1))
    outs = []
    for i, (buffer, ax) in enumerate(zip(grow(stacks, axes, 4), axes)):
        n = stacks[i].shape[ax]
        buffer = put(buffer, stacks[i], ax, coord * n)
        buffer = put(buffer, from_right[i], ax, ((coord + 1) % 4) * n)
        buffer = put(buffer, from_left[i], ax, ((coord + 3) % 4) * n)
        buffer = put(buffer, far_left[i], ax, ((coord + 2) % 4) * n)
        if split:
            buffer = put(buffer, far_right[i], ax, ((coord + 2) % 4) * n + n // 2)
        outs.append(buffer)
    return outs


def torus_gather(route_a, axes_a, route_b, axes_b):
    coord = fsdp_coords()
    route_a = ring_stage(route_a, axes_a, "y", coord["y"])
    route_b = ring_stage(route_b, axes_b, "x", coord["x"])
    both = pair_stage(route_a + route_b, axes_a + axes_b, coord["z"])
    route_a, route_b = both[: len(route_a)], both[len(route_a) :]
    return ring_stage(route_a, axes_a, "x", coord["x"]), ring_stage(route_b, axes_b, "y", coord["y"])


def hp_dot(left, right, spec):
    return jnp.einsum(spec, left, right, precision=highest, preferred_element_type=jnp.float32)


def per_device(
    tokens,
    cotangent,
    segments,
    adapter_id,
    w_qkv,
    w_out,
    w_gateup,
    w_down,
    gain_attn,
    gain_ffn,
    gain_sub,
    lambda_head,
    a_in,
    b_qkv,
    b_gateup,
    a_out,
    a_down,
    b_rows,
):
    tok_count = lax.axis_size("tok")
    fsdp_count = lax.axis_size("fsdp")
    me_tok = lax.axis_index("tok")
    seqs, local_len, _ = tokens.shape
    length = local_len * tok_count
    qw_here = w_qkv.shape[2]
    ff_here = w_gateup.shape[2]
    heads_here = qw_here // VALUE_DIM
    lambda_here = lax.dynamic_slice_in_dim(lambda_head, me_tok * heads_here, heads_here)
    positions = jnp.arange(length)
    offsets = adapter_id * RANK
    fsdp_rows = w_qkv.shape[1]
    groups_per_adapter = RANK // b_qkv.shape[1]

    a_in_tok = tok_gather(a_in)
    b_rows_tok = tok_gather(b_rows)
    small = [a_in_tok, b_rows_tok, b_qkv, b_gateup, a_out, a_down]
    small_flat = jnp.concatenate([p.reshape(-1, COLS) for p in small])
    (g_qkv, g_out, g_down, g_small), (g_gateup,) = torus_gather(
        [w_qkv[:, None], w_out[None], w_down[None], small_flat[None]],
        [1, 0, 0, 0],
        [w_gateup[:, None]],
        [1],
    )
    w_qkv_full = g_qkv.reshape(3, D, qw_here)
    w_out_full = jnp.moveaxis(g_out, 0, 1).reshape(qw_here, D)
    w_down_full = jnp.moveaxis(g_down, 0, 1).reshape(ff_here, D)
    w_gateup_perm = jnp.transpose(
        g_gateup.reshape(2, 4, 2, 4, D // fsdp_count, ff_here), (0, 3, 2, 1, 4, 5)
    ).reshape(2, D, ff_here)
    unpacked = []
    start = 0
    for p in small:
        rows = p.size // COLS
        unpacked.append(g_small[:, start : start + rows].reshape((fsdp_count,) + p.shape))
        start += rows
    (g_ain, g_brows, g_bqkv, g_bgateup, g_aout, g_adown) = unpacked
    a_in_full = jnp.transpose(g_ain, (2, 0, 1, 3, 4)).reshape(5, D, COLS)
    b_rows_full = jnp.transpose(g_brows, (2, 3, 0, 1, 4)).reshape(2, COLS, D)

    def to_yzx(values):
        lead = values.shape[:-1]
        split = values.reshape(lead + (4, 2, 4, D // fsdp_count))
        n = len(lead)
        order = tuple(range(n)) + (n + 2, n + 1, n, n + 3)
        return jnp.transpose(split, order).reshape(values.shape)

    def from_yzx(values):
        lead = values.shape[:-1]
        split = values.reshape(lead + (4, 2, 4, D // fsdp_count))
        n = len(lead)
        order = tuple(range(n)) + (n + 2, n + 1, n, n + 3)
        return jnp.transpose(split, order).reshape(values.shape)

    def pick_cols(values, axis):
        return jnp.stack(
            [lax.dynamic_slice_in_dim(values, offsets[s], RANK, axis) for s in range(seqs)]
        )

    def pick_groups(values):
        return jnp.stack(
            [
                lax.dynamic_slice_in_dim(values, adapter_id[s] * groups_per_adapter, groups_per_adapter, 0)
                for s in range(seqs)
            ]
        )

    a_in_sel = pick_cols(a_in_full, 2)
    b_rows_sel = pick_cols(b_rows_full, 1)
    b_qkv_sel = jnp.moveaxis(pick_groups(g_bqkv), 1, 2).reshape(seqs, 3, RANK, qw_here)
    b_gateup_sel = jnp.moveaxis(pick_groups(g_bgateup), 1, 2).reshape(seqs, 2, RANK, ff_here)
    a_out_sel = jnp.moveaxis(pick_groups(g_aout), 1, 2).reshape(seqs, qw_here, RANK)
    a_down_sel = jnp.moveaxis(pick_groups(g_adown), 1, 2).reshape(seqs, ff_here, RANK)

    def gather_rows(values):
        full = tok_gather(values, 1)
        return full.reshape(seqs, length, values.shape[-1])

    def scatter_rows(values):
        return tok_scatter(values.reshape(seqs, tok_count, local_len, values.shape[-1]), 1)

    def column_forward(rows_full, weight, down_sel, up_sel, rows_for_weight=None):
        if rows_for_weight is None:
            rows_for_weight = rows_full
        lowrank = jnp.einsum("std,sdr->str", rows_full, down_sel, preferred_element_type=jnp.float32)
        linear = jnp.einsum("std,de->ste", rows_for_weight, weight, preferred_element_type=jnp.float32)
        return linear + adapter_scale * hp_dot(lowrank, up_sel.astype(jnp.float32), "str,sre->ste"), lowrank

    def row_forward(rows_here, weight, down_sel, up_sel):
        lowrank = jnp.einsum("std,sdr->str", rows_here, down_sel, preferred_element_type=jnp.float32)
        main_part = jnp.einsum("std,de->ste", rows_here, weight, preferred_element_type=jnp.float32)
        total = main_part + adapter_scale * hp_dot(lowrank, up_sel.astype(jnp.float32), "str,sre->ste")
        return scatter_rows(total), lowrank

    inputs_rows = tokens.astype(jnp.float32)
    allowed = (segments[:, :, None] == segments[:, None, :]) & (
        positions[:, None] >= positions[None, :]
    )[None]
    grad_ffn_full = gather_rows(cotangent)
    normed_rows, norm_attn_pull = jax.vjp(partial(rows_norm, gain_vector=gain_attn), inputs_rows)
    normed_full = gather_rows(normed_rows.astype(jnp.bfloat16))
    proj_lin = []
    proj_low = []
    for p in range(3):
        lin, lowr = column_forward(normed_full, w_qkv_full[p], a_in_sel[:, p], b_qkv_sel[:, p])
        proj_lin.append(lin)
        proj_low.append(lowr)
    rotate = partial(rotary_heads, positions=positions, head_dim=HEAD_DIM)
    query_rot, query_pull = jax.vjp(rotate, proj_lin[0])
    key_rot, key_pull = jax.vjp(rotate, proj_lin[1])
    query_in = query_rot.astype(jnp.bfloat16).reshape(seqs, length, heads_here, 2, HEAD_DIM)
    key_in = key_rot.astype(jnp.bfloat16).reshape(seqs, length, heads_here, 2, HEAD_DIM)
    value_in = proj_lin[2].astype(jnp.bfloat16).reshape(seqs, length, heads_here, VALUE_DIM)
    heads_out, log_total = jax.vmap(attend, in_axes=(0, 0, 0, 0, None))(
        query_in, key_in, value_in, allowed, lambda_here
    )
    mixed_float, head_pull = jax.vjp(partial(head_norm, gain_vector=gain_sub), heads_out)
    mixed_rows = mixed_float.reshape(seqs, length, qw_here).astype(jnp.bfloat16)
    attn_rows, out_low = row_forward(mixed_rows, w_out_full, a_out_sel, b_rows_sel[:, 0])
    hidden = inputs_rows + attn_rows
    normed_ffn, norm_ffn_pull = jax.vjp(partial(rows_norm, gain_vector=gain_ffn), hidden)
    ffn_full = gather_rows(normed_ffn.astype(jnp.bfloat16))
    gate_lin, gate_low = column_forward(ffn_full, w_gateup_perm[0], a_in_sel[:, 3], b_gateup_sel[:, 0])
    up_lin, up_low = column_forward(ffn_full, w_gateup_perm[1], a_in_sel[:, 4], b_gateup_sel[:, 1])
    product_float, swiglu_pull = jax.vjp(swiglu, gate_lin, up_lin)
    product = product_float.astype(jnp.bfloat16)
    ffn_rows, down_low = row_forward(product, w_down_full, a_down_sel, b_rows_sel[:, 1])
    output = (hidden + ffn_rows).astype(jnp.bfloat16)
    row_lows = tok_sum(jnp.stack([out_low, down_low]))

    tangent = cotangent.astype(jnp.float32)

    def row_backward(grad_full, rows_here, weight, down_sel, up_sel):
        grad_float = grad_full.astype(jnp.float32)
        grad_low = adapter_scale * hp_dot(grad_float, up_sel.astype(jnp.float32), "ste,sre->str")
        grad_down = hp_dot(rows_here.astype(jnp.float32), grad_low, "std,str->sdr")
        grad_inputs = jnp.einsum(
            "ste,de->std", grad_full, weight, preferred_element_type=jnp.float32
        ) + hp_dot(grad_low, down_sel.astype(jnp.float32), "str,sdr->std")
        return grad_inputs, grad_down

    def column_backward(rows_full, entries, weight_order=None):
        running = None
        grad_lows = []
        grads_up = []
        for grad_rows, weight, down_sel, up_sel, lowrank in entries:
            grad_float = grad_rows.astype(jnp.float32)
            grad_low = adapter_scale * hp_dot(grad_float, up_sel.astype(jnp.float32), "ste,sre->str")
            grads_up.append(adapter_scale * hp_dot(lowrank, grad_float, "str,ste->sre"))
            grad_lows.append(grad_low)
            main_term = jnp.einsum("ste,de->std", grad_rows, weight, preferred_element_type=jnp.float32)
            if weight_order is not None:
                main_term = weight_order(main_term)
            term = main_term + hp_dot(grad_low, down_sel.astype(jnp.float32), "str,sdr->std")
            running = term if running is None else running + term
        return scatter_rows(running), grad_lows, grads_up

    def mine_of(values, axis):
        shape = values.shape
        split = values.reshape(
            shape[:axis] + (fsdp_count, tok_count, D // (fsdp_count * tok_count)) + shape[axis + 1 :]
        )
        return lax.dynamic_index_in_dim(split, me_tok, axis + 1, keepdims=False)

    grad_product, grad_a_down = row_backward(
        grad_ffn_full, product, w_down_full, a_down_sel, b_rows_sel[:, 1]
    )
    grad_gate, grad_up = swiglu_pull(grad_product)
    grad_ffn_rows, ffn_grad_lows, ffn_grads_up = column_backward(
        ffn_full,
        (
            (grad_gate.astype(jnp.bfloat16), w_gateup_perm[0], a_in_sel[:, 3], b_gateup_sel[:, 0], gate_low),
            (grad_up.astype(jnp.bfloat16), w_gateup_perm[1], a_in_sel[:, 4], b_gateup_sel[:, 1], up_low),
        ),
    )
    grad_hidden = tangent + norm_ffn_pull(grad_ffn_rows)[0]
    grad_attn_full = gather_rows(grad_hidden.astype(jnp.bfloat16))
    grad_mixed, grad_a_out = row_backward(
        grad_attn_full, mixed_rows, w_out_full, a_out_sel, b_rows_sel[:, 0]
    )
    grad_heads = head_pull(grad_mixed.reshape(seqs, length, heads_here, VALUE_DIM))[0].astype(
        jnp.bfloat16
    )
    grad_query_rot, grad_key_rot, grad_values = jax.vmap(
        attend_back, in_axes=(0, 0, 0, 0, None, 0, 0)
    )(query_in, key_in, value_in, allowed, lambda_here, log_total, grad_heads)
    grad_query = query_pull(grad_query_rot.reshape(seqs, length, qw_here))[0].astype(jnp.bfloat16)
    grad_key = key_pull(grad_key_rot.reshape(seqs, length, qw_here))[0].astype(jnp.bfloat16)
    grad_attn_rows, attn_grad_lows, attn_grads_up = column_backward(
        normed_full,
        (
            (grad_query, w_qkv_full[0], a_in_sel[:, 0], b_qkv_sel[:, 0], proj_low[0]),
            (grad_key, w_qkv_full[1], a_in_sel[:, 1], b_qkv_sel[:, 1], proj_low[1]),
            (grad_values.reshape(seqs, length, qw_here), w_qkv_full[2], a_in_sel[:, 2], b_qkv_sel[:, 2], proj_low[2]),
        ),
    )
    grad_tokens = grad_hidden + norm_attn_pull(grad_attn_rows)[0]

    grad_lows = tok_sum(jnp.stack(attn_grad_lows + ffn_grad_lows))
    onehot = (
        jnp.arange(COLS)[None, None, :] == offsets[:, None, None] + jnp.arange(RANK)[None, :, None]
    ).astype(jnp.float32)
    wide_lows = hp_dot(grad_lows, onehot, "pstr,src->pstc")
    dense_a_in = jnp.concatenate(
        [
            hp_dot(normed_full.astype(jnp.float32), wide_lows[:3], "std,pstc->pdc"),
            hp_dot(ffn_full.astype(jnp.float32), wide_lows[3:], "std,pstc->pdc"),
        ]
    )
    a_in_mine = lax.dynamic_index_in_dim(
        dense_a_in.reshape(5, fsdp_count, tok_count, RANK, COLS), me_tok, 2, keepdims=False
    )
    wide_row_lows = hp_dot(row_lows, onehot, "qstr,src->qstc")
    dense_b_rows = adapter_scale * hp_dot(
        wide_row_lows,
        jnp.stack([grad_attn_full, grad_ffn_full]).astype(jnp.float32),
        "qstc,qstd->qcd",
    )
    b_rows_mine = lax.dynamic_index_in_dim(
        dense_b_rows.reshape(2, COLS, fsdp_count, tok_count, RANK), me_tok, 3, keepdims=False
    )
    def reduce_to_owners(parts, kind):
        rows = [p.size // (fsdp_count * COLS) for p in parts]
        packed = jnp.concatenate(
            [p.reshape(fsdp_count, r, COLS) for p, r in zip(parts, rows)], axis=1
        ).astype(kind)
        total = lax.all_to_all(packed, "fsdp", 0, 0, tiled=False).astype(jnp.float32).sum(0)
        out = []
        start = 0
        for p, r in zip(parts, rows):
            out.append(total[start : start + r].reshape(p.shape[1:]))
            start += r
        return out

    per = COLS // fsdp_count
    dense_b_gateup = hp_dot(onehot, jnp.stack(ffn_grads_up, 1), "src,spre->pce")
    dense_a_down = hp_dot(grad_a_down, onehot, "sdr,src->dc")
    b_gateup_block, a_down_block = reduce_to_owners(
        [
            jnp.moveaxis(dense_b_gateup.reshape(2, fsdp_count, per, ff_here), 1, 0),
            jnp.moveaxis(dense_a_down.reshape(ff_here, fsdp_count, per), 1, 0),
        ],
        jnp.bfloat16,
    )
    dense_b_qkv = hp_dot(onehot, jnp.stack(attn_grads_up, 1), "src,spre->pce")
    dense_a_out = hp_dot(grad_a_out, onehot, "sdr,src->dc")
    b_qkv_block, a_out_block, a_in_block, b_rows_block = reduce_to_owners(
        [
            jnp.moveaxis(dense_b_qkv.reshape(3, fsdp_count, per, qw_here), 1, 0),
            jnp.moveaxis(dense_a_out.reshape(qw_here, fsdp_count, per), 1, 0),
            jnp.moveaxis(a_in_mine, 1, 0),
            jnp.moveaxis(b_rows_mine, 2, 0),
        ],
        jnp.bfloat16,
    )

    return (
        output,
        grad_tokens,
        a_in_block,
        b_qkv_block,
        b_gateup_block,
        a_out_block,
        a_down_block,
        b_rows_block,
    )


def solution(mesh):
    return jax.shard_map(
        per_device,
        mesh=mesh,
        in_specs=(
            P("fsdp", "tok", None),
            P("fsdp", "tok", None),
            P("fsdp", None),
            P("fsdp"),
            P(None, "fsdp", "tok"),
            P("tok", "fsdp"),
            P(None, "fsdp", "tok"),
            P("tok", "fsdp"),
            P(),
            P(),
            P(),
            P(),
            P(None, ("fsdp", "tok"), None),
            P(None, "fsdp", "tok"),
            P(None, "fsdp", "tok"),
            P("tok", "fsdp"),
            P("tok", "fsdp"),
            P(None, None, ("fsdp", "tok")),
        ),
        out_specs=(
            P("fsdp", "tok", None),
            P("fsdp", "tok", None),
            P(None, ("fsdp", "tok"), None),
            P(None, "fsdp", "tok"),
            P(None, "fsdp", "tok"),
            P("tok", "fsdp"),
            P("tok", "fsdp"),
            P(None, None, ("fsdp", "tok")),
        ),
        check_vma=False,
    )
```
